32 devices in a mesh: bins: 16 (over z, y, x), params: 2 (over core).
Axes of the slice: x: 2, y: 2, z: 4, core: 2. Of those that a mesh axis runs over, the one named last changes fastest.
Arguments:
- event_bins: int32 [49152], P('bins'), may hold values from 0 to 16383, as said below
- event_weights: bfloat16 [49152, 3072], P('bins', 'params'), may hold values from -6 to 6
- nominal: bfloat16 [49152], P('bins'), may hold values from 0.5 to 2
- background: float32 [16384], P('bins'), may hold values from 1 to 10
- observed: float32 [16384], P('bins'), may hold values from 1 to 100
Outputs:
- hessian: float32 [3072, 3072], P(('params', 'bins'))
The draws below stay inside these ranges and needn't reach their ends.
Inputs may be any that keep to these rules, and one draw needn't show every extreme that they name: `event_bins`: each index of bins holds 3072 consecutive events in ascending bin order. The owner of bin b is b // 1024; each owner's bins receive from one index of bins between 96 and 288 of its events, and in every draw every index of bins has some owner that receives exactly 288 of its events.
All inputs are finite; a program needn't handle non-finite values.
Results may differ from the reference program's by a relative error of at most 0.0016.
Values may be sent and summed in bfloat16 or wider, within the bound.
A program may use at most 128 MiB of HBM per device.

```python
import math
import jax
import jax.numpy as jnp
from jax import lax

P_SIZE = 3072
BINS_DEV = 1024
E_DEV = 3072
PG = 1536
NB = 16384
EVENTS = 49152
COLS = 3072
N_BINS = 16
N_PARAMS = 2


def draw_event_bins(key, part):
    base_count = E_DEV // N_BINS
    swing_most = base_count // 2

    def one_source(subkey):
        key_swing, key_perm, key_bins = jax.random.split(subkey, 3)
        swing = jax.random.randint(key_swing, (N_BINS // 2,), -swing_most, swing_most + 1)
        swing = swing.at[0].set(swing_most)
        profile = jnp.concatenate([base_count + swing, base_count - swing])
        counts = profile[jax.random.permutation(key_perm, N_BINS)]
        bounds = jnp.cumsum(counts)
        ordinal = jnp.arange(E_DEV, dtype=jnp.int32)
        target = jnp.sum((bounds[None, :] <= ordinal[:, None]).astype(jnp.int32), axis=1)
        inside = jax.random.randint(key_bins, (E_DEV,), 0, BINS_DEV)
        return jnp.sort(target * BINS_DEV + inside).astype(jnp.int32)
    source_keys = jax.random.split(jax.random.fold_in(key, 7), N_BINS)
    return jax.vmap(one_source)(source_keys).reshape(-1)


def steps_of(stream_key, shape, pieces, least, top_value):
    factor_of = 1.0
    for dim, parts in pieces:
        draws = jax.random.uniform(jax.random.fold_in(jax.random.fold_in(stream_key, 6), dim), (parts,), jnp.float32, least / len(pieces), top_value / len(pieces))
        factor_of = factor_of * jnp.repeat(jnp.exp(draws), shape[dim] // parts).reshape((-1,) + (1,) * (len(shape) - 1 - dim))
    return factor_of


def gaussian(key, extent, scale, limit, cuts=(), kind=jnp.bfloat16):
    result = scale * jax.random.normal(key, extent, jnp.float32)
    if cuts:
        result = result * steps_of(key, extent, cuts, -0.22, 0.18)
    return jnp.clip(result, -limit, limit).astype(kind)


def setup_inputs(seed: int = 0) -> dict:
    keys = jax.random.split(jax.random.key(seed), 6)
    return {
        "event_bins": draw_event_bins(jax.random.fold_in(keys[5], 71), 0),
        "event_weights": gaussian(keys[1], (EVENTS, P_SIZE), 1.0, 6.0, ((0, 16), (1, 2))),
        "nominal": jnp.clip(jnp.exp(math.log(2.0) - 1.3862944 * jax.random.uniform(keys[2], (EVENTS,), jnp.float32) ** steps_of(keys[2], (EVENTS,), ((0, 16),), -0.2, 0.2)), 0.5, 2.0).astype(jnp.bfloat16),
        "background": jnp.clip(jnp.exp(math.log(10.0) - 2.3025851 * jax.random.uniform(keys[3], (NB,), jnp.float32) ** steps_of(keys[3], (NB,), ((0, 16),), -0.2, 0.2)), 1.0, 10.0),
        "observed": jnp.clip(jnp.exp(math.log(100.0) - 4.6051702 * jax.random.uniform(keys[4], (NB,), jnp.float32) ** steps_of(keys[4], (NB,), ((0, 16),), -0.2, 0.2)), 1.0, 100.0),
    }


def reference(event_bins, event_weights, nominal, background, observed):
    bins_split = event_bins.reshape(N_BINS, E_DEV)
    weights_split = event_weights.reshape(N_BINS, E_DEV, P_SIZE)

    def add_source(carry, stacked):
        source_bins, source_weights = stacked
        part_sum = jax.ops.segment_sum(source_weights.astype(jnp.float32), source_bins, num_segments=NB)
        return carry + part_sum, None

    histogram, _ = lax.scan(add_source, jnp.zeros((NB, P_SIZE), jnp.float32), (bins_split, weights_split))
    templates = histogram.astype(jnp.bfloat16)
    nominal_sum = jax.ops.segment_sum(nominal.astype(jnp.float32), event_bins, num_segments=NB)
    yields = background + nominal_sum
    curvature = observed / (yields * yields)
    weighted = (curvature[:, None] * templates.astype(jnp.float32)).astype(jnp.bfloat16)
    dims = (((0,), (0,)), ((), ()))
    full = lax.dot_general(weighted, templates, dims, preferred_element_type=jnp.float32)
    full = full * (1.0 / NB)
    blocks = full.reshape(N_PARAMS, PG, N_PARAMS, PG)
    groups = jnp.arange(N_PARAMS, dtype=jnp.int32)
    tiles = []
    for offset in range(N_PARAMS // 2 + 1):
        tiles.append(blocks[groups, :, (groups + offset) % N_PARAMS, :])
    stacked_tiles = jnp.stack(tiles, axis=2)
    return stacked_tiles.reshape(P_SIZE, COLS)
```

```python
import functools
import math

import jax
import jax.numpy as jnp
from jax import lax
from jax.experimental import pallas as pl
from jax.experimental.pallas import tpu as pltpu
from jax.sharding import PartitionSpec as P

ALIGN = 8
MESH = pl.DeviceIdType.MESH


def from_behind(value, axis, steps):
    count = lax.axis_size(axis)
    pairs = [(source, (source + steps) % count) for source in range(count)]
    return lax.ppermute(value, axis, pairs)


def pack_kernel(owners, slot, first, width, starts_ref, rows_ref, out_ref, held, in_sems, out_sems):
    def fetch(o):
        start = pl.multiple_of(starts_ref[o] * ALIGN, ALIGN)
        return pltpu.make_async_copy(
            rows_ref.at[pl.ds(start, slot), pl.ds(first, width)], held.at[o], in_sems.at[o]
        )

    def store(o):
        return pltpu.make_async_copy(held.at[o], out_ref.at[o], out_sems.at[o])

    @pl.loop(0, owners)
    def _(o):
        fetch(o).start()

    @pl.loop(0, owners)
    def _(o):
        fetch(o).wait()
        store(o).start()

    @pl.loop(0, owners)
    def _(o):
        store(o).wait()


def pack(starts, rows, slot, first, width):
    owners = starts.shape[0]
    return pl.pallas_call(
        functools.partial(pack_kernel, owners, slot, first, width),
        out_shape=jax.ShapeDtypeStruct((owners, slot, width), rows.dtype),
        in_specs=[
            pl.BlockSpec(memory_space=pltpu.SMEM),
            pl.BlockSpec(memory_space=pl.ANY),
        ],
        out_specs=pl.BlockSpec(memory_space=pl.ANY),
        scratch_shapes=[
            pltpu.VMEM((owners, slot, width), rows.dtype),
            pltpu.SemaphoreType.DMA((owners,)),
            pltpu.SemaphoreType.DMA((owners,)),
        ],
        compiler_params=pltpu.CompilerParams(vmem_limit_bytes=32 << 20),
        cost_estimate=pl.CostEstimate(
            flops=0, bytes_accessed=4 * owners * slot * width, transcendentals=0
        ),
        name="pack",
    )(starts, rows)


def meta_kernel(bins_dev, starts_ref, table_ref, out_ref):
    owners, _, slot = out_ref.shape
    events = table_ref.shape[1]
    table = table_ref[...]

    @pl.loop(0, owners)
    def _(o):
        start = starts_ref[o] * ALIGN
        turned = pltpu.roll(table, lax.rem(events - start, events), axis=1)[:, :slot]
        bins = turned[0:1] - (o * bins_dev).astype(jnp.float32)
        inside = (bins >= 0) & (bins < bins_dev)
        out_ref[o, 0:1, :] = jnp.where(inside, bins, -1.0)
        out_ref[o, 1:2, :] = turned[1:2]


def pack_meta(starts, table, slot, bins_dev):
    owners = starts.shape[0]
    return pl.pallas_call(
        functools.partial(meta_kernel, bins_dev),
        out_shape=jax.ShapeDtypeStruct((owners, 2, slot), jnp.float32),
        in_specs=[
            pl.BlockSpec(memory_space=pltpu.SMEM),
            pl.BlockSpec(memory_space=pltpu.VMEM),
        ],
        out_specs=pl.BlockSpec(memory_space=pltpu.VMEM),
        name="pack_meta",
    )(starts, table)


def hist_kernel(chunk, tile, local_ref, rows_ref, out_ref, hot):
    bins, total = hot.shape

    @pl.when(pl.program_id(0) == 0)
    def _():
        ids = lax.broadcasted_iota(jnp.int32, (bins, chunk), 0)

        @pl.loop(0, total // chunk)
        def _(k):
            part = pl.ds(pl.multiple_of(k * chunk, chunk), chunk)
            hot[:, part] = (ids == local_ref[:, part]).astype(jnp.bfloat16)

    @pl.loop(0, bins // tile)
    def _(m):
        part = pl.ds(pl.multiple_of(m * tile, tile), tile)
        out_ref[part, :] = jnp.dot(
            hot[part, :], rows_ref[...], preferred_element_type=jnp.float32
        ).astype(out_ref.dtype)


def histogram_of(local, rows, bins, block, dtype):
    total, width = rows.shape
    return pl.pallas_call(
        functools.partial(hist_kernel, math.gcd(total, 128), math.gcd(bins, 256)),
        grid=(width // block,),
        out_shape=jax.ShapeDtypeStruct((bins, width), dtype),
        in_specs=[
            pl.BlockSpec((1, total), lambda j: (0, 0)),
            pl.BlockSpec((total, block), lambda j: (0, j)),
        ],
        out_specs=pl.BlockSpec((bins, block), lambda j: (0, j)),
        scratch_shapes=[pltpu.VMEM((bins, total), jnp.bfloat16)],
        compiler_params=pltpu.CompilerParams(
            vmem_limit_bytes=40 << 20, dimension_semantics=("arbitrary",)
        ),
        cost_estimate=pl.CostEstimate(
            flops=2 * bins * total * width, bytes_accessed=2 * total * width, transcendentals=0
        ),
        name="histogram",
    )(local, rows)


def reduce_kernel(
    piece, shares_ref, out_ref, own, got_near, sums, got_far,
    own_sem, near_send, near_recv, far_send, far_recv,
):
    far, near, rows, _ = shares_ref.shape
    me = lax.axis_index("bins")
    f, n = me // near, lax.rem(me, near)

    def near_peer(d):
        return lax.rem(n + d, near)

    def far_peer(d):
        return lax.rem(f + d, far)

    barrier = pltpu.get_barrier_semaphore()
    for d in range(1, near):
        pl.semaphore_signal(
            barrier, inc=1, device_id={"bins": f * near + near_peer(d)}, device_id_type=MESH
        )
    for d in range(1, far):
        pl.semaphore_signal(
            barrier, inc=1, device_id={"bins": far_peer(d) * near + n}, device_id_type=MESH
        )
    pl.semaphore_wait(barrier, near + far - 2)

    def part_of(c):
        return pl.ds(pl.multiple_of(c * piece, piece), piece)

    def near_copy(d, c):
        return pltpu.make_async_remote_copy(
            src_ref=shares_ref.at[:, near_peer(d), part_of(c), :],
            dst_ref=got_near.at[d - 1, :, part_of(c), :],
            send_sem=near_send.at[d - 1, c],
            recv_sem=near_recv.at[d - 1, c],
            device_id={"bins": f * near + near_peer(d)},
            device_id_type=MESH,
        )

    def far_copy(d, c):
        return pltpu.make_async_remote_copy(
            src_ref=sums.at[far_peer(d), part_of(c), :],
            dst_ref=got_far.at[d - 1, part_of(c), :],
            send_sem=far_send.at[d - 1, c],
            recv_sem=far_recv.at[d - 1, c],
            device_id={"bins": far_peer(d) * near + n},
            device_id_type=MESH,
        )

    own_copy = pltpu.make_async_copy(shares_ref.at[:, n], own, own_sem)
    own_copy.start()
    pieces = rows // piece

    @pl.loop(0, pieces)
    def _(c):
        for d in range(1, near):
            near_copy(d, c).start()

    own_copy.wait()

    @pl.loop(0, pieces)
    def _(c):
        part = part_of(c)
        for d in range(1, near):
            near_copy(d, c).wait_recv()

        @pl.loop(0, far)
        def _(k):
            total = own[k, part, :].astype(jnp.float32)
            for d in range(1, near):
                total += got_near[d - 1, k, part, :].astype(jnp.float32)
            sums[k, part, :] = total

        for d in range(1, far):
            far_copy(d, c).start()

    @pl.loop(0, pieces)
    def _(c):
        part = part_of(c)
        for d in range(1, far):
            far_copy(d, c).wait_recv()
        total = sums[f, part, :]
        for d in range(1, far):
            total += got_far[d - 1, part, :]
        out_ref[part, :] = total
        for d in range(1, near):
            near_copy(d, c).wait_send()
        for d in range(1, far):
            far_copy(d, c).wait_send()


def reduce_shares(shares):
    owners, rows, cols = shares.shape
    near = math.isqrt(owners)
    while owners % near:
        near -= 1
    far = owners // near
    piece = 16 if rows % 16 == 0 else rows
    pieces = rows // piece
    return pl.pallas_call(
        functools.partial(reduce_kernel, piece),
        out_shape=jax.ShapeDtypeStruct((rows, cols), jnp.float32),
        in_specs=[pl.BlockSpec(memory_space=pl.ANY)],
        out_specs=pl.BlockSpec(memory_space=pltpu.VMEM),
        scratch_shapes=[
            pltpu.VMEM((far, rows, cols), shares.dtype),
            pltpu.VMEM((near - 1, far, rows, cols), shares.dtype),
            pltpu.VMEM((far, rows, cols), jnp.float32),
            pltpu.VMEM((far - 1, rows, cols), jnp.float32),
            pltpu.SemaphoreType.DMA,
            pltpu.SemaphoreType.DMA((near - 1, pieces)),
            pltpu.SemaphoreType.DMA((near - 1, pieces)),
            pltpu.SemaphoreType.DMA((far - 1, pieces)),
            pltpu.SemaphoreType.DMA((far - 1, pieces)),
        ],
        compiler_params=pltpu.CompilerParams(
            collective_id=1, has_side_effects=True, vmem_limit_bytes=40 << 20
        ),
        name="reduce_shares",
    )(shares.reshape(far, near, rows, cols))


def body(event_bins, event_weights, nominal, background, observed):
    owners = lax.axis_size("bins")
    groups_count = lax.axis_size("params")
    events = event_bins.shape[0]
    width_g = event_weights.shape[1]
    bins_dev = background.shape[0]
    capacity = 3 * events // (2 * owners)
    slot = -(-capacity // ALIGN) * ALIGN + ALIGN
    chunks = 2 if width_g % 512 == 0 else 1
    width = width_g // chunks
    block = math.gcd(width, 256)

    destination = event_bins // bins_dev
    targets = jnp.arange(owners, dtype=jnp.int32)
    before = jnp.sum((destination[None, :] < targets[:, None]).astype(jnp.int32), axis=1)
    starts = jnp.minimum(before // ALIGN, (events - slot) // ALIGN)

    table = jnp.stack([event_bins.astype(jnp.float32), nominal.astype(jnp.float32)])
    table = jnp.concatenate([table, jnp.zeros((6, events), jnp.float32)], axis=0)
    meta = pack_meta(starts, table, slot, bins_dev)
    got_meta = lax.all_to_all(meta, "bins", split_axis=0, concat_axis=0, tiled=True)
    local = got_meta[:, 0].astype(jnp.int32).reshape(1, owners * slot)
    got_nominal = got_meta[:, 1].astype(jnp.bfloat16).reshape(owners * slot, 1)
    got_nominal = jnp.broadcast_to(got_nominal, (owners * slot, 128))
    nominal_sum = histogram_of(local, got_nominal, bins_dev, 128, jnp.float32)[:, 0]
    yields = background + nominal_sum
    curvature = observed / (yields * yields)

    parts = []
    for c in range(chunks):
        packed = pack(starts, event_weights, slot, c * width, width)
        got = lax.all_to_all(packed, "bins", split_axis=0, concat_axis=0, tiled=True)
        got = got.reshape(owners * slot, width)
        parts.append(histogram_of(local, got, bins_dev, block, jnp.bfloat16))
    templates = jnp.concatenate(parts, axis=1)
    weighted = (curvature[:, None] * templates.astype(jnp.float32)).astype(jnp.bfloat16)
    pieces = [templates]
    for shift_by in range(1, groups_count // 2 + 1):
        shifted = [from_behind(part, "params", -shift_by) for part in parts]
        pieces.append(jnp.concatenate(shifted, axis=1))
    partners = jnp.concatenate(pieces, axis=1)
    dims = (((0,), (0,)), ((), ()))
    full = lax.dot_general(weighted, partners, dims, preferred_element_type=jnp.float32)
    full = full.astype(jnp.bfloat16)
    shares = full.reshape(owners, width_g // owners, full.shape[1])
    summed = reduce_shares(shares)
    return summed * (1.0 / (bins_dev * owners))


LANES = 128
TILE = 256


def shift(value, pairs):
    return lax.ppermute(value, "bins", pairs)


def xor_of(a, b, count):
    total, bit = 0, 1
    while bit < count:
        total = total + bit * lax.rem(a // bit + b // bit, 2)
        bit *= 2
    return total


def diagonal():
    rows = lax.broadcasted_iota(jnp.int32, (LANES, LANES), 0)
    return rows == lax.broadcasted_iota(jnp.int32, (LANES, LANES), 1)


def fold_kernel(sources, steps, received, last, info_ref, before_ref, ids_ref, *refs):
    rows_refs = refs[:sources]
    got = refs[sources : sources + 2 * received]
    outs = refs[sources + 2 * received : -1]
    acc = refs[-1]
    events = ids_ref.shape[1]
    block = outs[0].shape[0]
    tiles = block // TILE
    bounds = before_ref.shape[0] // sources

    @pl.when(info_ref[1] == 1)
    def _():
        @pl.loop(0, tiles)
        def _(k):
            index = (info_ref[0] * steps + pl.program_id(0)) * tiles + k
            bins = index * TILE + lax.broadcasted_iota(jnp.int32, (TILE, LANES), 0)

            def product(s, start):
                ids = ids_ref[s : s + 1, pl.ds(start, LANES)]
                hot = (bins == ids).astype(jnp.bfloat16)
                return jnp.dot(
                    hot, rows_refs[s][pl.ds(start, LANES), :], preferred_element_type=jnp.float32
                )

            total = jnp.zeros((TILE, LANES), jnp.float32)
            firsts = []
            for s in range(sources):
                low = before_ref[s * bounds + index]
                first = jnp.minimum(low // LANES * LANES, events - 2 * LANES)
                first = pl.multiple_of(first, LANES)
                firsts.append(first)
                total += product(s, first)
                total += product(s, pl.multiple_of(first + LANES, LANES))
            acc[...] = total
            for s in range(sources):
                high = before_ref[s * bounds + index + 1]
                rest = jnp.maximum(high - firsts[s] - 2 * LANES + LANES - 1, 0) // LANES
                begin = firsts[s] + 2 * LANES

                @pl.loop(0, rest)
                def _(e):
                    acc[...] += product(s, pl.multiple_of(begin + e * LANES, LANES))

            eye = diagonal()
            for h in range(TILE // LANES):
                line = k * (TILE // LANES) + h
                part = pl.ds(pl.multiple_of(line * LANES, LANES), LANES)
                value = acc[h * LANES : (h + 1) * LANES, :]
                for n in range(received):
                    scale = got[2 * n + 1][pl.ds(line, 1), :]
                    scale = jnp.sum(jnp.where(eye, scale, 0.0), axis=1, keepdims=True)
                    value += got[2 * n][part, :].astype(jnp.int32).astype(jnp.float32) * scale
                if last:
                    outs[0][part, :] = value.astype(outs[0].dtype)
                else:
                    most = jnp.max(jnp.abs(value), axis=1, keepdims=True)
                    wide = most * (2.0**23 + 1.0)
                    step = (wide + (most - wide)) * 2.0**-14
                    factor = jnp.where(most > 1e-30, 1.0 / step, 0.0)
                    coded = jnp.round(value * factor).astype(jnp.int32)
                    outs[0][part, :] = coded.astype(outs[0].dtype)
                    scale = jnp.where(eye, step, 0.0)
                    outs[1][pl.ds(line, 1), :] = jnp.sum(scale, axis=0, keepdims=True)


def fold(info, before, ids, rows, got, bins, last):
    sources, events = ids.shape
    block = 8 * LANES
    steps = bins // block
    smem = pl.BlockSpec(memory_space=pltpu.SMEM)
    values = pl.BlockSpec((block, LANES), lambda j: (j, 0))
    scales = pl.BlockSpec((8, LANES), lambda j: (j, 0))
    whole_rows = pl.BlockSpec((events, LANES), lambda j: (0, 0))
    flat = [part for pair in got for part in pair]
    if last:
        out_shape = [jax.ShapeDtypeStruct((bins, LANES), jnp.bfloat16)]
        out_specs = [values]
    else:
        out_shape = [
            jax.ShapeDtypeStruct((bins, LANES), jnp.int16),
            jax.ShapeDtypeStruct((bins // LANES, LANES), jnp.float32),
        ]
        out_specs = [values, scales]
    return pl.pallas_call(
        functools.partial(fold_kernel, sources, steps, len(got), last),
        grid=(steps,),
        out_shape=out_shape,
        in_specs=[smem, smem, pl.BlockSpec((sources, events), lambda j: (0, 0))]
        + [whole_rows] * sources
        + [values, scales] * len(got),
        out_specs=out_specs,
        scratch_shapes=[pltpu.VMEM((TILE, LANES), jnp.float32)],
        compiler_params=pltpu.CompilerParams(
            vmem_limit_bytes=24 << 20, dimension_semantics=("arbitrary",)
        ),
        cost_estimate=pl.CostEstimate(
            flops=bins * 2 * sources * 256 * LANES,
            bytes_accessed=2 * sources * events * LANES + 4 * bins * LANES,
            transcendentals=0,
        ),
        name="fold_last" if last else "fold",
    )(info, before, ids, *rows, *flat)


def curve_kernel(lows_ref, ids_ref, nominal_ref, background_ref, observed_ref, out_ref, acc):
    sources = ids_ref.shape[0]
    bounds = lows_ref.shape[0] // sources
    index = pl.program_id(0)
    first_bin = lows_ref[sources * (bounds - 1)]
    bins = first_bin + index * TILE + lax.broadcasted_iota(jnp.int32, (TILE, LANES), 0)
    acc[...] = jnp.zeros_like(acc)

    @pl.loop(0, sources)
    def _(s):
        low = lows_ref[s * (bounds - 1) + index]
        high = lows_ref[s * (bounds - 1) + index + 1]

        @pl.loop(low // LANES, (high + LANES - 1) // LANES)
        def _(b):
            part = pl.ds(pl.multiple_of(b * LANES, LANES), LANES)
            hit = bins == ids_ref[s, :, part]
            acc[...] += jnp.where(hit, nominal_ref[s, :, part], 0.0)

    yields = background_ref[...] + jnp.sum(acc[...], axis=1, keepdims=True)
    out_ref[...] = observed_ref[...] / (yields * yields)


def curvature_of(lows, first_bin, ids, nominal, background, observed):
    sources, events = ids.shape
    bins = background.shape[0]
    table = jnp.concatenate(
        [lows.reshape(-1), first_bin.reshape(1), jnp.zeros((sources - 1,), jnp.int32)]
    )
    column = pl.BlockSpec((TILE, 1), lambda j: (j, 0))
    whole = pl.BlockSpec((sources, 1, events), lambda j: (0, 0, 0))
    return pl.pallas_call(
        curve_kernel,
        grid=(bins // TILE,),
        out_shape=jax.ShapeDtypeStruct((bins, 1), jnp.float32),
        in_specs=[pl.BlockSpec(memory_space=pltpu.SMEM), whole, whole, column, column],
        out_specs=column,
        scratch_shapes=[pltpu.VMEM((TILE, LANES), jnp.float32)],
        compiler_params=pltpu.CompilerParams(
            vmem_limit_bytes=8 << 20, dimension_semantics=("arbitrary",)
        ),
        name="curvature",
    )(
        table,
        ids.reshape(sources, 1, events),
        nominal.reshape(sources, 1, events),
        background.reshape(bins, 1),
        observed.reshape(bins, 1),
    )


def weigh_kernel(near, chunks, piece, me_ref, curve_ref, *refs):
    out_ref = refs[-1]
    rows = lax.broadcasted_iota(jnp.int32, (piece, LANES), 0) + me_ref[0] * piece
    lanes = lax.broadcasted_iota(jnp.int32, (piece, LANES), 1)
    for d in range(near):
        total = 0.0
        for c in range(chunks):
            pick = (rows == lanes + c * LANES).astype(jnp.bfloat16)
            value = curve_ref[...] * refs[d * chunks + c][...].astype(jnp.float32)
            total += lax.dot_general(
                pick, value.astype(jnp.bfloat16), (((1,), (1,)), ((), ())),
                preferred_element_type=jnp.float32,
            )
        out_ref[d * piece : (d + 1) * piece, :] = total.astype(out_ref.dtype)


def weigh(me, curve, templates, near, chunks, piece):
    bins = curve.shape[0]
    tile = 512
    return pl.pallas_call(
        functools.partial(weigh_kernel, near, chunks, piece),
        grid=(bins // tile,),
        out_shape=jax.ShapeDtypeStruct((near * piece, bins), jnp.bfloat16),
        in_specs=[
            pl.BlockSpec(memory_space=pltpu.SMEM),
            pl.BlockSpec((tile, 1), lambda j: (j, 0)),
        ]
        + [pl.BlockSpec((tile, LANES), lambda j: (j, 0))] * (near * chunks),
        out_specs=pl.BlockSpec((near * piece, tile), lambda j: (0, j)),
        compiler_params=pltpu.CompilerParams(
            vmem_limit_bytes=24 << 20, dimension_semantics=("arbitrary",)
        ),
        name="weigh",
    )(me, curve, *templates)


def hessian_kernel(count, weighted_ref, *refs):
    pieces = refs[:count]
    full_ref, coded_ref, held, sems = refs[count:]
    bins = held.shape[0]
    depth = math.gcd(bins, 1024)

    def fetch(n):
        return pltpu.make_async_copy(
            pieces[n], held.at[:, n * LANES : (n + 1) * LANES], sems.at[n]
        )

    for n in range(count):
        fetch(n).start()
    for n in range(0, count, 2):
        fetch(n).wait()
        fetch(n + 1).wait()
        columns = slice(n * LANES, (n + 2) * LANES)
        total = jnp.dot(
            weighted_ref[...], held[:, columns], preferred_element_type=jnp.float32
        )
        full_ref[:, columns] = total
        coded_ref[:, columns] = total.astype(coded_ref.dtype)


def hessian_of(weighted, pieces):
    rows, bins = weighted.shape
    count = len(pieces)
    shape = (rows, count * LANES)
    return pl.pallas_call(
        functools.partial(hessian_kernel, count),
        out_shape=[
            jax.ShapeDtypeStruct(shape, jnp.float32),
            jax.ShapeDtypeStruct(shape, jnp.bfloat16),
        ],
        in_specs=[pl.BlockSpec(memory_space=pltpu.VMEM)]
        + [pl.BlockSpec(memory_space=pl.ANY)] * count,
        out_specs=[pl.BlockSpec(memory_space=pltpu.VMEM)] * 2,
        scratch_shapes=[
            pltpu.VMEM((bins, count * LANES), jnp.bfloat16),
            pltpu.SemaphoreType.DMA((count,)),
        ],
        compiler_params=pltpu.CompilerParams(vmem_limit_bytes=48 << 20),
        cost_estimate=pl.CostEstimate(
            flops=2 * rows * bins * count * LANES,
            bytes_accessed=2 * bins * count * LANES,
            transcendentals=0,
        ),
        name="hessian",
    )(weighted, *pieces)


def sum_kernel(near, far, piece, run, full_ref, coded_ref, out_ref, own, got, own_sem, sends, recvs):
    here = lax.axis_index("bins")
    z, me = here // near, lax.rem(here, near)
    columns = out_ref.shape[1]

    def peer(k):
        return lax.rem(z + k, far)

    barrier = pltpu.get_barrier_semaphore()
    for k in range(1, far):
        pl.semaphore_signal(
            barrier, inc=1, device_id={"bins": peer(k) * near + me}, device_id_type=MESH
        )
    pl.semaphore_wait(barrier, far - 1)

    def rows_for(target):
        return pl.ds(pl.multiple_of(xor_of(me, target, near) * piece, piece), piece)

    def copy(k):
        return pltpu.make_async_remote_copy(
            src_ref=coded_ref.at[rows_for(peer(k)), :],
            dst_ref=got.at[k - 1],
            send_sem=sends.at[k - 1],
            recv_sem=recvs.at[k - 1],
            device_id={"bins": peer(k) * near + me},
            device_id_type=MESH,
        )

    for k in range(1, far):
        copy(k).start()
    own_copy = pltpu.make_async_copy(full_ref.at[rows_for(z), :], own, own_sem)
    own_copy.start()
    own_copy.wait()
    for k in range(1, far):
        copy(k).wait_recv()
    for n in range(columns // run):
        group, d = n // near, n % near
        total = own[:, n * run : (n + 1) * run]
        for k in range(1, far):
            total += got[k - 1, :, n * run : (n + 1) * run].astype(jnp.float32)
        start = (group * near + xor_of(me, d, near)) * run
        out_ref[:, pl.ds(pl.multiple_of(start, LANES), run)] = total
    for k in range(1, far):
        copy(k).wait_send()


def sum_over_planes(full, coded, near, far, run):
    rows, columns = full.shape
    piece = rows // far
    return pl.pallas_call(
        functools.partial(sum_kernel, near, far, piece, run),
        out_shape=jax.ShapeDtypeStruct((piece, columns), jnp.float32),
        in_specs=[pl.BlockSpec(memory_space=pl.ANY)] * 2,
        out_specs=pl.BlockSpec(memory_space=pltpu.VMEM),
        scratch_shapes=[
            pltpu.VMEM((piece, columns), jnp.float32),
            pltpu.VMEM((far - 1, piece, columns), coded.dtype),
            pltpu.SemaphoreType.DMA,
            pltpu.SemaphoreType.DMA((far - 1,)),
            pltpu.SemaphoreType.DMA((far - 1,)),
        ],
        compiler_params=pltpu.CompilerParams(
            collective_id=2, has_side_effects=True, vmem_limit_bytes=16 << 20
        ),
        name="sum_over_planes",
    )(full, coded)


def body_by_parameters(event_bins, event_weights, nominal, background, observed):
    owners = lax.axis_size("bins")
    near = math.isqrt(owners)
    far = owners // near
    events = event_bins.shape[0]
    bins_dev = background.shape[0]
    width = event_weights.shape[1] // near
    chunks = width // LANES
    bins = near * bins_dev
    here = lax.axis_index("bins")
    z, me = here // near, lax.rem(here, near)
    planes = range(far)
    around = [[(s, s // near * near + (s % near ^ d)) for s in range(owners)] for d in range(near)]

    def spread(value):
        return [value] + [shift(value, around[d]) for d in range(1, near)]

    meta = jnp.concatenate([event_bins.astype(jnp.float32), nominal.astype(jnp.float32)])
    meta = jnp.stack(spread(meta.reshape(2, events)))
    local = jnp.stack(spread(jnp.stack([background, observed])))
    ids = meta[:, 0].astype(jnp.int32)
    marks = jnp.arange(far * bins // TILE + 1, dtype=jnp.int32) * TILE
    before = jnp.sum((ids[:, None, :] < marks[None, :, None]).astype(jnp.int32), axis=2)
    before = before.reshape(-1)

    def chunk_of(weights, c):
        parts = []
        for d in range(near):
            start = (me ^ d) * width + c * LANES
            part = lax.dynamic_slice(weights, (0, start), (events, LANES))
            parts.append(part if d == 0 else shift(part, around[d]))
        return parts

    def info(target):
        valid = (target >= 0) & (target < far)
        return jnp.stack([jnp.clip(target, 0, far - 1), valid.astype(jnp.int32)])

    def up(r):
        return [(p * near + m, (p + 1) * near + m) for p in planes if p < r for m in range(near)]

    def down(r):
        return [
            (p * near + m, (p - 1) * near + m) for p in planes if p >= far - r for m in range(near)
        ]

    def send(pair, pairs):
        return tuple(shift(part, pairs) for part in pair)

    rows_of = []
    weights = event_weights
    for c in range(chunks):
        rows_of.append(chunk_of(weights, c))
        weights, _ = lax.optimization_barrier((weights, rows_of[c][1:]))

    own = [None] * chunks
    for c in range(chunks):
        rows = rows_of[c]
        rising, falling = [], []
        for r in range(1, far):
            rising = [send(fold(info(z + far - r), before, ids, rows, rising, bins, False), up(r))]
            falling = [
                send(fold(info(z - far + r), before, ids, rows, falling, bins, False), down(r))
            ]
        own[c] = fold(info(z), before, ids, rows, rising + falling, bins, True)[0]

    metas = [meta] + [
        shift(meta, [(s, (s + k * near) % owners) for s in range(owners)]) for k in range(1, far)
    ]
    metas = jnp.concatenate(metas)
    all_ids = metas[:, 0].astype(jnp.int32)
    first_bin = z * bins
    near_marks = first_bin + jnp.arange(bins // TILE + 1, dtype=jnp.int32) * TILE
    lows = jnp.sum((all_ids[:, None, :] < near_marks[None, :, None]).astype(jnp.int32), axis=2)
    places = jnp.arange(near, dtype=jnp.int32)
    match = (places[None, :] ^ me) == places[:, None]
    local = jnp.sum(jnp.where(match[:, :, None, None], local[None], 0.0), axis=1)
    curve = curvature_of(
        lows, first_bin, all_ids, metas[:, 1], local[:, 0].reshape(-1), local[:, 1].reshape(-1)
    )

    mine = [spread(own[c]) for c in range(chunks)]
    mine = [mine[c][d] for d in range(near) for c in range(chunks)]
    theirs = [from_behind(part, "params", 1) for part in mine]
    weighted = weigh(
        me.reshape(1).astype(jnp.int32), curve, mine, near, chunks, width // far
    )
    full, coded = hessian_of(weighted, mine + theirs)
    summed = sum_over_planes(full, coded, near, far, width)
    return summed * (1.0 / (bins_dev * owners))


def splits_by_parameters(mesh, event_bins, event_weights, background):
    owners, groups = mesh.shape["bins"], mesh.shape["params"]
    near = math.isqrt(owners)
    events = event_bins.shape[0] // owners
    width = event_weights.shape[1] // groups // max(near, 1)
    bins_dev = background.shape[0] // owners
    return (
        groups == 2
        and near > 1
        and near * near == owners
        and near & (near - 1) == 0
        and width % LANES == 0
        and width % (16 * near) == 0
        and events % LANES == 0
        and events >= 2 * LANES
        and bins_dev % (8 * LANES) == 0
    )


def solution(mesh):
    in_specs = (P("bins"), P("bins", "params"), P("bins"), P("bins"), P("bins"))
    out_specs = P(("params", "bins"), None)

    def run(event_bins, event_weights, nominal, background, observed):
        fits = splits_by_parameters(mesh, event_bins, event_weights, background)
        chosen = body_by_parameters if fits else body
        mapped = jax.shard_map(
            chosen, mesh=mesh, in_specs=in_specs, out_specs=out_specs, check_vma=False
        )
        return mapped(event_bins, event_weights, nominal, background, observed)

    return run
```

```python
import functools
import math

import jax
import jax.numpy as jnp
from jax import lax
from jax.experimental import pallas as pl
from jax.experimental.pallas import tpu as pltpu
from jax.sharding import PartitionSpec as P

ALIGN = 8
MESH = pl.DeviceIdType.MESH


def from_behind(value, axis, steps):
    count = lax.axis_size(axis)
    pairs = [(source, (source + steps) % count) for source in range(count)]
    return lax.ppermute(value, axis, pairs)


def pack_kernel(owners, slot, first, width, starts_ref, rows_ref, out_ref, held, in_sems, out_sems):
    def fetch(o):
        start = pl.multiple_of(starts_ref[o] * ALIGN, ALIGN)
        return pltpu.make_async_copy(
            rows_ref.at[pl.ds(start, slot), pl.ds(first, width)], held.at[o], in_sems.at[o]
        )

    def store(o):
        return pltpu.make_async_copy(held.at[o], out_ref.at[o], out_sems.at[o])

    @pl.loop(0, owners)
    def _(o):
        fetch(o).start()

    @pl.loop(0, owners)
    def _(o):
        fetch(o).wait()
        store(o).start()

    @pl.loop(0, owners)
    def _(o):
        store(o).wait()


def pack(starts, rows, slot, first, width):
    owners = starts.shape[0]
    return pl.pallas_call(
        functools.partial(pack_kernel, owners, slot, first, width),
        out_shape=jax.ShapeDtypeStruct((owners, slot, width), rows.dtype),
        in_specs=[
            pl.BlockSpec(memory_space=pltpu.SMEM),
            pl.BlockSpec(memory_space=pl.ANY),
        ],
        out_specs=pl.BlockSpec(memory_space=pl.ANY),
        scratch_shapes=[
            pltpu.VMEM((owners, slot, width), rows.dtype),
            pltpu.SemaphoreType.DMA((owners,)),
            pltpu.SemaphoreType.DMA((owners,)),
        ],
        compiler_params=pltpu.CompilerParams(vmem_limit_bytes=32 << 20),
        cost_estimate=pl.CostEstimate(
            flops=0, bytes_accessed=4 * owners * slot * width, transcendentals=0
        ),
        name="pack",
    )(starts, rows)


def meta_kernel(bins_dev, starts_ref, table_ref, out_ref):
    owners, _, slot = out_ref.shape
    events = table_ref.shape[1]
    table = table_ref[...]

    @pl.loop(0, owners)
    def _(o):
        start = starts_ref[o] * ALIGN
        turned = pltpu.roll(table, lax.rem(events - start, events), axis=1)[:, :slot]
        bins = turned[0:1] - (o * bins_dev).astype(jnp.float32)
        inside = (bins >= 0) & (bins < bins_dev)
        out_ref[o, 0:1, :] = jnp.where(inside, bins, -1.0)
        out_ref[o, 1:2, :] = turned[1:2]


def pack_meta(starts, table, slot, bins_dev):
    owners = starts.shape[0]
    return pl.pallas_call(
        functools.partial(meta_kernel, bins_dev),
        out_shape=jax.ShapeDtypeStruct((owners, 2, slot), jnp.float32),
        in_specs=[
            pl.BlockSpec(memory_space=pltpu.SMEM),
            pl.BlockSpec(memory_space=pltpu.VMEM),
        ],
        out_specs=pl.BlockSpec(memory_space=pltpu.VMEM),
        name="pack_meta",
    )(starts, table)


def hist_kernel(chunk, tile, local_ref, rows_ref, out_ref, hot):
    bins, total = hot.shape

    @pl.when(pl.program_id(0) == 0)
    def _():
        ids = lax.broadcasted_iota(jnp.int32, (bins, chunk), 0)

        @pl.loop(0, total // chunk)
        def _(k):
            part = pl.ds(pl.multiple_of(k * chunk, chunk), chunk)
            hot[:, part] = (ids == local_ref[:, part]).astype(jnp.bfloat16)

    @pl.loop(0, bins // tile)
    def _(m):
        part = pl.ds(pl.multiple_of(m * tile, tile), tile)
        out_ref[part, :] = jnp.dot(
            hot[part, :], rows_ref[...], preferred_element_type=jnp.float32
        ).astype(out_ref.dtype)


def histogram_of(local, rows, bins, block, dtype):
    total, width = rows.shape
    return pl.pallas_call(
        functools.partial(hist_kernel, math.gcd(total, 128), math.gcd(bins, 256)),
        grid=(width // block,),
        out_shape=jax.ShapeDtypeStruct((bins, width), dtype),
        in_specs=[
            pl.BlockSpec((1, total), lambda j: (0, 0)),
            pl.BlockSpec((total, block), lambda j: (0, j)),
        ],
        out_specs=pl.BlockSpec((bins, block), lambda j: (0, j)),
        scratch_shapes=[pltpu.VMEM((bins, total), jnp.bfloat16)],
        compiler_params=pltpu.CompilerParams(
            vmem_limit_bytes=40 << 20, dimension_semantics=("arbitrary",)
        ),
        cost_estimate=pl.CostEstimate(
            flops=2 * bins * total * width, bytes_accessed=2 * total * width, transcendentals=0
        ),
        name="histogram",
    )(local, rows)


def reduce_kernel(
    piece, shares_ref, out_ref, own, got_near, sums, got_far,
    own_sem, near_send, near_recv, far_send, far_recv,
):
    far, near, rows, _ = shares_ref.shape
    me = lax.axis_index("bins")
    f, n = me // near, lax.rem(me, near)

    def near_peer(d):
        return lax.rem(n + d, near)

    def far_peer(d):
        return lax.rem(f + d, far)

    barrier = pltpu.get_barrier_semaphore()
    for d in range(1, near):
        pl.semaphore_signal(
            barrier, inc=1, device_id={"bins": f * near + near_peer(d)}, device_id_type=MESH
        )
    for d in range(1, far):
        pl.semaphore_signal(
            barrier, inc=1, device_id={"bins": far_peer(d) * near + n}, device_id_type=MESH
        )
    pl.semaphore_wait(barrier, near + far - 2)

    def part_of(c):
        return pl.ds(pl.multiple_of(c * piece, piece), piece)

    def near_copy(d, c):
        return pltpu.make_async_remote_copy(
            src_ref=shares_ref.at[:, near_peer(d), part_of(c), :],
            dst_ref=got_near.at[d - 1, :, part_of(c), :],
            send_sem=near_send.at[d - 1, c],
            recv_sem=near_recv.at[d - 1, c],
            device_id={"bins": f * near + near_peer(d)},
            device_id_type=MESH,
        )

    def far_copy(d, c):
        return pltpu.make_async_remote_copy(
            src_ref=sums.at[far_peer(d), part_of(c), :],
            dst_ref=got_far.at[d - 1, part_of(c), :],
            send_sem=far_send.at[d - 1, c],
            recv_sem=far_recv.at[d - 1, c],
            device_id={"bins": far_peer(d) * near + n},
            device_id_type=MESH,
        )

    own_copy = pltpu.make_async_copy(shares_ref.at[:, n], own, own_sem)
    own_copy.start()
    pieces = rows // piece

    @pl.loop(0, pieces)
    def _(c):
        for d in range(1, near):
            near_copy(d, c).start()

    own_copy.wait()

    @pl.loop(0, pieces)
    def _(c):
        part = part_of(c)
        for d in range(1, near):
            near_copy(d, c).wait_recv()

        @pl.loop(0, far)
        def _(k):
            total = own[k, part, :].astype(jnp.float32)
            for d in range(1, near):
                total += got_near[d - 1, k, part, :].astype(jnp.float32)
            sums[k, part, :] = total

        for d in range(1, far):
            far_copy(d, c).start()

    @pl.loop(0, pieces)
    def _(c):
        part = part_of(c)
        for d in range(1, far):
            far_copy(d, c).wait_recv()
        total = sums[f, part, :]
        for d in range(1, far):
            total += got_far[d - 1, part, :]
        out_ref[part, :] = total
        for d in range(1, near):
            near_copy(d, c).wait_send()
        for d in range(1, far):
            far_copy(d, c).wait_send()


def reduce_shares(shares):
    owners, rows, cols = shares.shape
    near = math.isqrt(owners)
    while owners % near:
        near -= 1
    far = owners // near
    piece = 16 if rows % 16 == 0 else rows
    pieces = rows // piece
    return pl.pallas_call(
        functools.partial(reduce_kernel, piece),
        out_shape=jax.ShapeDtypeStruct((rows, cols), jnp.float32),
        in_specs=[pl.BlockSpec(memory_space=pl.ANY)],
        out_specs=pl.BlockSpec(memory_space=pltpu.VMEM),
        scratch_shapes=[
            pltpu.VMEM((far, rows, cols), shares.dtype),
            pltpu.VMEM((near - 1, far, rows, cols), shares.dtype),
            pltpu.VMEM((far, rows, cols), jnp.float32),
            pltpu.VMEM((far - 1, rows, cols), jnp.float32),
            pltpu.SemaphoreType.DMA,
            pltpu.SemaphoreType.DMA((near - 1, pieces)),
            pltpu.SemaphoreType.DMA((near - 1, pieces)),
            pltpu.SemaphoreType.DMA((far - 1, pieces)),
            pltpu.SemaphoreType.DMA((far - 1, pieces)),
        ],
        compiler_params=pltpu.CompilerParams(
            collective_id=1, has_side_effects=True, vmem_limit_bytes=40 << 20
        ),
        name="reduce_shares",
    )(shares.reshape(far, near, rows, cols))


def body(event_bins, event_weights, nominal, background, observed):
    owners = lax.axis_size("bins")
    groups_count = lax.axis_size("params")
    events = event_bins.shape[0]
    width_g = event_weights.shape[1]
    bins_dev = background.shape[0]
    capacity = 3 * events // (2 * owners)
    slot = -(-capacity // ALIGN) * ALIGN + ALIGN
    chunks = 2 if width_g % 512 == 0 else 1
    width = width_g // chunks
    block = math.gcd(width, 256)

    destination = event_bins // bins_dev
    targets = jnp.arange(owners, dtype=jnp.int32)
    before = jnp.sum((destination[None, :] < targets[:, None]).astype(jnp.int32), axis=1)
    starts = jnp.minimum(before // ALIGN, (events - slot) // ALIGN)

    table = jnp.stack([event_bins.astype(jnp.float32), nominal.astype(jnp.float32)])
    table = jnp.concatenate([table, jnp.zeros((6, events), jnp.float32)], axis=0)
    meta = pack_meta(starts, table, slot, bins_dev)
    got_meta = lax.all_to_all(meta, "bins", split_axis=0, concat_axis=0, tiled=True)
    local = got_meta[:, 0].astype(jnp.int32).reshape(1, owners * slot)
    got_nominal = got_meta[:, 1].astype(jnp.bfloat16).reshape(owners * slot, 1)
    got_nominal = jnp.broadcast_to(got_nominal, (owners * slot, 128))
    nominal_sum = histogram_of(local, got_nominal, bins_dev, 128, jnp.float32)[:, 0]
    yields = background + nominal_sum
    curvature = observed / (yields * yields)

    parts = []
    for c in range(chunks):
        packed = pack(starts, event_weights, slot, c * width, width)
        got = lax.all_to_all(packed, "bins", split_axis=0, concat_axis=0, tiled=True)
        got = got.reshape(owners * slot, width)
        parts.append(histogram_of(local, got, bins_dev, block, jnp.bfloat16))
    templates = jnp.concatenate(parts, axis=1)
    weighted = (curvature[:, None] * templates.astype(jnp.float32)).astype(jnp.bfloat16)
    pieces = [templates]
    for shift_by in range(1, groups_count // 2 + 1):
        shifted = [from_behind(part, "params", -shift_by) for part in parts]
        pieces.append(jnp.concatenate(shifted, axis=1))
    partners = jnp.concatenate(pieces, axis=1)
    dims = (((0,), (0,)), ((), ()))
    full = lax.dot_general(weighted, partners, dims, preferred_element_type=jnp.float32)
    full = full.astype(jnp.bfloat16)
    shares = full.reshape(owners, width_g // owners, full.shape[1])
    summed = reduce_shares(shares)
    return summed * (1.0 / (bins_dev * owners))


LANES = 128
TILE = 256


def shift(value, pairs):
    return lax.ppermute(value, "bins", pairs)


def xor_of(a, b, count):
    total, bit = 0, 1
    while bit < count:
        total = total + bit * lax.rem(a // bit + b // bit, 2)
        bit *= 2
    return total


def diagonal():
    rows = lax.broadcasted_iota(jnp.int32, (LANES, LANES), 0)
    return rows == lax.broadcasted_iota(jnp.int32, (LANES, LANES), 1)


def slots_kernel(bins_dev, starts_ref, table_ref, out_ref):
    owners, sources, slot = out_ref.shape
    events = table_ref.shape[1]
    table = table_ref[...]

    @pl.loop(0, owners)
    def _(o):
        for s in range(sources):
            start = starts_ref[s * owners + o] * 16
            turned = pltpu.roll(table, lax.rem(events - start, events), axis=1)[s : s + 1, :slot]
            bins = turned - (o * bins_dev).astype(jnp.float32)
            inside = (bins >= 0) & (bins < bins_dev)
            out_ref[o, s : s + 1, :] = jnp.where(inside, bins, -1.0)


def slots_of(starts, ids, owners, slot, bins_dev):
    sources, events = ids.shape
    table = jnp.concatenate([ids, jnp.zeros((8 - sources, events), jnp.float32)])
    return pl.pallas_call(
        functools.partial(slots_kernel, bins_dev),
        out_shape=jax.ShapeDtypeStruct((owners, sources, slot), jnp.float32),
        in_specs=[
            pl.BlockSpec(memory_space=pltpu.SMEM),
            pl.BlockSpec(memory_space=pltpu.VMEM),
        ],
        out_specs=pl.BlockSpec(memory_space=pltpu.VMEM),
        name="slots",
    )(starts, table)


def chain_kernel(near, far, chunks, pieces, slot, starts_ref, local_ref, weights_ref, *refs):
    firsts = refs[:near]
    out_ref = refs[near]
    rows_refs = refs[near + 1 : near + 1 + chunks]
    (
        window, acc, own, send_q, send_s, got_q, got_s,
        row_sem, row_send, row_recv, q_send, q_recv, s_send, s_recv,
        own_sem, side_send, side_recv, pair_send, pair_recv,
    ) = refs[near + 1 + chunks :]
    owners = near * far
    here = lax.axis_index("bins")
    core = lax.axis_index("params")
    z, me = here // near, lax.rem(here, near)
    bins_dev = own.shape[1] // near
    width = chunks * LANES
    held = near // pieces
    size = held * bins_dev
    lines = size // LANES

    def side(d):
        return z * near + xor_of(me, d, near)

    def along(way):
        return (z + 1 - 2 * way) * near + me

    barrier = pltpu.get_barrier_semaphore()
    for d in range(1, near):
        pl.semaphore_signal(barrier, inc=1, device_id={"bins": side(d)}, device_id_type=MESH)
    pl.semaphore_signal(barrier, inc=1, device_id={"params": 1 - core}, device_id_type=MESH)

    @pl.when(z < far - 1)
    def _():
        pl.semaphore_signal(barrier, inc=1, device_id={"bins": along(0)}, device_id_type=MESH)

    @pl.when(z > 0)
    def _():
        pl.semaphore_signal(barrier, inc=1, device_id={"bins": along(1)}, device_id_type=MESH)

    inner = (z > 0).astype(jnp.int32) + (z < far - 1).astype(jnp.int32)
    pl.semaphore_wait(barrier, near + inner)

    def quarter(d, c):
        start = xor_of(me, d, near) * width + c * LANES
        return weights_ref.at[:, pl.ds(pl.multiple_of(start, LANES), LANES)]

    def row_copy(c, d):
        return pltpu.make_async_remote_copy(
            src_ref=quarter(d, c),
            dst_ref=rows_refs[c].at[d],
            send_sem=row_send.at[c, d],
            recv_sem=row_recv.at[c, d],
            device_id={"bins": side(d)},
            device_id_type=MESH,
        )

    def row_local(c, d):
        source = firsts[d] if c == 0 else quarter(d, c)
        return pltpu.make_async_copy(source, rows_refs[c].at[d], row_sem.at[c, d])

    for d in range(near):
        row_local(0, d).start()
    for c in range(1, chunks):
        row_local(c, 0).start()
        for d in range(1, near):
            row_copy(c, d).start()

    def chain_copies(way, c, r, p):
        return [
            pltpu.make_async_remote_copy(
                src_ref=source.at[way, c, r - 1, p],
                dst_ref=target.at[way, c, r - 1, p],
                send_sem=sent.at[way, c, r - 1, p],
                recv_sem=landed.at[way, c, r - 1, p],
                device_id={"bins": along(way)},
                device_id_type=MESH,
            )
            for source, target, sent, landed in (
                (send_q, got_q, q_send, q_recv), (send_s, got_s, s_send, s_recv)
            )
        ]

    def fold(c, plane, p, inputs, finish):
        @pl.loop(0, held)
        def _(i):
            owner = plane * near + p * held + i
            for s in range(near):
                start = starts_ref[s * owners + owner] * 16
                window[s * slot : (s + 1) * slot, :] = rows_refs[c][s, pl.ds(start, slot), :]

            @pl.loop(0, bins_dev // TILE)
            def _(k):
                bins = k * TILE + lax.broadcasted_iota(jnp.int32, (TILE, near * slot), 0)
                hot = (bins == local_ref[owner]).astype(jnp.bfloat16)
                acc[...] = jnp.dot(hot, window[...], preferred_element_type=jnp.float32)
                base = i * (bins_dev // LANES) + k * (TILE // LANES)
                eye = diagonal()
                for way, r, has in inputs:
                    @pl.when(has)
                    def _():
                        for h in range(TILE // LANES):
                            line = base + h
                            part = pl.ds(pl.multiple_of(line * LANES, LANES), LANES)
                            step = got_s[way, c, r - 1, p, pl.ds(line, 1), :]
                            step = jnp.sum(jnp.where(eye, step, 0.0), axis=1, keepdims=True)
                            coded = got_q[way, c, r - 1, p, part, :].astype(jnp.int32)
                            acc[h * LANES : (h + 1) * LANES, :] += (
                                coded.astype(jnp.float32) * step
                            )
                for h in range(TILE // LANES):
                    line = base + h
                    part = pl.ds(pl.multiple_of(line * LANES, LANES), LANES)
                    finish(acc[h * LANES : (h + 1) * LANES, :], line, part, eye)

    def wait_chain(way, c, r, p):
        for copy in chain_copies(way, c, r, p):
            copy.wait_recv()

    def rounds(c, first, last):
        @pl.loop(first, last)
        def _(r):
            @pl.loop(0, pieces)
            def _(p):
                for way in range(2):
                    step_in = z if way == 0 else far - 1 - z

                    @pl.when(step_in < r)
                    def _():
                        has = step_in > 0

                        @pl.when(has)
                        def _():
                            wait_chain(way, c, r - 1, p)

                        def code(value, line, part, eye):
                            most = jnp.max(jnp.abs(value), axis=1, keepdims=True)
                            wide = most * (2.0**23 + 1.0)
                            step = (wide + (most - wide)) * 2.0**-14
                            factor = jnp.where(most > 1e-30, 1.0 / step, 0.0)
                            coded = jnp.round(value * factor).astype(jnp.int32)
                            send_q[way, c, r - 1, p, part, :] = coded.astype(send_q.dtype)
                            send_s[way, c, r - 1, p, pl.ds(line, 1), :] = jnp.sum(
                                jnp.where(eye, step, 0.0), axis=0, keepdims=True
                            )

                        plane = z + (far - r) * (1 - 2 * way)
                        fold(c, plane, p, [(way, r - 1, has)], code)
                        for copy in chain_copies(way, c, r, p):
                            copy.start()

    def rows_part(p):
        return pl.ds(pl.multiple_of(p * size, size), size)

    def side_copy(c, d, p):
        return pltpu.make_async_remote_copy(
            src_ref=own.at[c, rows_part(p), :],
            dst_ref=out_ref.at[0, d, c, rows_part(p), :],
            send_sem=side_send.at[c, d, p],
            recv_sem=side_recv.at[c, d, p],
            device_id={"bins": side(d)},
            device_id_type=MESH,
        )

    def pair_copy(c, d, p):
        source = own.at[c] if d == 0 else out_ref.at[0, d, c]
        return pltpu.make_async_remote_copy(
            src_ref=source.at[rows_part(p), :],
            dst_ref=out_ref.at[1, d, c, rows_part(p), :],
            send_sem=pair_send.at[c, d, p],
            recv_sem=pair_recv.at[c, d, p],
            device_id={"params": 1 - core},
            device_id_type=MESH,
        )

    def keep_copy(c, p):
        return pltpu.make_async_copy(
            own.at[c, rows_part(p), :], out_ref.at[0, 0, c, rows_part(p), :], own_sem.at[c, p]
        )

    def finish(c):
        @pl.loop(0, pieces)
        def _(p):
            @pl.when(z > 0)
            def _():
                wait_chain(0, c, far - 1, p)

            @pl.when(z < far - 1)
            def _():
                wait_chain(1, c, far - 1, p)

            def store(value, line, part, eye):
                row = pl.ds(pl.multiple_of(p * size + line * LANES, LANES), LANES)
                own[c, row, :] = value.astype(own.dtype)

            fold(c, z, p, [(0, far - 1, z > 0), (1, far - 1, z < far - 1)], store)
            for d in range(1, near):
                side_copy(c, d, p).start()
            pair_copy(c, 0, p).start()
            keep_copy(c, p).start()

    def relay(c):
        @pl.loop(0, pieces)
        def _(p):
            for d in range(1, near):
                side_copy(c, d, p).wait_recv()
                pair_copy(c, d, p).start()

    for c in range(chunks):
        row_local(c, 0).wait()
        for d in range(1, near):
            if c == 0:
                row_local(c, d).wait()
            else:
                row_copy(c, d).wait_recv()
        rounds(c, 1, 2)
        if c > 0:
            finish(c - 1)
        rounds(c, 2, far)
        if 0 < c < chunks - 1:
            relay(c - 1)
    finish(chunks - 1)
    for c in range(max(chunks - 2, 0), chunks):
        relay(c)

    for c in range(chunks):
        if c > 0:
            for d in range(1, near):
                row_copy(c, d).wait_send()

        @pl.loop(0, pieces)
        def _(p):
            keep_copy(c, p).wait()
            for d in range(1, near):
                side_copy(c, d, p).wait_send()
            for d in range(near):
                pair_copy(c, d, p).wait_send()
                pair_copy(c, d, p).wait_recv()

            @pl.loop(1, far)
            def _(r):
                for way in range(2):
                    step_in = z if way == 0 else far - 1 - z

                    @pl.when(step_in < r)
                    def _():
                        for copy in chain_copies(way, c, r, p):
                            copy.wait_send()


def chain(starts, local, weights, firsts, near, far, chunks, slot, bins_dev):
    events = weights.shape[0]
    pieces = 2
    bins = near * bins_dev
    size = bins // pieces
    hops = (2, chunks, far - 1, pieces)
    dma = pltpu.SemaphoreType.DMA
    return pl.pallas_call(
        functools.partial(chain_kernel, near, far, chunks, pieces, slot),
        out_shape=jax.ShapeDtypeStruct((2, near, chunks, bins, LANES), jnp.bfloat16),
        in_specs=[
            pl.BlockSpec(memory_space=pltpu.SMEM),
            pl.BlockSpec(memory_space=pltpu.VMEM),
        ]
        + [pl.BlockSpec(memory_space=pl.ANY)] * (1 + near),
        out_specs=pl.BlockSpec(memory_space=pl.ANY),
        scratch_shapes=[pltpu.VMEM((near, events, LANES), jnp.bfloat16)] * chunks
        + [
            pltpu.VMEM((near * slot, LANES), jnp.bfloat16),
            pltpu.VMEM((TILE, LANES), jnp.float32),
            pltpu.VMEM((chunks, bins, LANES), jnp.bfloat16),
            pltpu.VMEM(hops + (size, LANES), jnp.int16),
            pltpu.VMEM(hops + (size // LANES, LANES), jnp.float32),
            pltpu.VMEM(hops + (size, LANES), jnp.int16),
            pltpu.VMEM(hops + (size // LANES, LANES), jnp.float32),
            dma((chunks, near)),
            dma((chunks, near)),
            dma((chunks, near)),
            dma(hops),
            dma(hops),
            dma(hops),
            dma(hops),
            dma((chunks, pieces)),
            dma((chunks, near, pieces)),
            dma((chunks, near, pieces)),
            dma((chunks, near, pieces)),
            dma((chunks, near, pieces)),
        ],
        compiler_params=pltpu.CompilerParams(
            collective_id=3, has_side_effects=True, vmem_limit_bytes=60 << 20
        ),
        name="chain",
    )(starts, local, weights, *firsts)


def curve_kernel(lows_ref, ids_ref, nominal_ref, background_ref, observed_ref, out_ref, acc):
    sources = ids_ref.shape[0]
    bounds = lows_ref.shape[0] // sources
    index = pl.program_id(0)
    first_bin = lows_ref[sources * (bounds - 1)]
    bins = first_bin + index * TILE + lax.broadcasted_iota(jnp.int32, (TILE, LANES), 0)
    acc[...] = jnp.zeros_like(acc)

    @pl.loop(0, sources)
    def _(s):
        low = lows_ref[s * (bounds - 1) + index]
        high = lows_ref[s * (bounds - 1) + index + 1]

        @pl.loop(low // LANES, (high + LANES - 1) // LANES)
        def _(b):
            part = pl.ds(pl.multiple_of(b * LANES, LANES), LANES)
            hit = bins == ids_ref[s, :, part]
            acc[...] += jnp.where(hit, nominal_ref[s, :, part], 0.0)

    yields = background_ref[...] + jnp.sum(acc[...], axis=1, keepdims=True)
    out_ref[...] = observed_ref[...] / (yields * yields)


def curvature_of(lows, first_bin, ids, nominal, background, observed):
    sources, events = ids.shape
    bins = background.shape[0]
    table = jnp.concatenate(
        [lows.reshape(-1), first_bin.reshape(1), jnp.zeros((sources - 1,), jnp.int32)]
    )
    column = pl.BlockSpec((TILE, 1), lambda j: (j, 0))
    whole = pl.BlockSpec((sources, 1, events), lambda j: (0, 0, 0))
    return pl.pallas_call(
        curve_kernel,
        grid=(bins // TILE,),
        out_shape=jax.ShapeDtypeStruct((bins, 1), jnp.float32),
        in_specs=[pl.BlockSpec(memory_space=pltpu.SMEM), whole, whole, column, column],
        out_specs=column,
        scratch_shapes=[pltpu.VMEM((TILE, LANES), jnp.float32)],
        compiler_params=pltpu.CompilerParams(
            vmem_limit_bytes=8 << 20, dimension_semantics=("arbitrary",)
        ),
        name="curvature",
    )(
        table,
        ids.reshape(sources, 1, events),
        nominal.reshape(sources, 1, events),
        background.reshape(bins, 1),
        observed.reshape(bins, 1),
    )


def weigh_kernel(piece, me_ref, curve_ref, templates_ref, out_ref):
    _, near, chunks, _, _ = templates_ref.shape
    rows = lax.broadcasted_iota(jnp.int32, (piece, LANES), 0) + me_ref[0] * piece
    lanes = lax.broadcasted_iota(jnp.int32, (piece, LANES), 1)
    for d in range(near):
        total = 0.0
        for c in range(chunks):
            pick = (rows == lanes + c * LANES).astype(jnp.bfloat16)
            value = curve_ref[...] * templates_ref[0, d, c].astype(jnp.float32)
            total += lax.dot_general(
                pick, value.astype(jnp.bfloat16), (((1,), (1,)), ((), ())),
                preferred_element_type=jnp.float32,
            )
        out_ref[d * piece : (d + 1) * piece, :] = total.astype(out_ref.dtype)


def weigh(me, curve, templates, piece):
    _, near, chunks, bins, _ = templates.shape
    tile = 512
    return pl.pallas_call(
        functools.partial(weigh_kernel, piece),
        grid=(bins // tile,),
        out_shape=jax.ShapeDtypeStruct((near * piece, bins), jnp.bfloat16),
        in_specs=[
            pl.BlockSpec(memory_space=pltpu.SMEM),
            pl.BlockSpec((tile, 1), lambda j: (j, 0)),
            pl.BlockSpec((1, near, chunks, tile, LANES), lambda j: (0, 0, 0, j, 0)),
        ],
        out_specs=pl.BlockSpec((near * piece, tile), lambda j: (0, j)),
        compiler_params=pltpu.CompilerParams(
            vmem_limit_bytes=24 << 20, dimension_semantics=("arbitrary",)
        ),
        name="weigh",
    )(me, curve, templates)


def hessian_kernel(weighted_ref, templates_ref, full_ref, coded_ref, held, sems):
    groups, near, chunks, _, _ = templates_ref.shape
    places = [(k, d, c) for k in range(groups) for d in range(near) for c in range(chunks)]

    def fetch(n):
        return pltpu.make_async_copy(
            templates_ref.at[places[n]], held.at[:, n * LANES : (n + 1) * LANES], sems.at[n]
        )

    for n in range(len(places)):
        fetch(n).start()
    for n in range(0, len(places), 2):
        fetch(n).wait()
        fetch(n + 1).wait()
        columns = slice(n * LANES, (n + 2) * LANES)
        total = jnp.dot(
            weighted_ref[...], held[:, columns], preferred_element_type=jnp.float32
        )
        full_ref[:, columns] = total
        coded_ref[:, columns] = total.astype(coded_ref.dtype)


def hessian_of(weighted, templates):
    rows, bins = weighted.shape
    count = math.prod(templates.shape[:3])
    shape = (rows, count * LANES)
    return pl.pallas_call(
        hessian_kernel,
        out_shape=[
            jax.ShapeDtypeStruct(shape, jnp.float32),
            jax.ShapeDtypeStruct(shape, jnp.bfloat16),
        ],
        in_specs=[pl.BlockSpec(memory_space=pltpu.VMEM), pl.BlockSpec(memory_space=pl.ANY)],
        out_specs=[pl.BlockSpec(memory_space=pltpu.VMEM)] * 2,
        scratch_shapes=[
            pltpu.VMEM((bins, count * LANES), jnp.bfloat16),
            pltpu.SemaphoreType.DMA((count,)),
        ],
        compiler_params=pltpu.CompilerParams(vmem_limit_bytes=48 << 20),
        cost_estimate=pl.CostEstimate(
            flops=2 * rows * bins * count * LANES,
            bytes_accessed=2 * bins * count * LANES,
            transcendentals=0,
        ),
        name="hessian",
    )(weighted, templates)


def sum_kernel(near, far, piece, run, full_ref, coded_ref, out_ref, own, got, own_sem, sends, recvs):
    here = lax.axis_index("bins")
    z, me = here // near, lax.rem(here, near)
    columns = out_ref.shape[1]

    def peer(k):
        return lax.rem(z + k, far)

    barrier = pltpu.get_barrier_semaphore()
    for k in range(1, far):
        pl.semaphore_signal(
            barrier, inc=1, device_id={"bins": peer(k) * near + me}, device_id_type=MESH
        )
    pl.semaphore_wait(barrier, far - 1)

    def rows_for(target):
        return pl.ds(pl.multiple_of(xor_of(me, target, near) * piece, piece), piece)

    def copy(k):
        return pltpu.make_async_remote_copy(
            src_ref=coded_ref.at[rows_for(peer(k)), :],
            dst_ref=got.at[k - 1],
            send_sem=sends.at[k - 1],
            recv_sem=recvs.at[k - 1],
            device_id={"bins": peer(k) * near + me},
            device_id_type=MESH,
        )

    for k in range(1, far):
        copy(k).start()
    own_copy = pltpu.make_async_copy(full_ref.at[rows_for(z), :], own, own_sem)
    own_copy.start()
    own_copy.wait()
    for k in range(1, far):
        copy(k).wait_recv()
    for n in range(columns // run):
        group, d = n // near, n % near
        total = own[:, n * run : (n + 1) * run]
        for k in range(1, far):
            total += got[k - 1, :, n * run : (n + 1) * run].astype(jnp.float32)
        start = (group * near + xor_of(me, d, near)) * run
        out_ref[:, pl.ds(pl.multiple_of(start, LANES), run)] = total
    for k in range(1, far):
        copy(k).wait_send()


def sum_over_planes(full, coded, near, far, run):
    rows, columns = full.shape
    piece = rows // far
    return pl.pallas_call(
        functools.partial(sum_kernel, near, far, piece, run),
        out_shape=jax.ShapeDtypeStruct((piece, columns), jnp.float32),
        in_specs=[pl.BlockSpec(memory_space=pl.ANY)] * 2,
        out_specs=pl.BlockSpec(memory_space=pltpu.VMEM),
        scratch_shapes=[
            pltpu.VMEM((piece, columns), jnp.float32),
            pltpu.VMEM((far - 1, piece, columns), coded.dtype),
            pltpu.SemaphoreType.DMA,
            pltpu.SemaphoreType.DMA((far - 1,)),
            pltpu.SemaphoreType.DMA((far - 1,)),
        ],
        compiler_params=pltpu.CompilerParams(
            collective_id=2, has_side_effects=True, vmem_limit_bytes=16 << 20
        ),
        name="sum_over_planes",
    )(full, coded)


def body_by_parameters(event_bins, event_weights, nominal, background, observed):
    owners = lax.axis_size("bins")
    near = math.isqrt(owners)
    far = owners // near
    events = event_bins.shape[0]
    bins_dev = background.shape[0]
    width = event_weights.shape[1] // near
    chunks = width // LANES
    bins = near * bins_dev
    capacity = 3 * events // (2 * owners)
    slot = -(-capacity // 16) * 16 + 16
    here = lax.axis_index("bins")
    z, me = here // near, lax.rem(here, near)
    around = [[(s, s // near * near + (s % near ^ d)) for s in range(owners)] for d in range(near)]

    def spread(value):
        return [value] + [shift(value, around[d]) for d in range(1, near)]

    meta = jnp.concatenate([event_bins.astype(jnp.float32), nominal.astype(jnp.float32)])
    meta = jnp.stack(spread(meta.reshape(2, events)))
    local = jnp.stack(spread(jnp.stack([background, observed])))
    ids = meta[:, 0]
    marks = (jnp.arange(owners, dtype=jnp.int32) * bins_dev).astype(jnp.float32)
    before = jnp.sum((ids[:, None, :] < marks[None, :, None]).astype(jnp.int32), axis=2)
    starts = jnp.minimum(before // 16, (events - slot) // 16).reshape(-1)
    places = slots_of(starts, ids, owners, slot, bins_dev)
    places = places.astype(jnp.int32).reshape(owners, 1, near * slot)

    firsts = []
    for d in range(near):
        part = lax.dynamic_slice(event_weights, (0, (me ^ d) * width), (events, LANES))
        firsts.append(part if d == 0 else shift(part, around[d]))

    metas = [meta] + [
        shift(meta, [(s, (s + k * near) % owners) for s in range(owners)]) for k in range(1, far)
    ]
    metas = jnp.concatenate(metas)
    all_ids = metas[:, 0].astype(jnp.int32)
    first_bin = z * bins
    near_marks = first_bin + jnp.arange(bins // TILE + 1, dtype=jnp.int32) * TILE
    lows = jnp.sum((all_ids[:, None, :] < near_marks[None, :, None]).astype(jnp.int32), axis=2)
    index = jnp.arange(near, dtype=jnp.int32)
    match = (index[None, :] ^ me) == index[:, None]
    local = jnp.sum(jnp.where(match[:, :, None, None], local[None], 0.0), axis=1)
    curve = curvature_of(
        lows, first_bin, all_ids, metas[:, 1], local[:, 0].reshape(-1), local[:, 1].reshape(-1)
    )

    starts, curve = lax.optimization_barrier((starts, curve))
    templates = chain(starts, places, event_weights, firsts, near, far, chunks, slot, bins_dev)
    weighted = weigh(me.reshape(1).astype(jnp.int32), curve, templates, width // far)
    full, coded = hessian_of(weighted, templates)
    summed = sum_over_planes(full, coded, near, far, width)
    return summed * (1.0 / (bins_dev * owners))


def splits_by_parameters(mesh, event_bins, event_weights, background):
    owners, groups = mesh.shape["bins"], mesh.shape["params"]
    near = math.isqrt(owners)
    events = event_bins.shape[0] // owners
    width = event_weights.shape[1] // groups // max(near, 1)
    bins_dev = background.shape[0] // owners
    return (
        groups == 2
        and near > 1
        and near * near == owners
        and near & (near - 1) == 0
        and width % LANES == 0
        and width % (16 * near) == 0
        and events % LANES == 0
        and events >= 2 * LANES
        and bins_dev % (8 * LANES) == 0
    )


def solution(mesh):
    in_specs = (P("bins"), P("bins", "params"), P("bins"), P("bins"), P("bins"))
    out_specs = P(("params", "bins"), None)

    def run(event_bins, event_weights, nominal, background, observed):
        fits = splits_by_parameters(mesh, event_bins, event_weights, background)
        chosen = body_by_parameters if fits else body
        mapped = jax.shard_map(
            chosen, mesh=mesh, in_specs=in_specs, out_specs=out_specs, check_vma=False
        )
        return mapped(event_bins, event_weights, nominal, background, observed)

    return run
```

```python
import functools
import math

import jax
import jax.numpy as jnp
from jax import lax
from jax.experimental import pallas as pl
from jax.experimental.pallas import tpu as pltpu
from jax.sharding import PartitionSpec as P

ALIGN = 8
MESH = pl.DeviceIdType.MESH


def from_behind(value, axis, steps):
    count = lax.axis_size(axis)
    pairs = [(source, (source + steps) % count) for source in range(count)]
    return lax.ppermute(value, axis, pairs)


def pack_kernel(owners, slot, first, width, starts_ref, rows_ref, out_ref, held, in_sems, out_sems):
    def fetch(o):
        start = pl.multiple_of(starts_ref[o] * ALIGN, ALIGN)
        return pltpu.make_async_copy(
            rows_ref.at[pl.ds(start, slot), pl.ds(first, width)], held.at[o], in_sems.at[o]
        )

    def store(o):
        return pltpu.make_async_copy(held.at[o], out_ref.at[o], out_sems.at[o])

    @pl.loop(0, owners)
    def _(o):
        fetch(o).start()

    @pl.loop(0, owners)
    def _(o):
        fetch(o).wait()
        store(o).start()

    @pl.loop(0, owners)
    def _(o):
        store(o).wait()


def pack(starts, rows, slot, first, width):
    owners = starts.shape[0]
    return pl.pallas_call(
        functools.partial(pack_kernel, owners, slot, first, width),
        out_shape=jax.ShapeDtypeStruct((owners, slot, width), rows.dtype),
        in_specs=[
            pl.BlockSpec(memory_space=pltpu.SMEM),
            pl.BlockSpec(memory_space=pl.ANY),
        ],
        out_specs=pl.BlockSpec(memory_space=pl.ANY),
        scratch_shapes=[
            pltpu.VMEM((owners, slot, width), rows.dtype),
            pltpu.SemaphoreType.DMA((owners,)),
            pltpu.SemaphoreType.DMA((owners,)),
        ],
        compiler_params=pltpu.CompilerParams(vmem_limit_bytes=32 << 20),
        cost_estimate=pl.CostEstimate(
            flops=0, bytes_accessed=4 * owners * slot * width, transcendentals=0
        ),
        name="pack",
    )(starts, rows)


def meta_kernel(bins_dev, starts_ref, table_ref, out_ref):
    owners, _, slot = out_ref.shape
    events = table_ref.shape[1]
    table = table_ref[...]

    @pl.loop(0, owners)
    def _(o):
        start = starts_ref[o] * ALIGN
        turned = pltpu.roll(table, lax.rem(events - start, events), axis=1)[:, :slot]
        bins = turned[0:1] - (o * bins_dev).astype(jnp.float32)
        inside = (bins >= 0) & (bins < bins_dev)
        out_ref[o, 0:1, :] = jnp.where(inside, bins, -1.0)
        out_ref[o, 1:2, :] = turned[1:2]


def pack_meta(starts, table, slot, bins_dev):
    owners = starts.shape[0]
    return pl.pallas_call(
        functools.partial(meta_kernel, bins_dev),
        out_shape=jax.ShapeDtypeStruct((owners, 2, slot), jnp.float32),
        in_specs=[
            pl.BlockSpec(memory_space=pltpu.SMEM),
            pl.BlockSpec(memory_space=pltpu.VMEM),
        ],
        out_specs=pl.BlockSpec(memory_space=pltpu.VMEM),
        name="pack_meta",
    )(starts, table)


def hist_kernel(chunk, tile, local_ref, rows_ref, out_ref, hot):
    bins, total = hot.shape

    @pl.when(pl.program_id(0) == 0)
    def _():
        ids = lax.broadcasted_iota(jnp.int32, (bins, chunk), 0)

        @pl.loop(0, total // chunk)
        def _(k):
            part = pl.ds(pl.multiple_of(k * chunk, chunk), chunk)
            hot[:, part] = (ids == local_ref[:, part]).astype(jnp.bfloat16)

    @pl.loop(0, bins // tile)
    def _(m):
        part = pl.ds(pl.multiple_of(m * tile, tile), tile)
        out_ref[part, :] = jnp.dot(
            hot[part, :], rows_ref[...], preferred_element_type=jnp.float32
        ).astype(out_ref.dtype)


def histogram_of(local, rows, bins, block, dtype):
    total, width = rows.shape
    return pl.pallas_call(
        functools.partial(hist_kernel, math.gcd(total, 128), math.gcd(bins, 256)),
        grid=(width // block,),
        out_shape=jax.ShapeDtypeStruct((bins, width), dtype),
        in_specs=[
            pl.BlockSpec((1, total), lambda j: (0, 0)),
            pl.BlockSpec((total, block), lambda j: (0, j)),
        ],
        out_specs=pl.BlockSpec((bins, block), lambda j: (0, j)),
        scratch_shapes=[pltpu.VMEM((bins, total), jnp.bfloat16)],
        compiler_params=pltpu.CompilerParams(
            vmem_limit_bytes=40 << 20, dimension_semantics=("arbitrary",)
        ),
        cost_estimate=pl.CostEstimate(
            flops=2 * bins * total * width, bytes_accessed=2 * total * width, transcendentals=0
        ),
        name="histogram",
    )(local, rows)


def reduce_kernel(
    piece, shares_ref, out_ref, own, got_near, sums, got_far,
    own_sem, near_send, near_recv, far_send, far_recv,
):
    far, near, rows, _ = shares_ref.shape
    me = lax.axis_index("bins")
    f, n = me // near, lax.rem(me, near)

    def near_peer(d):
        return lax.rem(n + d, near)

    def far_peer(d):
        return lax.rem(f + d, far)

    barrier = pltpu.get_barrier_semaphore()
    for d in range(1, near):
        pl.semaphore_signal(
            barrier, inc=1, device_id={"bins": f * near + near_peer(d)}, device_id_type=MESH
        )
    for d in range(1, far):
        pl.semaphore_signal(
            barrier, inc=1, device_id={"bins": far_peer(d) * near + n}, device_id_type=MESH
        )
    pl.semaphore_wait(barrier, near + far - 2)

    def part_of(c):
        return pl.ds(pl.multiple_of(c * piece, piece), piece)

    def near_copy(d, c):
        return pltpu.make_async_remote_copy(
            src_ref=shares_ref.at[:, near_peer(d), part_of(c), :],
            dst_ref=got_near.at[d - 1, :, part_of(c), :],
            send_sem=near_send.at[d - 1, c],
            recv_sem=near_recv.at[d - 1, c],
            device_id={"bins": f * near + near_peer(d)},
            device_id_type=MESH,
        )

    def far_copy(d, c):
        return pltpu.make_async_remote_copy(
            src_ref=sums.at[far_peer(d), part_of(c), :],
            dst_ref=got_far.at[d - 1, part_of(c), :],
            send_sem=far_send.at[d - 1, c],
            recv_sem=far_recv.at[d - 1, c],
            device_id={"bins": far_peer(d) * near + n},
            device_id_type=MESH,
        )

    own_copy = pltpu.make_async_copy(shares_ref.at[:, n], own, own_sem)
    own_copy.start()
    pieces = rows // piece

    @pl.loop(0, pieces)
    def _(c):
        for d in range(1, near):
            near_copy(d, c).start()

    own_copy.wait()

    @pl.loop(0, pieces)
    def _(c):
        part = part_of(c)
        for d in range(1, near):
            near_copy(d, c).wait_recv()

        @pl.loop(0, far)
        def _(k):
            total = own[k, part, :].astype(jnp.float32)
            for d in range(1, near):
                total += got_near[d - 1, k, part, :].astype(jnp.float32)
            sums[k, part, :] = total

        for d in range(1, far):
            far_copy(d, c).start()

    @pl.loop(0, pieces)
    def _(c):
        part = part_of(c)
        for d in range(1, far):
            far_copy(d, c).wait_recv()
        total = sums[f, part, :]
        for d in range(1, far):
            total += got_far[d - 1, part, :]
        out_ref[part, :] = total
        for d in range(1, near):
            near_copy(d, c).wait_send()
        for d in range(1, far):
            far_copy(d, c).wait_send()


def reduce_shares(shares):
    owners, rows, cols = shares.shape
    near = math.isqrt(owners)
    while owners % near:
        near -= 1
    far = owners // near
    piece = 16 if rows % 16 == 0 else rows
    pieces = rows // piece
    return pl.pallas_call(
        functools.partial(reduce_kernel, piece),
        out_shape=jax.ShapeDtypeStruct((rows, cols), jnp.float32),
        in_specs=[pl.BlockSpec(memory_space=pl.ANY)],
        out_specs=pl.BlockSpec(memory_space=pltpu.VMEM),
        scratch_shapes=[
            pltpu.VMEM((far, rows, cols), shares.dtype),
            pltpu.VMEM((near - 1, far, rows, cols), shares.dtype),
            pltpu.VMEM((far, rows, cols), jnp.float32),
            pltpu.VMEM((far - 1, rows, cols), jnp.float32),
            pltpu.SemaphoreType.DMA,
            pltpu.SemaphoreType.DMA((near - 1, pieces)),
            pltpu.SemaphoreType.DMA((near - 1, pieces)),
            pltpu.SemaphoreType.DMA((far - 1, pieces)),
            pltpu.SemaphoreType.DMA((far - 1, pieces)),
        ],
        compiler_params=pltpu.CompilerParams(
            collective_id=1, has_side_effects=True, vmem_limit_bytes=40 << 20
        ),
        name="reduce_shares",
    )(shares.reshape(far, near, rows, cols))


def body(event_bins, event_weights, nominal, background, observed):
    owners = lax.axis_size("bins")
    groups_count = lax.axis_size("params")
    events = event_bins.shape[0]
    width_g = event_weights.shape[1]
    bins_dev = background.shape[0]
    capacity = 3 * events // (2 * owners)
    slot = -(-capacity // ALIGN) * ALIGN + ALIGN
    chunks = 2 if width_g % 512 == 0 else 1
    width = width_g // chunks
    block = math.gcd(width, 256)

    destination = event_bins // bins_dev
    targets = jnp.arange(owners, dtype=jnp.int32)
    before = jnp.sum((destination[None, :] < targets[:, None]).astype(jnp.int32), axis=1)
    starts = jnp.minimum(before // ALIGN, (events - slot) // ALIGN)

    table = jnp.stack([event_bins.astype(jnp.float32), nominal.astype(jnp.float32)])
    table = jnp.concatenate([table, jnp.zeros((6, events), jnp.float32)], axis=0)
    meta = pack_meta(starts, table, slot, bins_dev)
    got_meta = lax.all_to_all(meta, "bins", split_axis=0, concat_axis=0, tiled=True)
    local = got_meta[:, 0].astype(jnp.int32).reshape(1, owners * slot)
    got_nominal = got_meta[:, 1].astype(jnp.bfloat16).reshape(owners * slot, 1)
    got_nominal = jnp.broadcast_to(got_nominal, (owners * slot, 128))
    nominal_sum = histogram_of(local, got_nominal, bins_dev, 128, jnp.float32)[:, 0]
    yields = background + nominal_sum
    curvature = observed / (yields * yields)

    parts = []
    for c in range(chunks):
        packed = pack(starts, event_weights, slot, c * width, width)
        got = lax.all_to_all(packed, "bins", split_axis=0, concat_axis=0, tiled=True)
        got = got.reshape(owners * slot, width)
        parts.append(histogram_of(local, got, bins_dev, block, jnp.bfloat16))
    templates = jnp.concatenate(parts, axis=1)
    weighted = (curvature[:, None] * templates.astype(jnp.float32)).astype(jnp.bfloat16)
    pieces = [templates]
    for shift_by in range(1, groups_count // 2 + 1):
        shifted = [from_behind(part, "params", -shift_by) for part in parts]
        pieces.append(jnp.concatenate(shifted, axis=1))
    partners = jnp.concatenate(pieces, axis=1)
    dims = (((0,), (0,)), ((), ()))
    full = lax.dot_general(weighted, partners, dims, preferred_element_type=jnp.float32)
    full = full.astype(jnp.bfloat16)
    shares = full.reshape(owners, width_g // owners, full.shape[1])
    summed = reduce_shares(shares)
    return summed * (1.0 / (bins_dev * owners))


LANES = 128
TILE = 256


def shift(value, pairs):
    return lax.ppermute(value, "bins", pairs)


def xor_of(a, b, count):
    total, bit = 0, 1
    while bit < count:
        total = total + bit * lax.rem(a // bit + b // bit, 2)
        bit *= 2
    return total


def diagonal():
    rows = lax.broadcasted_iota(jnp.int32, (LANES, LANES), 0)
    return rows == lax.broadcasted_iota(jnp.int32, (LANES, LANES), 1)


def slots_kernel(bins_dev, starts_ref, table_ref, out_ref):
    owners, slot = out_ref.shape
    events = table_ref.shape[1]
    table = table_ref[...]

    @pl.loop(0, owners)
    def _(o):
        start = starts_ref[o] * 16
        turned = pltpu.roll(table, lax.rem(events - start, events), axis=1)[0:1, :slot]
        bins = turned - (o * bins_dev).astype(jnp.float32)
        inside = (bins >= 0) & (bins < bins_dev)
        out_ref[pl.ds(o, 1), :] = jnp.where(inside, bins, -1.0)


def slots_of(starts, table, slot, bins_dev):
    return pl.pallas_call(
        functools.partial(slots_kernel, bins_dev),
        out_shape=jax.ShapeDtypeStruct((starts.shape[0], slot), jnp.float32),
        in_specs=[
            pl.BlockSpec(memory_space=pltpu.SMEM),
            pl.BlockSpec(memory_space=pltpu.VMEM),
        ],
        out_specs=pl.BlockSpec(memory_space=pltpu.VMEM),
        name="slots",
    )(starts, table)


def nominal_kernel(lows_ref, table_ref, out_ref, acc):
    events = table_ref.shape[1]
    groups = TILE // LANES

    @pl.loop(0, out_ref.shape[0] // groups)
    def _(k):
        bins = (k * TILE + lax.broadcasted_iota(jnp.int32, (TILE, LANES), 0)).astype(jnp.float32)

        def sums(start):
            part = pl.ds(pl.multiple_of(start, LANES), LANES)
            return jnp.where(bins == table_ref[0:1, part], table_ref[1:2, part], 0.0)

        first = jnp.minimum(lows_ref[k] // LANES * LANES, events - 2 * LANES)
        acc[...] = sums(first) + sums(first + LANES)
        rest = jnp.maximum(lows_ref[k + 1] - first - LANES - 1, 0) // LANES

        @pl.loop(0, rest)
        def _(e):
            acc[...] += sums(first + (2 + e) * LANES)

        for h in range(groups):
            total = jnp.sum(acc[h * LANES : (h + 1) * LANES, :], axis=1, keepdims=True)
            total = jnp.sum(jnp.where(diagonal(), total, 0.0), axis=0, keepdims=True)
            out_ref[pl.ds(k * groups + h, 1), :] = total


def nominal_sums(lows, table):
    bins = (lows.shape[0] - 1) * TILE
    return pl.pallas_call(
        nominal_kernel,
        out_shape=jax.ShapeDtypeStruct((bins // LANES, LANES), jnp.float32),
        in_specs=[
            pl.BlockSpec(memory_space=pltpu.SMEM),
            pl.BlockSpec(memory_space=pltpu.VMEM),
        ],
        out_specs=pl.BlockSpec(memory_space=pltpu.VMEM),
        scratch_shapes=[pltpu.VMEM((TILE, LANES), jnp.float32)],
        name="nominal",
    )(lows, table)


def chain_kernel(
    near, far, chunks, pieces, slot, starts_ref, local_ref, nominal_ref, data_ref, weights_ref, *refs
):
    firsts = refs[:near]
    out_ref, curve_ref = refs[near : near + 2]
    rows_refs = refs[near + 2 : near + 2 + chunks]
    (
        heads, sums, got_sums, got_side, got_data, levels,
        head_sem, head_keep, rest_sem, sums_send, sums_recv, total_send, total_recv,
        data_send, data_recv,
        window, acc, own, send_q, send_s, got_q, got_s,
        row_sem, row_send, row_recv, q_send, q_recv, s_send, s_recv,
        own_sem, side_send, side_recv, pair_send, pair_recv,
    ) = refs[near + 2 + chunks :]
    owners = near * far
    here = lax.axis_index("bins")
    core = lax.axis_index("params")
    z, me = here // near, lax.rem(here, near)
    bins_dev = own.shape[1] // near
    width = chunks * LANES
    held = near // pieces
    size = held * bins_dev
    direct = [d for d in range(1, near) if near != 4 or d != 3]

    def side(d):
        return z * near + xor_of(me, d, near)

    def along(way):
        return (z + 1 - 2 * way) * near + me

    def peer(k):
        return lax.rem(z + k, far)

    barrier = pltpu.get_barrier_semaphore()
    for d in range(1, near):
        pl.semaphore_signal(barrier, inc=1, device_id={"bins": side(d)}, device_id_type=MESH)
    for k in range(1, far):
        pl.semaphore_signal(
            barrier, inc=1, device_id={"bins": peer(k) * near + me}, device_id_type=MESH
        )
    pl.semaphore_signal(barrier, inc=1, device_id={"params": 1 - core}, device_id_type=MESH)
    pl.semaphore_wait(barrier, near + far - 1)

    events = weights_ref.shape[0]
    ahead = firsts[0].shape[0]
    lower = (z < far // 2).astype(jnp.int32)
    head_start = lower * (events - ahead)
    rest_start = (1 - lower) * ahead

    def quarter(d, c):
        start = xor_of(me, d, near) * width + c * LANES
        return pl.ds(pl.multiple_of(start, LANES), LANES)

    def row_part(c):
        if c > 0:
            return pl.ds(0, events)
        return pl.ds(pl.multiple_of(rest_start, 16), events - ahead)

    def row_copy(c, d):
        return pltpu.make_async_remote_copy(
            src_ref=weights_ref.at[row_part(c), quarter(d, c)],
            dst_ref=rows_refs[c].at[d, row_part(c), :],
            send_sem=row_send.at[c, d],
            recv_sem=row_recv.at[c, d],
            device_id={"bins": side(d)},
            device_id_type=MESH,
        )

    def row_local(c):
        return pltpu.make_async_copy(
            weights_ref.at[row_part(c), quarter(0, c)],
            rows_refs[c].at[0, row_part(c), :],
            row_sem.at[c],
        )

    def head_local(d):
        return pltpu.make_async_copy(firsts[d], heads.at[d], head_sem.at[d])

    def head_stay(d):
        part = pl.ds(pl.multiple_of(head_start, 16), ahead)
        return pltpu.make_async_copy(firsts[d], rows_refs[0].at[d, part, :], head_keep.at[d])

    def sums_copy(k):
        lines_from = pl.ds(pl.multiple_of(peer(k) * curve_ref.shape[0], 8), curve_ref.shape[0])
        return pltpu.make_async_remote_copy(
            src_ref=nominal_ref.at[lines_from, :],
            dst_ref=got_sums.at[k - 1],
            send_sem=sums_send.at[k - 1],
            recv_sem=sums_recv.at[k - 1],
            device_id={"bins": peer(k) * near + me},
            device_id_type=MESH,
        )

    def total_copy(d):
        return pltpu.make_async_remote_copy(
            src_ref=sums,
            dst_ref=got_side.at[d - 1],
            send_sem=total_send.at[d - 1],
            recv_sem=total_recv.at[d - 1],
            device_id={"bins": side(d)},
            device_id_type=MESH,
        )

    def data_copy(d):
        return pltpu.make_async_remote_copy(
            src_ref=data_ref,
            dst_ref=got_data.at[d - 1],
            send_sem=data_send.at[d - 1],
            recv_sem=data_recv.at[d - 1],
            device_id={"bins": side(d)},
            device_id_type=MESH,
        )

    for d in range(near):
        head_local(d).start()
    for k in range(1, far):
        sums_copy(k).start()
    for d in range(1, near):
        data_copy(d).start()
    for c in range(chunks):
        for d in range(1, near):
            row_copy(c, d).start()
    for c in range(chunks):
        row_local(c).start()
    for d in range(near):
        head_stay(d).start()

    def gather_sums():
        own_lines = pl.ds(pl.multiple_of(z * curve_ref.shape[0], 8), curve_ref.shape[0])
        total = nominal_ref[own_lines, :]
        for k in range(1, far):
            sums_copy(k).wait_recv()
            total += got_sums[k - 1]
        sums[...] = total
        for d in range(1, near):
            total_copy(d).start()

    def finish_sums():
        total = sums[...]
        for d in range(1, near):
            total_copy(d).wait_recv()
            total += got_side[d - 1]
        lines_dev = bins_dev // LANES
        levels[0, pl.ds(pl.multiple_of(me * lines_dev, 8), lines_dev), :] = data_ref[0:lines_dev, :]
        levels[1, pl.ds(pl.multiple_of(me * lines_dev, 8), lines_dev), :] = data_ref[
            lines_dev : 2 * lines_dev, :
        ]
        for d in range(1, near):
            data_copy(d).wait_recv()
            part = pl.ds(pl.multiple_of(xor_of(me, d, near) * lines_dev, 8), lines_dev)
            levels[0, part, :] = got_data[d - 1, 0:lines_dev, :]
            levels[1, part, :] = got_data[d - 1, lines_dev : 2 * lines_dev, :]
        yields = levels[0] + total
        curve_ref[...] = levels[1] / (yields * yields)

    def chain_copies(way, c, r, p):
        return [
            pltpu.make_async_remote_copy(
                src_ref=source.at[way, c, r - 1, p],
                dst_ref=target.at[way, c, r - 1, p],
                send_sem=sent.at[way, c, r - 1, p],
                recv_sem=landed.at[way, c, r - 1, p],
                device_id={"bins": along(way)},
                device_id_type=MESH,
            )
            for source, target, sent, landed in (
                (send_q, got_q, q_send, q_recv), (send_s, got_s, s_send, s_recv)
            )
        ]

    def fold(c, plane, p, inputs, finish, early=False):
        @pl.loop(0, held)
        def _(i):
            owner = plane * near + p * held + i
            for s in range(near):
                start = starts_ref[s * owners + owner]
                if early:
                    start = jnp.maximum(start - lower * ((events - ahead) // 16), 0)
                    part = heads[s, pl.ds(start * 16, slot), :]
                else:
                    part = rows_refs[c][s, pl.ds(start * 16, slot), :]
                window[s * slot : (s + 1) * slot, :] = part

            @pl.loop(0, bins_dev // TILE)
            def _(k):
                bins = k * TILE + lax.broadcasted_iota(jnp.int32, (TILE, near * slot), 0)
                hot = (bins == local_ref[owner]).astype(jnp.bfloat16)
                acc[...] = jnp.dot(hot, window[...], preferred_element_type=jnp.float32)
                base = i * (bins_dev // LANES) + k * (TILE // LANES)
                eye = diagonal()
                for way, r, has in inputs:
                    @pl.when(has)
                    def _():
                        for h in range(TILE // LANES):
                            line = base + h
                            part = pl.ds(pl.multiple_of(line * LANES, LANES), LANES)
                            step = got_s[way, c, r - 1, p, pl.ds(line, 1), :]
                            step = jnp.sum(jnp.where(eye, step, 0.0), axis=1, keepdims=True)
                            coded = got_q[way, c, r - 1, p, part, :].astype(jnp.int32)
                            acc[h * LANES : (h + 1) * LANES, :] += (
                                coded.astype(jnp.float32) * step
                            )
                for h in range(TILE // LANES):
                    line = base + h
                    part = pl.ds(pl.multiple_of(line * LANES, LANES), LANES)
                    finish(acc[h * LANES : (h + 1) * LANES, :], line, part, eye)

    def wait_chain(way, c, r, p):
        for copy in chain_copies(way, c, r, p):
            copy.wait_recv()

    def rounds(c, first, last):
        @pl.loop(first, last)
        def _(r):
            @pl.loop(0, pieces)
            def _(p):
                for way in range(2):
                    step_in = z if way == 0 else far - 1 - z

                    @pl.when(step_in < r)
                    def _():
                        has = step_in > 0

                        if first > 1:
                            @pl.when(has)
                            def _():
                                wait_chain(way, c, r - 1, p)

                        def code(value, line, part, eye):
                            most = jnp.max(jnp.abs(value), axis=1, keepdims=True)
                            wide = most * (2.0**23 + 1.0)
                            step = (wide + (most - wide)) * 2.0**-14
                            factor = jnp.where(most > 1e-30, 1.0 / step, 0.0)
                            coded = jnp.round(value * factor).astype(jnp.int32)
                            send_q[way, c, r - 1, p, part, :] = coded.astype(send_q.dtype)
                            send_s[way, c, r - 1, p, pl.ds(line, 1), :] = jnp.sum(
                                jnp.where(eye, step, 0.0), axis=0, keepdims=True
                            )

                        plane = z + (far - r) * (1 - 2 * way)
                        early = c == 0 and first == 1
                        fold(c, plane, p, [] if first == 1 else [(way, r - 1, has)], code, early)
                        for copy in chain_copies(way, c, r, p):
                            copy.start()

    def rows_part(p):
        return pl.ds(pl.multiple_of(p * size, size), size)

    def side_copy(c, d, p, source=0, hop=None):
        hop = d if hop is None else hop
        origin = own.at[c] if source == 0 else out_ref.at[0, source, c]
        return pltpu.make_async_remote_copy(
            src_ref=origin.at[rows_part(p), :],
            dst_ref=out_ref.at[0, d, c, rows_part(p), :],
            send_sem=side_send.at[c, d, p],
            recv_sem=side_recv.at[c, d, p],
            device_id={"bins": side(hop)},
            device_id_type=MESH,
        )

    def pair_copy(c, d, p):
        source = own.at[c] if d == 0 else out_ref.at[0, d, c]
        return pltpu.make_async_remote_copy(
            src_ref=source.at[rows_part(p), :],
            dst_ref=out_ref.at[1, d, c, rows_part(p), :],
            send_sem=pair_send.at[c, d, p],
            recv_sem=pair_recv.at[c, d, p],
            device_id={"params": 1 - core},
            device_id_type=MESH,
        )

    def keep_copy(c, p):
        return pltpu.make_async_copy(
            own.at[c, rows_part(p), :], out_ref.at[0, 0, c, rows_part(p), :], own_sem.at[c, p]
        )

    def finish(c):
        @pl.loop(0, pieces)
        def _(p):
            @pl.when(z > 0)
            def _():
                wait_chain(0, c, far - 1, p)

            @pl.when(z < far - 1)
            def _():
                wait_chain(1, c, far - 1, p)

            def store(value, line, part, eye):
                row = pl.ds(pl.multiple_of(p * size + line * LANES, LANES), LANES)
                own[c, row, :] = value.astype(own.dtype)

            fold(c, z, p, [(0, far - 1, z > 0), (1, far - 1, z < far - 1)], store)
            for d in direct:
                side_copy(c, d, p).start()
            pair_copy(c, 0, p).start()
            keep_copy(c, p).start()

    def forward(c, p, act):
        if near == 4:
            @pl.when(lax.rem(p, 2) == 0)
            def _():
                act(side_copy(c, 3, p, 1, 2))

            @pl.when(lax.rem(p, 2) == 1)
            def _():
                act(side_copy(c, 3, p, 2, 1))

    def relay(c):
        @pl.loop(0, pieces)
        def _(p):
            for d in direct:
                side_copy(c, d, p).wait_recv()
            forward(c, p, lambda copy: copy.start())
            for d in direct:
                pair_copy(c, d, p).start()

    def relay_last(c):
        @pl.loop(0, pieces)
        def _(p):
            for d in range(1, near):
                if d not in direct:
                    side_copy(c, d, p).wait_recv()
                    pair_copy(c, d, p).start()

    for d in range(near):
        head_local(d).wait()
    for c in range(chunks):
        if c > 0:
            row_local(c).wait()
            for d in range(1, near):
                row_copy(c, d).wait_recv()
        rounds(c, 1, 2)
        if c == 0:
            row_local(c).wait()
            head_stay(0).wait()
            for d in range(1, near):
                head_stay(d).wait()
                row_copy(c, d).wait_recv()
        if c > 0:
            finish(c - 1)
        rounds(c, 2, far)
        if c == 0:
            gather_sums()
        if c == 1:
            finish_sums()
        if c > 0:
            relay(c - 1)
        if c > 1:
            relay_last(c - 2)
    if chunks == 1:
        finish_sums()
    finish(chunks - 1)
    if chunks > 1:
        relay_last(chunks - 2)
    relay(chunks - 1)
    relay_last(chunks - 1)

    for k in range(1, far):
        sums_copy(k).wait_send()
    for d in range(1, near):
        total_copy(d).wait_send()
        data_copy(d).wait_send()
    for c in range(chunks):
        for d in range(1, near):
            row_copy(c, d).wait_send()

        @pl.loop(0, pieces)
        def _(p):
            keep_copy(c, p).wait()
            for d in direct:
                side_copy(c, d, p).wait_send()
            forward(c, p, lambda copy: copy.wait_send())
            for d in range(near):
                pair_copy(c, d, p).wait_send()
                pair_copy(c, d, p).wait_recv()

            @pl.loop(1, far)
            def _(r):
                for way in range(2):
                    step_in = z if way == 0 else far - 1 - z

                    @pl.when(step_in < r)
                    def _():
                        for copy in chain_copies(way, c, r, p):
                            copy.wait_send()


def chain(starts, local, nominal, data, weights, firsts, near, far, chunks, slot, bins_dev):
    events = weights.shape[0]
    ahead = firsts[0].shape[0]
    pieces = near
    bins = near * bins_dev
    size = bins // pieces
    hops = (2, chunks, far - 1, pieces)
    lines = bins // LANES
    dma = pltpu.SemaphoreType.DMA
    rows = jnp.bfloat16
    table = jnp.float32
    return pl.pallas_call(
        functools.partial(chain_kernel, near, far, chunks, pieces, slot),
        out_shape=[
            jax.ShapeDtypeStruct((2, near, chunks, bins, LANES), rows),
            jax.ShapeDtypeStruct((lines, LANES), table),
        ],
        in_specs=[pl.BlockSpec(memory_space=pltpu.SMEM)]
        + [pl.BlockSpec(memory_space=pltpu.VMEM)] * 3
        + [pl.BlockSpec(memory_space=pl.ANY)] * (1 + near),
        out_specs=[
            pl.BlockSpec(memory_space=pl.ANY),
            pl.BlockSpec(memory_space=pltpu.VMEM),
        ],
        scratch_shapes=[pltpu.VMEM((near, events, LANES), rows)] * chunks
        + [
            pltpu.VMEM((near, ahead, LANES), rows),
            pltpu.VMEM((lines, LANES), table),
            pltpu.VMEM((far - 1, lines, LANES), table),
            pltpu.VMEM((near - 1, lines, LANES), table),
            pltpu.VMEM((near - 1,) + data.shape, table),
            pltpu.VMEM((2, lines, LANES), table),
            dma((near,)),
            dma((near,)),
            dma((1,)),
            dma((far - 1,)),
            dma((far - 1,)),
            dma((near - 1,)),
            dma((near - 1,)),
            dma((near - 1,)),
            dma((near - 1,)),
            pltpu.VMEM((near * slot, LANES), rows),
            pltpu.VMEM((TILE, LANES), table),
            pltpu.VMEM((chunks, bins, LANES), rows),
            pltpu.VMEM(hops + (size, LANES), jnp.int16),
            pltpu.VMEM(hops + (size // LANES, LANES), table),
            pltpu.VMEM(hops + (size, LANES), jnp.int16),
            pltpu.VMEM(hops + (size // LANES, LANES), table),
            dma((chunks,)),
            dma((chunks, near)),
            dma((chunks, near)),
            dma(hops),
            dma(hops),
            dma(hops),
            dma(hops),
            dma((chunks, pieces)),
            dma((chunks, near, pieces)),
            dma((chunks, near, pieces)),
            dma((chunks, near, pieces)),
            dma((chunks, near, pieces)),
        ],
        compiler_params=pltpu.CompilerParams(
            collective_id=3, has_side_effects=True, vmem_limit_bytes=62 << 20
        ),
        name="chain",
    )(starts, local, nominal, data, weights, *firsts)


def tail_kernel(
    near, far, templates_ref, curve_ref, out_ref, held, weighted, total, coded, own, got,
    sems, sends, recvs,
):
    groups, _, chunks, bins, _ = templates_ref.shape
    here = lax.axis_index("bins")
    z, me = here // near, lax.rem(here, near)
    piece = own.shape[0]
    count = groups * near * chunks
    step = 2 * LANES
    depth = 4 * LANES

    def peer(k):
        return lax.rem(z + k, far)

    barrier = pltpu.get_barrier_semaphore()
    for k in range(1, far):
        pl.semaphore_signal(
            barrier, inc=1, device_id={"bins": peer(k) * near + me}, device_id_type=MESH
        )

    def fetch(n):
        part = templates_ref.at[n // (near * chunks), lax.rem(n // chunks, near), lax.rem(n, chunks)]
        return pltpu.make_async_copy(
            part, held.at[:, pl.ds(pl.multiple_of(n * LANES, LANES), LANES)], sems.at[n]
        )

    @pl.loop(0, count)
    def _(n):
        fetch(n).start()

    pl.semaphore_wait(barrier, far - 1)
    rows = lax.broadcasted_iota(jnp.int32, (piece, LANES), 0) + me * piece
    lanes = lax.broadcasted_iota(jnp.int32, (piece, LANES), 1)

    @pl.loop(0, near * chunks)
    def _(n):
        fetch(n).wait()

    @pl.loop(0, bins // depth)
    def _(b):
        eye = diagonal()
        curves = []
        for h in range(depth // LANES):
            line = curve_ref[pl.ds(b * (depth // LANES) + h, 1), :]
            curves.append(jnp.sum(jnp.where(eye, line, 0.0), axis=1, keepdims=True))
        curve = jnp.concatenate(curves, axis=0)
        part = pl.ds(pl.multiple_of(b * depth, depth), depth)
        for d in range(near):
            picked = 0.0
            for c in range(chunks):
                pick = (rows == lanes + c * LANES).astype(jnp.bfloat16)
                columns = slice((d * chunks + c) * LANES, (d * chunks + c + 1) * LANES)
                value = curve * held[part, columns].astype(jnp.float32)
                picked += lax.dot_general(
                    pick, value.astype(jnp.bfloat16), (((1,), (1,)), ((), ())),
                    preferred_element_type=jnp.float32,
                )
            weighted[d * piece : (d + 1) * piece, part] = picked.astype(weighted.dtype)

    def rows_for(target):
        return pl.ds(pl.multiple_of(xor_of(me, target, near) * piece, 16), piece)

    def columns_of(n):
        return pl.ds(pl.multiple_of(n * step, step), step)

    def copy(k, n):
        return pltpu.make_async_remote_copy(
            src_ref=coded.at[rows_for(peer(k)), columns_of(n)],
            dst_ref=got.at[k - 1, :, columns_of(n)],
            send_sem=sends.at[k - 1, n],
            recv_sem=recvs.at[k - 1, n],
            device_id={"bins": peer(k) * near + me},
            device_id_type=MESH,
        )

    @pl.loop(0, count // 2)
    def _(n):
        @pl.when(n >= near * chunks // 2)
        def _():
            fetch(2 * n).wait()
            fetch(2 * n + 1).wait()

        total[...] = jnp.dot(
            weighted[...], held[:, columns_of(n)], preferred_element_type=jnp.float32
        )
        coded[:, columns_of(n)] = total[...].astype(coded.dtype)
        own[:, columns_of(n)] = total[rows_for(z), :]
        for k in range(1, far):
            copy(k, n).start()

    @pl.loop(0, count // 2)
    def _(n):
        for k in range(1, far):
            copy(k, n).wait_recv()
        for half in range(2):
            place = 2 * n + half
            group = place // (near * chunks)
            d = lax.rem(place // chunks, near)
            start = ((group * near + xor_of(me, d, near)) * chunks + lax.rem(place, chunks)) * LANES
            part = pl.ds(pl.multiple_of(place * LANES, LANES), LANES)
            value = own[:, part]
            for k in range(1, far):
                value += got[k - 1, :, part].astype(jnp.float32)
            out_ref[:, pl.ds(pl.multiple_of(start, LANES), LANES)] = value

    @pl.loop(0, count // 2)
    def _(n):
        for k in range(1, far):
            copy(k, n).wait_send()


def tail(templates, curve, near, far):
    groups, _, chunks, bins, _ = templates.shape
    piece = chunks * LANES // far
    columns = groups * near * chunks * LANES
    count = groups * near * chunks
    return pl.pallas_call(
        functools.partial(tail_kernel, near, far),
        out_shape=jax.ShapeDtypeStruct((piece, columns), jnp.float32),
        in_specs=[pl.BlockSpec(memory_space=pl.ANY), pl.BlockSpec(memory_space=pltpu.VMEM)],
        out_specs=pl.BlockSpec(memory_space=pltpu.VMEM),
        scratch_shapes=[
            pltpu.VMEM((bins, columns), jnp.bfloat16),
            pltpu.VMEM((near * piece, bins), jnp.bfloat16),
            pltpu.VMEM((near * piece, 2 * LANES), jnp.float32),
            pltpu.VMEM((near * piece, columns), jnp.bfloat16),
            pltpu.VMEM((piece, columns), jnp.float32),
            pltpu.VMEM((far - 1, piece, columns), jnp.bfloat16),
            pltpu.SemaphoreType.DMA((count,)),
            pltpu.SemaphoreType.DMA((far - 1, count // 2)),
            pltpu.SemaphoreType.DMA((far - 1, count // 2)),
        ],
        compiler_params=pltpu.CompilerParams(
            collective_id=2, has_side_effects=True, vmem_limit_bytes=60 << 20
        ),
        name="tail",
    )(templates, curve)


def body_by_parameters(event_bins, event_weights, nominal, background, observed):
    owners = lax.axis_size("bins")
    near = math.isqrt(owners)
    far = owners // near
    events = event_bins.shape[0]
    bins_dev = background.shape[0]
    width = event_weights.shape[1] // near
    chunks = width // LANES
    capacity = 3 * events // (2 * owners)
    slot = -(-capacity // 16) * 16 + 16
    ahead = min(-(-near * capacity // 16) * 16 + 16, events - 16)
    here = lax.axis_index("bins")
    z, me = here // near, lax.rem(here, near)
    around = [[(s, s // near * near + (s % near ^ d)) for s in range(owners)] for d in range(near)]

    def spread(value):
        return [value] + [shift(value, around[d]) for d in range(1, near)]

    marks = jnp.arange(owners * bins_dev // TILE + 1, dtype=jnp.int32) * TILE
    lows = jnp.sum((event_bins[None, :] < marks[:, None]).astype(jnp.int32), axis=1)
    starts = jnp.minimum(lows[: -1 : bins_dev // TILE] // 16, (events - slot) // 16)
    table = jnp.stack([event_bins.astype(jnp.float32), nominal.astype(jnp.float32)])
    table = jnp.concatenate([table, jnp.zeros((6, events), jnp.float32)])
    places = slots_of(starts, table, slot, bins_dev)
    line = jnp.pad(starts.astype(jnp.float32), (0, slot - owners)).reshape(1, slot)
    places = jnp.stack(spread(jnp.concatenate([places, line])))

    firsts = []
    first_row = jnp.where(z < far // 2, events - ahead, 0)
    for d in range(near):
        corner = (first_row, (me ^ d) * width)
        part = lax.dynamic_slice(event_weights, corner, (ahead, LANES))
        firsts.append(part if d == 0 else shift(part, around[d]))

    sums = nominal_sums(lows, table)
    starts = places[:, owners, :owners].astype(jnp.int32).reshape(-1)
    places = places[:, :owners].astype(jnp.int32).transpose(1, 0, 2)
    places = places.reshape(owners, 1, near * slot)
    data = jnp.concatenate([background, observed]).reshape(-1, LANES)
    templates, curve = chain(
        starts, places, sums, data, event_weights, firsts, near, far, chunks, slot, bins_dev
    )
    summed = tail(templates, curve, near, far)
    return summed * (1.0 / (bins_dev * owners))


def splits_by_parameters(mesh, event_bins, event_weights, background):
    owners, groups = mesh.shape["bins"], mesh.shape["params"]
    near = math.isqrt(owners)
    events = event_bins.shape[0] // owners
    width = event_weights.shape[1] // groups // max(near, 1)
    bins_dev = background.shape[0] // owners
    return (
        groups == 2
        and near > 1
        and near * near == owners
        and near & (near - 1) == 0
        and width % LANES == 0
        and width % (16 * near) == 0
        and events % LANES == 0
        and events >= 2 * LANES
        and bins_dev % (8 * LANES) == 0
    )


def solution(mesh):
    in_specs = (P("bins"), P("bins", "params"), P("bins"), P("bins"), P("bins"))
    out_specs = P(("params", "bins"), None)

    def run(event_bins, event_weights, nominal, background, observed):
        fits = splits_by_parameters(mesh, event_bins, event_weights, background)
        chosen = body_by_parameters if fits else body
        mapped = jax.shard_map(
            chosen, mesh=mesh, in_specs=in_specs, out_specs=out_specs, check_vma=False
        )
        return mapped(event_bins, event_weights, nominal, background, observed)

    return run
```

```python
import functools
import math

import jax
import jax.numpy as jnp
from jax import lax
from jax.experimental import pallas as pl
from jax.experimental.pallas import tpu as pltpu
from jax.sharding import PartitionSpec as P

ALIGN = 8
MESH = pl.DeviceIdType.MESH


def from_behind(value, axis, steps):
    count = lax.axis_size(axis)
    pairs = [(source, (source + steps) % count) for source in range(count)]
    return lax.ppermute(value, axis, pairs)


def pack_kernel(owners, slot, first, width, starts_ref, rows_ref, out_ref, held, in_sems, out_sems):
    def fetch(o):
        start = pl.multiple_of(starts_ref[o] * ALIGN, ALIGN)
        return pltpu.make_async_copy(
            rows_ref.at[pl.ds(start, slot), pl.ds(first, width)], held.at[o], in_sems.at[o]
        )

    def store(o):
        return pltpu.make_async_copy(held.at[o], out_ref.at[o], out_sems.at[o])

    @pl.loop(0, owners)
    def _(o):
        fetch(o).start()

    @pl.loop(0, owners)
    def _(o):
        fetch(o).wait()
        store(o).start()

    @pl.loop(0, owners)
    def _(o):
        store(o).wait()


def pack(starts, rows, slot, first, width):
    owners = starts.shape[0]
    return pl.pallas_call(
        functools.partial(pack_kernel, owners, slot, first, width),
        out_shape=jax.ShapeDtypeStruct((owners, slot, width), rows.dtype),
        in_specs=[
            pl.BlockSpec(memory_space=pltpu.SMEM),
            pl.BlockSpec(memory_space=pl.ANY),
        ],
        out_specs=pl.BlockSpec(memory_space=pl.ANY),
        scratch_shapes=[
            pltpu.VMEM((owners, slot, width), rows.dtype),
            pltpu.SemaphoreType.DMA((owners,)),
            pltpu.SemaphoreType.DMA((owners,)),
        ],
        compiler_params=pltpu.CompilerParams(vmem_limit_bytes=32 << 20),
        cost_estimate=pl.CostEstimate(
            flops=0, bytes_accessed=4 * owners * slot * width, transcendentals=0
        ),
        name="pack",
    )(starts, rows)


def meta_kernel(bins_dev, starts_ref, table_ref, out_ref):
    owners, _, slot = out_ref.shape
    events = table_ref.shape[1]
    table = table_ref[...]

    @pl.loop(0, owners)
    def _(o):
        start = starts_ref[o] * ALIGN
        turned = pltpu.roll(table, lax.rem(events - start, events), axis=1)[:, :slot]
        bins = turned[0:1] - (o * bins_dev).astype(jnp.float32)
        inside = (bins >= 0) & (bins < bins_dev)
        out_ref[o, 0:1, :] = jnp.where(inside, bins, -1.0)
        out_ref[o, 1:2, :] = turned[1:2]


def pack_meta(starts, table, slot, bins_dev):
    owners = starts.shape[0]
    return pl.pallas_call(
        functools.partial(meta_kernel, bins_dev),
        out_shape=jax.ShapeDtypeStruct((owners, 2, slot), jnp.float32),
        in_specs=[
            pl.BlockSpec(memory_space=pltpu.SMEM),
            pl.BlockSpec(memory_space=pltpu.VMEM),
        ],
        out_specs=pl.BlockSpec(memory_space=pltpu.VMEM),
        name="pack_meta",
    )(starts, table)


def hist_kernel(chunk, tile, local_ref, rows_ref, out_ref, hot):
    bins, total = hot.shape

    @pl.when(pl.program_id(0) == 0)
    def _():
        ids = lax.broadcasted_iota(jnp.int32, (bins, chunk), 0)

        @pl.loop(0, total // chunk)
        def _(k):
            part = pl.ds(pl.multiple_of(k * chunk, chunk), chunk)
            hot[:, part] = (ids == local_ref[:, part]).astype(jnp.bfloat16)

    @pl.loop(0, bins // tile)
    def _(m):
        part = pl.ds(pl.multiple_of(m * tile, tile), tile)
        out_ref[part, :] = jnp.dot(
            hot[part, :], rows_ref[...], preferred_element_type=jnp.float32
        ).astype(out_ref.dtype)


def histogram_of(local, rows, bins, block, dtype):
    total, width = rows.shape
    return pl.pallas_call(
        functools.partial(hist_kernel, math.gcd(total, 128), math.gcd(bins, 256)),
        grid=(width // block,),
        out_shape=jax.ShapeDtypeStruct((bins, width), dtype),
        in_specs=[
            pl.BlockSpec((1, total), lambda j: (0, 0)),
            pl.BlockSpec((total, block), lambda j: (0, j)),
        ],
        out_specs=pl.BlockSpec((bins, block), lambda j: (0, j)),
        scratch_shapes=[pltpu.VMEM((bins, total), jnp.bfloat16)],
        compiler_params=pltpu.CompilerParams(
            vmem_limit_bytes=40 << 20, dimension_semantics=("arbitrary",)
        ),
        cost_estimate=pl.CostEstimate(
            flops=2 * bins * total * width, bytes_accessed=2 * total * width, transcendentals=0
        ),
        name="histogram",
    )(local, rows)


def reduce_kernel(
    piece, shares_ref, out_ref, own, got_near, sums, got_far,
    own_sem, near_send, near_recv, far_send, far_recv,
):
    far, near, rows, _ = shares_ref.shape
    me = lax.axis_index("bins")
    f, n = me // near, lax.rem(me, near)

    def near_peer(d):
        return lax.rem(n + d, near)

    def far_peer(d):
        return lax.rem(f + d, far)

    barrier = pltpu.get_barrier_semaphore()
    for d in range(1, near):
        pl.semaphore_signal(
            barrier, inc=1, device_id={"bins": f * near + near_peer(d)}, device_id_type=MESH
        )
    for d in range(1, far):
        pl.semaphore_signal(
            barrier, inc=1, device_id={"bins": far_peer(d) * near + n}, device_id_type=MESH
        )
    pl.semaphore_wait(barrier, near + far - 2)

    def part_of(c):
        return pl.ds(pl.multiple_of(c * piece, piece), piece)

    def near_copy(d, c):
        return pltpu.make_async_remote_copy(
            src_ref=shares_ref.at[:, near_peer(d), part_of(c), :],
            dst_ref=got_near.at[d - 1, :, part_of(c), :],
            send_sem=near_send.at[d - 1, c],
            recv_sem=near_recv.at[d - 1, c],
            device_id={"bins": f * near + near_peer(d)},
            device_id_type=MESH,
        )

    def far_copy(d, c):
        return pltpu.make_async_remote_copy(
            src_ref=sums.at[far_peer(d), part_of(c), :],
            dst_ref=got_far.at[d - 1, part_of(c), :],
            send_sem=far_send.at[d - 1, c],
            recv_sem=far_recv.at[d - 1, c],
            device_id={"bins": far_peer(d) * near + n},
            device_id_type=MESH,
        )

    own_copy = pltpu.make_async_copy(shares_ref.at[:, n], own, own_sem)
    own_copy.start()
    pieces = rows // piece

    @pl.loop(0, pieces)
    def _(c):
        for d in range(1, near):
            near_copy(d, c).start()

    own_copy.wait()

    @pl.loop(0, pieces)
    def _(c):
        part = part_of(c)
        for d in range(1, near):
            near_copy(d, c).wait_recv()

        @pl.loop(0, far)
        def _(k):
            total = own[k, part, :].astype(jnp.float32)
            for d in range(1, near):
                total += got_near[d - 1, k, part, :].astype(jnp.float32)
            sums[k, part, :] = total

        for d in range(1, far):
            far_copy(d, c).start()

    @pl.loop(0, pieces)
    def _(c):
        part = part_of(c)
        for d in range(1, far):
            far_copy(d, c).wait_recv()
        total = sums[f, part, :]
        for d in range(1, far):
            total += got_far[d - 1, part, :]
        out_ref[part, :] = total
        for d in range(1, near):
            near_copy(d, c).wait_send()
        for d in range(1, far):
            far_copy(d, c).wait_send()


def reduce_shares(shares):
    owners, rows, cols = shares.shape
    near = math.isqrt(owners)
    while owners % near:
        near -= 1
    far = owners // near
    piece = 16 if rows % 16 == 0 else rows
    pieces = rows // piece
    return pl.pallas_call(
        functools.partial(reduce_kernel, piece),
        out_shape=jax.ShapeDtypeStruct((rows, cols), jnp.float32),
        in_specs=[pl.BlockSpec(memory_space=pl.ANY)],
        out_specs=pl.BlockSpec(memory_space=pltpu.VMEM),
        scratch_shapes=[
            pltpu.VMEM((far, rows, cols), shares.dtype),
            pltpu.VMEM((near - 1, far, rows, cols), shares.dtype),
            pltpu.VMEM((far, rows, cols), jnp.float32),
            pltpu.VMEM((far - 1, rows, cols), jnp.float32),
            pltpu.SemaphoreType.DMA,
            pltpu.SemaphoreType.DMA((near - 1, pieces)),
            pltpu.SemaphoreType.DMA((near - 1, pieces)),
            pltpu.SemaphoreType.DMA((far - 1, pieces)),
            pltpu.SemaphoreType.DMA((far - 1, pieces)),
        ],
        compiler_params=pltpu.CompilerParams(
            collective_id=1, has_side_effects=True, vmem_limit_bytes=40 << 20
        ),
        name="reduce_shares",
    )(shares.reshape(far, near, rows, cols))


def body(event_bins, event_weights, nominal, background, observed):
    owners = lax.axis_size("bins")
    groups_count = lax.axis_size("params")
    events = event_bins.shape[0]
    width_g = event_weights.shape[1]
    bins_dev = background.shape[0]
    capacity = 3 * events // (2 * owners)
    slot = -(-capacity // ALIGN) * ALIGN + ALIGN
    chunks = 2 if width_g % 512 == 0 else 1
    width = width_g // chunks
    block = math.gcd(width, 256)

    destination = event_bins // bins_dev
    targets = jnp.arange(owners, dtype=jnp.int32)
    before = jnp.sum((destination[None, :] < targets[:, None]).astype(jnp.int32), axis=1)
    starts = jnp.minimum(before // ALIGN, (events - slot) // ALIGN)

    table = jnp.stack([event_bins.astype(jnp.float32), nominal.astype(jnp.float32)])
    table = jnp.concatenate([table, jnp.zeros((6, events), jnp.float32)], axis=0)
    meta = pack_meta(starts, table, slot, bins_dev)
    got_meta = lax.all_to_all(meta, "bins", split_axis=0, concat_axis=0, tiled=True)
    local = got_meta[:, 0].astype(jnp.int32).reshape(1, owners * slot)
    got_nominal = got_meta[:, 1].astype(jnp.bfloat16).reshape(owners * slot, 1)
    got_nominal = jnp.broadcast_to(got_nominal, (owners * slot, 128))
    nominal_sum = histogram_of(local, got_nominal, bins_dev, 128, jnp.float32)[:, 0]
    yields = background + nominal_sum
    curvature = observed / (yields * yields)

    parts = []
    for c in range(chunks):
        packed = pack(starts, event_weights, slot, c * width, width)
        got = lax.all_to_all(packed, "bins", split_axis=0, concat_axis=0, tiled=True)
        got = got.reshape(owners * slot, width)
        parts.append(histogram_of(local, got, bins_dev, block, jnp.bfloat16))
    templates = jnp.concatenate(parts, axis=1)
    weighted = (curvature[:, None] * templates.astype(jnp.float32)).astype(jnp.bfloat16)
    pieces = [templates]
    for shift_by in range(1, groups_count // 2 + 1):
        shifted = [from_behind(part, "params", -shift_by) for part in parts]
        pieces.append(jnp.concatenate(shifted, axis=1))
    partners = jnp.concatenate(pieces, axis=1)
    dims = (((0,), (0,)), ((), ()))
    full = lax.dot_general(weighted, partners, dims, preferred_element_type=jnp.float32)
    full = full.astype(jnp.bfloat16)
    shares = full.reshape(owners, width_g // owners, full.shape[1])
    summed = reduce_shares(shares)
    return summed * (1.0 / (bins_dev * owners))


LANES = 128
TILE = 256


def shift(value, pairs):
    return lax.ppermute(value, "bins", pairs)


def xor_of(a, b, count):
    total, bit = 0, 1
    while bit < count:
        total = total + bit * lax.rem(a // bit + b // bit, 2)
        bit *= 2
    return total


def diagonal():
    rows = lax.broadcasted_iota(jnp.int32, (LANES, LANES), 0)
    return rows == lax.broadcasted_iota(jnp.int32, (LANES, LANES), 1)


def slots_kernel(bins_dev, starts_ref, table_ref, out_ref):
    owners = starts_ref.shape[0]
    slot = out_ref.shape[1]
    events = table_ref.shape[1]
    table = table_ref[...]

    @pl.loop(0, owners)
    def _(o):
        start = starts_ref[o] * 16
        turned = pltpu.roll(table, lax.rem(events - start, events), axis=1)
        bins = turned[0:1, :slot] - (o * bins_dev).astype(jnp.float32)
        inside = (bins >= 0) & (bins < bins_dev)
        out_ref[pl.ds(o, 1), :] = jnp.where(inside, bins, -1.0)
        out_ref[pl.ds(owners + o, 1), :] = turned[1:2, :slot]


def slots_of(starts, table, slot, bins_dev):
    return pl.pallas_call(
        functools.partial(slots_kernel, bins_dev),
        out_shape=jax.ShapeDtypeStruct((2 * starts.shape[0], slot), jnp.float32),
        in_specs=[
            pl.BlockSpec(memory_space=pltpu.SMEM),
            pl.BlockSpec(memory_space=pltpu.VMEM),
        ],
        out_specs=pl.BlockSpec(memory_space=pltpu.VMEM),
        name="slots",
    )(starts, table)


def chain_kernel(
    near, far, chunks, pieces, slot, starts_ref, local_ref, worth_ref, data_ref, weights_ref, *refs
):
    firsts = refs[:near]
    out_ref, curve_ref = refs[near : near + 2]
    rows_refs = refs[near + 2 : near + 2 + chunks]
    (
        heads, sums, got_sums, got_data, levels,
        head_sem, head_keep, sums_send, sums_recv, data_send, data_recv,
        window, acc, own, send_q, send_s, got_q, got_s,
        row_sem, row_send, row_recv, q_send, q_recv, s_send, s_recv,
        own_sem, side_send, side_recv, pair_send, pair_recv,
    ) = refs[near + 2 + chunks :]
    owners = near * far
    here = lax.axis_index("bins")
    core = lax.axis_index("params")
    z, me = here // near, lax.rem(here, near)
    bins_dev = own.shape[1] // near
    width = chunks * LANES
    held = near // pieces
    size = held * bins_dev
    direct = [d for d in range(1, near) if near != 4 or d != 3]

    def side(d):
        return z * near + xor_of(me, d, near)

    def along(way):
        return (z + 1 - 2 * way) * near + me

    def peer(k):
        return lax.rem(z + k, far)

    barrier = pltpu.get_barrier_semaphore()
    for d in range(1, near):
        pl.semaphore_signal(barrier, inc=1, device_id={"bins": side(d)}, device_id_type=MESH)
    for k in range(1, far):
        pl.semaphore_signal(
            barrier, inc=1, device_id={"bins": peer(k) * near + me}, device_id_type=MESH
        )
    pl.semaphore_signal(barrier, inc=1, device_id={"params": 1 - core}, device_id_type=MESH)
    pl.semaphore_wait(barrier, near + far - 1)

    events = weights_ref.shape[0]
    ahead = firsts[0].shape[0]
    lower = (z < far // 2).astype(jnp.int32)
    head_start = lower * (events - ahead)
    rest_start = (1 - lower) * ahead

    def quarter(d, c):
        start = xor_of(me, d, near) * width + c * LANES
        return pl.ds(pl.multiple_of(start, LANES), LANES)

    def row_part(c):
        if c > 0:
            return pl.ds(0, events)
        return pl.ds(pl.multiple_of(rest_start, 16), events - ahead)

    def row_copy(c, d):
        return pltpu.make_async_remote_copy(
            src_ref=weights_ref.at[row_part(c), quarter(d, c)],
            dst_ref=rows_refs[c].at[d, row_part(c), :],
            send_sem=row_send.at[c, d],
            recv_sem=row_recv.at[c, d],
            device_id={"bins": side(d)},
            device_id_type=MESH,
        )

    def row_local(c):
        return pltpu.make_async_copy(
            weights_ref.at[row_part(c), quarter(0, c)],
            rows_refs[c].at[0, row_part(c), :],
            row_sem.at[c],
        )

    def head_local(d):
        return pltpu.make_async_copy(firsts[d], heads.at[d], head_sem.at[d])

    def head_stay(d):
        part = pl.ds(pl.multiple_of(head_start, 16), ahead)
        return pltpu.make_async_copy(firsts[d], rows_refs[0].at[d, part, :], head_keep.at[d])

    def sums_copy(k):
        lines_from = pl.ds(pl.multiple_of(peer(k) * curve_ref.shape[0], 8), curve_ref.shape[0])
        return pltpu.make_async_remote_copy(
            src_ref=sums.at[lines_from, :],
            dst_ref=got_sums.at[k - 1],
            send_sem=sums_send.at[k - 1],
            recv_sem=sums_recv.at[k - 1],
            device_id={"bins": peer(k) * near + me},
            device_id_type=MESH,
        )

    def data_copy(d):
        return pltpu.make_async_remote_copy(
            src_ref=data_ref,
            dst_ref=got_data.at[d - 1],
            send_sem=data_send.at[d - 1],
            recv_sem=data_recv.at[d - 1],
            device_id={"bins": side(d)},
            device_id_type=MESH,
        )

    for d in range(near):
        head_local(d).start()
    for d in range(1, near):
        data_copy(d).start()
    for c in range(chunks):
        for d in range(1, near):
            row_copy(c, d).start()
    for c in range(chunks):
        row_local(c).start()
    for d in range(near):
        head_stay(d).start()

    def nominal_sums():
        @pl.loop(0, owners)
        def _(o):
            @pl.loop(0, bins_dev // TILE)
            def _(k):
                bins = k * TILE + lax.broadcasted_iota(jnp.int32, (TILE, near * slot), 0)
                total = jnp.sum(
                    jnp.where(bins == local_ref[o], worth_ref[o], 0.0), axis=1, keepdims=True
                )
                for h in range(TILE // LANES):
                    part = total[h * LANES : (h + 1) * LANES]
                    line = o * (bins_dev // LANES) + k * (TILE // LANES) + h
                    sums[pl.ds(line, 1), :] = jnp.sum(
                        jnp.where(diagonal(), part, 0.0), axis=0, keepdims=True
                    )
        for k in range(1, far):
            sums_copy(k).start()

    def finish_sums():
        own_lines = pl.ds(pl.multiple_of(z * curve_ref.shape[0], 8), curve_ref.shape[0])
        total = sums[own_lines, :]
        for k in range(1, far):
            sums_copy(k).wait_recv()
            total += got_sums[k - 1]
        lines_dev = bins_dev // LANES
        levels[0, pl.ds(pl.multiple_of(me * lines_dev, 8), lines_dev), :] = data_ref[0:lines_dev, :]
        levels[1, pl.ds(pl.multiple_of(me * lines_dev, 8), lines_dev), :] = data_ref[
            lines_dev : 2 * lines_dev, :
        ]
        for d in range(1, near):
            data_copy(d).wait_recv()
            part = pl.ds(pl.multiple_of(xor_of(me, d, near) * lines_dev, 8), lines_dev)
            levels[0, part, :] = got_data[d - 1, 0:lines_dev, :]
            levels[1, part, :] = got_data[d - 1, lines_dev : 2 * lines_dev, :]
        yields = levels[0] + total
        curve_ref[...] = levels[1] / (yields * yields)

    def chain_copies(way, c, r, p):
        return [
            pltpu.make_async_remote_copy(
                src_ref=source.at[way, c, r - 1, p],
                dst_ref=target.at[way, c, r - 1, p],
                send_sem=sent.at[way, c, r - 1, p],
                recv_sem=landed.at[way, c, r - 1, p],
                device_id={"bins": along(way)},
                device_id_type=MESH,
            )
            for source, target, sent, landed in (
                (send_q, got_q, q_send, q_recv), (send_s, got_s, s_send, s_recv)
            )
        ]

    def fold(c, plane, p, inputs, finish, early=False):
        @pl.loop(0, held)
        def _(i):
            owner = plane * near + p * held + i
            for s in range(near):
                start = starts_ref[s * owners + owner]
                if early:
                    start = jnp.maximum(start - lower * ((events - ahead) // 16), 0)
                    part = heads[s, pl.ds(start * 16, slot), :]
                else:
                    part = rows_refs[c][s, pl.ds(start * 16, slot), :]
                window[s * slot : (s + 1) * slot, :] = part

            @pl.loop(0, bins_dev // TILE)
            def _(k):
                bins = k * TILE + lax.broadcasted_iota(jnp.int32, (TILE, near * slot), 0)
                hot = (bins == local_ref[owner]).astype(jnp.bfloat16)
                acc[...] = jnp.dot(hot, window[...], preferred_element_type=jnp.float32)
                base = i * (bins_dev // LANES) + k * (TILE // LANES)
                eye = diagonal()
                for way, r, has in inputs:
                    @pl.when(has)
                    def _():
                        for h in range(TILE // LANES):
                            line = base + h
                            part = pl.ds(pl.multiple_of(line * LANES, LANES), LANES)
                            step = got_s[way, c, r - 1, p, pl.ds(line, 1), :]
                            step = jnp.sum(jnp.where(eye, step, 0.0), axis=1, keepdims=True)
                            coded = got_q[way, c, r - 1, p, part, :].astype(jnp.int32)
                            acc[h * LANES : (h + 1) * LANES, :] += (
                                coded.astype(jnp.float32) * step
                            )
                for h in range(TILE // LANES):
                    line = base + h
                    part = pl.ds(pl.multiple_of(line * LANES, LANES), LANES)
                    finish(acc[h * LANES : (h + 1) * LANES, :], line, part, eye)

    def wait_chain(way, c, r, p):
        for copy in chain_copies(way, c, r, p):
            copy.wait_recv()

    def rounds(c, p, first, last, when, early=False):
        @pl.loop(first, last)
        def _(r):
            for way in range(2):
                step_in = z if way == 0 else far - 1 - z

                @pl.when(when(step_in, r))
                def _():
                    inputs = []
                    if when is not at_end:
                        has = step_in > 0
                        inputs = [(way, r - 1, has)]

                        @pl.when(has)
                        def _():
                            wait_chain(way, c, r - 1, p)

                    def code(value, line, part, eye):
                        most = jnp.max(jnp.abs(value), axis=1, keepdims=True)
                        wide = most * (2.0**23 + 1.0)
                        step = (wide + (most - wide)) * 2.0**-14
                        factor = jnp.where(most > 1e-30, 1.0 / step, 0.0)
                        coded = jnp.round(value * factor).astype(jnp.int32)
                        send_q[way, c, r - 1, p, part, :] = coded.astype(send_q.dtype)
                        send_s[way, c, r - 1, p, pl.ds(line, 1), :] = jnp.sum(
                            jnp.where(eye, step, 0.0), axis=0, keepdims=True
                        )

                    plane = z + (far - r) * (1 - 2 * way)
                    fold(c, plane, p, inputs, code, early)
                    for copy in chain_copies(way, c, r, p):
                        copy.start()

    def at_end(step_in, r):
        return step_in == 0

    def inside(step_in, r):
        return (step_in < r) & ((step_in > 0) | (r == far - 1))

    def rows_part(p):
        return pl.ds(pl.multiple_of(p * size, size), size)

    def side_copy(c, d, p, source=0, hop=None):
        hop = d if hop is None else hop
        origin = own.at[c] if source == 0 else out_ref.at[0, source, c]
        return pltpu.make_async_remote_copy(
            src_ref=origin.at[rows_part(p), :],
            dst_ref=out_ref.at[0, d, c, rows_part(p), :],
            send_sem=side_send.at[c, d, p],
            recv_sem=side_recv.at[c, d, p],
            device_id={"bins": side(hop)},
            device_id_type=MESH,
        )

    def pair_copy(c, d, p):
        source = own.at[c] if d == 0 else out_ref.at[0, d, c]
        return pltpu.make_async_remote_copy(
            src_ref=source.at[rows_part(p), :],
            dst_ref=out_ref.at[1, d, c, rows_part(p), :],
            send_sem=pair_send.at[c, d, p],
            recv_sem=pair_recv.at[c, d, p],
            device_id={"params": 1 - core},
            device_id_type=MESH,
        )

    def keep_copy(c, p):
        return pltpu.make_async_copy(
            own.at[c, rows_part(p), :], out_ref.at[0, 0, c, rows_part(p), :], own_sem.at[c, p]
        )

    def finish(c, p):
        @pl.when(z > 0)
        def _():
            wait_chain(0, c, far - 1, p)

        @pl.when(z < far - 1)
        def _():
            wait_chain(1, c, far - 1, p)

        def store(value, line, part, eye):
            row = pl.ds(pl.multiple_of(p * size + line * LANES, LANES), LANES)
            own[c, row, :] = value.astype(own.dtype)

        fold(c, z, p, [(0, far - 1, z > 0), (1, far - 1, z < far - 1)], store)
        for d in direct:
            side_copy(c, d, p).start()
        pair_copy(c, 0, p).start()
        keep_copy(c, p).start()

    def forward(c, p, act):
        if near == 4:
            @pl.when(lax.rem(p, 2) == 0)
            def _():
                act(side_copy(c, 3, p, 1, 2))

            @pl.when(lax.rem(p, 2) == 1)
            def _():
                act(side_copy(c, 3, p, 2, 1))

    def relay(u):
        @pl.when(u >= 0)
        def _():
            c, p = jnp.maximum(u, 0) // pieces, lax.rem(jnp.maximum(u, 0), pieces)
            for d in direct:
                side_copy(c, d, p).wait_recv()
            forward(c, p, lambda copy: copy.start())
            for d in direct:
                pair_copy(c, d, p).start()

    def relay_last(u):
        @pl.when(u >= 0)
        def _():
            c, p = jnp.maximum(u, 0) // pieces, lax.rem(jnp.maximum(u, 0), pieces)
            for d in range(1, near):
                if d not in direct:
                    side_copy(c, d, p).wait_recv()
                    pair_copy(c, d, p).start()

    for d in range(near):
        head_local(d).wait()

    @pl.loop(0, pieces)
    def _(p):
        rounds(0, p, 1, 2, at_end, True)

    nominal_sums()
    row_local(0).wait()
    head_stay(0).wait()
    for d in range(1, near):
        head_stay(d).wait()
        row_copy(0, d).wait_recv()
    for c in range(chunks):
        if c > 0:
            row_local(c).wait()
            for d in range(1, near):
                row_copy(c, d).wait_recv()
        rounds(c, 0, 2 if c == 0 else 1, far - 1, at_end)
        if c > 0:
            finish(c - 1, pieces - 1)
        rounds(c, 0, 2, far, inside)
        if c > 0:
            relay(jnp.int32(c * pieces - 2))
            relay_last(jnp.int32(c * pieces - 3))

        @pl.loop(1, pieces)
        def _(p):
            rounds(c, p, 2 if c == 0 else 1, far - 1, at_end)
            finish(c, p - 1)
            rounds(c, p, 2, far, inside)
            relay(c * pieces + p - 2)
            relay_last(c * pieces + p - 3)
        if c == 0:
            finish_sums()
    finish(chunks - 1, pieces - 1)
    units = chunks * pieces
    relay(jnp.int32(units - 2))
    relay_last(jnp.int32(units - 3))
    relay(jnp.int32(units - 1))
    relay_last(jnp.int32(units - 2))
    relay_last(jnp.int32(units - 1))

    for k in range(1, far):
        sums_copy(k).wait_send()
    for d in range(1, near):
        data_copy(d).wait_send()
    for c in range(chunks):
        for d in range(1, near):
            row_copy(c, d).wait_send()

        @pl.loop(0, pieces)
        def _(p):
            keep_copy(c, p).wait()
            for d in direct:
                side_copy(c, d, p).wait_send()
            forward(c, p, lambda copy: copy.wait_send())
            for d in range(near):
                pair_copy(c, d, p).wait_send()
                pair_copy(c, d, p).wait_recv()

            @pl.loop(1, far)
            def _(r):
                for way in range(2):
                    step_in = z if way == 0 else far - 1 - z

                    @pl.when(step_in < r)
                    def _():
                        for copy in chain_copies(way, c, r, p):
                            copy.wait_send()


def chain(starts, local, worth, data, weights, firsts, near, far, chunks, slot, bins_dev):
    events = weights.shape[0]
    ahead = firsts[0].shape[0]
    pieces = near
    bins = near * bins_dev
    size = bins // pieces
    hops = (2, chunks, far - 1, pieces)
    lines = bins // LANES
    dma = pltpu.SemaphoreType.DMA
    rows = jnp.bfloat16
    table = jnp.float32
    return pl.pallas_call(
        functools.partial(chain_kernel, near, far, chunks, pieces, slot),
        out_shape=[
            jax.ShapeDtypeStruct((2, near, chunks, bins, LANES), rows),
            jax.ShapeDtypeStruct((lines, LANES), table),
        ],
        in_specs=[pl.BlockSpec(memory_space=pltpu.SMEM)]
        + [pl.BlockSpec(memory_space=pltpu.VMEM)] * 3
        + [pl.BlockSpec(memory_space=pl.ANY)] * (1 + near),
        out_specs=[
            pl.BlockSpec(memory_space=pl.ANY),
            pl.BlockSpec(memory_space=pltpu.VMEM),
        ],
        scratch_shapes=[pltpu.VMEM((near, events, LANES), rows)] * chunks
        + [
            pltpu.VMEM((near, ahead, LANES), rows),
            pltpu.VMEM((far * lines, LANES), table),
            pltpu.VMEM((far - 1, lines, LANES), table),
            pltpu.VMEM((near - 1,) + data.shape, table),
            pltpu.VMEM((2, lines, LANES), table),
            dma((near,)),
            dma((near,)),
            dma((far - 1,)),
            dma((far - 1,)),
            dma((near - 1,)),
            dma((near - 1,)),
            pltpu.VMEM((near * slot, LANES), rows),
            pltpu.VMEM((TILE, LANES), table),
            pltpu.VMEM((chunks, bins, LANES), rows),
            pltpu.VMEM(hops + (size, LANES), jnp.int16),
            pltpu.VMEM(hops + (size // LANES, LANES), table),
            pltpu.VMEM(hops + (size, LANES), jnp.int16),
            pltpu.VMEM(hops + (size // LANES, LANES), table),
            dma((chunks,)),
            dma((chunks, near)),
            dma((chunks, near)),
            dma(hops),
            dma(hops),
            dma(hops),
            dma(hops),
            dma((chunks, pieces)),
            dma((chunks, near, pieces)),
            dma((chunks, near, pieces)),
            dma((chunks, near, pieces)),
            dma((chunks, near, pieces)),
        ],
        compiler_params=pltpu.CompilerParams(
            collective_id=3, has_side_effects=True, vmem_limit_bytes=62 << 20
        ),
        name="chain",
    )(starts, local, worth, data, weights, *firsts)


def tail_kernel(
    near, far, templates_ref, curve_ref, out_ref, held, weighted, total, coded, own, got,
    sems, sends, recvs,
):
    groups, _, chunks, bins, _ = templates_ref.shape
    here = lax.axis_index("bins")
    z, me = here // near, lax.rem(here, near)
    piece = own.shape[0]
    count = groups * near * chunks
    step = 2 * LANES
    depth = 4 * LANES

    def peer(k):
        return lax.rem(z + k, far)

    barrier = pltpu.get_barrier_semaphore()
    for k in range(1, far):
        pl.semaphore_signal(
            barrier, inc=1, device_id={"bins": peer(k) * near + me}, device_id_type=MESH
        )

    def fetch(n):
        part = templates_ref.at[n // (near * chunks), lax.rem(n // chunks, near), lax.rem(n, chunks)]
        return pltpu.make_async_copy(
            part, held.at[:, pl.ds(pl.multiple_of(n * LANES, LANES), LANES)], sems.at[n]
        )

    @pl.loop(0, count)
    def _(n):
        fetch(n).start()

    pl.semaphore_wait(barrier, far - 1)
    rows = lax.broadcasted_iota(jnp.int32, (piece, LANES), 0) + me * piece
    lanes = lax.broadcasted_iota(jnp.int32, (piece, LANES), 1)

    @pl.loop(0, near * chunks)
    def _(n):
        fetch(n).wait()

    @pl.loop(0, bins // depth)
    def _(b):
        eye = diagonal()
        curves = []
        for h in range(depth // LANES):
            line = curve_ref[pl.ds(b * (depth // LANES) + h, 1), :]
            curves.append(jnp.sum(jnp.where(eye, line, 0.0), axis=1, keepdims=True))
        curve = jnp.concatenate(curves, axis=0)
        part = pl.ds(pl.multiple_of(b * depth, depth), depth)
        for d in range(near):
            picked = 0.0
            for c in range(chunks):
                pick = (rows == lanes + c * LANES).astype(jnp.bfloat16)
                columns = slice((d * chunks + c) * LANES, (d * chunks + c + 1) * LANES)
                value = curve * held[part, columns].astype(jnp.float32)
                picked += lax.dot_general(
                    pick, value.astype(jnp.bfloat16), (((1,), (1,)), ((), ())),
                    preferred_element_type=jnp.float32,
                )
            weighted[d * piece : (d + 1) * piece, part] = picked.astype(weighted.dtype)

    def rows_for(target):
        return pl.ds(pl.multiple_of(xor_of(me, target, near) * piece, 16), piece)

    def columns_of(n):
        return pl.ds(pl.multiple_of(n * step, step), step)

    def copy(k, n):
        return pltpu.make_async_remote_copy(
            src_ref=coded.at[rows_for(peer(k)), columns_of(n)],
            dst_ref=got.at[k - 1, :, columns_of(n)],
            send_sem=sends.at[k - 1, n],
            recv_sem=recvs.at[k - 1, n],
            device_id={"bins": peer(k) * near + me},
            device_id_type=MESH,
        )

    @pl.loop(0, count // 2)
    def _(n):
        @pl.when(n >= near * chunks // 2)
        def _():
            fetch(2 * n).wait()
            fetch(2 * n + 1).wait()

        total[...] = jnp.dot(
            weighted[...], held[:, columns_of(n)], preferred_element_type=jnp.float32
        )
        coded[:, columns_of(n)] = total[...].astype(coded.dtype)
        own[:, columns_of(n)] = total[rows_for(z), :]
        for k in range(1, far):
            copy(k, n).start()

    @pl.loop(0, count // 2)
    def _(n):
        for k in range(1, far):
            copy(k, n).wait_recv()
        for half in range(2):
            place = 2 * n + half
            group = place // (near * chunks)
            d = lax.rem(place // chunks, near)
            start = ((group * near + xor_of(me, d, near)) * chunks + lax.rem(place, chunks)) * LANES
            part = pl.ds(pl.multiple_of(place * LANES, LANES), LANES)
            value = own[:, part]
            for k in range(1, far):
                value += got[k - 1, :, part].astype(jnp.float32)
            out_ref[:, pl.ds(pl.multiple_of(start, LANES), LANES)] = value

    @pl.loop(0, count // 2)
    def _(n):
        for k in range(1, far):
            copy(k, n).wait_send()


def tail(templates, curve, near, far):
    groups, _, chunks, bins, _ = templates.shape
    piece = chunks * LANES // far
    columns = groups * near * chunks * LANES
    count = groups * near * chunks
    return pl.pallas_call(
        functools.partial(tail_kernel, near, far),
        out_shape=jax.ShapeDtypeStruct((piece, columns), jnp.float32),
        in_specs=[pl.BlockSpec(memory_space=pl.ANY), pl.BlockSpec(memory_space=pltpu.VMEM)],
        out_specs=pl.BlockSpec(memory_space=pltpu.VMEM),
        scratch_shapes=[
            pltpu.VMEM((bins, columns), jnp.bfloat16),
            pltpu.VMEM((near * piece, bins), jnp.bfloat16),
            pltpu.VMEM((near * piece, 2 * LANES), jnp.float32),
            pltpu.VMEM((near * piece, columns), jnp.bfloat16),
            pltpu.VMEM((piece, columns), jnp.float32),
            pltpu.VMEM((far - 1, piece, columns), jnp.bfloat16),
            pltpu.SemaphoreType.DMA((count,)),
            pltpu.SemaphoreType.DMA((far - 1, count // 2)),
            pltpu.SemaphoreType.DMA((far - 1, count // 2)),
        ],
        compiler_params=pltpu.CompilerParams(
            collective_id=2, has_side_effects=True, vmem_limit_bytes=60 << 20
        ),
        name="tail",
    )(templates, curve)


def body_by_parameters(event_bins, event_weights, nominal, background, observed):
    owners = lax.axis_size("bins")
    near = math.isqrt(owners)
    far = owners // near
    events = event_bins.shape[0]
    bins_dev = background.shape[0]
    width = event_weights.shape[1] // near
    chunks = width // LANES
    capacity = 3 * events // (2 * owners)
    slot = -(-capacity // 16) * 16 + 16
    ahead = min(-(-near * capacity // 16) * 16 + 16, events - 16)
    here = lax.axis_index("bins")
    z, me = here // near, lax.rem(here, near)
    around = [[(s, s // near * near + (s % near ^ d)) for s in range(owners)] for d in range(near)]

    def spread(value):
        return [value] + [shift(value, around[d]) for d in range(1, near)]

    marks = jnp.arange(owners * bins_dev // TILE + 1, dtype=jnp.int32) * TILE
    lows = jnp.sum((event_bins[None, :] < marks[:, None]).astype(jnp.int32), axis=1)
    starts = jnp.minimum(lows[: -1 : bins_dev // TILE] // 16, (events - slot) // 16)
    table = jnp.stack([event_bins.astype(jnp.float32), nominal.astype(jnp.float32)])
    table = jnp.concatenate([table, jnp.zeros((6, events), jnp.float32)])
    places = slots_of(starts, table, slot, bins_dev)
    line = jnp.pad(starts.astype(jnp.float32), (0, slot - owners)).reshape(1, slot)
    places = jnp.stack(spread(jnp.concatenate([places, line])))

    firsts = []
    first_row = jnp.where(z < far // 2, events - ahead, 0)
    for d in range(near):
        corner = (first_row, (me ^ d) * width)
        part = lax.dynamic_slice(event_weights, corner, (ahead, LANES))
        firsts.append(part if d == 0 else shift(part, around[d]))

    starts = places[:, 2 * owners, :owners].astype(jnp.int32).reshape(-1)
    places = places[:, : 2 * owners].transpose(1, 0, 2).reshape(2 * owners, 1, near * slot)
    worth = places[owners:]
    places = places[:owners].astype(jnp.int32)
    data = jnp.concatenate([background, observed]).reshape(-1, LANES)
    templates, curve = chain(
        starts, places, worth, data, event_weights, firsts, near, far, chunks, slot, bins_dev
    )
    summed = tail(templates, curve, near, far)
    return summed * (1.0 / (bins_dev * owners))


def splits_by_parameters(mesh, event_bins, event_weights, background):
    owners, groups = mesh.shape["bins"], mesh.shape["params"]
    near = math.isqrt(owners)
    events = event_bins.shape[0] // owners
    width = event_weights.shape[1] // groups // max(near, 1)
    bins_dev = background.shape[0] // owners
    return (
        groups == 2
        and near >= 4
        and near * near == owners
        and near & (near - 1) == 0
        and width % LANES == 0
        and width % (16 * near) == 0
        and events % LANES == 0
        and events >= 2 * LANES
        and bins_dev % (8 * LANES) == 0
    )


def solution(mesh):
    in_specs = (P("bins"), P("bins", "params"), P("bins"), P("bins"), P("bins"))
    out_specs = P(("params", "bins"), None)

    def run(event_bins, event_weights, nominal, background, observed):
        fits = splits_by_parameters(mesh, event_bins, event_weights, background)
        chosen = body_by_parameters if fits else body
        mapped = jax.shard_map(
            chosen, mesh=mesh, in_specs=in_specs, out_specs=out_specs, check_vma=False
        )
        return mapped(event_bins, event_weights, nominal, background, observed)

    return run
```

```python
import functools
import math

import jax
import jax.numpy as jnp
from jax import lax
from jax.experimental import pallas as pl
from jax.experimental.pallas import tpu as pltpu
from jax.sharding import PartitionSpec as P

ALIGN = 8
MESH = pl.DeviceIdType.MESH


def from_behind(value, axis, steps):
    count = lax.axis_size(axis)
    pairs = [(source, (source + steps) % count) for source in range(count)]
    return lax.ppermute(value, axis, pairs)


def pack_kernel(owners, slot, first, width, starts_ref, rows_ref, out_ref, held, in_sems, out_sems):
    def fetch(o):
        start = pl.multiple_of(starts_ref[o] * ALIGN, ALIGN)
        return pltpu.make_async_copy(
            rows_ref.at[pl.ds(start, slot), pl.ds(first, width)], held.at[o], in_sems.at[o]
        )

    def store(o):
        return pltpu.make_async_copy(held.at[o], out_ref.at[o], out_sems.at[o])

    @pl.loop(0, owners)
    def _(o):
        fetch(o).start()

    @pl.loop(0, owners)
    def _(o):
        fetch(o).wait()
        store(o).start()

    @pl.loop(0, owners)
    def _(o):
        store(o).wait()


def pack(starts, rows, slot, first, width):
    owners = starts.shape[0]
    return pl.pallas_call(
        functools.partial(pack_kernel, owners, slot, first, width),
        out_shape=jax.ShapeDtypeStruct((owners, slot, width), rows.dtype),
        in_specs=[
            pl.BlockSpec(memory_space=pltpu.SMEM),
            pl.BlockSpec(memory_space=pl.ANY),
        ],
        out_specs=pl.BlockSpec(memory_space=pl.ANY),
        scratch_shapes=[
            pltpu.VMEM((owners, slot, width), rows.dtype),
            pltpu.SemaphoreType.DMA((owners,)),
            pltpu.SemaphoreType.DMA((owners,)),
        ],
        compiler_params=pltpu.CompilerParams(vmem_limit_bytes=32 << 20),
        cost_estimate=pl.CostEstimate(
            flops=0, bytes_accessed=4 * owners * slot * width, transcendentals=0
        ),
        name="pack",
    )(starts, rows)


def meta_kernel(bins_dev, starts_ref, table_ref, out_ref):
    owners, _, slot = out_ref.shape
    events = table_ref.shape[1]
    table = table_ref[...]

    @pl.loop(0, owners)
    def _(o):
        start = starts_ref[o] * ALIGN
        turned = pltpu.roll(table, lax.rem(events - start, events), axis=1)[:, :slot]
        bins = turned[0:1] - (o * bins_dev).astype(jnp.float32)
        inside = (bins >= 0) & (bins < bins_dev)
        out_ref[o, 0:1, :] = jnp.where(inside, bins, -1.0)
        out_ref[o, 1:2, :] = turned[1:2]


def pack_meta(starts, table, slot, bins_dev):
    owners = starts.shape[0]
    return pl.pallas_call(
        functools.partial(meta_kernel, bins_dev),
        out_shape=jax.ShapeDtypeStruct((owners, 2, slot), jnp.float32),
        in_specs=[
            pl.BlockSpec(memory_space=pltpu.SMEM),
            pl.BlockSpec(memory_space=pltpu.VMEM),
        ],
        out_specs=pl.BlockSpec(memory_space=pltpu.VMEM),
        name="pack_meta",
    )(starts, table)


def hist_kernel(chunk, tile, local_ref, rows_ref, out_ref, hot):
    bins, total = hot.shape

    @pl.when(pl.program_id(0) == 0)
    def _():
        ids = lax.broadcasted_iota(jnp.int32, (bins, chunk), 0)

        @pl.loop(0, total // chunk)
        def _(k):
            part = pl.ds(pl.multiple_of(k * chunk, chunk), chunk)
            hot[:, part] = (ids == local_ref[:, part]).astype(jnp.bfloat16)

    @pl.loop(0, bins // tile)
    def _(m):
        part = pl.ds(pl.multiple_of(m * tile, tile), tile)
        out_ref[part, :] = jnp.dot(
            hot[part, :], rows_ref[...], preferred_element_type=jnp.float32
        ).astype(out_ref.dtype)


def histogram_of(local, rows, bins, block, dtype):
    total, width = rows.shape
    return pl.pallas_call(
        functools.partial(hist_kernel, math.gcd(total, 128), math.gcd(bins, 256)),
        grid=(width // block,),
        out_shape=jax.ShapeDtypeStruct((bins, width), dtype),
        in_specs=[
            pl.BlockSpec((1, total), lambda j: (0, 0)),
            pl.BlockSpec((total, block), lambda j: (0, j)),
        ],
        out_specs=pl.BlockSpec((bins, block), lambda j: (0, j)),
        scratch_shapes=[pltpu.VMEM((bins, total), jnp.bfloat16)],
        compiler_params=pltpu.CompilerParams(
            vmem_limit_bytes=40 << 20, dimension_semantics=("arbitrary",)
        ),
        cost_estimate=pl.CostEstimate(
            flops=2 * bins * total * width, bytes_accessed=2 * total * width, transcendentals=0
        ),
        name="histogram",
    )(local, rows)


def reduce_kernel(
    piece, shares_ref, out_ref, own, got_near, sums, got_far,
    own_sem, near_send, near_recv, far_send, far_recv,
):
    far, near, rows, _ = shares_ref.shape
    me = lax.axis_index("bins")
    f, n = me // near, lax.rem(me, near)

    def near_peer(d):
        return lax.rem(n + d, near)

    def far_peer(d):
        return lax.rem(f + d, far)

    barrier = pltpu.get_barrier_semaphore()
    for d in range(1, near):
        pl.semaphore_signal(
            barrier, inc=1, device_id={"bins": f * near + near_peer(d)}, device_id_type=MESH
        )
    for d in range(1, far):
        pl.semaphore_signal(
            barrier, inc=1, device_id={"bins": far_peer(d) * near + n}, device_id_type=MESH
        )
    pl.semaphore_wait(barrier, near + far - 2)

    def part_of(c):
        return pl.ds(pl.multiple_of(c * piece, piece), piece)

    def near_copy(d, c):
        return pltpu.make_async_remote_copy(
            src_ref=shares_ref.at[:, near_peer(d), part_of(c), :],
            dst_ref=got_near.at[d - 1, :, part_of(c), :],
            send_sem=near_send.at[d - 1, c],
            recv_sem=near_recv.at[d - 1, c],
            device_id={"bins": f * near + near_peer(d)},
            device_id_type=MESH,
        )

    def far_copy(d, c):
        return pltpu.make_async_remote_copy(
            src_ref=sums.at[far_peer(d), part_of(c), :],
            dst_ref=got_far.at[d - 1, part_of(c), :],
            send_sem=far_send.at[d - 1, c],
            recv_sem=far_recv.at[d - 1, c],
            device_id={"bins": far_peer(d) * near + n},
            device_id_type=MESH,
        )

    own_copy = pltpu.make_async_copy(shares_ref.at[:, n], own, own_sem)
    own_copy.start()
    pieces = rows // piece

    @pl.loop(0, pieces)
    def _(c):
        for d in range(1, near):
            near_copy(d, c).start()

    own_copy.wait()

    @pl.loop(0, pieces)
    def _(c):
        part = part_of(c)
        for d in range(1, near):
            near_copy(d, c).wait_recv()

        @pl.loop(0, far)
        def _(k):
            total = own[k, part, :].astype(jnp.float32)
            for d in range(1, near):
                total += got_near[d - 1, k, part, :].astype(jnp.float32)
            sums[k, part, :] = total

        for d in range(1, far):
            far_copy(d, c).start()

    @pl.loop(0, pieces)
    def _(c):
        part = part_of(c)
        for d in range(1, far):
            far_copy(d, c).wait_recv()
        total = sums[f, part, :]
        for d in range(1, far):
            total += got_far[d - 1, part, :]
        out_ref[part, :] = total
        for d in range(1, near):
            near_copy(d, c).wait_send()
        for d in range(1, far):
            far_copy(d, c).wait_send()


def reduce_shares(shares):
    owners, rows, cols = shares.shape
    near = math.isqrt(owners)
    while owners % near:
        near -= 1
    far = owners // near
    piece = 16 if rows % 16 == 0 else rows
    pieces = rows // piece
    return pl.pallas_call(
        functools.partial(reduce_kernel, piece),
        out_shape=jax.ShapeDtypeStruct((rows, cols), jnp.float32),
        in_specs=[pl.BlockSpec(memory_space=pl.ANY)],
        out_specs=pl.BlockSpec(memory_space=pltpu.VMEM),
        scratch_shapes=[
            pltpu.VMEM((far, rows, cols), shares.dtype),
            pltpu.VMEM((near - 1, far, rows, cols), shares.dtype),
            pltpu.VMEM((far, rows, cols), jnp.float32),
            pltpu.VMEM((far - 1, rows, cols), jnp.float32),
            pltpu.SemaphoreType.DMA,
            pltpu.SemaphoreType.DMA((near - 1, pieces)),
            pltpu.SemaphoreType.DMA((near - 1, pieces)),
            pltpu.SemaphoreType.DMA((far - 1, pieces)),
            pltpu.SemaphoreType.DMA((far - 1, pieces)),
        ],
        compiler_params=pltpu.CompilerParams(
            collective_id=1, has_side_effects=True, vmem_limit_bytes=40 << 20
        ),
        name="reduce_shares",
    )(shares.reshape(far, near, rows, cols))


def body(event_bins, event_weights, nominal, background, observed):
    owners = lax.axis_size("bins")
    groups_count = lax.axis_size("params")
    events = event_bins.shape[0]
    width_g = event_weights.shape[1]
    bins_dev = background.shape[0]
    capacity = 3 * events // (2 * owners)
    slot = -(-capacity // ALIGN) * ALIGN + ALIGN
    chunks = 2 if width_g % 512 == 0 else 1
    width = width_g // chunks
    block = math.gcd(width, 256)

    destination = event_bins // bins_dev
    targets = jnp.arange(owners, dtype=jnp.int32)
    before = jnp.sum((destination[None, :] < targets[:, None]).astype(jnp.int32), axis=1)
    starts = jnp.minimum(before // ALIGN, (events - slot) // ALIGN)

    table = jnp.stack([event_bins.astype(jnp.float32), nominal.astype(jnp.float32)])
    table = jnp.concatenate([table, jnp.zeros((6, events), jnp.float32)], axis=0)
    meta = pack_meta(starts, table, slot, bins_dev)
    got_meta = lax.all_to_all(meta, "bins", split_axis=0, concat_axis=0, tiled=True)
    local = got_meta[:, 0].astype(jnp.int32).reshape(1, owners * slot)
    got_nominal = got_meta[:, 1].astype(jnp.bfloat16).reshape(owners * slot, 1)
    got_nominal = jnp.broadcast_to(got_nominal, (owners * slot, 128))
    nominal_sum = histogram_of(local, got_nominal, bins_dev, 128, jnp.float32)[:, 0]
    yields = background + nominal_sum
    curvature = observed / (yields * yields)

    parts = []
    for c in range(chunks):
        packed = pack(starts, event_weights, slot, c * width, width)
        got = lax.all_to_all(packed, "bins", split_axis=0, concat_axis=0, tiled=True)
        got = got.reshape(owners * slot, width)
        parts.append(histogram_of(local, got, bins_dev, block, jnp.bfloat16))
    templates = jnp.concatenate(parts, axis=1)
    weighted = (curvature[:, None] * templates.astype(jnp.float32)).astype(jnp.bfloat16)
    pieces = [templates]
    for shift_by in range(1, groups_count // 2 + 1):
        shifted = [from_behind(part, "params", -shift_by) for part in parts]
        pieces.append(jnp.concatenate(shifted, axis=1))
    partners = jnp.concatenate(pieces, axis=1)
    dims = (((0,), (0,)), ((), ()))
    full = lax.dot_general(weighted, partners, dims, preferred_element_type=jnp.float32)
    full = full.astype(jnp.bfloat16)
    shares = full.reshape(owners, width_g // owners, full.shape[1])
    summed = reduce_shares(shares)
    return summed * (1.0 / (bins_dev * owners))


LANES = 128
TILE = 256


def shift(value, pairs):
    return lax.ppermute(value, "bins", pairs)


def xor_of(a, b, count):
    total, bit = 0, 1
    while bit < count:
        total = total + bit * lax.rem(a // bit + b // bit, 2)
        bit *= 2
    return total


def diagonal():
    rows = lax.broadcasted_iota(jnp.int32, (LANES, LANES), 0)
    return rows == lax.broadcasted_iota(jnp.int32, (LANES, LANES), 1)


def slots_kernel(bins_dev, starts_ref, table_ref, out_ref):
    owners = starts_ref.shape[0]
    slot = out_ref.shape[1]
    events = table_ref.shape[1]
    table = table_ref[...]

    @pl.loop(0, owners)
    def _(o):
        start = starts_ref[o] * 16
        turned = pltpu.roll(table, lax.rem(events - start, events), axis=1)
        bins = turned[0:1, :slot] - (o * bins_dev).astype(jnp.float32)
        inside = (bins >= 0) & (bins < bins_dev)
        out_ref[pl.ds(o, 1), :] = jnp.where(inside, bins, -1.0)
        out_ref[pl.ds(owners + o, 1), :] = turned[1:2, :slot]


def slots_of(starts, table, slot, bins_dev):
    return pl.pallas_call(
        functools.partial(slots_kernel, bins_dev),
        out_shape=jax.ShapeDtypeStruct((2 * starts.shape[0], slot), jnp.float32),
        in_specs=[
            pl.BlockSpec(memory_space=pltpu.SMEM),
            pl.BlockSpec(memory_space=pltpu.VMEM),
        ],
        out_specs=pl.BlockSpec(memory_space=pltpu.VMEM),
        name="slots",
    )(starts, table)


def chain_kernel(
    near, far, chunks, pieces, slot, starts_ref, local_ref, worth_ref, data_ref, weights_ref, *refs
):
    firsts = refs[:near]
    out_ref, curve_ref = refs[near : near + 2]
    rows_refs = refs[near + 2 : near + 2 + chunks]
    (
        heads, sums, got_sums, got_data, levels,
        head_sem, head_keep, sums_send, sums_recv, data_send, data_recv,
        window, acc, own, send_q, send_s, got_q, got_s,
        row_sem, row_send, row_recv, q_send, q_recv, s_send, s_recv,
        own_sem, side_send, side_recv, pair_send, pair_recv,
    ) = refs[near + 2 + chunks :]
    owners = near * far
    here = lax.axis_index("bins")
    core = lax.axis_index("params")
    z, me = here // near, lax.rem(here, near)
    bins_dev = own.shape[1] // near
    width = chunks * LANES
    held = near // pieces
    size = held * bins_dev
    direct = [d for d in range(1, near) if near != 4 or d != 3]

    def side(d):
        return z * near + xor_of(me, d, near)

    def along(way):
        return (z + 1 - 2 * way) * near + me

    def peer(k):
        return lax.rem(z + k, far)

    barrier = pltpu.get_barrier_semaphore()
    for d in range(1, near):
        pl.semaphore_signal(barrier, inc=1, device_id={"bins": side(d)}, device_id_type=MESH)
    for k in range(1, far):
        pl.semaphore_signal(
            barrier, inc=1, device_id={"bins": peer(k) * near + me}, device_id_type=MESH
        )
    pl.semaphore_signal(barrier, inc=1, device_id={"params": 1 - core}, device_id_type=MESH)
    pl.semaphore_wait(barrier, near + far - 1)

    events = weights_ref.shape[0]
    ahead = firsts[0].shape[0]
    lower = (z < far // 2).astype(jnp.int32)
    head_start = lower * (events - ahead)
    rest_start = (1 - lower) * ahead

    def quarter(d, c):
        start = xor_of(me, d, near) * width + c * LANES
        return pl.ds(pl.multiple_of(start, LANES), LANES)

    def row_part(c):
        if c > 0:
            return pl.ds(0, events)
        return pl.ds(pl.multiple_of(rest_start, 16), events - ahead)

    def row_copy(c, d):
        return pltpu.make_async_remote_copy(
            src_ref=weights_ref.at[row_part(c), quarter(d, c)],
            dst_ref=rows_refs[c].at[d, row_part(c), :],
            send_sem=row_send.at[c, d],
            recv_sem=row_recv.at[c, d],
            device_id={"bins": side(d)},
            device_id_type=MESH,
        )

    def row_local(c):
        return pltpu.make_async_copy(
            weights_ref.at[row_part(c), quarter(0, c)],
            rows_refs[c].at[0, row_part(c), :],
            row_sem.at[c],
        )

    def head_local(d):
        return pltpu.make_async_copy(firsts[d], heads.at[d], head_sem.at[d])

    def head_stay(d):
        part = pl.ds(pl.multiple_of(head_start, 16), ahead)
        return pltpu.make_async_copy(firsts[d], rows_refs[0].at[d, part, :], head_keep.at[d])

    def sums_copy(k):
        lines_from = pl.ds(pl.multiple_of(peer(k) * curve_ref.shape[0], 8), curve_ref.shape[0])
        return pltpu.make_async_remote_copy(
            src_ref=sums.at[lines_from, :],
            dst_ref=got_sums.at[k - 1],
            send_sem=sums_send.at[k - 1],
            recv_sem=sums_recv.at[k - 1],
            device_id={"bins": peer(k) * near + me},
            device_id_type=MESH,
        )

    def data_copy(d):
        return pltpu.make_async_remote_copy(
            src_ref=data_ref,
            dst_ref=got_data.at[d - 1],
            send_sem=data_send.at[d - 1],
            recv_sem=data_recv.at[d - 1],
            device_id={"bins": side(d)},
            device_id_type=MESH,
        )

    for d in range(near):
        head_local(d).start()
    for d in range(1, near):
        data_copy(d).start()
    for c in range(chunks):
        for d in range(1, near):
            row_copy(c, d).start()
    for c in range(chunks):
        row_local(c).start()
    for d in range(near):
        head_stay(d).start()

    def nominal_sums():
        @pl.loop(0, owners)
        def _(o):
            @pl.loop(0, bins_dev // TILE)
            def _(k):
                bins = k * TILE + lax.broadcasted_iota(jnp.int32, (TILE, near * slot), 0)
                total = jnp.sum(
                    jnp.where(bins == local_ref[o], worth_ref[o], 0.0), axis=1, keepdims=True
                )
                for h in range(TILE // LANES):
                    part = total[h * LANES : (h + 1) * LANES]
                    line = o * (bins_dev // LANES) + k * (TILE // LANES) + h
                    sums[pl.ds(line, 1), :] = jnp.sum(
                        jnp.where(diagonal(), part, 0.0), axis=0, keepdims=True
                    )
        for k in range(1, far):
            sums_copy(k).start()

    def finish_sums():
        own_lines = pl.ds(pl.multiple_of(z * curve_ref.shape[0], 8), curve_ref.shape[0])
        total = sums[own_lines, :]
        for k in range(1, far):
            sums_copy(k).wait_recv()
            total += got_sums[k - 1]
        lines_dev = bins_dev // LANES
        levels[0, pl.ds(pl.multiple_of(me * lines_dev, 8), lines_dev), :] = data_ref[0:lines_dev, :]
        levels[1, pl.ds(pl.multiple_of(me * lines_dev, 8), lines_dev), :] = data_ref[
            lines_dev : 2 * lines_dev, :
        ]
        for d in range(1, near):
            data_copy(d).wait_recv()
            part = pl.ds(pl.multiple_of(xor_of(me, d, near) * lines_dev, 8), lines_dev)
            levels[0, part, :] = got_data[d - 1, 0:lines_dev, :]
            levels[1, part, :] = got_data[d - 1, lines_dev : 2 * lines_dev, :]
        yields = levels[0] + total
        curve_ref[...] = levels[1] / (yields * yields)

    def chain_copies(way, c, r, p):
        return [
            pltpu.make_async_remote_copy(
                src_ref=source.at[way, c, r - 1, p],
                dst_ref=target.at[way, c, r - 1, p],
                send_sem=sent.at[way, c, r - 1, p],
                recv_sem=landed.at[way, c, r - 1, p],
                device_id={"bins": along(way)},
                device_id_type=MESH,
            )
            for source, target, sent, landed in (
                (send_q, got_q, q_send, q_recv), (send_s, got_s, s_send, s_recv)
            )
        ]

    def fold(c, plane, p, inputs, finish, early=False):
        @pl.loop(0, held)
        def _(i):
            owner = plane * near + p * held + i
            for s in range(near):
                start = starts_ref[s * owners + owner]
                if early:
                    start = jnp.maximum(start - lower * ((events - ahead) // 16), 0)
                    part = heads[s, pl.ds(start * 16, slot), :]
                else:
                    part = rows_refs[c][s, pl.ds(start * 16, slot), :]
                window[s * slot : (s + 1) * slot, :] = part

            @pl.loop(0, bins_dev // TILE)
            def _(k):
                bins = k * TILE + lax.broadcasted_iota(jnp.int32, (TILE, near * slot), 0)
                hot = (bins == local_ref[owner]).astype(jnp.bfloat16)
                acc[...] = jnp.dot(hot, window[...], preferred_element_type=jnp.float32)
                base = i * (bins_dev // LANES) + k * (TILE // LANES)
                eye = diagonal()
                for way, r, has in inputs:
                    @pl.when(has)
                    def _():
                        for h in range(TILE // LANES):
                            line = base + h
                            part = pl.ds(pl.multiple_of(line * LANES, LANES), LANES)
                            step = got_s[way, c, r - 1, p, pl.ds(line, 1), :]
                            step = jnp.sum(jnp.where(eye, step, 0.0), axis=1, keepdims=True)
                            coded = got_q[way, c, r - 1, p, part, :].astype(jnp.int32)
                            acc[h * LANES : (h + 1) * LANES, :] += (
                                coded.astype(jnp.float32) * step
                            )
                for h in range(TILE // LANES):
                    line = base + h
                    part = pl.ds(pl.multiple_of(line * LANES, LANES), LANES)
                    finish(acc[h * LANES : (h + 1) * LANES, :], line, part, eye)

    def wait_chain(way, c, r, p):
        for copy in chain_copies(way, c, r, p):
            copy.wait_recv()

    def rounds(c, span, first, last, early=False):
        low, high = span

        @pl.loop(first, last)
        def _(r):
            @pl.loop(low, high)
            def _(p):
                for way in range(2):
                    step_in = z if way == 0 else far - 1 - z

                    @pl.when(step_in < r)
                    def _():
                        inputs = []
                        if first > 1:
                            has = step_in > 0
                            inputs = [(way, r - 1, has)]

                            @pl.when(has)
                            def _():
                                wait_chain(way, c, r - 1, p)

                        def code(value, line, part, eye):
                            most = jnp.max(jnp.abs(value), axis=1, keepdims=True)
                            wide = most * (2.0**23 + 1.0)
                            step = (wide + (most - wide)) * 2.0**-14
                            factor = jnp.where(most > 1e-30, 1.0 / step, 0.0)
                            coded = jnp.round(value * factor).astype(jnp.int32)
                            send_q[way, c, r - 1, p, part, :] = coded.astype(send_q.dtype)
                            send_s[way, c, r - 1, p, pl.ds(line, 1), :] = jnp.sum(
                                jnp.where(eye, step, 0.0), axis=0, keepdims=True
                            )

                        plane = z + (far - r) * (1 - 2 * way)
                        fold(c, plane, p, inputs, code, early)
                        for copy in chain_copies(way, c, r, p):
                            copy.start()

    def rows_part(p):
        return pl.ds(pl.multiple_of(p * size, size), size)

    def side_copy(c, d, p, source=0, hop=None):
        hop = d if hop is None else hop
        origin = own.at[c] if source == 0 else out_ref.at[0, source, c]
        return pltpu.make_async_remote_copy(
            src_ref=origin.at[rows_part(p), :],
            dst_ref=out_ref.at[0, d, c, rows_part(p), :],
            send_sem=side_send.at[c, d, p],
            recv_sem=side_recv.at[c, d, p],
            device_id={"bins": side(hop)},
            device_id_type=MESH,
        )

    def pair_copy(c, d, p):
        source = own.at[c] if d == 0 else out_ref.at[0, d, c]
        return pltpu.make_async_remote_copy(
            src_ref=source.at[rows_part(p), :],
            dst_ref=out_ref.at[1, d, c, rows_part(p), :],
            send_sem=pair_send.at[c, d, p],
            recv_sem=pair_recv.at[c, d, p],
            device_id={"params": 1 - core},
            device_id_type=MESH,
        )

    def keep_copy(c, p):
        return pltpu.make_async_copy(
            own.at[c, rows_part(p), :], out_ref.at[0, 0, c, rows_part(p), :], own_sem.at[c, p]
        )

    def finish(c, p):
        @pl.when(z > 0)
        def _():
            wait_chain(0, c, far - 1, p)

        @pl.when(z < far - 1)
        def _():
            wait_chain(1, c, far - 1, p)

        def store(value, line, part, eye):
            row = pl.ds(pl.multiple_of(p * size + line * LANES, LANES), LANES)
            own[c, row, :] = value.astype(own.dtype)

        fold(c, z, p, [(0, far - 1, z > 0), (1, far - 1, z < far - 1)], store)
        for d in direct:
            side_copy(c, d, p).start()
        pair_copy(c, 0, p).start()
        keep_copy(c, p).start()

    def forward(c, p, act):
        if near == 4:
            @pl.when(lax.rem(p, 2) == 0)
            def _():
                act(side_copy(c, 3, p, 1, 2))

            @pl.when(lax.rem(p, 2) == 1)
            def _():
                act(side_copy(c, 3, p, 2, 1))

    def over(c, span, act):
        @pl.loop(span[0], span[1])
        def _(p):
            act(c, p)

    def relay(c, p):
        for d in direct:
            side_copy(c, d, p).wait_recv()
        forward(c, p, lambda copy: copy.start())
        for d in direct:
            pair_copy(c, d, p).start()

    def relay_last(c, p):
        for d in range(1, near):
            if d not in direct:
                side_copy(c, d, p).wait_recv()
                pair_copy(c, d, p).start()

    every = (0, pieces)
    groups = [(c, every) for c in range(chunks - 1)]
    groups += [(chunks - 1, (0, pieces // 2)), (chunks - 1, (pieces // 2, pieces))]
    for d in range(near):
        head_local(d).wait()
    for g, (c, span) in enumerate(groups):
        new = g == 0 or groups[g - 1][0] != c
        if new and c > 0:
            row_local(c).wait()
            for d in range(1, near):
                row_copy(c, d).wait_recv()
        rounds(c, span, 1, 2, g == 0)
        if g == 0:
            nominal_sums()
            row_local(0).wait()
            head_stay(0).wait()
            for d in range(1, near):
                head_stay(d).wait()
                row_copy(0, d).wait_recv()
        if g > 0:
            over(*groups[g - 1], finish)
        rounds(c, span, 2, far)
        if g == 0:
            finish_sums()
        if g > 0:
            over(*groups[g - 1], relay)
        if g > 1:
            over(*groups[g - 2], relay_last)
    over(*groups[-1], finish)
    over(*groups[-2], relay_last)
    over(*groups[-1], relay)
    over(*groups[-1], relay_last)

    for k in range(1, far):
        sums_copy(k).wait_send()
    for d in range(1, near):
        data_copy(d).wait_send()
    for c in range(chunks):
        for d in range(1, near):
            row_copy(c, d).wait_send()

        @pl.loop(0, pieces)
        def _(p):
            keep_copy(c, p).wait()
            for d in direct:
                side_copy(c, d, p).wait_send()
            forward(c, p, lambda copy: copy.wait_send())
            for d in range(near):
                pair_copy(c, d, p).wait_send()
                pair_copy(c, d, p).wait_recv()

            @pl.loop(1, far)
            def _(r):
                for way in range(2):
                    step_in = z if way == 0 else far - 1 - z

                    @pl.when(step_in < r)
                    def _():
                        for copy in chain_copies(way, c, r, p):
                            copy.wait_send()


def chain(starts, local, worth, data, weights, firsts, near, far, chunks, slot, bins_dev):
    events = weights.shape[0]
    ahead = firsts[0].shape[0]
    pieces = near
    bins = near * bins_dev
    size = bins // pieces
    hops = (2, chunks, far - 1, pieces)
    lines = bins // LANES
    dma = pltpu.SemaphoreType.DMA
    rows = jnp.bfloat16
    table = jnp.float32
    return pl.pallas_call(
        functools.partial(chain_kernel, near, far, chunks, pieces, slot),
        out_shape=[
            jax.ShapeDtypeStruct((2, near, chunks, bins, LANES), rows),
            jax.ShapeDtypeStruct((lines, LANES), table),
        ],
        in_specs=[pl.BlockSpec(memory_space=pltpu.SMEM)]
        + [pl.BlockSpec(memory_space=pltpu.VMEM)] * 3
        + [pl.BlockSpec(memory_space=pl.ANY)] * (1 + near),
        out_specs=[
            pl.BlockSpec(memory_space=pl.ANY),
            pl.BlockSpec(memory_space=pltpu.VMEM),
        ],
        scratch_shapes=[pltpu.VMEM((near, events, LANES), rows)] * chunks
        + [
            pltpu.VMEM((near, ahead, LANES), rows),
            pltpu.VMEM((far * lines, LANES), table),
            pltpu.VMEM((far - 1, lines, LANES), table),
            pltpu.VMEM((near - 1,) + data.shape, table),
            pltpu.VMEM((2, lines, LANES), table),
            dma((near,)),
            dma((near,)),
            dma((far - 1,)),
            dma((far - 1,)),
            dma((near - 1,)),
            dma((near - 1,)),
            pltpu.VMEM((near * slot, LANES), rows),
            pltpu.VMEM((TILE, LANES), table),
            pltpu.VMEM((chunks, bins, LANES), rows),
            pltpu.VMEM(hops + (size, LANES), jnp.int16),
            pltpu.VMEM(hops + (size // LANES, LANES), table),
            pltpu.VMEM(hops + (size, LANES), jnp.int16),
            pltpu.VMEM(hops + (size // LANES, LANES), table),
            dma((chunks,)),
            dma((chunks, near)),
            dma((chunks, near)),
            dma(hops),
            dma(hops),
            dma(hops),
            dma(hops),
            dma((chunks, pieces)),
            dma((chunks, near, pieces)),
            dma((chunks, near, pieces)),
            dma((chunks, near, pieces)),
            dma((chunks, near, pieces)),
        ],
        compiler_params=pltpu.CompilerParams(
            collective_id=3, has_side_effects=True, vmem_limit_bytes=62 << 20
        ),
        name="chain",
    )(starts, local, worth, data, weights, *firsts)


def tail_kernel(
    near, far, templates_ref, curve_ref, out_ref, held, weighted, total, coded, own, got,
    hand, kept, merged, sems, sends, recvs, hand_recvs,
):
    groups, _, chunks, bins, _ = templates_ref.shape
    here = lax.axis_index("bins")
    z, me = here // near, lax.rem(here, near)
    piece = own.shape[0]
    count = groups * near * chunks
    step = 2 * LANES
    depth = 4 * LANES

    def peer(k):
        return lax.rem(z + k, far)

    barrier = pltpu.get_barrier_semaphore()
    for k in range(1, far):
        pl.semaphore_signal(
            barrier, inc=1, device_id={"bins": peer(k) * near + me}, device_id_type=MESH
        )

    def fetch(n):
        part = templates_ref.at[n // (near * chunks), lax.rem(n // chunks, near), lax.rem(n, chunks)]
        return pltpu.make_async_copy(
            part, held.at[:, pl.ds(pl.multiple_of(n * LANES, LANES), LANES)], sems.at[n]
        )

    @pl.loop(0, count)
    def _(n):
        fetch(n).start()

    pl.semaphore_wait(barrier, far - 1)
    rows = lax.broadcasted_iota(jnp.int32, (piece, LANES), 0) + me * piece
    lanes = lax.broadcasted_iota(jnp.int32, (piece, LANES), 1)

    @pl.loop(0, near * chunks)
    def _(n):
        fetch(n).wait()

    @pl.loop(0, bins // depth)
    def _(b):
        eye = diagonal()
        curves = []
        for h in range(depth // LANES):
            line = curve_ref[pl.ds(b * (depth // LANES) + h, 1), :]
            curves.append(jnp.sum(jnp.where(eye, line, 0.0), axis=1, keepdims=True))
        curve = jnp.concatenate(curves, axis=0)
        part = pl.ds(pl.multiple_of(b * depth, depth), depth)
        for d in range(near):
            picked = 0.0
            for c in range(chunks):
                pick = (rows == lanes + c * LANES).astype(jnp.bfloat16)
                columns = slice((d * chunks + c) * LANES, (d * chunks + c + 1) * LANES)
                value = curve * held[part, columns].astype(jnp.float32)
                picked += lax.dot_general(
                    pick, value.astype(jnp.bfloat16), (((1,), (1,)), ((), ())),
                    preferred_element_type=jnp.float32,
                )
            weighted[d * piece : (d + 1) * piece, part] = picked.astype(weighted.dtype)

    def rows_for(target):
        return pl.ds(pl.multiple_of(xor_of(me, target, near) * piece, 16), piece)

    def columns_of(n):
        return pl.ds(pl.multiple_of(n * step, step), step)

    def send(source, target, landed, j, n, to):
        return pltpu.make_async_remote_copy(
            src_ref=source,
            dst_ref=target.at[:, columns_of(n)],
            send_sem=sends.at[j, n],
            recv_sem=landed,
            device_id={"bins": to * near + me},
            device_id_type=MESH,
        )

    half = z // 2
    at_end = (z == 0) | (z == far - 1)
    within = 1 + half
    end = half * (far - 1)

    def to_inner(j, n):
        target = (far - 1 - within, far - 1 - z, within)[j]
        source = coded.at[rows_for(target), columns_of(n)]
        if j == 2:
            return send(source, got.at[half], recvs.at[half, n], j, n, within)
        return send(source, hand.at[j], hand_recvs.at[j, n], j, n, within)

    def from_inner(j, n):
        target = (far - 1 - z, far - 1 - end, end)[j]
        if j == 2:
            source = coded.at[rows_for(target), columns_of(n)]
        else:
            source = merged.at[j, :, columns_of(n)]
        return send(source, got.at[half], recvs.at[half, n], j, n, target)

    def merge(n):
        for j in range(2):
            to_inner(j, n).wait_recv()
            part = kept[j, :, columns_of(n)] + hand[j, :, columns_of(n)].astype(jnp.float32)
            merged[j, :, columns_of(n)] = part.astype(merged.dtype)
            from_inner(j, n).start()

    inner = jnp.logical_not(at_end)
    lag = 2

    @pl.loop(0, count // 2)
    def _(n):
        @pl.when(n >= near * chunks // 2)
        def _():
            fetch(2 * n).wait()
            fetch(2 * n + 1).wait()

        total[...] = jnp.dot(
            weighted[...], held[:, columns_of(n)], preferred_element_type=jnp.float32
        )
        coded[:, columns_of(n)] = total[...].astype(coded.dtype)
        own[:, columns_of(n)] = total[rows_for(z), :]

        @pl.when(at_end)
        def _():
            for j in range(3):
                to_inner(j, n).start()

        @pl.when(inner)
        def _():
            from_inner(2, n).start()
            kept[0, :, columns_of(n)] = total[rows_for(far - 1 - z), :]
            kept[1, :, columns_of(n)] = total[rows_for(far - 1 - end), :]

        @pl.when(inner & (n >= lag))
        def _():
            merge(n - lag)

    @pl.when(inner)
    def _():
        @pl.loop(count // 2 - lag, count // 2)
        def _(n):
            merge(n)

    @pl.loop(0, count // 2)
    def _(n):
        for j in range(2):
            send(merged.at[0, :, columns_of(n)], got.at[j], recvs.at[j, n], 0, n, within).wait_recv()
        for side in range(2):
            place = 2 * n + side
            group = place // (near * chunks)
            d = lax.rem(place // chunks, near)
            start = ((group * near + xor_of(me, d, near)) * chunks + lax.rem(place, chunks)) * LANES
            part = pl.ds(pl.multiple_of(place * LANES, LANES), LANES)
            value = own[:, part]
            for j in range(2):
                value += got[j, :, part].astype(jnp.float32)
            out_ref[:, pl.ds(pl.multiple_of(start, LANES), LANES)] = value

    @pl.loop(0, count // 2)
    def _(n):
        for j in range(3):
            @pl.when(at_end)
            def _():
                to_inner(j, n).wait_send()

            @pl.when(inner)
            def _():
                from_inner(j, n).wait_send()


def tail(templates, curve, near, far):
    groups, _, chunks, bins, _ = templates.shape
    piece = chunks * LANES // far
    columns = groups * near * chunks * LANES
    count = groups * near * chunks
    return pl.pallas_call(
        functools.partial(tail_kernel, near, far),
        out_shape=jax.ShapeDtypeStruct((piece, columns), jnp.float32),
        in_specs=[pl.BlockSpec(memory_space=pl.ANY), pl.BlockSpec(memory_space=pltpu.VMEM)],
        out_specs=pl.BlockSpec(memory_space=pltpu.VMEM),
        scratch_shapes=[
            pltpu.VMEM((bins, columns), jnp.bfloat16),
            pltpu.VMEM((near * piece, bins), jnp.bfloat16),
            pltpu.VMEM((near * piece, 2 * LANES), jnp.float32),
            pltpu.VMEM((near * piece, columns), jnp.bfloat16),
            pltpu.VMEM((piece, columns), jnp.float32),
            pltpu.VMEM((2, piece, columns), jnp.bfloat16),
            pltpu.VMEM((2, piece, columns), jnp.bfloat16),
            pltpu.VMEM((2, piece, columns), jnp.float32),
            pltpu.VMEM((2, piece, columns), jnp.bfloat16),
            pltpu.SemaphoreType.DMA((count,)),
            pltpu.SemaphoreType.DMA((3, count // 2)),
            pltpu.SemaphoreType.DMA((2, count // 2)),
            pltpu.SemaphoreType.DMA((2, count // 2)),
        ],
        compiler_params=pltpu.CompilerParams(
            collective_id=2, has_side_effects=True, vmem_limit_bytes=60 << 20
        ),
        name="tail",
    )(templates, curve)


def body_by_parameters(event_bins, event_weights, nominal, background, observed):
    owners = lax.axis_size("bins")
    near = math.isqrt(owners)
    far = owners // near
    events = event_bins.shape[0]
    bins_dev = background.shape[0]
    width = event_weights.shape[1] // near
    chunks = width // LANES
    capacity = 3 * events // (2 * owners)
    slot = -(-capacity // 16) * 16 + 16
    ahead = min(-(-near * capacity // 16) * 16 + 16, events - 16)
    here = lax.axis_index("bins")
    z, me = here // near, lax.rem(here, near)
    around = [[(s, s // near * near + (s % near ^ d)) for s in range(owners)] for d in range(near)]

    def spread(value):
        return [value] + [shift(value, around[d]) for d in range(1, near)]

    marks = jnp.arange(owners * bins_dev // TILE + 1, dtype=jnp.int32) * TILE
    lows = jnp.sum((event_bins[None, :] < marks[:, None]).astype(jnp.int32), axis=1)
    starts = jnp.minimum(lows[: -1 : bins_dev // TILE] // 16, (events - slot) // 16)
    table = jnp.stack([event_bins.astype(jnp.float32), nominal.astype(jnp.float32)])
    table = jnp.concatenate([table, jnp.zeros((6, events), jnp.float32)])
    places = slots_of(starts, table, slot, bins_dev)
    line = jnp.pad(starts.astype(jnp.float32), (0, slot - owners)).reshape(1, slot)
    places = jnp.stack(spread(jnp.concatenate([places, line])))

    firsts = []
    first_row = jnp.where(z < far // 2, events - ahead, 0)
    for d in range(near):
        corner = (first_row, (me ^ d) * width)
        part = lax.dynamic_slice(event_weights, corner, (ahead, LANES))
        firsts.append(part if d == 0 else shift(part, around[d]))

    starts = places[:, 2 * owners, :owners].astype(jnp.int32).reshape(-1)
    places = places[:, : 2 * owners].transpose(1, 0, 2).reshape(2 * owners, 1, near * slot)
    worth = places[owners:]
    places = places[:owners].astype(jnp.int32)
    data = jnp.concatenate([background, observed]).reshape(-1, LANES)
    templates, curve = chain(
        starts, places, worth, data, event_weights, firsts, near, far, chunks, slot, bins_dev
    )
    summed = tail(templates, curve, near, far)
    return summed * (1.0 / (bins_dev * owners))


def splits_by_parameters(mesh, event_bins, event_weights, background):
    owners, groups = mesh.shape["bins"], mesh.shape["params"]
    near = math.isqrt(owners)
    events = event_bins.shape[0] // owners
    width = event_weights.shape[1] // groups // max(near, 1)
    bins_dev = background.shape[0] // owners
    return (
        groups == 2
        and near == 4
        and near * near == owners
        and near & (near - 1) == 0
        and width % LANES == 0
        and width % (16 * near) == 0
        and events % LANES == 0
        and events >= 2 * LANES
        and bins_dev % (8 * LANES) == 0
    )


def solution(mesh):
    in_specs = (P("bins"), P("bins", "params"), P("bins"), P("bins"), P("bins"))
    out_specs = P(("params", "bins"), None)

    def run(event_bins, event_weights, nominal, background, observed):
        fits = splits_by_parameters(mesh, event_bins, event_weights, background)
        chosen = body_by_parameters if fits else body
        mapped = jax.shard_map(
            chosen, mesh=mesh, in_specs=in_specs, out_specs=out_specs, check_vma=False
        )
        return mapped(event_bins, event_weights, nominal, background, observed)

    return run
```

```python
import functools
import math

import jax
import jax.numpy as jnp
from jax import lax
from jax.experimental import pallas as pl
from jax.experimental.pallas import tpu as pltpu
from jax.sharding import PartitionSpec as P

ALIGN = 8
MESH = pl.DeviceIdType.MESH


def from_behind(value, axis, steps):
    count = lax.axis_size(axis)
    pairs = [(source, (source + steps) % count) for source in range(count)]
    return lax.ppermute(value, axis, pairs)


def pack_kernel(owners, slot, first, width, starts_ref, rows_ref, out_ref, held, in_sems, out_sems):
    def fetch(o):
        start = pl.multiple_of(starts_ref[o] * ALIGN, ALIGN)
        return pltpu.make_async_copy(
            rows_ref.at[pl.ds(start, slot), pl.ds(first, width)], held.at[o], in_sems.at[o]
        )

    def store(o):
        return pltpu.make_async_copy(held.at[o], out_ref.at[o], out_sems.at[o])

    @pl.loop(0, owners)
    def _(o):
        fetch(o).start()

    @pl.loop(0, owners)
    def _(o):
        fetch(o).wait()
        store(o).start()

    @pl.loop(0, owners)
    def _(o):
        store(o).wait()


def pack(starts, rows, slot, first, width):
    owners = starts.shape[0]
    return pl.pallas_call(
        functools.partial(pack_kernel, owners, slot, first, width),
        out_shape=jax.ShapeDtypeStruct((owners, slot, width), rows.dtype),
        in_specs=[
            pl.BlockSpec(memory_space=pltpu.SMEM),
            pl.BlockSpec(memory_space=pl.ANY),
        ],
        out_specs=pl.BlockSpec(memory_space=pl.ANY),
        scratch_shapes=[
            pltpu.VMEM((owners, slot, width), rows.dtype),
            pltpu.SemaphoreType.DMA((owners,)),
            pltpu.SemaphoreType.DMA((owners,)),
        ],
        compiler_params=pltpu.CompilerParams(vmem_limit_bytes=32 << 20),
        cost_estimate=pl.CostEstimate(
            flops=0, bytes_accessed=4 * owners * slot * width, transcendentals=0
        ),
        name="pack",
    )(starts, rows)


def meta_kernel(bins_dev, starts_ref, table_ref, out_ref):
    owners, _, slot = out_ref.shape
    events = table_ref.shape[1]
    table = table_ref[...]

    @pl.loop(0, owners)
    def _(o):
        start = starts_ref[o] * ALIGN
        turned = pltpu.roll(table, lax.rem(events - start, events), axis=1)[:, :slot]
        bins = turned[0:1] - (o * bins_dev).astype(jnp.float32)
        inside = (bins >= 0) & (bins < bins_dev)
        out_ref[o, 0:1, :] = jnp.where(inside, bins, -1.0)
        out_ref[o, 1:2, :] = turned[1:2]


def pack_meta(starts, table, slot, bins_dev):
    owners = starts.shape[0]
    return pl.pallas_call(
        functools.partial(meta_kernel, bins_dev),
        out_shape=jax.ShapeDtypeStruct((owners, 2, slot), jnp.float32),
        in_specs=[
            pl.BlockSpec(memory_space=pltpu.SMEM),
            pl.BlockSpec(memory_space=pltpu.VMEM),
        ],
        out_specs=pl.BlockSpec(memory_space=pltpu.VMEM),
        name="pack_meta",
    )(starts, table)


def hist_kernel(chunk, tile, local_ref, rows_ref, out_ref, hot):
    bins, total = hot.shape

    @pl.when(pl.program_id(0) == 0)
    def _():
        ids = lax.broadcasted_iota(jnp.int32, (bins, chunk), 0)

        @pl.loop(0, total // chunk)
        def _(k):
            part = pl.ds(pl.multiple_of(k * chunk, chunk), chunk)
            hot[:, part] = (ids == local_ref[:, part]).astype(jnp.bfloat16)

    @pl.loop(0, bins // tile)
    def _(m):
        part = pl.ds(pl.multiple_of(m * tile, tile), tile)
        out_ref[part, :] = jnp.dot(
            hot[part, :], rows_ref[...], preferred_element_type=jnp.float32
        ).astype(out_ref.dtype)


def histogram_of(local, rows, bins, block, dtype):
    total, width = rows.shape
    return pl.pallas_call(
        functools.partial(hist_kernel, math.gcd(total, 128), math.gcd(bins, 256)),
        grid=(width // block,),
        out_shape=jax.ShapeDtypeStruct((bins, width), dtype),
        in_specs=[
            pl.BlockSpec((1, total), lambda j: (0, 0)),
            pl.BlockSpec((total, block), lambda j: (0, j)),
        ],
        out_specs=pl.BlockSpec((bins, block), lambda j: (0, j)),
        scratch_shapes=[pltpu.VMEM((bins, total), jnp.bfloat16)],
        compiler_params=pltpu.CompilerParams(
            vmem_limit_bytes=40 << 20, dimension_semantics=("arbitrary",)
        ),
        cost_estimate=pl.CostEstimate(
            flops=2 * bins * total * width, bytes_accessed=2 * total * width, transcendentals=0
        ),
        name="histogram",
    )(local, rows)


def reduce_kernel(
    piece, shares_ref, out_ref, own, got_near, sums, got_far,
    own_sem, near_send, near_recv, far_send, far_recv,
):
    far, near, rows, _ = shares_ref.shape
    me = lax.axis_index("bins")
    f, n = me // near, lax.rem(me, near)

    def near_peer(d):
        return lax.rem(n + d, near)

    def far_peer(d):
        return lax.rem(f + d, far)

    barrier = pltpu.get_barrier_semaphore()
    for d in range(1, near):
        pl.semaphore_signal(
            barrier, inc=1, device_id={"bins": f * near + near_peer(d)}, device_id_type=MESH
        )
    for d in range(1, far):
        pl.semaphore_signal(
            barrier, inc=1, device_id={"bins": far_peer(d) * near + n}, device_id_type=MESH
        )
    pl.semaphore_wait(barrier, near + far - 2)

    def part_of(c):
        return pl.ds(pl.multiple_of(c * piece, piece), piece)

    def near_copy(d, c):
        return pltpu.make_async_remote_copy(
            src_ref=shares_ref.at[:, near_peer(d), part_of(c), :],
            dst_ref=got_near.at[d - 1, :, part_of(c), :],
            send_sem=near_send.at[d - 1, c],
            recv_sem=near_recv.at[d - 1, c],
            device_id={"bins": f * near + near_peer(d)},
            device_id_type=MESH,
        )

    def far_copy(d, c):
        return pltpu.make_async_remote_copy(
            src_ref=sums.at[far_peer(d), part_of(c), :],
            dst_ref=got_far.at[d - 1, part_of(c), :],
            send_sem=far_send.at[d - 1, c],
            recv_sem=far_recv.at[d - 1, c],
            device_id={"bins": far_peer(d) * near + n},
            device_id_type=MESH,
        )

    own_copy = pltpu.make_async_copy(shares_ref.at[:, n], own, own_sem)
    own_copy.start()
    pieces = rows // piece

    @pl.loop(0, pieces)
    def _(c):
        for d in range(1, near):
            near_copy(d, c).start()

    own_copy.wait()

    @pl.loop(0, pieces)
    def _(c):
        part = part_of(c)
        for d in range(1, near):
            near_copy(d, c).wait_recv()

        @pl.loop(0, far)
        def _(k):
            total = own[k, part, :].astype(jnp.float32)
            for d in range(1, near):
                total += got_near[d - 1, k, part, :].astype(jnp.float32)
            sums[k, part, :] = total

        for d in range(1, far):
            far_copy(d, c).start()

    @pl.loop(0, pieces)
    def _(c):
        part = part_of(c)
        for d in range(1, far):
            far_copy(d, c).wait_recv()
        total = sums[f, part, :]
        for d in range(1, far):
            total += got_far[d - 1, part, :]
        out_ref[part, :] = total
        for d in range(1, near):
            near_copy(d, c).wait_send()
        for d in range(1, far):
            far_copy(d, c).wait_send()


def reduce_shares(shares):
    owners, rows, cols = shares.shape
    near = math.isqrt(owners)
    while owners % near:
        near -= 1
    far = owners // near
    piece = 16 if rows % 16 == 0 else rows
    pieces = rows // piece
    return pl.pallas_call(
        functools.partial(reduce_kernel, piece),
        out_shape=jax.ShapeDtypeStruct((rows, cols), jnp.float32),
        in_specs=[pl.BlockSpec(memory_space=pl.ANY)],
        out_specs=pl.BlockSpec(memory_space=pltpu.VMEM),
        scratch_shapes=[
            pltpu.VMEM((far, rows, cols), shares.dtype),
            pltpu.VMEM((near - 1, far, rows, cols), shares.dtype),
            pltpu.VMEM((far, rows, cols), jnp.float32),
            pltpu.VMEM((far - 1, rows, cols), jnp.float32),
            pltpu.SemaphoreType.DMA,
            pltpu.SemaphoreType.DMA((near - 1, pieces)),
            pltpu.SemaphoreType.DMA((near - 1, pieces)),
            pltpu.SemaphoreType.DMA((far - 1, pieces)),
            pltpu.SemaphoreType.DMA((far - 1, pieces)),
        ],
        compiler_params=pltpu.CompilerParams(
            collective_id=1, has_side_effects=True, vmem_limit_bytes=40 << 20
        ),
        name="reduce_shares",
    )(shares.reshape(far, near, rows, cols))


def body(event_bins, event_weights, nominal, background, observed):
    owners = lax.axis_size("bins")
    groups_count = lax.axis_size("params")
    events = event_bins.shape[0]
    width_g = event_weights.shape[1]
    bins_dev = background.shape[0]
    capacity = 3 * events // (2 * owners)
    slot = -(-capacity // ALIGN) * ALIGN + ALIGN
    chunks = 2 if width_g % 512 == 0 else 1
    width = width_g // chunks
    block = math.gcd(width, 256)

    destination = event_bins // bins_dev
    targets = jnp.arange(owners, dtype=jnp.int32)
    before = jnp.sum((destination[None, :] < targets[:, None]).astype(jnp.int32), axis=1)
    starts = jnp.minimum(before // ALIGN, (events - slot) // ALIGN)

    table = jnp.stack([event_bins.astype(jnp.float32), nominal.astype(jnp.float32)])
    table = jnp.concatenate([table, jnp.zeros((6, events), jnp.float32)], axis=0)
    meta = pack_meta(starts, table, slot, bins_dev)
    got_meta = lax.all_to_all(meta, "bins", split_axis=0, concat_axis=0, tiled=True)
    local = got_meta[:, 0].astype(jnp.int32).reshape(1, owners * slot)
    got_nominal = got_meta[:, 1].astype(jnp.bfloat16).reshape(owners * slot, 1)
    got_nominal = jnp.broadcast_to(got_nominal, (owners * slot, 128))
    nominal_sum = histogram_of(local, got_nominal, bins_dev, 128, jnp.float32)[:, 0]
    yields = background + nominal_sum
    curvature = observed / (yields * yields)

    parts = []
    for c in range(chunks):
        packed = pack(starts, event_weights, slot, c * width, width)
        got = lax.all_to_all(packed, "bins", split_axis=0, concat_axis=0, tiled=True)
        got = got.reshape(owners * slot, width)
        parts.append(histogram_of(local, got, bins_dev, block, jnp.bfloat16))
    templates = jnp.concatenate(parts, axis=1)
    weighted = (curvature[:, None] * templates.astype(jnp.float32)).astype(jnp.bfloat16)
    pieces = [templates]
    for shift_by in range(1, groups_count // 2 + 1):
        shifted = [from_behind(part, "params", -shift_by) for part in parts]
        pieces.append(jnp.concatenate(shifted, axis=1))
    partners = jnp.concatenate(pieces, axis=1)
    dims = (((0,), (0,)), ((), ()))
    full = lax.dot_general(weighted, partners, dims, preferred_element_type=jnp.float32)
    full = full.astype(jnp.bfloat16)
    shares = full.reshape(owners, width_g // owners, full.shape[1])
    summed = reduce_shares(shares)
    return summed * (1.0 / (bins_dev * owners))


LANES = 128
TILE = 256


def shift(value, pairs):
    return lax.ppermute(value, "bins", pairs)


def xor_of(a, b, count):
    total, bit = 0, 1
    while bit < count:
        total = total + bit * lax.rem(a // bit + b // bit, 2)
        bit *= 2
    return total


def diagonal():
    rows = lax.broadcasted_iota(jnp.int32, (LANES, LANES), 0)
    return rows == lax.broadcasted_iota(jnp.int32, (LANES, LANES), 1)


def slots_kernel(bins_dev, starts_ref, table_ref, out_ref):
    owners = starts_ref.shape[0]
    slot = out_ref.shape[1]
    events = table_ref.shape[1]
    table = table_ref[...]

    @pl.loop(0, owners)
    def _(o):
        start = starts_ref[o] * 16
        turned = pltpu.roll(table, lax.rem(events - start, events), axis=1)
        bins = turned[0:1, :slot] - (o * bins_dev).astype(jnp.float32)
        inside = (bins >= 0) & (bins < bins_dev)
        out_ref[pl.ds(o, 1), :] = jnp.where(inside, bins, -1.0)
        out_ref[pl.ds(owners + o, 1), :] = turned[1:2, :slot]


def slots_of(starts, table, slot, bins_dev):
    return pl.pallas_call(
        functools.partial(slots_kernel, bins_dev),
        out_shape=jax.ShapeDtypeStruct((2 * starts.shape[0], slot), jnp.float32),
        in_specs=[
            pl.BlockSpec(memory_space=pltpu.SMEM),
            pl.BlockSpec(memory_space=pltpu.VMEM),
        ],
        out_specs=pl.BlockSpec(memory_space=pltpu.VMEM),
        name="slots",
    )(starts, table)


def chain_kernel(
    near, far, chunks, pieces, slot, starts_ref, local_ref, worth_ref, data_ref, weights_ref, *refs
):
    firsts = refs[:near]
    out_ref, weighted_ref = refs[near : near + 2]
    rows_refs = refs[near + 2 : near + 2 + chunks]
    (
        heads, sums, got_sums, got_data, levels, curve_ref, stage, stage_sem,
        head_sem, head_keep, sums_send, sums_recv, data_send, data_recv,
        window, acc, own, send_q, send_s, got_q, got_s,
        row_sem, row_send, row_recv, q_send, q_recv, s_send, s_recv,
        own_sem, side_send, side_recv, pair_send, pair_recv,
    ) = refs[near + 2 + chunks :]
    owners = near * far
    here = lax.axis_index("bins")
    core = lax.axis_index("params")
    z, me = here // near, lax.rem(here, near)
    bins_dev = own.shape[1] // near
    width = chunks * LANES
    held = near // pieces
    size = held * bins_dev
    direct = [d for d in range(1, near) if near != 4 or d != 3]

    def side(d):
        return z * near + xor_of(me, d, near)

    def along(way):
        return (z + 1 - 2 * way) * near + me

    def peer(k):
        return lax.rem(z + k, far)

    barrier = pltpu.get_barrier_semaphore()
    for d in range(1, near):
        pl.semaphore_signal(barrier, inc=1, device_id={"bins": side(d)}, device_id_type=MESH)
    for k in range(1, far):
        pl.semaphore_signal(
            barrier, inc=1, device_id={"bins": peer(k) * near + me}, device_id_type=MESH
        )
    pl.semaphore_signal(barrier, inc=1, device_id={"params": 1 - core}, device_id_type=MESH)
    pl.semaphore_wait(barrier, near + far - 1)

    events = weights_ref.shape[0]
    ahead = firsts[0].shape[0]
    lower = (z < far // 2).astype(jnp.int32)
    head_start = lower * (events - ahead)
    rest_start = (1 - lower) * ahead

    def quarter(d, c):
        start = xor_of(me, d, near) * width + c * LANES
        return pl.ds(pl.multiple_of(start, LANES), LANES)

    def row_part(c):
        if c > 0:
            return pl.ds(0, events)
        return pl.ds(pl.multiple_of(rest_start, 16), events - ahead)

    def row_copy(c, d):
        return pltpu.make_async_remote_copy(
            src_ref=weights_ref.at[row_part(c), quarter(d, c)],
            dst_ref=rows_refs[c].at[d, row_part(c), :],
            send_sem=row_send.at[c, d],
            recv_sem=row_recv.at[c, d],
            device_id={"bins": side(d)},
            device_id_type=MESH,
        )

    def row_local(c):
        return pltpu.make_async_copy(
            weights_ref.at[row_part(c), quarter(0, c)],
            rows_refs[c].at[0, row_part(c), :],
            row_sem.at[c],
        )

    def head_local(d):
        return pltpu.make_async_copy(firsts[d], heads.at[d], head_sem.at[d])

    def head_stay(d):
        part = pl.ds(pl.multiple_of(head_start, 16), ahead)
        return pltpu.make_async_copy(firsts[d], rows_refs[0].at[d, part, :], head_keep.at[d])

    def sums_copy(k):
        lines_from = pl.ds(pl.multiple_of(peer(k) * curve_ref.shape[0], 8), curve_ref.shape[0])
        return pltpu.make_async_remote_copy(
            src_ref=sums.at[lines_from, :],
            dst_ref=got_sums.at[k - 1],
            send_sem=sums_send.at[k - 1],
            recv_sem=sums_recv.at[k - 1],
            device_id={"bins": peer(k) * near + me},
            device_id_type=MESH,
        )

    def data_copy(d):
        return pltpu.make_async_remote_copy(
            src_ref=data_ref,
            dst_ref=got_data.at[d - 1],
            send_sem=data_send.at[d - 1],
            recv_sem=data_recv.at[d - 1],
            device_id={"bins": side(d)},
            device_id_type=MESH,
        )

    for d in range(near):
        head_local(d).start()
    for d in range(1, near):
        data_copy(d).start()
    for c in range(chunks):
        for d in range(1, near):
            row_copy(c, d).start()
    for c in range(chunks):
        row_local(c).start()
    for d in range(near):
        head_stay(d).start()

    def nominal_sums():
        @pl.loop(0, owners)
        def _(o):
            @pl.loop(0, bins_dev // TILE)
            def _(k):
                bins = k * TILE + lax.broadcasted_iota(jnp.int32, (TILE, near * slot), 0)
                total = jnp.sum(
                    jnp.where(bins == local_ref[o], worth_ref[o], 0.0), axis=1, keepdims=True
                )
                for h in range(TILE // LANES):
                    part = total[h * LANES : (h + 1) * LANES]
                    line = o * (bins_dev // LANES) + k * (TILE // LANES) + h
                    sums[pl.ds(line, 1), :] = jnp.sum(
                        jnp.where(diagonal(), part, 0.0), axis=0, keepdims=True
                    )
        for k in range(1, far):
            sums_copy(k).start()

    def finish_sums():
        own_lines = pl.ds(pl.multiple_of(z * curve_ref.shape[0], 8), curve_ref.shape[0])
        total = sums[own_lines, :]
        for k in range(1, far):
            sums_copy(k).wait_recv()
            total += got_sums[k - 1]
        lines_dev = bins_dev // LANES
        levels[0, pl.ds(pl.multiple_of(me * lines_dev, 8), lines_dev), :] = data_ref[0:lines_dev, :]
        levels[1, pl.ds(pl.multiple_of(me * lines_dev, 8), lines_dev), :] = data_ref[
            lines_dev : 2 * lines_dev, :
        ]
        for d in range(1, near):
            data_copy(d).wait_recv()
            part = pl.ds(pl.multiple_of(xor_of(me, d, near) * lines_dev, 8), lines_dev)
            levels[0, part, :] = got_data[d - 1, 0:lines_dev, :]
            levels[1, part, :] = got_data[d - 1, lines_dev : 2 * lines_dev, :]
        yields = levels[0] + total
        curve_ref[...] = levels[1] / (yields * yields)

    def chain_copies(way, c, r, p):
        return [
            pltpu.make_async_remote_copy(
                src_ref=source.at[way, c, r - 1, p],
                dst_ref=target.at[way, c, r - 1, p],
                send_sem=sent.at[way, c, r - 1, p],
                recv_sem=landed.at[way, c, r - 1, p],
                device_id={"bins": along(way)},
                device_id_type=MESH,
            )
            for source, target, sent, landed in (
                (send_q, got_q, q_send, q_recv), (send_s, got_s, s_send, s_recv)
            )
        ]

    def fold(c, plane, p, inputs, finish, early=False):
        @pl.loop(0, held)
        def _(i):
            owner = plane * near + p * held + i
            for s in range(near):
                start = starts_ref[s * owners + owner]
                if early:
                    start = jnp.maximum(start - lower * ((events - ahead) // 16), 0)
                    part = heads[s, pl.ds(start * 16, slot), :]
                else:
                    part = rows_refs[c][s, pl.ds(start * 16, slot), :]
                window[s * slot : (s + 1) * slot, :] = part

            @pl.loop(0, bins_dev // TILE)
            def _(k):
                bins = k * TILE + lax.broadcasted_iota(jnp.int32, (TILE, near * slot), 0)
                hot = (bins == local_ref[owner]).astype(jnp.bfloat16)
                acc[...] = jnp.dot(hot, window[...], preferred_element_type=jnp.float32)
                base = i * (bins_dev // LANES) + k * (TILE // LANES)
                eye = diagonal()
                for way, r, has in inputs:
                    @pl.when(has)
                    def _():
                        for h in range(TILE // LANES):
                            line = base + h
                            part = pl.ds(pl.multiple_of(line * LANES, LANES), LANES)
                            step = got_s[way, c, r - 1, p, pl.ds(line, 1), :]
                            step = jnp.sum(jnp.where(eye, step, 0.0), axis=1, keepdims=True)
                            coded = got_q[way, c, r - 1, p, part, :].astype(jnp.int32)
                            acc[h * LANES : (h + 1) * LANES, :] += (
                                coded.astype(jnp.float32) * step
                            )
                for h in range(TILE // LANES):
                    line = base + h
                    part = pl.ds(pl.multiple_of(line * LANES, LANES), LANES)
                    finish(acc[h * LANES : (h + 1) * LANES, :], line, part, eye)

    def wait_chain(way, c, r, p):
        for copy in chain_copies(way, c, r, p):
            copy.wait_recv()

    def rounds(c, span, first, last, early=False):
        low, high = span

        @pl.loop(first, last)
        def _(r):
            @pl.loop(low, high)
            def _(p):
                for way in range(2):
                    step_in = z if way == 0 else far - 1 - z

                    @pl.when(step_in < r)
                    def _():
                        inputs = []
                        if first > 1:
                            has = step_in > 0
                            inputs = [(way, r - 1, has)]

                            @pl.when(has)
                            def _():
                                wait_chain(way, c, r - 1, p)

                        def code(value, line, part, eye):
                            most = jnp.max(jnp.abs(value), axis=1, keepdims=True)
                            wide = most * (2.0**23 + 1.0)
                            step = (wide + (most - wide)) * 2.0**-14
                            factor = jnp.where(most > 1e-30, 1.0 / step, 0.0)
                            coded = jnp.round(value * factor).astype(jnp.int32)
                            send_q[way, c, r - 1, p, part, :] = coded.astype(send_q.dtype)
                            send_s[way, c, r - 1, p, pl.ds(line, 1), :] = jnp.sum(
                                jnp.where(eye, step, 0.0), axis=0, keepdims=True
                            )

                        plane = z + (far - r) * (1 - 2 * way)
                        fold(c, plane, p, inputs, code, early)
                        for copy in chain_copies(way, c, r, p):
                            copy.start()

    def rows_part(p):
        return pl.ds(pl.multiple_of(p * size, size), size)

    def side_copy(c, d, p, source=0, hop=None):
        hop = d if hop is None else hop
        origin = own.at[c] if source == 0 else out_ref.at[0, source, c]
        return pltpu.make_async_remote_copy(
            src_ref=origin.at[rows_part(p), :],
            dst_ref=out_ref.at[0, d, c, rows_part(p), :],
            send_sem=side_send.at[c, d, p],
            recv_sem=side_recv.at[c, d, p],
            device_id={"bins": side(hop)},
            device_id_type=MESH,
        )

    def pair_copy(c, d, p):
        source = own.at[c] if d == 0 else out_ref.at[0, d, c]
        return pltpu.make_async_remote_copy(
            src_ref=source.at[rows_part(p), :],
            dst_ref=out_ref.at[1, d, c, rows_part(p), :],
            send_sem=pair_send.at[c, d, p],
            recv_sem=pair_recv.at[c, d, p],
            device_id={"params": 1 - core},
            device_id_type=MESH,
        )

    def keep_copy(c, p):
        return pltpu.make_async_copy(
            own.at[c, rows_part(p), :], out_ref.at[0, 0, c, rows_part(p), :], own_sem.at[c, p]
        )

    def finish(c, p):
        @pl.when(z > 0)
        def _():
            wait_chain(0, c, far - 1, p)

        @pl.when(z < far - 1)
        def _():
            wait_chain(1, c, far - 1, p)

        def store(value, line, part, eye):
            row = pl.ds(pl.multiple_of(p * size + line * LANES, LANES), LANES)
            own[c, row, :] = value.astype(own.dtype)

        fold(c, z, p, [(0, far - 1, z > 0), (1, far - 1, z < far - 1)], store)
        for d in direct:
            side_copy(c, d, p).start()
        pair_copy(c, 0, p).start()
        keep_copy(c, p).start()

    def forward(c, p, act):
        if near == 4:
            @pl.when(lax.rem(p, 2) == 0)
            def _():
                act(side_copy(c, 3, p, 1, 2))

            @pl.when(lax.rem(p, 2) == 1)
            def _():
                act(side_copy(c, 3, p, 2, 1))

    def over(c, span, act):
        @pl.loop(span[0], span[1])
        def _(p):
            act(c, p)

    def relay(c, p):
        for d in direct:
            side_copy(c, d, p).wait_recv()
        forward(c, p, lambda copy: copy.start())
        for d in direct:
            pair_copy(c, d, p).start()

    def relay_last(c, p):
        for d in range(1, near):
            if d not in direct:
                side_copy(c, d, p).wait_recv()
                pair_copy(c, d, p).start()

    def stage_copy(c, d, p):
        return pltpu.make_async_copy(
            out_ref.at[0, d, c, rows_part(p), :], stage.at[p, d - 1], stage_sem.at[p, d - 1]
        )

    def fetch(c, p):
        for d in range(1, near):
            stage_copy(c, d, p).start()

    def weigh(c, p):
        for d in range(1, near):
            stage_copy(c, d, p).wait()
        piece = weighted_ref.shape[0] // near
        depth = 4 * LANES
        rows = lax.broadcasted_iota(jnp.int32, (piece, LANES), 0) + me * piece
        lanes = lax.broadcasted_iota(jnp.int32, (piece, LANES), 1) + c * LANES
        pick = (rows == lanes).astype(jnp.bfloat16)

        @pl.loop(0, size // depth)
        def _(b):
            eye = diagonal()
            curves = []
            for h in range(depth // LANES):
                at = p * (size // LANES) + b * (depth // LANES) + h
                line = curve_ref[pl.ds(at, 1), :]
                curves.append(jnp.sum(jnp.where(eye, line, 0.0), axis=1, keepdims=True))
            curve = jnp.concatenate(curves, axis=0)
            here_part = pl.ds(pl.multiple_of(b * depth, depth), depth)
            part = pl.ds(pl.multiple_of(p * size + b * depth, depth), depth)
            for d in range(near):
                if d == 0:
                    value = own[c, part, :]
                else:
                    value = stage[p, d - 1, here_part, :]
                value = (curve * value.astype(jnp.float32)).astype(jnp.bfloat16)
                picked = lax.dot_general(
                    pick, value, (((1,), (1,)), ((), ())), preferred_element_type=jnp.float32
                ).astype(weighted_ref.dtype)
                block = slice(d * piece, (d + 1) * piece)
                if c == 0:
                    weighted_ref[block, part] = picked
                else:
                    weighted_ref[block, part] += picked

    def weigh_all(c, span):
        over(c, span, relay_last)
        over(c, span, fetch)
        over(c, span, weigh)

    every = (0, pieces)
    groups = [(c, every) for c in range(chunks - 1)]
    groups += [(chunks - 1, (0, pieces // 2)), (chunks - 1, (pieces // 2, pieces))]
    for d in range(near):
        head_local(d).wait()
    for g, (c, span) in enumerate(groups):
        new = g == 0 or groups[g - 1][0] != c
        if new and c > 0:
            row_local(c).wait()
            for d in range(1, near):
                row_copy(c, d).wait_recv()
        rounds(c, span, 1, 2, g == 0)
        if g == 0:
            nominal_sums()
            row_local(0).wait()
            head_stay(0).wait()
            for d in range(1, near):
                head_stay(d).wait()
                row_copy(0, d).wait_recv()
        if g > 0:
            over(*groups[g - 1], finish)
        rounds(c, span, 2, far)
        if g == 0:
            finish_sums()
        if g > 0:
            over(*groups[g - 1], relay)
        if g > 1:
            weigh_all(*groups[g - 2])
    over(*groups[-1], finish)
    weigh_all(*groups[-2])
    over(*groups[-1], relay)
    weigh_all(*groups[-1])

    for k in range(1, far):
        sums_copy(k).wait_send()
    for d in range(1, near):
        data_copy(d).wait_send()
    for c in range(chunks):
        for d in range(1, near):
            row_copy(c, d).wait_send()

        @pl.loop(0, pieces)
        def _(p):
            keep_copy(c, p).wait()
            for d in direct:
                side_copy(c, d, p).wait_send()
            forward(c, p, lambda copy: copy.wait_send())
            for d in range(near):
                pair_copy(c, d, p).wait_send()
                pair_copy(c, d, p).wait_recv()

            @pl.loop(1, far)
            def _(r):
                for way in range(2):
                    step_in = z if way == 0 else far - 1 - z

                    @pl.when(step_in < r)
                    def _():
                        for copy in chain_copies(way, c, r, p):
                            copy.wait_send()


def chain(starts, local, worth, data, weights, firsts, near, far, chunks, slot, bins_dev):
    events = weights.shape[0]
    ahead = firsts[0].shape[0]
    pieces = near
    bins = near * bins_dev
    size = bins // pieces
    hops = (2, chunks, far - 1, pieces)
    lines = bins // LANES
    dma = pltpu.SemaphoreType.DMA
    rows = jnp.bfloat16
    table = jnp.float32
    return pl.pallas_call(
        functools.partial(chain_kernel, near, far, chunks, pieces, slot),
        out_shape=[
            jax.ShapeDtypeStruct((2, near, chunks, bins, LANES), rows),
            jax.ShapeDtypeStruct((chunks * LANES * near // far, bins), rows),
        ],
        in_specs=[pl.BlockSpec(memory_space=pltpu.SMEM)]
        + [pl.BlockSpec(memory_space=pltpu.VMEM)] * 3
        + [pl.BlockSpec(memory_space=pl.ANY)] * (1 + near),
        out_specs=[
            pl.BlockSpec(memory_space=pl.ANY),
            pl.BlockSpec(memory_space=pltpu.VMEM),
        ],
        scratch_shapes=[pltpu.VMEM((near, events, LANES), rows)] * chunks
        + [
            pltpu.VMEM((near, ahead, LANES), rows),
            pltpu.VMEM((far * lines, LANES), table),
            pltpu.VMEM((far - 1, lines, LANES), table),
            pltpu.VMEM((near - 1,) + data.shape, table),
            pltpu.VMEM((2, lines, LANES), table),
            pltpu.VMEM((lines, LANES), table),
            pltpu.VMEM((pieces, near - 1, size, LANES), rows),
            dma((pieces, near - 1)),
            dma((near,)),
            dma((near,)),
            dma((far - 1,)),
            dma((far - 1,)),
            dma((near - 1,)),
            dma((near - 1,)),
            pltpu.VMEM((near * slot, LANES), rows),
            pltpu.VMEM((TILE, LANES), table),
            pltpu.VMEM((chunks, bins, LANES), rows),
            pltpu.VMEM(hops + (size, LANES), jnp.int16),
            pltpu.VMEM(hops + (size // LANES, LANES), table),
            pltpu.VMEM(hops + (size, LANES), jnp.int16),
            pltpu.VMEM(hops + (size // LANES, LANES), table),
            dma((chunks,)),
            dma((chunks, near)),
            dma((chunks, near)),
            dma(hops),
            dma(hops),
            dma(hops),
            dma(hops),
            dma((chunks, pieces)),
            dma((chunks, near, pieces)),
            dma((chunks, near, pieces)),
            dma((chunks, near, pieces)),
            dma((chunks, near, pieces)),
        ],
        compiler_params=pltpu.CompilerParams(
            collective_id=3, has_side_effects=True, vmem_limit_bytes=62 << 20
        ),
        name="chain",
    )(starts, local, worth, data, weights, *firsts)


def tail_kernel(
    near, far, templates_ref, weighted, out_ref, held, total, coded, own, got,
    hand, kept, merged, sems, sends, recvs, hand_recvs,
):
    groups, _, chunks, bins, _ = templates_ref.shape
    here = lax.axis_index("bins")
    z, me = here // near, lax.rem(here, near)
    piece = own.shape[0]
    count = groups * near * chunks
    step = 2 * LANES

    def peer(k):
        return lax.rem(z + k, far)

    barrier = pltpu.get_barrier_semaphore()
    for k in range(1, far):
        pl.semaphore_signal(
            barrier, inc=1, device_id={"bins": peer(k) * near + me}, device_id_type=MESH
        )

    def fetch(n):
        part = templates_ref.at[n // (near * chunks), lax.rem(n // chunks, near), lax.rem(n, chunks)]
        return pltpu.make_async_copy(
            part, held.at[:, pl.ds(pl.multiple_of(n * LANES, LANES), LANES)], sems.at[n]
        )

    @pl.loop(0, count)
    def _(n):
        fetch(n).start()

    pl.semaphore_wait(barrier, far - 1)

    def rows_for(target):
        return pl.ds(pl.multiple_of(xor_of(me, target, near) * piece, 16), piece)

    def columns_of(n):
        return pl.ds(pl.multiple_of(n * step, step), step)

    def send(source, target, landed, j, n, to):
        return pltpu.make_async_remote_copy(
            src_ref=source,
            dst_ref=target.at[:, columns_of(n)],
            send_sem=sends.at[j, n],
            recv_sem=landed,
            device_id={"bins": to * near + me},
            device_id_type=MESH,
        )

    half = z // 2
    at_end = (z == 0) | (z == far - 1)
    within = 1 + half
    end = half * (far - 1)

    def to_inner(j, n):
        target = (far - 1 - within, far - 1 - z, within)[j]
        source = coded.at[rows_for(target), columns_of(n)]
        if j == 2:
            return send(source, got.at[half], recvs.at[half, n], j, n, within)
        return send(source, hand.at[j], hand_recvs.at[j, n], j, n, within)

    def from_inner(j, n):
        target = (far - 1 - z, far - 1 - end, end)[j]
        if j == 2:
            source = coded.at[rows_for(target), columns_of(n)]
        else:
            source = merged.at[j, :, columns_of(n)]
        return send(source, got.at[half], recvs.at[half, n], j, n, target)

    def merge(n):
        for j in range(2):
            to_inner(j, n).wait_recv()
            part = kept[j, :, columns_of(n)] + hand[j, :, columns_of(n)].astype(jnp.float32)
            merged[j, :, columns_of(n)] = part.astype(merged.dtype)
            from_inner(j, n).start()

    inner = jnp.logical_not(at_end)
    lag = 2

    @pl.loop(0, count // 2)
    def _(n):
        fetch(2 * n).wait()
        fetch(2 * n + 1).wait()
        total[...] = jnp.dot(
            weighted[...], held[:, columns_of(n)], preferred_element_type=jnp.float32
        )
        coded[:, columns_of(n)] = total[...].astype(coded.dtype)
        own[:, columns_of(n)] = total[rows_for(z), :]

        @pl.when(at_end)
        def _():
            for j in range(3):
                to_inner(j, n).start()

        @pl.when(inner)
        def _():
            from_inner(2, n).start()
            kept[0, :, columns_of(n)] = total[rows_for(far - 1 - z), :]
            kept[1, :, columns_of(n)] = total[rows_for(far - 1 - end), :]

        @pl.when(inner & (n >= lag))
        def _():
            merge(n - lag)

    @pl.when(inner)
    def _():
        @pl.loop(count // 2 - lag, count // 2)
        def _(n):
            merge(n)

    @pl.loop(0, count // 2)
    def _(n):
        for j in range(2):
            send(merged.at[0, :, columns_of(n)], got.at[j], recvs.at[j, n], 0, n, within).wait_recv()
        for side in range(2):
            place = 2 * n + side
            group = place // (near * chunks)
            d = lax.rem(place // chunks, near)
            start = ((group * near + xor_of(me, d, near)) * chunks + lax.rem(place, chunks)) * LANES
            part = pl.ds(pl.multiple_of(place * LANES, LANES), LANES)
            value = own[:, part]
            for j in range(2):
                value += got[j, :, part].astype(jnp.float32)
            out_ref[:, pl.ds(pl.multiple_of(start, LANES), LANES)] = value

    @pl.loop(0, count // 2)
    def _(n):
        for j in range(3):
            @pl.when(at_end)
            def _():
                to_inner(j, n).wait_send()

            @pl.when(inner)
            def _():
                from_inner(j, n).wait_send()


def tail(templates, weighted, near, far):
    groups, _, chunks, bins, _ = templates.shape
    piece = chunks * LANES // far
    columns = groups * near * chunks * LANES
    count = groups * near * chunks
    return pl.pallas_call(
        functools.partial(tail_kernel, near, far),
        out_shape=jax.ShapeDtypeStruct((piece, columns), jnp.float32),
        in_specs=[pl.BlockSpec(memory_space=pl.ANY), pl.BlockSpec(memory_space=pltpu.VMEM)],
        out_specs=pl.BlockSpec(memory_space=pltpu.VMEM),
        scratch_shapes=[
            pltpu.VMEM((bins, columns), jnp.bfloat16),
            pltpu.VMEM((near * piece, 2 * LANES), jnp.float32),
            pltpu.VMEM((near * piece, columns), jnp.bfloat16),
            pltpu.VMEM((piece, columns), jnp.float32),
            pltpu.VMEM((2, piece, columns), jnp.bfloat16),
            pltpu.VMEM((2, piece, columns), jnp.bfloat16),
            pltpu.VMEM((2, piece, columns), jnp.float32),
            pltpu.VMEM((2, piece, columns), jnp.bfloat16),
            pltpu.SemaphoreType.DMA((count,)),
            pltpu.SemaphoreType.DMA((3, count // 2)),
            pltpu.SemaphoreType.DMA((2, count // 2)),
            pltpu.SemaphoreType.DMA((2, count // 2)),
        ],
        compiler_params=pltpu.CompilerParams(
            collective_id=2, has_side_effects=True, vmem_limit_bytes=60 << 20
        ),
        name="tail",
    )(templates, weighted)


def body_by_parameters(event_bins, event_weights, nominal, background, observed):
    owners = lax.axis_size("bins")
    near = math.isqrt(owners)
    far = owners // near
    events = event_bins.shape[0]
    bins_dev = background.shape[0]
    width = event_weights.shape[1] // near
    chunks = width // LANES
    capacity = 3 * events // (2 * owners)
    slot = -(-capacity // 16) * 16 + 16
    ahead = min(-(-near * capacity // 16) * 16 + 16, events - 16)
    here = lax.axis_index("bins")
    z, me = here // near, lax.rem(here, near)
    around = [[(s, s // near * near + (s % near ^ d)) for s in range(owners)] for d in range(near)]

    def spread(value):
        return [value] + [shift(value, around[d]) for d in range(1, near)]

    marks = jnp.arange(owners * bins_dev // TILE + 1, dtype=jnp.int32) * TILE
    lows = jnp.sum((event_bins[None, :] < marks[:, None]).astype(jnp.int32), axis=1)
    starts = jnp.minimum(lows[: -1 : bins_dev // TILE] // 16, (events - slot) // 16)
    table = jnp.stack([event_bins.astype(jnp.float32), nominal.astype(jnp.float32)])
    table = jnp.concatenate([table, jnp.zeros((6, events), jnp.float32)])
    places = slots_of(starts, table, slot, bins_dev)
    line = jnp.pad(starts.astype(jnp.float32), (0, slot - owners)).reshape(1, slot)
    places = jnp.stack(spread(jnp.concatenate([places, line])))

    firsts = []
    first_row = jnp.where(z < far // 2, events - ahead, 0)
    for d in range(near):
        corner = (first_row, (me ^ d) * width)
        part = lax.dynamic_slice(event_weights, corner, (ahead, LANES))
        firsts.append(part if d == 0 else shift(part, around[d]))

    starts = places[:, 2 * owners, :owners].astype(jnp.int32).reshape(-1)
    places = places[:, : 2 * owners].transpose(1, 0, 2).reshape(2 * owners, 1, near * slot)
    worth = places[owners:]
    places = places[:owners].astype(jnp.int32)
    data = jnp.concatenate([background, observed]).reshape(-1, LANES)
    templates, weighted = chain(
        starts, places, worth, data, event_weights, firsts, near, far, chunks, slot, bins_dev
    )
    summed = tail(templates, weighted, near, far)
    return summed * (1.0 / (bins_dev * owners))


def splits_by_parameters(mesh, event_bins, event_weights, background):
    owners, groups = mesh.shape["bins"], mesh.shape["params"]
    near = math.isqrt(owners)
    events = event_bins.shape[0] // owners
    width = event_weights.shape[1] // groups // max(near, 1)
    bins_dev = background.shape[0] // owners
    return (
        groups == 2
        and near == 4
        and near * near == owners
        and near & (near - 1) == 0
        and width % LANES == 0
        and width % (16 * near) == 0
        and events % LANES == 0
        and events >= 2 * LANES
        and bins_dev % (8 * LANES) == 0
    )


def solution(mesh):
    in_specs = (P("bins"), P("bins", "params"), P("bins"), P("bins"), P("bins"))
    out_specs = P(("params", "bins"), None)

    def run(event_bins, event_weights, nominal, background, observed):
        fits = splits_by_parameters(mesh, event_bins, event_weights, background)
        chosen = body_by_parameters if fits else body
        mapped = jax.shard_map(
            chosen, mesh=mesh, in_specs=in_specs, out_specs=out_specs, check_vma=False
        )
        return mapped(event_bins, event_weights, nominal, background, observed)

    return run
```

```python
import functools
import math

import jax
import jax.numpy as jnp
from jax import lax
from jax.experimental import pallas as pl
from jax.experimental.pallas import tpu as pltpu
from jax.sharding import PartitionSpec as P

ALIGN = 8
MESH = pl.DeviceIdType.MESH


def from_behind(value, axis, steps):
    count = lax.axis_size(axis)
    pairs = [(source, (source + steps) % count) for source in range(count)]
    return lax.ppermute(value, axis, pairs)


def pack_kernel(owners, slot, first, width, starts_ref, rows_ref, out_ref, held, in_sems, out_sems):
    def fetch(o):
        start = pl.multiple_of(starts_ref[o] * ALIGN, ALIGN)
        return pltpu.make_async_copy(
            rows_ref.at[pl.ds(start, slot), pl.ds(first, width)], held.at[o], in_sems.at[o]
        )

    def store(o):
        return pltpu.make_async_copy(held.at[o], out_ref.at[o], out_sems.at[o])

    @pl.loop(0, owners)
    def _(o):
        fetch(o).start()

    @pl.loop(0, owners)
    def _(o):
        fetch(o).wait()
        store(o).start()

    @pl.loop(0, owners)
    def _(o):
        store(o).wait()


def pack(starts, rows, slot, first, width):
    owners = starts.shape[0]
    return pl.pallas_call(
        functools.partial(pack_kernel, owners, slot, first, width),
        out_shape=jax.ShapeDtypeStruct((owners, slot, width), rows.dtype),
        in_specs=[
            pl.BlockSpec(memory_space=pltpu.SMEM),
            pl.BlockSpec(memory_space=pl.ANY),
        ],
        out_specs=pl.BlockSpec(memory_space=pl.ANY),
        scratch_shapes=[
            pltpu.VMEM((owners, slot, width), rows.dtype),
            pltpu.SemaphoreType.DMA((owners,)),
            pltpu.SemaphoreType.DMA((owners,)),
        ],
        compiler_params=pltpu.CompilerParams(vmem_limit_bytes=32 << 20),
        cost_estimate=pl.CostEstimate(
            flops=0, bytes_accessed=4 * owners * slot * width, transcendentals=0
        ),
        name="pack",
    )(starts, rows)


def meta_kernel(bins_dev, starts_ref, table_ref, out_ref):
    owners, _, slot = out_ref.shape
    events = table_ref.shape[1]
    table = table_ref[...]

    @pl.loop(0, owners)
    def _(o):
        start = starts_ref[o] * ALIGN
        turned = pltpu.roll(table, lax.rem(events - start, events), axis=1)[:, :slot]
        bins = turned[0:1] - (o * bins_dev).astype(jnp.float32)
        inside = (bins >= 0) & (bins < bins_dev)
        out_ref[o, 0:1, :] = jnp.where(inside, bins, -1.0)
        out_ref[o, 1:2, :] = turned[1:2]


def pack_meta(starts, table, slot, bins_dev):
    owners = starts.shape[0]
    return pl.pallas_call(
        functools.partial(meta_kernel, bins_dev),
        out_shape=jax.ShapeDtypeStruct((owners, 2, slot), jnp.float32),
        in_specs=[
            pl.BlockSpec(memory_space=pltpu.SMEM),
            pl.BlockSpec(memory_space=pltpu.VMEM),
        ],
        out_specs=pl.BlockSpec(memory_space=pltpu.VMEM),
        name="pack_meta",
    )(starts, table)


def hist_kernel(chunk, tile, local_ref, rows_ref, out_ref, hot):
    bins, total = hot.shape

    @pl.when(pl.program_id(0) == 0)
    def _():
        ids = lax.broadcasted_iota(jnp.int32, (bins, chunk), 0)

        @pl.loop(0, total // chunk)
        def _(k):
            part = pl.ds(pl.multiple_of(k * chunk, chunk), chunk)
            hot[:, part] = (ids == local_ref[:, part]).astype(jnp.bfloat16)

    @pl.loop(0, bins // tile)
    def _(m):
        part = pl.ds(pl.multiple_of(m * tile, tile), tile)
        out_ref[part, :] = jnp.dot(
            hot[part, :], rows_ref[...], preferred_element_type=jnp.float32
        ).astype(out_ref.dtype)


def histogram_of(local, rows, bins, block, dtype):
    total, width = rows.shape
    return pl.pallas_call(
        functools.partial(hist_kernel, math.gcd(total, 128), math.gcd(bins, 256)),
        grid=(width // block,),
        out_shape=jax.ShapeDtypeStruct((bins, width), dtype),
        in_specs=[
            pl.BlockSpec((1, total), lambda j: (0, 0)),
            pl.BlockSpec((total, block), lambda j: (0, j)),
        ],
        out_specs=pl.BlockSpec((bins, block), lambda j: (0, j)),
        scratch_shapes=[pltpu.VMEM((bins, total), jnp.bfloat16)],
        compiler_params=pltpu.CompilerParams(
            vmem_limit_bytes=40 << 20, dimension_semantics=("arbitrary",)
        ),
        cost_estimate=pl.CostEstimate(
            flops=2 * bins * total * width, bytes_accessed=2 * total * width, transcendentals=0
        ),
        name="histogram",
    )(local, rows)


def reduce_kernel(
    piece, shares_ref, out_ref, own, got_near, sums, got_far,
    own_sem, near_send, near_recv, far_send, far_recv,
):
    far, near, rows, _ = shares_ref.shape
    me = lax.axis_index("bins")
    f, n = me // near, lax.rem(me, near)

    def near_peer(d):
        return lax.rem(n + d, near)

    def far_peer(d):
        return lax.rem(f + d, far)

    barrier = pltpu.get_barrier_semaphore()
    for d in range(1, near):
        pl.semaphore_signal(
            barrier, inc=1, device_id={"bins": f * near + near_peer(d)}, device_id_type=MESH
        )
    for d in range(1, far):
        pl.semaphore_signal(
            barrier, inc=1, device_id={"bins": far_peer(d) * near + n}, device_id_type=MESH
        )
    pl.semaphore_wait(barrier, near + far - 2)

    def part_of(c):
        return pl.ds(pl.multiple_of(c * piece, piece), piece)

    def near_copy(d, c):
        return pltpu.make_async_remote_copy(
            src_ref=shares_ref.at[:, near_peer(d), part_of(c), :],
            dst_ref=got_near.at[d - 1, :, part_of(c), :],
            send_sem=near_send.at[d - 1, c],
            recv_sem=near_recv.at[d - 1, c],
            device_id={"bins": f * near + near_peer(d)},
            device_id_type=MESH,
        )

    def far_copy(d, c):
        return pltpu.make_async_remote_copy(
            src_ref=sums.at[far_peer(d), part_of(c), :],
            dst_ref=got_far.at[d - 1, part_of(c), :],
            send_sem=far_send.at[d - 1, c],
            recv_sem=far_recv.at[d - 1, c],
            device_id={"bins": far_peer(d) * near + n},
            device_id_type=MESH,
        )

    own_copy = pltpu.make_async_copy(shares_ref.at[:, n], own, own_sem)
    own_copy.start()
    pieces = rows // piece

    @pl.loop(0, pieces)
    def _(c):
        for d in range(1, near):
            near_copy(d, c).start()

    own_copy.wait()

    @pl.loop(0, pieces)
    def _(c):
        part = part_of(c)
        for d in range(1, near):
            near_copy(d, c).wait_recv()

        @pl.loop(0, far)
        def _(k):
            total = own[k, part, :].astype(jnp.float32)
            for d in range(1, near):
                total += got_near[d - 1, k, part, :].astype(jnp.float32)
            sums[k, part, :] = total

        for d in range(1, far):
            far_copy(d, c).start()

    @pl.loop(0, pieces)
    def _(c):
        part = part_of(c)
        for d in range(1, far):
            far_copy(d, c).wait_recv()
        total = sums[f, part, :]
        for d in range(1, far):
            total += got_far[d - 1, part, :]
        out_ref[part, :] = total
        for d in range(1, near):
            near_copy(d, c).wait_send()
        for d in range(1, far):
            far_copy(d, c).wait_send()


def reduce_shares(shares):
    owners, rows, cols = shares.shape
    near = math.isqrt(owners)
    while owners % near:
        near -= 1
    far = owners // near
    piece = 16 if rows % 16 == 0 else rows
    pieces = rows // piece
    return pl.pallas_call(
        functools.partial(reduce_kernel, piece),
        out_shape=jax.ShapeDtypeStruct((rows, cols), jnp.float32),
        in_specs=[pl.BlockSpec(memory_space=pl.ANY)],
        out_specs=pl.BlockSpec(memory_space=pltpu.VMEM),
        scratch_shapes=[
            pltpu.VMEM((far, rows, cols), shares.dtype),
            pltpu.VMEM((near - 1, far, rows, cols), shares.dtype),
            pltpu.VMEM((far, rows, cols), jnp.float32),
            pltpu.VMEM((far - 1, rows, cols), jnp.float32),
            pltpu.SemaphoreType.DMA,
            pltpu.SemaphoreType.DMA((near - 1, pieces)),
            pltpu.SemaphoreType.DMA((near - 1, pieces)),
            pltpu.SemaphoreType.DMA((far - 1, pieces)),
            pltpu.SemaphoreType.DMA((far - 1, pieces)),
        ],
        compiler_params=pltpu.CompilerParams(
            collective_id=1, has_side_effects=True, vmem_limit_bytes=40 << 20
        ),
        name="reduce_shares",
    )(shares.reshape(far, near, rows, cols))


def body(event_bins, event_weights, nominal, background, observed):
    owners = lax.axis_size("bins")
    groups_count = lax.axis_size("params")
    events = event_bins.shape[0]
    width_g = event_weights.shape[1]
    bins_dev = background.shape[0]
    capacity = 3 * events // (2 * owners)
    slot = -(-capacity // ALIGN) * ALIGN + ALIGN
    chunks = 2 if width_g % 512 == 0 else 1
    width = width_g // chunks
    block = math.gcd(width, 256)

    destination = event_bins // bins_dev
    targets = jnp.arange(owners, dtype=jnp.int32)
    before = jnp.sum((destination[None, :] < targets[:, None]).astype(jnp.int32), axis=1)
    starts = jnp.minimum(before // ALIGN, (events - slot) // ALIGN)

    table = jnp.stack([event_bins.astype(jnp.float32), nominal.astype(jnp.float32)])
    table = jnp.concatenate([table, jnp.zeros((6, events), jnp.float32)], axis=0)
    meta = pack_meta(starts, table, slot, bins_dev)
    got_meta = lax.all_to_all(meta, "bins", split_axis=0, concat_axis=0, tiled=True)
    local = got_meta[:, 0].astype(jnp.int32).reshape(1, owners * slot)
    got_nominal = got_meta[:, 1].astype(jnp.bfloat16).reshape(owners * slot, 1)
    got_nominal = jnp.broadcast_to(got_nominal, (owners * slot, 128))
    nominal_sum = histogram_of(local, got_nominal, bins_dev, 128, jnp.float32)[:, 0]
    yields = background + nominal_sum
    curvature = observed / (yields * yields)

    parts = []
    for c in range(chunks):
        packed = pack(starts, event_weights, slot, c * width, width)
        got = lax.all_to_all(packed, "bins", split_axis=0, concat_axis=0, tiled=True)
        got = got.reshape(owners * slot, width)
        parts.append(histogram_of(local, got, bins_dev, block, jnp.bfloat16))
    templates = jnp.concatenate(parts, axis=1)
    weighted = (curvature[:, None] * templates.astype(jnp.float32)).astype(jnp.bfloat16)
    pieces = [templates]
    for shift_by in range(1, groups_count // 2 + 1):
        shifted = [from_behind(part, "params", -shift_by) for part in parts]
        pieces.append(jnp.concatenate(shifted, axis=1))
    partners = jnp.concatenate(pieces, axis=1)
    dims = (((0,), (0,)), ((), ()))
    full = lax.dot_general(weighted, partners, dims, preferred_element_type=jnp.float32)
    full = full.astype(jnp.bfloat16)
    shares = full.reshape(owners, width_g // owners, full.shape[1])
    summed = reduce_shares(shares)
    return summed * (1.0 / (bins_dev * owners))


LANES = 128
TILE = 256


def shift(value, pairs):
    return lax.ppermute(value, "bins", pairs)


def xor_of(a, b, count):
    total, bit = 0, 1
    while bit < count:
        total = total + bit * lax.rem(a // bit + b // bit, 2)
        bit *= 2
    return total


def diagonal():
    rows = lax.broadcasted_iota(jnp.int32, (LANES, LANES), 0)
    return rows == lax.broadcasted_iota(jnp.int32, (LANES, LANES), 1)


def slots_kernel(bins_dev, starts_ref, ids_ref, nominal_ref, out_ref):
    owners = starts_ref.shape[0]
    slot = out_ref.shape[1]
    events = ids_ref.shape[1]
    first = lax.broadcasted_iota(jnp.int32, (8, events), 0) == 0
    table = jnp.where(first, ids_ref[...].astype(jnp.float32), nominal_ref[...].astype(jnp.float32))
    lanes = lax.broadcasted_iota(jnp.int32, (1, slot), 1)
    out_ref[pl.ds(2 * owners, 1), :] = jnp.zeros((1, slot), jnp.float32)

    @pl.loop(0, owners)
    def _(o):
        start = starts_ref[o]
        turned = pltpu.roll(table, lax.rem(events - start * 16, events), axis=1)
        bins = turned[0:1, :slot] - (o * bins_dev).astype(jnp.float32)
        inside = (bins >= 0) & (bins < bins_dev)
        out_ref[pl.ds(o, 1), :] = jnp.where(inside, bins, -1.0)
        out_ref[pl.ds(owners + o, 1), :] = turned[1:2, :slot]
        out_ref[pl.ds(2 * owners, 1), :] += jnp.where(lanes == o, start.astype(jnp.float32), 0.0)


def slots_of(starts, ids, nominal, slot, bins_dev):
    owners, events = starts.shape[0], ids.shape[0]
    return pl.pallas_call(
        functools.partial(slots_kernel, bins_dev),
        out_shape=jax.ShapeDtypeStruct((2 * owners + 1, slot), jnp.float32),
        in_specs=[pl.BlockSpec(memory_space=pltpu.SMEM)]
        + [pl.BlockSpec(memory_space=pltpu.VMEM)] * 2,
        out_specs=pl.BlockSpec(memory_space=pltpu.VMEM),
        name="slots",
    )(starts, ids.reshape(1, events), nominal.reshape(1, events))


def chain_kernel(
    near, far, chunks, pieces, slot, starts_ref, local_ref, worth_ref, data_ref, weights_ref, *refs
):
    firsts = refs[:near]
    out_ref, weighted_ref = refs[near : near + 2]
    rows_refs = refs[near + 2 : near + 2 + chunks]
    (
        heads, sums, got_sums, got_data, levels, curve_ref, stage, stage_sem,
        head_sem, head_keep, sums_send, sums_recv, data_send, data_recv,
        window, acc, own, send_q, send_s, got_q, got_s,
        row_sem, row_send, row_recv, q_send, q_recv, s_send, s_recv,
        own_sem, side_send, side_recv, pair_send, pair_recv,
    ) = refs[near + 2 + chunks :]
    owners = near * far
    here = lax.axis_index("bins")
    core = lax.axis_index("params")
    z, me = here // near, lax.rem(here, near)
    bins_dev = own.shape[1] // near
    width = chunks * LANES
    held = near // pieces
    size = held * bins_dev
    direct = [d for d in range(1, near) if near != 4 or d != 3]

    def side(d):
        return z * near + xor_of(me, d, near)

    def along(way):
        return (z + 1 - 2 * way) * near + me

    def peer(k):
        return lax.rem(z + k, far)

    barrier = pltpu.get_barrier_semaphore()
    for d in range(1, near):
        pl.semaphore_signal(barrier, inc=1, device_id={"bins": side(d)}, device_id_type=MESH)
    for k in range(1, far):
        pl.semaphore_signal(
            barrier, inc=1, device_id={"bins": peer(k) * near + me}, device_id_type=MESH
        )
    pl.semaphore_signal(barrier, inc=1, device_id={"params": 1 - core}, device_id_type=MESH)
    pl.semaphore_wait(barrier, near + far - 1)

    events = weights_ref.shape[0]
    ahead = firsts[0].shape[0]
    lower = (z < far // 2).astype(jnp.int32)
    head_start = lower * (events - ahead)
    rest_start = (1 - lower) * ahead

    def quarter(d, c):
        start = xor_of(me, d, near) * width + c * LANES
        return pl.ds(pl.multiple_of(start, LANES), LANES)

    def row_part(c):
        if c > 0:
            return pl.ds(0, events)
        return pl.ds(pl.multiple_of(rest_start, 16), events - ahead)

    def row_copy(c, d):
        return pltpu.make_async_remote_copy(
            src_ref=weights_ref.at[row_part(c), quarter(d, c)],
            dst_ref=rows_refs[c].at[d, row_part(c), :],
            send_sem=row_send.at[c, d],
            recv_sem=row_recv.at[c, d],
            device_id={"bins": side(d)},
            device_id_type=MESH,
        )

    def row_local(c):
        return pltpu.make_async_copy(
            weights_ref.at[row_part(c), quarter(0, c)],
            rows_refs[c].at[0, row_part(c), :],
            row_sem.at[c],
        )

    def head_local(d):
        return pltpu.make_async_copy(firsts[d], heads.at[d], head_sem.at[d])

    def head_stay(d):
        part = pl.ds(pl.multiple_of(head_start, 16), ahead)
        return pltpu.make_async_copy(firsts[d], rows_refs[0].at[d, part, :], head_keep.at[d])

    def sums_copy(k):
        lines_from = pl.ds(pl.multiple_of(peer(k) * curve_ref.shape[0], 8), curve_ref.shape[0])
        return pltpu.make_async_remote_copy(
            src_ref=sums.at[lines_from, :],
            dst_ref=got_sums.at[k - 1],
            send_sem=sums_send.at[k - 1],
            recv_sem=sums_recv.at[k - 1],
            device_id={"bins": peer(k) * near + me},
            device_id_type=MESH,
        )

    def data_copy(d):
        return pltpu.make_async_remote_copy(
            src_ref=data_ref,
            dst_ref=got_data.at[d - 1],
            send_sem=data_send.at[d - 1],
            recv_sem=data_recv.at[d - 1],
            device_id={"bins": side(d)},
            device_id_type=MESH,
        )

    for d in range(near):
        head_local(d).start()
    for d in range(1, near):
        data_copy(d).start()
    for c in range(chunks):
        for d in range(1, near):
            row_copy(c, d).start()
    for c in range(chunks):
        row_local(c).start()
    for d in range(near):
        head_stay(d).start()

    def nominal_sums():
        @pl.loop(0, owners)
        def _(o):
            @pl.loop(0, bins_dev // TILE)
            def _(k):
                bins = k * TILE + lax.broadcasted_iota(jnp.int32, (TILE, near * slot), 0)
                total = jnp.sum(
                    jnp.where(bins == local_ref[o], worth_ref[o], 0.0), axis=1, keepdims=True
                )
                for h in range(TILE // LANES):
                    part = total[h * LANES : (h + 1) * LANES]
                    line = o * (bins_dev // LANES) + k * (TILE // LANES) + h
                    sums[pl.ds(line, 1), :] = jnp.sum(
                        jnp.where(diagonal(), part, 0.0), axis=0, keepdims=True
                    )
        for k in range(1, far):
            sums_copy(k).start()

    def finish_sums():
        own_lines = pl.ds(pl.multiple_of(z * curve_ref.shape[0], 8), curve_ref.shape[0])
        total = sums[own_lines, :]
        for k in range(1, far):
            sums_copy(k).wait_recv()
            total += got_sums[k - 1]
        lines_dev = bins_dev // LANES
        levels[0, pl.ds(pl.multiple_of(me * lines_dev, 8), lines_dev), :] = data_ref[0:lines_dev, :]
        levels[1, pl.ds(pl.multiple_of(me * lines_dev, 8), lines_dev), :] = data_ref[
            lines_dev : 2 * lines_dev, :
        ]
        for d in range(1, near):
            data_copy(d).wait_recv()
            part = pl.ds(pl.multiple_of(xor_of(me, d, near) * lines_dev, 8), lines_dev)
            levels[0, part, :] = got_data[d - 1, 0:lines_dev, :]
            levels[1, part, :] = got_data[d - 1, lines_dev : 2 * lines_dev, :]
        yields = levels[0] + total
        curve_ref[...] = levels[1] / (yields * yields)

    def chain_copies(way, c, r, p):
        return [
            pltpu.make_async_remote_copy(
                src_ref=source.at[way, c, r - 1, p],
                dst_ref=target.at[way, c, r - 1, p],
                send_sem=sent.at[way, c, r - 1, p],
                recv_sem=landed.at[way, c, r - 1, p],
                device_id={"bins": along(way)},
                device_id_type=MESH,
            )
            for source, target, sent, landed in (
                (send_q, got_q, q_send, q_recv), (send_s, got_s, s_send, s_recv)
            )
        ]

    def fold(c, plane, p, inputs, finish, early=False):
        @pl.loop(0, held)
        def _(i):
            owner = plane * near + p * held + i
            for s in range(near):
                start = starts_ref[s * owners + owner]
                if early:
                    start = jnp.maximum(start - lower * ((events - ahead) // 16), 0)
                    part = heads[s, pl.ds(start * 16, slot), :]
                else:
                    part = rows_refs[c][s, pl.ds(start * 16, slot), :]
                window[s * slot : (s + 1) * slot, :] = part

            @pl.loop(0, bins_dev // TILE)
            def _(k):
                bins = k * TILE + lax.broadcasted_iota(jnp.int32, (TILE, near * slot), 0)
                hot = (bins == local_ref[owner]).astype(jnp.bfloat16)
                acc[...] = jnp.dot(hot, window[...], preferred_element_type=jnp.float32)
                base = i * (bins_dev // LANES) + k * (TILE // LANES)
                eye = diagonal()
                for way, r, has in inputs:
                    @pl.when(has)
                    def _():
                        for h in range(TILE // LANES):
                            line = base + h
                            part = pl.ds(pl.multiple_of(line * LANES, LANES), LANES)
                            step = got_s[way, c, r - 1, p, pl.ds(line, 1), :]
                            step = jnp.sum(jnp.where(eye, step, 0.0), axis=1, keepdims=True)
                            coded = got_q[way, c, r - 1, p, part, :].astype(jnp.int32)
                            acc[h * LANES : (h + 1) * LANES, :] += (
                                coded.astype(jnp.float32) * step
                            )
                for h in range(TILE // LANES):
                    line = base + h
                    part = pl.ds(pl.multiple_of(line * LANES, LANES), LANES)
                    finish(acc[h * LANES : (h + 1) * LANES, :], line, part, eye)

    def wait_chain(way, c, r, p):
        for copy in chain_copies(way, c, r, p):
            copy.wait_recv()

    def rounds(c, span, first, last, early=False):
        low, high = span

        @pl.loop(first, last)
        def _(r):
            @pl.loop(low, high)
            def _(p):
                for way in range(2):
                    step_in = z if way == 0 else far - 1 - z

                    @pl.when(step_in < r)
                    def _():
                        inputs = []
                        if first > 1:
                            has = step_in > 0
                            inputs = [(way, r - 1, has)]

                            @pl.when(has)
                            def _():
                                wait_chain(way, c, r - 1, p)

                        def code(value, line, part, eye):
                            most = jnp.max(jnp.abs(value), axis=1, keepdims=True)
                            wide = most * (2.0**23 + 1.0)
                            step = (wide + (most - wide)) * 2.0**-14
                            factor = jnp.where(most > 1e-30, 1.0 / step, 0.0)
                            coded = jnp.round(value * factor).astype(jnp.int32)
                            send_q[way, c, r - 1, p, part, :] = coded.astype(send_q.dtype)
                            send_s[way, c, r - 1, p, pl.ds(line, 1), :] = jnp.sum(
                                jnp.where(eye, step, 0.0), axis=0, keepdims=True
                            )

                        plane = z + (far - r) * (1 - 2 * way)
                        fold(c, plane, p, inputs, code, early)
                        for copy in chain_copies(way, c, r, p):
                            copy.start()

    def rows_part(p):
        return pl.ds(pl.multiple_of(p * size, size), size)

    def side_copy(c, d, p, source=0, hop=None):
        hop = d if hop is None else hop
        origin = own.at[c] if source == 0 else out_ref.at[0, source, c]
        return pltpu.make_async_remote_copy(
            src_ref=origin.at[rows_part(p), :],
            dst_ref=out_ref.at[0, d, c, rows_part(p), :],
            send_sem=side_send.at[c, d, p],
            recv_sem=side_recv.at[c, d, p],
            device_id={"bins": side(hop)},
            device_id_type=MESH,
        )

    def pair_copy(c, d, p):
        source = own.at[c] if d == 0 else out_ref.at[0, d, c]
        return pltpu.make_async_remote_copy(
            src_ref=source.at[rows_part(p), :],
            dst_ref=out_ref.at[1, d, c, rows_part(p), :],
            send_sem=pair_send.at[c, d, p],
            recv_sem=pair_recv.at[c, d, p],
            device_id={"params": 1 - core},
            device_id_type=MESH,
        )

    def keep_copy(c, p):
        return pltpu.make_async_copy(
            own.at[c, rows_part(p), :], out_ref.at[0, 0, c, rows_part(p), :], own_sem.at[c, p]
        )

    def finish(c, p):
        @pl.when(z > 0)
        def _():
            wait_chain(0, c, far - 1, p)

        @pl.when(z < far - 1)
        def _():
            wait_chain(1, c, far - 1, p)

        def store(value, line, part, eye):
            row = pl.ds(pl.multiple_of(p * size + line * LANES, LANES), LANES)
            own[c, row, :] = value.astype(own.dtype)

        fold(c, z, p, [(0, far - 1, z > 0), (1, far - 1, z < far - 1)], store)
        for d in direct:
            side_copy(c, d, p).start()
        pair_copy(c, 0, p).start()
        keep_copy(c, p).start()

    def forward(c, p, act):
        if near == 4:
            @pl.when(lax.rem(p, 2) == 0)
            def _():
                act(side_copy(c, 3, p, 1, 2))

            @pl.when(lax.rem(p, 2) == 1)
            def _():
                act(side_copy(c, 3, p, 2, 1))

    def over(c, span, act):
        @pl.loop(span[0], span[1])
        def _(p):
            act(c, p)

    def relay(c, p):
        for d in direct:
            side_copy(c, d, p).wait_recv()
        forward(c, p, lambda copy: copy.start())
        for d in direct:
            pair_copy(c, d, p).start()

    def relay_last(c, p):
        for d in range(1, near):
            if d not in direct:
                side_copy(c, d, p).wait_recv()
                pair_copy(c, d, p).start()

    def stage_copy(c, d, p):
        return pltpu.make_async_copy(
            out_ref.at[0, d, c, rows_part(p), :], stage.at[p, d - 1], stage_sem.at[p, d - 1]
        )

    def fetch(c, p):
        for d in range(1, near):
            stage_copy(c, d, p).start()

    def weigh(c, p):
        for d in range(1, near):
            stage_copy(c, d, p).wait()
        piece = weighted_ref.shape[0] // near
        depth = 4 * LANES
        rows = lax.broadcasted_iota(jnp.int32, (piece, LANES), 0) + me * piece
        lanes = lax.broadcasted_iota(jnp.int32, (piece, LANES), 1) + c * LANES
        pick = (rows == lanes).astype(jnp.bfloat16)

        @pl.loop(0, size // depth)
        def _(b):
            eye = diagonal()
            curves = []
            for h in range(depth // LANES):
                at = p * (size // LANES) + b * (depth // LANES) + h
                line = curve_ref[pl.ds(at, 1), :]
                curves.append(jnp.sum(jnp.where(eye, line, 0.0), axis=1, keepdims=True))
            curve = jnp.concatenate(curves, axis=0)
            here_part = pl.ds(pl.multiple_of(b * depth, depth), depth)
            part = pl.ds(pl.multiple_of(p * size + b * depth, depth), depth)
            for d in range(near):
                if d == 0:
                    value = own[c, part, :]
                else:
                    value = stage[p, d - 1, here_part, :]
                value = (curve * value.astype(jnp.float32)).astype(jnp.bfloat16)
                picked = lax.dot_general(
                    pick, value, (((1,), (1,)), ((), ())), preferred_element_type=jnp.float32
                ).astype(weighted_ref.dtype)
                block = slice(d * piece, (d + 1) * piece)
                if c == 0:
                    weighted_ref[block, part] = picked
                else:
                    weighted_ref[block, part] += picked

    def weigh_all(c, span):
        over(c, span, relay_last)
        over(c, span, fetch)
        over(c, span, weigh)

    every = (0, pieces)
    groups = [(c, every) for c in range(chunks - 1)]
    groups += [(chunks - 1, (0, pieces // 2)), (chunks - 1, (pieces // 2, pieces))]
    for d in range(near):
        head_local(d).wait()
    for g, (c, span) in enumerate(groups):
        new = g == 0 or groups[g - 1][0] != c
        if new and c > 0:
            row_local(c).wait()
            for d in range(1, near):
                row_copy(c, d).wait_recv()
        rounds(c, span, 1, 2, g == 0)
        if g == 0:
            nominal_sums()
            row_local(0).wait()
            head_stay(0).wait()
            for d in range(1, near):
                head_stay(d).wait()
                row_copy(0, d).wait_recv()
        if g > 0:
            over(*groups[g - 1], finish)
        rounds(c, span, 2, far)
        if g == 0:
            finish_sums()
        if g > 0:
            over(*groups[g - 1], relay)
        if g > 1:
            weigh_all(*groups[g - 2])
    over(*groups[-1], finish)
    weigh_all(*groups[-2])
    over(*groups[-1], relay)
    weigh_all(*groups[-1])

    for k in range(1, far):
        sums_copy(k).wait_send()
    for d in range(1, near):
        data_copy(d).wait_send()
    for c in range(chunks):
        for d in range(1, near):
            row_copy(c, d).wait_send()

        @pl.loop(0, pieces)
        def _(p):
            keep_copy(c, p).wait()
            for d in direct:
                side_copy(c, d, p).wait_send()
            forward(c, p, lambda copy: copy.wait_send())
            for d in range(near):
                pair_copy(c, d, p).wait_send()
                pair_copy(c, d, p).wait_recv()

            @pl.loop(1, far)
            def _(r):
                for way in range(2):
                    step_in = z if way == 0 else far - 1 - z

                    @pl.when(step_in < r)
                    def _():
                        for copy in chain_copies(way, c, r, p):
                            copy.wait_send()


def chain(starts, local, worth, data, weights, firsts, near, far, chunks, slot, bins_dev):
    events = weights.shape[0]
    ahead = firsts[0].shape[0]
    pieces = near
    bins = near * bins_dev
    size = bins // pieces
    hops = (2, chunks, far - 1, pieces)
    lines = bins // LANES
    dma = pltpu.SemaphoreType.DMA
    rows = jnp.bfloat16
    table = jnp.float32
    return pl.pallas_call(
        functools.partial(chain_kernel, near, far, chunks, pieces, slot),
        out_shape=[
            jax.ShapeDtypeStruct((2, near, chunks, bins, LANES), rows),
            jax.ShapeDtypeStruct((chunks * LANES * near // far, bins), rows),
        ],
        in_specs=[pl.BlockSpec(memory_space=pltpu.SMEM)]
        + [pl.BlockSpec(memory_space=pltpu.VMEM)] * 3
        + [pl.BlockSpec(memory_space=pl.ANY)] * (1 + near),
        out_specs=[
            pl.BlockSpec(memory_space=pl.ANY),
            pl.BlockSpec(memory_space=pltpu.VMEM),
        ],
        scratch_shapes=[pltpu.VMEM((near, events, LANES), rows)] * chunks
        + [
            pltpu.VMEM((near, ahead, LANES), rows),
            pltpu.VMEM((far * lines, LANES), table),
            pltpu.VMEM((far - 1, lines, LANES), table),
            pltpu.VMEM((near - 1,) + data.shape, table),
            pltpu.VMEM((2, lines, LANES), table),
            pltpu.VMEM((lines, LANES), table),
            pltpu.VMEM((pieces, near - 1, size, LANES), rows),
            dma((pieces, near - 1)),
            dma((near,)),
            dma((near,)),
            dma((far - 1,)),
            dma((far - 1,)),
            dma((near - 1,)),
            dma((near - 1,)),
            pltpu.VMEM((near * slot, LANES), rows),
            pltpu.VMEM((TILE, LANES), table),
            pltpu.VMEM((chunks, bins, LANES), rows),
            pltpu.VMEM(hops + (size, LANES), jnp.int16),
            pltpu.VMEM(hops + (size // LANES, LANES), table),
            pltpu.VMEM(hops + (size, LANES), jnp.int16),
            pltpu.VMEM(hops + (size // LANES, LANES), table),
            dma((chunks,)),
            dma((chunks, near)),
            dma((chunks, near)),
            dma(hops),
            dma(hops),
            dma(hops),
            dma(hops),
            dma((chunks, pieces)),
            dma((chunks, near, pieces)),
            dma((chunks, near, pieces)),
            dma((chunks, near, pieces)),
            dma((chunks, near, pieces)),
        ],
        compiler_params=pltpu.CompilerParams(
            collective_id=3, has_side_effects=True, vmem_limit_bytes=62 << 20
        ),
        name="chain",
    )(starts, local, worth, data, weights, *firsts)


def tail_kernel(
    near, far, templates_ref, weighted, out_ref, held, total, coded, own, got,
    hand, kept, merged, sems, sends, recvs, hand_recvs,
):
    groups, _, chunks, bins, _ = templates_ref.shape
    here = lax.axis_index("bins")
    z, me = here // near, lax.rem(here, near)
    piece = own.shape[0]
    count = groups * near * chunks
    step = 2 * LANES

    def peer(k):
        return lax.rem(z + k, far)

    barrier = pltpu.get_barrier_semaphore()
    for k in range(1, far):
        pl.semaphore_signal(
            barrier, inc=1, device_id={"bins": peer(k) * near + me}, device_id_type=MESH
        )

    def fetch(n):
        part = templates_ref.at[n // (near * chunks), lax.rem(n // chunks, near), lax.rem(n, chunks)]
        return pltpu.make_async_copy(
            part, held.at[:, pl.ds(pl.multiple_of(n * LANES, LANES), LANES)], sems.at[n]
        )

    @pl.loop(0, count)
    def _(n):
        fetch(n).start()

    pl.semaphore_wait(barrier, far - 1)

    def rows_for(target):
        return pl.ds(pl.multiple_of(xor_of(me, target, near) * piece, 16), piece)

    def columns_of(n):
        return pl.ds(pl.multiple_of(n * step, step), step)

    def send(source, target, landed, j, n, to):
        return pltpu.make_async_remote_copy(
            src_ref=source,
            dst_ref=target.at[:, columns_of(n)],
            send_sem=sends.at[j, n],
            recv_sem=landed,
            device_id={"bins": to * near + me},
            device_id_type=MESH,
        )

    half = z // 2
    at_end = (z == 0) | (z == far - 1)
    within = 1 + half
    end = half * (far - 1)

    def to_inner(j, n):
        target = (far - 1 - within, far - 1 - z, within)[j]
        source = coded.at[rows_for(target), columns_of(n)]
        if j == 2:
            return send(source, got.at[half], recvs.at[half, n], j, n, within)
        return send(source, hand.at[j], hand_recvs.at[j, n], j, n, within)

    def from_inner(j, n):
        target = (far - 1 - z, far - 1 - end, end)[j]
        if j == 2:
            source = coded.at[rows_for(target), columns_of(n)]
        else:
            source = merged.at[j, :, columns_of(n)]
        return send(source, got.at[half], recvs.at[half, n], j, n, target)

    def merge(n):
        for j in range(2):
            to_inner(j, n).wait_recv()
            part = kept[j, :, columns_of(n)] + hand[j, :, columns_of(n)].astype(jnp.float32)
            merged[j, :, columns_of(n)] = part.astype(merged.dtype)
            from_inner(j, n).start()

    inner = jnp.logical_not(at_end)
    lag = 2

    @pl.loop(0, count // 2)
    def _(n):
        fetch(2 * n).wait()
        fetch(2 * n + 1).wait()
        total[...] = jnp.dot(
            weighted[...], held[:, columns_of(n)], preferred_element_type=jnp.float32
        )
        coded[:, columns_of(n)] = total[...].astype(coded.dtype)
        own[:, columns_of(n)] = total[rows_for(z), :]

        @pl.when(at_end)
        def _():
            for j in range(3):
                to_inner(j, n).start()

        @pl.when(inner)
        def _():
            from_inner(2, n).start()
            kept[0, :, columns_of(n)] = total[rows_for(far - 1 - z), :]
            kept[1, :, columns_of(n)] = total[rows_for(far - 1 - end), :]

        @pl.when(inner & (n >= lag))
        def _():
            merge(n - lag)

    @pl.when(inner)
    def _():
        @pl.loop(count // 2 - lag, count // 2)
        def _(n):
            merge(n)

    @pl.loop(0, count // 2)
    def _(n):
        for j in range(2):
            send(merged.at[0, :, columns_of(n)], got.at[j], recvs.at[j, n], 0, n, within).wait_recv()
        for side in range(2):
            place = 2 * n + side
            group = place // (near * chunks)
            d = lax.rem(place // chunks, near)
            start = ((group * near + xor_of(me, d, near)) * chunks + lax.rem(place, chunks)) * LANES
            part = pl.ds(pl.multiple_of(place * LANES, LANES), LANES)
            value = own[:, part]
            for j in range(2):
                value += got[j, :, part].astype(jnp.float32)
            out_ref[:, pl.ds(pl.multiple_of(start, LANES), LANES)] = value

    @pl.loop(0, count // 2)
    def _(n):
        for j in range(3):
            @pl.when(at_end)
            def _():
                to_inner(j, n).wait_send()

            @pl.when(inner)
            def _():
                from_inner(j, n).wait_send()


def tail(templates, weighted, near, far):
    groups, _, chunks, bins, _ = templates.shape
    piece = chunks * LANES // far
    columns = groups * near * chunks * LANES
    count = groups * near * chunks
    return pl.pallas_call(
        functools.partial(tail_kernel, near, far),
        out_shape=jax.ShapeDtypeStruct((piece, columns), jnp.float32),
        in_specs=[pl.BlockSpec(memory_space=pl.ANY), pl.BlockSpec(memory_space=pltpu.VMEM)],
        out_specs=pl.BlockSpec(memory_space=pltpu.VMEM),
        scratch_shapes=[
            pltpu.VMEM((bins, columns), jnp.bfloat16),
            pltpu.VMEM((near * piece, 2 * LANES), jnp.float32),
            pltpu.VMEM((near * piece, columns), jnp.bfloat16),
            pltpu.VMEM((piece, columns), jnp.float32),
            pltpu.VMEM((2, piece, columns), jnp.bfloat16),
            pltpu.VMEM((2, piece, columns), jnp.bfloat16),
            pltpu.VMEM((2, piece, columns), jnp.float32),
            pltpu.VMEM((2, piece, columns), jnp.bfloat16),
            pltpu.SemaphoreType.DMA((count,)),
            pltpu.SemaphoreType.DMA((3, count // 2)),
            pltpu.SemaphoreType.DMA((2, count // 2)),
            pltpu.SemaphoreType.DMA((2, count // 2)),
        ],
        compiler_params=pltpu.CompilerParams(
            collective_id=2, has_side_effects=True, vmem_limit_bytes=60 << 20
        ),
        name="tail",
    )(templates, weighted)


def body_by_parameters(event_bins, event_weights, nominal, background, observed):
    owners = lax.axis_size("bins")
    near = math.isqrt(owners)
    far = owners // near
    events = event_bins.shape[0]
    bins_dev = background.shape[0]
    width = event_weights.shape[1] // near
    chunks = width // LANES
    capacity = 3 * events // (2 * owners)
    slot = -(-capacity // 16) * 16 + 16
    ahead = min(-(-near * capacity // 16) * 16 + 16, events - 16)
    here = lax.axis_index("bins")
    z, me = here // near, lax.rem(here, near)
    around = [[(s, s // near * near + (s % near ^ d)) for s in range(owners)] for d in range(near)]

    def spread(value):
        return [value] + [shift(value, around[d]) for d in range(1, near)]

    firsts = []
    first_row = jnp.where(z < far // 2, events - ahead, 0)
    for d in range(near):
        corner = (first_row, (me ^ d) * width)
        firsts.append(lax.dynamic_slice(event_weights, corner, (ahead, LANES)))
    event_bins, firsts = lax.optimization_barrier((event_bins, firsts))
    firsts = [part if d == 0 else shift(part, around[d]) for d, part in enumerate(firsts)]

    marks = jnp.arange(owners, dtype=jnp.int32) * bins_dev
    before = jnp.sum((event_bins[None, :] < marks[:, None]).astype(jnp.int32), axis=1)
    starts = jnp.minimum(before // 16, (events - slot) // 16)
    places = slots_of(starts, event_bins, nominal, slot, bins_dev)
    places = jnp.stack(spread(places))

    starts = places[:, 2 * owners, :owners].astype(jnp.int32).reshape(-1)
    places = places[:, : 2 * owners].transpose(1, 0, 2).reshape(2 * owners, 1, near * slot)
    worth = places[owners:]
    places = places[:owners].astype(jnp.int32)
    data = jnp.concatenate([background, observed]).reshape(-1, LANES)
    templates, weighted = chain(
        starts, places, worth, data, event_weights, firsts, near, far, chunks, slot, bins_dev
    )
    summed = tail(templates, weighted, near, far)
    return summed * (1.0 / (bins_dev * owners))


def splits_by_parameters(mesh, event_bins, event_weights, background):
    owners, groups = mesh.shape["bins"], mesh.shape["params"]
    near = math.isqrt(owners)
    events = event_bins.shape[0] // owners
    width = event_weights.shape[1] // groups // max(near, 1)
    bins_dev = background.shape[0] // owners
    return (
        groups == 2
        and near == 4
        and near * near == owners
        and near & (near - 1) == 0
        and width % LANES == 0
        and width % (16 * near) == 0
        and events % LANES == 0
        and events >= 2 * LANES
        and bins_dev % (8 * LANES) == 0
    )


def solution(mesh):
    in_specs = (P("bins"), P("bins", "params"), P("bins"), P("bins"), P("bins"))
    out_specs = P(("params", "bins"), None)

    def run(event_bins, event_weights, nominal, background, observed):
        fits = splits_by_parameters(mesh, event_bins, event_weights, background)
        chosen = body_by_parameters if fits else body
        mapped = jax.shard_map(
            chosen, mesh=mesh, in_specs=in_specs, out_specs=out_specs, check_vma=False
        )
        return mapped(event_bins, event_weights, nominal, background, observed)

    return run
```

```python
import functools
import math

import jax
import jax.numpy as jnp
from jax import lax
from jax.experimental import pallas as pl
from jax.experimental.pallas import tpu as pltpu
from jax.sharding import PartitionSpec as P


ALIGN = 8
MESH = pl.DeviceIdType.MESH


def from_behind(value, axis, steps):
    count = lax.axis_size(axis)
    pairs = [(source, (source + steps) % count) for source in range(count)]
    return lax.ppermute(value, axis, pairs)


def pack_kernel(owners, slot, first, width, starts_ref, rows_ref, out_ref, held, in_sems, out_sems):
    def fetch(o):
        start = pl.multiple_of(starts_ref[o] * ALIGN, ALIGN)
        return pltpu.make_async_copy(
            rows_ref.at[pl.ds(start, slot), pl.ds(first, width)], held.at[o], in_sems.at[o]
        )

    def store(o):
        return pltpu.make_async_copy(held.at[o], out_ref.at[o], out_sems.at[o])

    @pl.loop(0, owners)
    def _(o):
        fetch(o).start()

    @pl.loop(0, owners)
    def _(o):
        fetch(o).wait()
        store(o).start()

    @pl.loop(0, owners)
    def _(o):
        store(o).wait()


def pack(starts, rows, slot, first, width):
    owners = starts.shape[0]
    return pl.pallas_call(
        functools.partial(pack_kernel, owners, slot, first, width),
        out_shape=jax.ShapeDtypeStruct((owners, slot, width), rows.dtype),
        in_specs=[
            pl.BlockSpec(memory_space=pltpu.SMEM),
            pl.BlockSpec(memory_space=pl.ANY),
        ],
        out_specs=pl.BlockSpec(memory_space=pl.ANY),
        scratch_shapes=[
            pltpu.VMEM((owners, slot, width), rows.dtype),
            pltpu.SemaphoreType.DMA((owners,)),
            pltpu.SemaphoreType.DMA((owners,)),
        ],
        compiler_params=pltpu.CompilerParams(vmem_limit_bytes=32 << 20),
        cost_estimate=pl.CostEstimate(
            flops=0, bytes_accessed=4 * owners * slot * width, transcendentals=0
        ),
        name="pack",
    )(starts, rows)


def meta_kernel(bins_dev, starts_ref, table_ref, out_ref):
    owners, _, slot = out_ref.shape
    events = table_ref.shape[1]
    table = table_ref[...]

    @pl.loop(0, owners)
    def _(o):
        start = starts_ref[o] * ALIGN
        turned = pltpu.roll(table, lax.rem(events - start, events), axis=1)[:, :slot]
        bins = turned[0:1] - (o * bins_dev).astype(jnp.float32)
        inside = (bins >= 0) & (bins < bins_dev)
        out_ref[o, 0:1, :] = jnp.where(inside, bins, -1.0)
        out_ref[o, 1:2, :] = turned[1:2]


def pack_meta(starts, table, slot, bins_dev):
    owners = starts.shape[0]
    return pl.pallas_call(
        functools.partial(meta_kernel, bins_dev),
        out_shape=jax.ShapeDtypeStruct((owners, 2, slot), jnp.float32),
        in_specs=[
            pl.BlockSpec(memory_space=pltpu.SMEM),
            pl.BlockSpec(memory_space=pltpu.VMEM),
        ],
        out_specs=pl.BlockSpec(memory_space=pltpu.VMEM),
        name="pack_meta",
    )(starts, table)


def hist_kernel(chunk, tile, local_ref, rows_ref, out_ref, hot):
    bins, total = hot.shape

    @pl.when(pl.program_id(0) == 0)
    def _():
        ids = lax.broadcasted_iota(jnp.int32, (bins, chunk), 0)

        @pl.loop(0, total // chunk)
        def _(k):
            part = pl.ds(pl.multiple_of(k * chunk, chunk), chunk)
            hot[:, part] = (ids == local_ref[:, part]).astype(jnp.bfloat16)

    @pl.loop(0, bins // tile)
    def _(m):
        part = pl.ds(pl.multiple_of(m * tile, tile), tile)
        out_ref[part, :] = jnp.dot(
            hot[part, :], rows_ref[...], preferred_element_type=jnp.float32
        ).astype(out_ref.dtype)


def histogram_of(local, rows, bins, block, dtype):
    total, width = rows.shape
    return pl.pallas_call(
        functools.partial(hist_kernel, math.gcd(total, 128), math.gcd(bins, 256)),
        grid=(width // block,),
        out_shape=jax.ShapeDtypeStruct((bins, width), dtype),
        in_specs=[
            pl.BlockSpec((1, total), lambda j: (0, 0)),
            pl.BlockSpec((total, block), lambda j: (0, j)),
        ],
        out_specs=pl.BlockSpec((bins, block), lambda j: (0, j)),
        scratch_shapes=[pltpu.VMEM((bins, total), jnp.bfloat16)],
        compiler_params=pltpu.CompilerParams(
            vmem_limit_bytes=40 << 20, dimension_semantics=("arbitrary",)
        ),
        cost_estimate=pl.CostEstimate(
            flops=2 * bins * total * width, bytes_accessed=2 * total * width, transcendentals=0
        ),
        name="histogram",
    )(local, rows)


def reduce_kernel(
    piece, shares_ref, out_ref, own, got_near, sums, got_far,
    own_sem, near_send, near_recv, far_send, far_recv,
):
    far, near, rows, _ = shares_ref.shape
    me = lax.axis_index("bins")
    f, n = me // near, lax.rem(me, near)

    def near_peer(d):
        return lax.rem(n + d, near)

    def far_peer(d):
        return lax.rem(f + d, far)

    barrier = pltpu.get_barrier_semaphore()
    for d in range(1, near):
        pl.semaphore_signal(
            barrier, inc=1, device_id={"bins": f * near + near_peer(d)}, device_id_type=MESH
        )
    for d in range(1, far):
        pl.semaphore_signal(
            barrier, inc=1, device_id={"bins": far_peer(d) * near + n}, device_id_type=MESH
        )
    pl.semaphore_wait(barrier, near + far - 2)

    def part_of(c):
        return pl.ds(pl.multiple_of(c * piece, piece), piece)

    def near_copy(d, c):
        return pltpu.make_async_remote_copy(
            src_ref=shares_ref.at[:, near_peer(d), part_of(c), :],
            dst_ref=got_near.at[d - 1, :, part_of(c), :],
            send_sem=near_send.at[d - 1, c],
            recv_sem=near_recv.at[d - 1, c],
            device_id={"bins": f * near + near_peer(d)},
            device_id_type=MESH,
        )

    def far_copy(d, c):
        return pltpu.make_async_remote_copy(
            src_ref=sums.at[far_peer(d), part_of(c), :],
            dst_ref=got_far.at[d - 1, part_of(c), :],
            send_sem=far_send.at[d - 1, c],
            recv_sem=far_recv.at[d - 1, c],
            device_id={"bins": far_peer(d) * near + n},
            device_id_type=MESH,
        )

    own_copy = pltpu.make_async_copy(shares_ref.at[:, n], own, own_sem)
    own_copy.start()
    pieces = rows // piece

    @pl.loop(0, pieces)
    def _(c):
        for d in range(1, near):
            near_copy(d, c).start()

    own_copy.wait()

    @pl.loop(0, pieces)
    def _(c):
        part = part_of(c)
        for d in range(1, near):
            near_copy(d, c).wait_recv()

        @pl.loop(0, far)
        def _(k):
            total = own[k, part, :].astype(jnp.float32)
            for d in range(1, near):
                total += got_near[d - 1, k, part, :].astype(jnp.float32)
            sums[k, part, :] = total

        for d in range(1, far):
            far_copy(d, c).start()

    @pl.loop(0, pieces)
    def _(c):
        part = part_of(c)
        for d in range(1, far):
            far_copy(d, c).wait_recv()
        total = sums[f, part, :]
        for d in range(1, far):
            total += got_far[d - 1, part, :]
        out_ref[part, :] = total
        for d in range(1, near):
            near_copy(d, c).wait_send()
        for d in range(1, far):
            far_copy(d, c).wait_send()


def reduce_shares(shares):
    owners, rows, cols = shares.shape
    near = math.isqrt(owners)
    while owners % near:
        near -= 1
    far = owners // near
    piece = 16 if rows % 16 == 0 else rows
    pieces = rows // piece
    return pl.pallas_call(
        functools.partial(reduce_kernel, piece),
        out_shape=jax.ShapeDtypeStruct((rows, cols), jnp.float32),
        in_specs=[pl.BlockSpec(memory_space=pl.ANY)],
        out_specs=pl.BlockSpec(memory_space=pltpu.VMEM),
        scratch_shapes=[
            pltpu.VMEM((far, rows, cols), shares.dtype),
            pltpu.VMEM((near - 1, far, rows, cols), shares.dtype),
            pltpu.VMEM((far, rows, cols), jnp.float32),
            pltpu.VMEM((far - 1, rows, cols), jnp.float32),
            pltpu.SemaphoreType.DMA,
            pltpu.SemaphoreType.DMA((near - 1, pieces)),
            pltpu.SemaphoreType.DMA((near - 1, pieces)),
            pltpu.SemaphoreType.DMA((far - 1, pieces)),
            pltpu.SemaphoreType.DMA((far - 1, pieces)),
        ],
        compiler_params=pltpu.CompilerParams(
            collective_id=1, has_side_effects=True, vmem_limit_bytes=40 << 20
        ),
        name="reduce_shares",
    )(shares.reshape(far, near, rows, cols))


def body(event_bins, event_weights, nominal, background, observed):
    owners = lax.axis_size("bins")
    groups_count = lax.axis_size("params")
    events = event_bins.shape[0]
    width_g = event_weights.shape[1]
    bins_dev = background.shape[0]
    capacity = 3 * events // (2 * owners)
    slot = -(-capacity // ALIGN) * ALIGN + ALIGN
    chunks = 2 if width_g % 512 == 0 else 1
    width = width_g // chunks
    block = math.gcd(width, 256)

    destination = event_bins // bins_dev
    targets = jnp.arange(owners, dtype=jnp.int32)
    before = jnp.sum((destination[None, :] < targets[:, None]).astype(jnp.int32), axis=1)
    starts = jnp.minimum(before // ALIGN, (events - slot) // ALIGN)

    table = jnp.stack([event_bins.astype(jnp.float32), nominal.astype(jnp.float32)])
    table = jnp.concatenate([table, jnp.zeros((6, events), jnp.float32)], axis=0)
    meta = pack_meta(starts, table, slot, bins_dev)
    got_meta = lax.all_to_all(meta, "bins", split_axis=0, concat_axis=0, tiled=True)
    local = got_meta[:, 0].astype(jnp.int32).reshape(1, owners * slot)
    got_nominal = got_meta[:, 1].astype(jnp.bfloat16).reshape(owners * slot, 1)
    got_nominal = jnp.broadcast_to(got_nominal, (owners * slot, 128))
    nominal_sum = histogram_of(local, got_nominal, bins_dev, 128, jnp.float32)[:, 0]
    yields = background + nominal_sum
    curvature = observed / (yields * yields)

    parts = []
    for c in range(chunks):
        packed = pack(starts, event_weights, slot, c * width, width)
        got = lax.all_to_all(packed, "bins", split_axis=0, concat_axis=0, tiled=True)
        got = got.reshape(owners * slot, width)
        parts.append(histogram_of(local, got, bins_dev, block, jnp.bfloat16))
    templates = jnp.concatenate(parts, axis=1)
    weighted = (curvature[:, None] * templates.astype(jnp.float32)).astype(jnp.bfloat16)
    pieces = [templates]
    for shift_by in range(1, groups_count // 2 + 1):
        shifted = [from_behind(part, "params", -shift_by) for part in parts]
        pieces.append(jnp.concatenate(shifted, axis=1))
    partners = jnp.concatenate(pieces, axis=1)
    dims = (((0,), (0,)), ((), ()))
    full = lax.dot_general(weighted, partners, dims, preferred_element_type=jnp.float32)
    full = full.astype(jnp.bfloat16)
    shares = full.reshape(owners, width_g // owners, full.shape[1])
    summed = reduce_shares(shares)
    return summed * (1.0 / (bins_dev * owners))


LANES = 128
TILE = 256


def shift(value, pairs):
    return lax.ppermute(value, "bins", pairs)


def xor_of(a, b, count):
    total, bit = 0, 1
    while bit < count:
        total = total + bit * lax.rem(a // bit + b // bit, 2)
        bit *= 2
    return total


def diagonal():
    rows = lax.broadcasted_iota(jnp.int32, (LANES, LANES), 0)
    return rows == lax.broadcasted_iota(jnp.int32, (LANES, LANES), 1)


def slots_kernel(bins_dev, starts_ref, ids_ref, nominal_ref, out_ref):
    owners = starts_ref.shape[0]
    slot = out_ref.shape[1]
    events = ids_ref.shape[1]
    first = lax.broadcasted_iota(jnp.int32, (8, events), 0) == 0
    table = jnp.where(first, ids_ref[...].astype(jnp.float32), nominal_ref[...].astype(jnp.float32))
    lanes = lax.broadcasted_iota(jnp.int32, (1, slot), 1)
    out_ref[pl.ds(2 * owners, 1), :] = jnp.zeros((1, slot), jnp.float32)

    @pl.loop(0, owners)
    def _(o):
        start = starts_ref[o]
        turned = pltpu.roll(table, lax.rem(events - start * 16, events), axis=1)
        bins = turned[0:1, :slot] - (o * bins_dev).astype(jnp.float32)
        inside = (bins >= 0) & (bins < bins_dev)
        out_ref[pl.ds(o, 1), :] = jnp.where(inside, bins, -1.0)
        out_ref[pl.ds(owners + o, 1), :] = turned[1:2, :slot]
        out_ref[pl.ds(2 * owners, 1), :] += jnp.where(lanes == o, start.astype(jnp.float32), 0.0)


def slots_of(starts, ids, nominal, slot, bins_dev):
    owners, events = starts.shape[0], ids.shape[0]
    return pl.pallas_call(
        functools.partial(slots_kernel, bins_dev),
        out_shape=jax.ShapeDtypeStruct((2 * owners + 1, slot), jnp.float32),
        in_specs=[pl.BlockSpec(memory_space=pltpu.SMEM)]
        + [pl.BlockSpec(memory_space=pltpu.VMEM)] * 2,
        out_specs=pl.BlockSpec(memory_space=pltpu.VMEM),
        name="slots",
    )(starts, ids.reshape(1, events), nominal.reshape(1, events))


def chain_kernel(
    near, far, chunks, pieces, slot, starts_ref, local_ref, worth_ref, data_ref, weights_ref, *refs
):
    firsts = refs[:near]
    out_ref, weighted_ref = refs[near : near + 2]
    rows_refs = refs[near + 2 : near + 2 + chunks]
    (
        heads, sums, got_sums, got_data, levels, curve_ref, stage, stage_sem,
        head_sem, head_keep, sums_send, sums_recv, data_send, data_recv,
        window, acc, own, send_q, send_s, got_q, got_s,
        row_sem, row_send, row_recv, q_send, q_recv, s_send, s_recv,
        own_sem, side_send, side_recv, pair_send, pair_recv,
    ) = refs[near + 2 + chunks :]
    owners = near * far
    here = lax.axis_index("bins")
    core = lax.axis_index("params")
    z, me = here // near, lax.rem(here, near)
    bins_dev = own.shape[1] // near
    width = chunks * LANES
    held = near // pieces
    size = held * bins_dev
    direct = [d for d in range(1, near) if near != 4 or d != 3]

    def side(d):
        return z * near + xor_of(me, d, near)

    def along(way):
        return (z + 1 - 2 * way) * near + me

    def peer(k):
        return lax.rem(z + k, far)

    barrier = pltpu.get_barrier_semaphore()
    for d in range(1, near):
        pl.semaphore_signal(barrier, inc=1, device_id={"bins": side(d)}, device_id_type=MESH)
    for k in range(1, far):
        pl.semaphore_signal(
            barrier, inc=1, device_id={"bins": peer(k) * near + me}, device_id_type=MESH
        )
    pl.semaphore_signal(barrier, inc=1, device_id={"params": 1 - core}, device_id_type=MESH)
    pl.semaphore_wait(barrier, near + far - 1)

    events = weights_ref.shape[0]
    ahead = firsts[0].shape[0]
    lower = (z < far // 2).astype(jnp.int32)
    head_start = lower * (events - ahead)
    rest_start = (1 - lower) * ahead

    def quarter(d, c):
        start = xor_of(me, d, near) * width + c * LANES
        return pl.ds(pl.multiple_of(start, LANES), LANES)

    def row_part(c):
        if c > 0:
            return pl.ds(0, events)
        return pl.ds(pl.multiple_of(rest_start, 16), events - ahead)

    def row_copy(c, d):
        return pltpu.make_async_remote_copy(
            src_ref=weights_ref.at[row_part(c), quarter(d, c)],
            dst_ref=rows_refs[c].at[d, row_part(c), :],
            send_sem=row_send.at[c, d],
            recv_sem=row_recv.at[c, d],
            device_id={"bins": side(d)},
            device_id_type=MESH,
        )

    def row_local(c):
        return pltpu.make_async_copy(
            weights_ref.at[row_part(c), quarter(0, c)],
            rows_refs[c].at[0, row_part(c), :],
            row_sem.at[c],
        )

    def head_local(d):
        return pltpu.make_async_copy(firsts[d], heads.at[d], head_sem.at[d])

    def head_stay(d):
        part = pl.ds(pl.multiple_of(head_start, 16), ahead)
        return pltpu.make_async_copy(firsts[d], rows_refs[0].at[d, part, :], head_keep.at[d])

    def sums_copy(k):
        lines_from = pl.ds(pl.multiple_of(peer(k) * curve_ref.shape[0], 8), curve_ref.shape[0])
        return pltpu.make_async_remote_copy(
            src_ref=sums.at[lines_from, :],
            dst_ref=got_sums.at[k - 1],
            send_sem=sums_send.at[k - 1],
            recv_sem=sums_recv.at[k - 1],
            device_id={"bins": peer(k) * near + me},
            device_id_type=MESH,
        )

    def data_copy(d):
        return pltpu.make_async_remote_copy(
            src_ref=data_ref,
            dst_ref=got_data.at[d - 1],
            send_sem=data_send.at[d - 1],
            recv_sem=data_recv.at[d - 1],
            device_id={"bins": side(d)},
            device_id_type=MESH,
        )

    for d in range(near):
        head_local(d).start()
    for d in range(1, near):
        data_copy(d).start()
    for c in range(chunks):
        for d in range(1, near):
            row_copy(c, d).start()
    for c in range(chunks):
        row_local(c).start()
    for d in range(near):
        head_stay(d).start()

    def nominal_sums():
        @pl.loop(0, owners)
        def _(o):
            @pl.loop(0, bins_dev // TILE)
            def _(k):
                bins = k * TILE + lax.broadcasted_iota(jnp.int32, (TILE, near * slot), 0)
                total = jnp.sum(
                    jnp.where(bins == local_ref[o], worth_ref[o], 0.0), axis=1, keepdims=True
                )
                for h in range(TILE // LANES):
                    part = total[h * LANES : (h + 1) * LANES]
                    line = o * (bins_dev // LANES) + k * (TILE // LANES) + h
                    sums[pl.ds(line, 1), :] = jnp.sum(
                        jnp.where(diagonal(), part, 0.0), axis=0, keepdims=True
                    )

        for k in range(1, far):
            sums_copy(k).start()

    def finish_sums():
        own_lines = pl.ds(pl.multiple_of(z * curve_ref.shape[0], 8), curve_ref.shape[0])
        total = sums[own_lines, :]
        for k in range(1, far):
            sums_copy(k).wait_recv()
            total += got_sums[k - 1]
        lines_dev = bins_dev // LANES
        levels[0, pl.ds(pl.multiple_of(me * lines_dev, 8), lines_dev), :] = data_ref[0:lines_dev, :]
        levels[1, pl.ds(pl.multiple_of(me * lines_dev, 8), lines_dev), :] = data_ref[
            lines_dev : 2 * lines_dev, :
        ]
        for d in range(1, near):
            data_copy(d).wait_recv()
            part = pl.ds(pl.multiple_of(xor_of(me, d, near) * lines_dev, 8), lines_dev)
            levels[0, part, :] = got_data[d - 1, 0:lines_dev, :]
            levels[1, part, :] = got_data[d - 1, lines_dev : 2 * lines_dev, :]
        yields = levels[0] + total
        curve_ref[...] = levels[1] / (yields * yields)

    def chain_copies(way, c, r, p):
        return [
            pltpu.make_async_remote_copy(
                src_ref=source.at[way, c, r - 1, p],
                dst_ref=target.at[way, c, r - 1, p],
                send_sem=sent.at[way, c, r - 1, p],
                recv_sem=landed.at[way, c, r - 1, p],
                device_id={"bins": along(way)},
                device_id_type=MESH,
            )
            for source, target, sent, landed in (
                (send_q, got_q, q_send, q_recv), (send_s, got_s, s_send, s_recv)
            )
        ]

    def fold(c, plane, p, inputs, finish, early=False):
        @pl.loop(0, held)
        def _(i):
            owner = plane * near + p * held + i
            for s in range(near):
                start = starts_ref[s * owners + owner]
                if early:
                    start = jnp.maximum(start - lower * ((events - ahead) // 16), 0)
                    part = heads[s, pl.ds(start * 16, slot), :]
                else:
                    part = rows_refs[c][s, pl.ds(start * 16, slot), :]
                window[s * slot : (s + 1) * slot, :] = part

            @pl.loop(0, bins_dev // TILE)
            def _(k):
                bins = k * TILE + lax.broadcasted_iota(jnp.int32, (TILE, near * slot), 0)
                hot = (bins == local_ref[owner]).astype(jnp.bfloat16)
                acc[...] = jnp.dot(hot, window[...], preferred_element_type=jnp.float32)
                base = i * (bins_dev // LANES) + k * (TILE // LANES)
                eye = diagonal()
                for way, r, has in inputs:
                    @pl.when(has)
                    def _():
                        for h in range(TILE // LANES):
                            line = base + h
                            part = pl.ds(pl.multiple_of(line * LANES, LANES), LANES)
                            step = got_s[way, c, r - 1, p, pl.ds(line, 1), :]
                            step = jnp.sum(jnp.where(eye, step, 0.0), axis=1, keepdims=True)
                            coded = got_q[way, c, r - 1, p, part, :].astype(jnp.int32)
                            acc[h * LANES : (h + 1) * LANES, :] += (
                                coded.astype(jnp.float32) * step
                            )
                for h in range(TILE // LANES):
                    line = base + h
                    part = pl.ds(pl.multiple_of(line * LANES, LANES), LANES)
                    finish(acc[h * LANES : (h + 1) * LANES, :], line, part, eye)

    def wait_chain(way, c, r, p):
        for copy in chain_copies(way, c, r, p):
            copy.wait_recv()

    def rounds(c, span, first, last, early=False):
        low, high = span

        @pl.loop(first, last)
        def _(r):
            @pl.loop(low, high)
            def _(p):
                for way in range(2):
                    step_in = z if way == 0 else far - 1 - z

                    @pl.when(step_in < r)
                    def _():
                        inputs = []
                        if first > 1:
                            has = step_in > 0
                            inputs = [(way, r - 1, has)]

                            @pl.when(has)
                            def _():
                                wait_chain(way, c, r - 1, p)

                        def code(value, line, part, eye):
                            most = jnp.max(jnp.abs(value), axis=1, keepdims=True)
                            wide = most * (2.0**23 + 1.0)
                            step = (wide + (most - wide)) * 2.0**-14
                            factor = jnp.where(most > 1e-30, 1.0 / step, 0.0)
                            coded = jnp.round(value * factor).astype(jnp.int32)
                            send_q[way, c, r - 1, p, part, :] = coded.astype(send_q.dtype)
                            send_s[way, c, r - 1, p, pl.ds(line, 1), :] = jnp.sum(
                                jnp.where(eye, step, 0.0), axis=0, keepdims=True
                            )

                        plane = z + (far - r) * (1 - 2 * way)
                        fold(c, plane, p, inputs, code, early)
                        for copy in chain_copies(way, c, r, p):
                            copy.start()

    def rows_part(p):
        return pl.ds(pl.multiple_of(p * size, size), size)

    def side_copy(c, d, p, source=0, hop=None):
        hop = d if hop is None else hop
        origin = own.at[c] if source == 0 else out_ref.at[0, source, c]
        return pltpu.make_async_remote_copy(
            src_ref=origin.at[rows_part(p), :],
            dst_ref=out_ref.at[0, d, c, rows_part(p), :],
            send_sem=side_send.at[c, d, p],
            recv_sem=side_recv.at[c, d, p],
            device_id={"bins": side(hop)},
            device_id_type=MESH,
        )

    def pair_copy(c, d, p):
        source = own.at[c] if d == 0 else out_ref.at[0, d, c]
        return pltpu.make_async_remote_copy(
            src_ref=source.at[rows_part(p), :],
            dst_ref=out_ref.at[1, d, c, rows_part(p), :],
            send_sem=pair_send.at[c, d, p],
            recv_sem=pair_recv.at[c, d, p],
            device_id={"params": 1 - core},
            device_id_type=MESH,
        )

    def keep_copy(c, p):
        return pltpu.make_async_copy(
            own.at[c, rows_part(p), :], out_ref.at[0, 0, c, rows_part(p), :], own_sem.at[c, p]
        )

    def finish(c, p):
        @pl.when(z > 0)
        def _():
            wait_chain(0, c, far - 1, p)

        @pl.when(z < far - 1)
        def _():
            wait_chain(1, c, far - 1, p)

        def store(value, line, part, eye):
            row = pl.ds(pl.multiple_of(p * size + line * LANES, LANES), LANES)
            own[c, row, :] = value.astype(own.dtype)

        fold(c, z, p, [(0, far - 1, z > 0), (1, far - 1, z < far - 1)], store)
        for d in direct:
            side_copy(c, d, p).start()
        pair_copy(c, 0, p).start()
        keep_copy(c, p).start()

    def forward(c, p, act):
        if near == 4:
            @pl.when(lax.rem(p, 2) == 0)
            def _():
                act(side_copy(c, 3, p, 1, 2))

            @pl.when(lax.rem(p, 2) == 1)
            def _():
                act(side_copy(c, 3, p, 2, 1))

    def over(c, span, act):
        @pl.loop(span[0], span[1])
        def _(p):
            act(c, p)

    def relay(c, p):
        for d in direct:
            side_copy(c, d, p).wait_recv()
        forward(c, p, lambda copy: copy.start())
        for d in direct:
            pair_copy(c, d, p).start()

    def relay_last(c, p):
        for d in range(1, near):
            if d not in direct:
                side_copy(c, d, p).wait_recv()
                pair_copy(c, d, p).start()

    def stage_copy(c, d, p):
        return pltpu.make_async_copy(
            out_ref.at[0, d, c, rows_part(p), :], stage.at[p, d - 1], stage_sem.at[p, d - 1]
        )

    def fetch(c, p):
        for d in range(1, near):
            stage_copy(c, d, p).start()

    def weigh(c, p):
        for d in range(1, near):
            stage_copy(c, d, p).wait()
        piece = weighted_ref.shape[0] // near
        depth = 4 * LANES
        rows = lax.broadcasted_iota(jnp.int32, (piece, LANES), 0) + me * piece
        lanes = lax.broadcasted_iota(jnp.int32, (piece, LANES), 1) + c * LANES
        pick = (rows == lanes).astype(jnp.bfloat16)

        @pl.loop(0, size // depth)
        def _(b):
            eye = diagonal()
            curves = []
            for h in range(depth // LANES):
                at = p * (size // LANES) + b * (depth // LANES) + h
                line = curve_ref[pl.ds(at, 1), :]
                curves.append(jnp.sum(jnp.where(eye, line, 0.0), axis=1, keepdims=True))
            curve = jnp.concatenate(curves, axis=0)
            here_part = pl.ds(pl.multiple_of(b * depth, depth), depth)
            part = pl.ds(pl.multiple_of(p * size + b * depth, depth), depth)
            for d in range(near):
                if d == 0:
                    value = own[c, part, :]
                else:
                    value = stage[p, d - 1, here_part, :]
                value = (curve * value.astype(jnp.float32)).astype(jnp.bfloat16)
                picked = lax.dot_general(
                    pick, value, (((1,), (1,)), ((), ())), preferred_element_type=jnp.float32
                ).astype(weighted_ref.dtype)
                block = slice(d * piece, (d + 1) * piece)
                if c == 0:
                    weighted_ref[block, part] = picked
                else:
                    weighted_ref[block, part] += picked

    def weigh_all(c, span):
        over(c, span, relay_last)
        over(c, span, fetch)
        over(c, span, weigh)

    every = (0, pieces)
    groups = [(c, every) for c in range(chunks - 1)]
    groups += [(chunks - 1, (0, pieces // 2)), (chunks - 1, (pieces // 2, pieces))]
    for d in range(near):
        head_local(d).wait()
    for g, (c, span) in enumerate(groups):
        new = g == 0 or groups[g - 1][0] != c
        if new and c > 0:
            row_local(c).wait()
            for d in range(1, near):
                row_copy(c, d).wait_recv()
        rounds(c, span, 1, 2, g == 0)
        if g == 0:
            nominal_sums()
            row_local(0).wait()
            head_stay(0).wait()
            for d in range(1, near):
                head_stay(d).wait()
                row_copy(0, d).wait_recv()
        if g > 0:
            over(*groups[g - 1], finish)
        rounds(c, span, 2, far)
        if g == 0:
            finish_sums()
        if g > 0:
            over(*groups[g - 1], relay)
        if g > 1:
            weigh_all(*groups[g - 2])
    over(*groups[-1], finish)
    weigh_all(*groups[-2])
    over(*groups[-1], relay)
    weigh_all(*groups[-1])

    for k in range(1, far):
        sums_copy(k).wait_send()
    for d in range(1, near):
        data_copy(d).wait_send()
    for c in range(chunks):
        for d in range(1, near):
            row_copy(c, d).wait_send()

        @pl.loop(0, pieces)
        def _(p):
            keep_copy(c, p).wait()
            for d in direct:
                side_copy(c, d, p).wait_send()
            forward(c, p, lambda copy: copy.wait_send())
            for d in range(near):
                pair_copy(c, d, p).wait_send()
                pair_copy(c, d, p).wait_recv()

            @pl.loop(1, far)
            def _(r):
                for way in range(2):
                    step_in = z if way == 0 else far - 1 - z

                    @pl.when(step_in < r)
                    def _():
                        for copy in chain_copies(way, c, r, p):
                            copy.wait_send()


def chain(starts, local, worth, data, weights, firsts, near, far, chunks, slot, bins_dev):
    events = weights.shape[0]
    ahead = firsts[0].shape[0]
    pieces = near
    bins = near * bins_dev
    size = bins // pieces
    hops = (2, chunks, far - 1, pieces)
    lines = bins // LANES
    dma = pltpu.SemaphoreType.DMA
    rows = jnp.bfloat16
    table = jnp.float32
    return pl.pallas_call(
        functools.partial(chain_kernel, near, far, chunks, pieces, slot),
        out_shape=[
            jax.ShapeDtypeStruct((2, near, chunks, bins, LANES), rows),
            jax.ShapeDtypeStruct((chunks * LANES * near // far, bins), rows),
        ],
        in_specs=[pl.BlockSpec(memory_space=pltpu.SMEM)]
        + [pl.BlockSpec(memory_space=pltpu.VMEM)] * 3
        + [pl.BlockSpec(memory_space=pl.ANY)] * (1 + near),
        out_specs=[
            pl.BlockSpec(memory_space=pl.ANY),
            pl.BlockSpec(memory_space=pltpu.VMEM),
        ],
        scratch_shapes=[pltpu.VMEM((near, events, LANES), rows)] * chunks
        + [
            pltpu.VMEM((near, ahead, LANES), rows),
            pltpu.VMEM((far * lines, LANES), table),
            pltpu.VMEM((far - 1, lines, LANES), table),
            pltpu.VMEM((near - 1,) + data.shape, table),
            pltpu.VMEM((2, lines, LANES), table),
            pltpu.VMEM((lines, LANES), table),
            pltpu.VMEM((pieces, near - 1, size, LANES), rows),
            dma((pieces, near - 1)),
            dma((near,)),
            dma((near,)),
            dma((far - 1,)),
            dma((far - 1,)),
            dma((near - 1,)),
            dma((near - 1,)),
            pltpu.VMEM((near * slot, LANES), rows),
            pltpu.VMEM((TILE, LANES), table),
            pltpu.VMEM((chunks, bins, LANES), rows),
            pltpu.VMEM(hops + (size, LANES), jnp.int16),
            pltpu.VMEM(hops + (size // LANES, LANES), table),
            pltpu.VMEM(hops + (size, LANES), jnp.int16),
            pltpu.VMEM(hops + (size // LANES, LANES), table),
            dma((chunks,)),
            dma((chunks, near)),
            dma((chunks, near)),
            dma(hops),
            dma(hops),
            dma(hops),
            dma(hops),
            dma((chunks, pieces)),
            dma((chunks, near, pieces)),
            dma((chunks, near, pieces)),
            dma((chunks, near, pieces)),
            dma((chunks, near, pieces)),
        ],
        compiler_params=pltpu.CompilerParams(
            collective_id=3, has_side_effects=True, vmem_limit_bytes=62 << 20
        ),
        name="chain",
    )(starts, local, worth, data, weights, *firsts)


def tail_kernel(
    near, far, templates_ref, weighted, out_ref, held, total, coded, own, got,
    hand, kept, merged, sems, sends, recvs, hand_recvs,
):
    groups, _, chunks, _, _ = templates_ref.shape
    here = lax.axis_index("bins")
    z, me = here // near, lax.rem(here, near)
    piece = own.shape[0]
    count = groups * near * chunks
    step = 2 * LANES

    def peer(k):
        return lax.rem(z + k, far)

    barrier = pltpu.get_barrier_semaphore()
    for k in range(1, far):
        pl.semaphore_signal(
            barrier, inc=1, device_id={"bins": peer(k) * near + me}, device_id_type=MESH
        )

    def fetch(n):
        part = templates_ref.at[n // (near * chunks), lax.rem(n // chunks, near), lax.rem(n, chunks)]
        return pltpu.make_async_copy(
            part, held.at[:, pl.ds(pl.multiple_of(n * LANES, LANES), LANES)], sems.at[n]
        )

    @pl.loop(0, count)
    def _(n):
        fetch(n).start()

    pl.semaphore_wait(barrier, far - 1)

    def rows_for(target):
        return pl.ds(pl.multiple_of(xor_of(me, target, near) * piece, 16), piece)

    def columns_of(n):
        return pl.ds(pl.multiple_of(n * step, step), step)

    def send(source, target, landed, j, n, to):
        return pltpu.make_async_remote_copy(
            src_ref=source,
            dst_ref=target.at[:, columns_of(n)],
            send_sem=sends.at[j, n],
            recv_sem=landed,
            device_id={"bins": to * near + me},
            device_id_type=MESH,
        )

    half = z // 2
    at_end = (z == 0) | (z == far - 1)
    within = 1 + half
    end = half * (far - 1)

    def to_inner(j, n):
        target = (far - 1 - within, far - 1 - z, within)[j]
        source = coded.at[rows_for(target), columns_of(n)]
        if j == 2:
            return send(source, got.at[half], recvs.at[half, n], j, n, within)
        return send(source, hand.at[j], hand_recvs.at[j, n], j, n, within)

    def from_inner(j, n):
        target = (far - 1 - z, far - 1 - end, end)[j]
        if j == 2:
            source = coded.at[rows_for(target), columns_of(n)]
        else:
            source = merged.at[j, :, columns_of(n)]
        return send(source, got.at[half], recvs.at[half, n], j, n, target)

    def merge(n):
        for j in range(2):
            to_inner(j, n).wait_recv()
            part = kept[j, :, columns_of(n)] + hand[j, :, columns_of(n)].astype(jnp.float32)
            merged[j, :, columns_of(n)] = part.astype(merged.dtype)
            from_inner(j, n).start()

    inner = jnp.logical_not(at_end)
    lag = 2

    @pl.loop(0, count // 2)
    def _(n):
        fetch(2 * n).wait()
        fetch(2 * n + 1).wait()
        total[...] = jnp.dot(
            weighted[...], held[:, columns_of(n)], preferred_element_type=jnp.float32
        )
        coded[:, columns_of(n)] = total[...].astype(coded.dtype)
        own[:, columns_of(n)] = total[rows_for(z), :]

        @pl.when(at_end)
        def _():
            for j in range(3):
                to_inner(j, n).start()

        @pl.when(inner)
        def _():
            from_inner(2, n).start()
            kept[0, :, columns_of(n)] = total[rows_for(far - 1 - z), :]
            kept[1, :, columns_of(n)] = total[rows_for(far - 1 - end), :]

        @pl.when(inner & (n >= lag))
        def _():
            merge(n - lag)

    @pl.when(inner)
    def _():
        @pl.loop(count // 2 - lag, count // 2)
        def _(n):
            merge(n)

    @pl.loop(0, count // 2)
    def _(n):
        for j in range(2):
            send(merged.at[0, :, columns_of(n)], got.at[j], recvs.at[j, n], 0, n, within).wait_recv()
        for side in range(2):
            place = 2 * n + side
            group = place // (near * chunks)
            d = lax.rem(place // chunks, near)
            start = ((group * near + xor_of(me, d, near)) * chunks + lax.rem(place, chunks)) * LANES
            part = pl.ds(pl.multiple_of(place * LANES, LANES), LANES)
            value = own[:, part]
            for j in range(2):
                value += got[j, :, part].astype(jnp.float32)
            out_ref[:, pl.ds(pl.multiple_of(start, LANES), LANES)] = value

    @pl.loop(0, count // 2)
    def _(n):
        for j in range(3):
            @pl.when(at_end)
            def _():
                to_inner(j, n).wait_send()

            @pl.when(inner)
            def _():
                from_inner(j, n).wait_send()


def tail(templates, weighted, near, far):
    groups, _, chunks, bins, _ = templates.shape
    piece = chunks * LANES // far
    columns = groups * near * chunks * LANES
    count = groups * near * chunks
    return pl.pallas_call(
        functools.partial(tail_kernel, near, far),
        out_shape=jax.ShapeDtypeStruct((piece, columns), jnp.float32),
        in_specs=[pl.BlockSpec(memory_space=pl.ANY), pl.BlockSpec(memory_space=pltpu.VMEM)],
        out_specs=pl.BlockSpec(memory_space=pltpu.VMEM),
        scratch_shapes=[
            pltpu.VMEM((bins, columns), jnp.bfloat16),
            pltpu.VMEM((near * piece, 2 * LANES), jnp.float32),
            pltpu.VMEM((near * piece, columns), jnp.bfloat16),
            pltpu.VMEM((piece, columns), jnp.float32),
            pltpu.VMEM((2, piece, columns), jnp.bfloat16),
            pltpu.VMEM((2, piece, columns), jnp.bfloat16),
            pltpu.VMEM((2, piece, columns), jnp.float32),
            pltpu.VMEM((2, piece, columns), jnp.bfloat16),
            pltpu.SemaphoreType.DMA((count,)),
            pltpu.SemaphoreType.DMA((3, count // 2)),
            pltpu.SemaphoreType.DMA((2, count // 2)),
            pltpu.SemaphoreType.DMA((2, count // 2)),
        ],
        compiler_params=pltpu.CompilerParams(
            collective_id=2, has_side_effects=True, vmem_limit_bytes=60 << 20
        ),
        name="tail",
    )(templates, weighted)


def body_by_parameters(event_bins, event_weights, nominal, background, observed):
    owners = lax.axis_size("bins")
    near = math.isqrt(owners)
    far = owners // near
    events = event_bins.shape[0]
    bins_dev = background.shape[0]
    width = event_weights.shape[1] // near
    chunks = width // LANES
    capacity = 3 * events // (2 * owners)
    slot = -(-capacity // 16) * 16 + 16
    ahead = min(-(-near * capacity // 16) * 16 + 16, events - 16)
    here = lax.axis_index("bins")
    z, me = here // near, lax.rem(here, near)
    around = [[(s, s // near * near + (s % near ^ d)) for s in range(owners)] for d in range(near)]

    def spread(value):
        return [value] + [shift(value, around[d]) for d in range(1, near)]

    firsts = []
    first_row = jnp.where(z < far // 2, events - ahead, 0)
    for d in range(near):
        corner = (first_row, (me ^ d) * width)
        firsts.append(lax.dynamic_slice(event_weights, corner, (ahead, LANES)))
    event_bins, firsts = lax.optimization_barrier((event_bins, firsts))
    for d in range(1, near):
        firsts[d] = shift(firsts[d], around[d])

    marks = jnp.arange(owners, dtype=jnp.int32) * bins_dev
    before = jnp.sum((event_bins[None, :] < marks[:, None]).astype(jnp.int32), axis=1)
    starts = jnp.minimum(before // 16, (events - slot) // 16)
    places = slots_of(starts, event_bins, nominal, slot, bins_dev)
    places = jnp.stack(spread(places))

    starts = places[:, 2 * owners, :owners].astype(jnp.int32).reshape(-1)
    places = places[:, : 2 * owners].transpose(1, 0, 2).reshape(2 * owners, 1, near * slot)
    worth = places[owners:]
    places = places[:owners].astype(jnp.int32)
    data = jnp.concatenate([background, observed]).reshape(-1, LANES)
    templates, weighted = chain(
        starts, places, worth, data, event_weights, firsts, near, far, chunks, slot, bins_dev
    )
    summed = tail(templates, weighted, near, far)
    return summed * (1.0 / (bins_dev * owners))


def splits_by_parameters(mesh, event_bins, event_weights, background):
    owners, groups = mesh.shape["bins"], mesh.shape["params"]
    near = math.isqrt(owners)
    events = event_bins.shape[0] // owners
    width = event_weights.shape[1] // groups // max(near, 1)
    bins_dev = background.shape[0] // owners
    return (
        groups == 2
        and near == 4
        and near * near == owners
        and near & (near - 1) == 0
        and width % LANES == 0
        and width % (16 * near) == 0
        and events % LANES == 0
        and events >= 2 * LANES
        and bins_dev % (8 * LANES) == 0
    )


def solution(mesh):
    in_specs = (P("bins"), P("bins", "params"), P("bins"), P("bins"), P("bins"))
    out_specs = P(("params", "bins"), None)

    def run(event_bins, event_weights, nominal, background, observed):
        fits = splits_by_parameters(mesh, event_bins, event_weights, background)
        chosen = body_by_parameters if fits else body
        mapped = jax.shard_map(
            chosen, mesh=mesh, in_specs=in_specs, out_specs=out_specs, check_vma=False
        )
        return mapped(event_bins, event_weights, nominal, background, observed)

    return run
```

```python
import functools
import math

import jax
import jax.numpy as jnp
from jax import lax
from jax.experimental import pallas as pl
from jax.experimental.pallas import tpu as pltpu
from jax.sharding import PartitionSpec as P


ALIGN = 8
MESH = pl.DeviceIdType.MESH


def from_behind(value, axis, steps):
    count = lax.axis_size(axis)
    pairs = [(source, (source + steps) % count) for source in range(count)]
    return lax.ppermute(value, axis, pairs)


def pack_kernel(owners, slot, first, width, starts_ref, rows_ref, out_ref, held, in_sems, out_sems):
    def fetch(o):
        start = pl.multiple_of(starts_ref[o] * ALIGN, ALIGN)
        return pltpu.make_async_copy(
            rows_ref.at[pl.ds(start, slot), pl.ds(first, width)], held.at[o], in_sems.at[o]
        )

    def store(o):
        return pltpu.make_async_copy(held.at[o], out_ref.at[o], out_sems.at[o])

    @pl.loop(0, owners)
    def _(o):
        fetch(o).start()

    @pl.loop(0, owners)
    def _(o):
        fetch(o).wait()
        store(o).start()

    @pl.loop(0, owners)
    def _(o):
        store(o).wait()


def pack(starts, rows, slot, first, width):
    owners = starts.shape[0]
    return pl.pallas_call(
        functools.partial(pack_kernel, owners, slot, first, width),
        out_shape=jax.ShapeDtypeStruct((owners, slot, width), rows.dtype),
        in_specs=[
            pl.BlockSpec(memory_space=pltpu.SMEM),
            pl.BlockSpec(memory_space=pl.ANY),
        ],
        out_specs=pl.BlockSpec(memory_space=pl.ANY),
        scratch_shapes=[
            pltpu.VMEM((owners, slot, width), rows.dtype),
            pltpu.SemaphoreType.DMA((owners,)),
            pltpu.SemaphoreType.DMA((owners,)),
        ],
        compiler_params=pltpu.CompilerParams(vmem_limit_bytes=32 << 20),
        cost_estimate=pl.CostEstimate(
            flops=0, bytes_accessed=4 * owners * slot * width, transcendentals=0
        ),
        name="pack",
    )(starts, rows)


def meta_kernel(bins_dev, starts_ref, table_ref, out_ref):
    owners, _, slot = out_ref.shape
    events = table_ref.shape[1]
    table = table_ref[...]

    @pl.loop(0, owners)
    def _(o):
        start = starts_ref[o] * ALIGN
        turned = pltpu.roll(table, lax.rem(events - start, events), axis=1)[:, :slot]
        bins = turned[0:1] - (o * bins_dev).astype(jnp.float32)
        inside = (bins >= 0) & (bins < bins_dev)
        out_ref[o, 0:1, :] = jnp.where(inside, bins, -1.0)
        out_ref[o, 1:2, :] = turned[1:2]


def pack_meta(starts, table, slot, bins_dev):
    owners = starts.shape[0]
    return pl.pallas_call(
        functools.partial(meta_kernel, bins_dev),
        out_shape=jax.ShapeDtypeStruct((owners, 2, slot), jnp.float32),
        in_specs=[
            pl.BlockSpec(memory_space=pltpu.SMEM),
            pl.BlockSpec(memory_space=pltpu.VMEM),
        ],
        out_specs=pl.BlockSpec(memory_space=pltpu.VMEM),
        name="pack_meta",
    )(starts, table)


def hist_kernel(chunk, tile, local_ref, rows_ref, out_ref, hot):
    bins, total = hot.shape

    @pl.when(pl.program_id(0) == 0)
    def _():
        ids = lax.broadcasted_iota(jnp.int32, (bins, chunk), 0)

        @pl.loop(0, total // chunk)
        def _(k):
            part = pl.ds(pl.multiple_of(k * chunk, chunk), chunk)
            hot[:, part] = (ids == local_ref[:, part]).astype(jnp.bfloat16)

    @pl.loop(0, bins // tile)
    def _(m):
        part = pl.ds(pl.multiple_of(m * tile, tile), tile)
        out_ref[part, :] = jnp.dot(
            hot[part, :], rows_ref[...], preferred_element_type=jnp.float32
        ).astype(out_ref.dtype)


def histogram_of(local, rows, bins, block, dtype):
    total, width = rows.shape
    return pl.pallas_call(
        functools.partial(hist_kernel, math.gcd(total, 128), math.gcd(bins, 256)),
        grid=(width // block,),
        out_shape=jax.ShapeDtypeStruct((bins, width), dtype),
        in_specs=[
            pl.BlockSpec((1, total), lambda j: (0, 0)),
            pl.BlockSpec((total, block), lambda j: (0, j)),
        ],
        out_specs=pl.BlockSpec((bins, block), lambda j: (0, j)),
        scratch_shapes=[pltpu.VMEM((bins, total), jnp.bfloat16)],
        compiler_params=pltpu.CompilerParams(
            vmem_limit_bytes=40 << 20, dimension_semantics=("arbitrary",)
        ),
        cost_estimate=pl.CostEstimate(
            flops=2 * bins * total * width, bytes_accessed=2 * total * width, transcendentals=0
        ),
        name="histogram",
    )(local, rows)


def reduce_kernel(
    piece, shares_ref, out_ref, own, got_near, sums, got_far,
    own_sem, near_send, near_recv, far_send, far_recv,
):
    far, near, rows, _ = shares_ref.shape
    me = lax.axis_index("bins")
    f, n = me // near, lax.rem(me, near)

    def near_peer(d):
        return lax.rem(n + d, near)

    def far_peer(d):
        return lax.rem(f + d, far)

    barrier = pltpu.get_barrier_semaphore()
    for d in range(1, near):
        pl.semaphore_signal(
            barrier, inc=1, device_id={"bins": f * near + near_peer(d)}, device_id_type=MESH
        )
    for d in range(1, far):
        pl.semaphore_signal(
            barrier, inc=1, device_id={"bins": far_peer(d) * near + n}, device_id_type=MESH
        )
    pl.semaphore_wait(barrier, near + far - 2)

    def part_of(c):
        return pl.ds(pl.multiple_of(c * piece, piece), piece)

    def near_copy(d, c):
        return pltpu.make_async_remote_copy(
            src_ref=shares_ref.at[:, near_peer(d), part_of(c), :],
            dst_ref=got_near.at[d - 1, :, part_of(c), :],
            send_sem=near_send.at[d - 1, c],
            recv_sem=near_recv.at[d - 1, c],
            device_id={"bins": f * near + near_peer(d)},
            device_id_type=MESH,
        )

    def far_copy(d, c):
        return pltpu.make_async_remote_copy(
            src_ref=sums.at[far_peer(d), part_of(c), :],
            dst_ref=got_far.at[d - 1, part_of(c), :],
            send_sem=far_send.at[d - 1, c],
            recv_sem=far_recv.at[d - 1, c],
            device_id={"bins": far_peer(d) * near + n},
            device_id_type=MESH,
        )

    own_copy = pltpu.make_async_copy(shares_ref.at[:, n], own, own_sem)
    own_copy.start()
    pieces = rows // piece

    @pl.loop(0, pieces)
    def _(c):
        for d in range(1, near):
            near_copy(d, c).start()

    own_copy.wait()

    @pl.loop(0, pieces)
    def _(c):
        part = part_of(c)
        for d in range(1, near):
            near_copy(d, c).wait_recv()

        @pl.loop(0, far)
        def _(k):
            total = own[k, part, :].astype(jnp.float32)
            for d in range(1, near):
                total += got_near[d - 1, k, part, :].astype(jnp.float32)
            sums[k, part, :] = total

        for d in range(1, far):
            far_copy(d, c).start()

    @pl.loop(0, pieces)
    def _(c):
        part = part_of(c)
        for d in range(1, far):
            far_copy(d, c).wait_recv()
        total = sums[f, part, :]
        for d in range(1, far):
            total += got_far[d - 1, part, :]
        out_ref[part, :] = total
        for d in range(1, near):
            near_copy(d, c).wait_send()
        for d in range(1, far):
            far_copy(d, c).wait_send()


def reduce_shares(shares):
    owners, rows, cols = shares.shape
    near = math.isqrt(owners)
    while owners % near:
        near -= 1
    far = owners // near
    piece = 16 if rows % 16 == 0 else rows
    pieces = rows // piece
    return pl.pallas_call(
        functools.partial(reduce_kernel, piece),
        out_shape=jax.ShapeDtypeStruct((rows, cols), jnp.float32),
        in_specs=[pl.BlockSpec(memory_space=pl.ANY)],
        out_specs=pl.BlockSpec(memory_space=pltpu.VMEM),
        scratch_shapes=[
            pltpu.VMEM((far, rows, cols), shares.dtype),
            pltpu.VMEM((near - 1, far, rows, cols), shares.dtype),
            pltpu.VMEM((far, rows, cols), jnp.float32),
            pltpu.VMEM((far - 1, rows, cols), jnp.float32),
            pltpu.SemaphoreType.DMA,
            pltpu.SemaphoreType.DMA((near - 1, pieces)),
            pltpu.SemaphoreType.DMA((near - 1, pieces)),
            pltpu.SemaphoreType.DMA((far - 1, pieces)),
            pltpu.SemaphoreType.DMA((far - 1, pieces)),
        ],
        compiler_params=pltpu.CompilerParams(
            collective_id=1, has_side_effects=True, vmem_limit_bytes=40 << 20
        ),
        name="reduce_shares",
    )(shares.reshape(far, near, rows, cols))


def body(event_bins, event_weights, nominal, background, observed):
    owners = lax.axis_size("bins")
    groups_count = lax.axis_size("params")
    events = event_bins.shape[0]
    width_g = event_weights.shape[1]
    bins_dev = background.shape[0]
    capacity = 3 * events // (2 * owners)
    slot = -(-capacity // ALIGN) * ALIGN + ALIGN
    chunks = 2 if width_g % 512 == 0 else 1
    width = width_g // chunks
    block = math.gcd(width, 256)

    destination = event_bins // bins_dev
    targets = jnp.arange(owners, dtype=jnp.int32)
    before = jnp.sum((destination[None, :] < targets[:, None]).astype(jnp.int32), axis=1)
    starts = jnp.minimum(before // ALIGN, (events - slot) // ALIGN)

    table = jnp.stack([event_bins.astype(jnp.float32), nominal.astype(jnp.float32)])
    table = jnp.concatenate([table, jnp.zeros((6, events), jnp.float32)], axis=0)
    meta = pack_meta(starts, table, slot, bins_dev)
    got_meta = lax.all_to_all(meta, "bins", split_axis=0, concat_axis=0, tiled=True)
    local = got_meta[:, 0].astype(jnp.int32).reshape(1, owners * slot)
    got_nominal = got_meta[:, 1].astype(jnp.bfloat16).reshape(owners * slot, 1)
    got_nominal = jnp.broadcast_to(got_nominal, (owners * slot, 128))
    nominal_sum = histogram_of(local, got_nominal, bins_dev, 128, jnp.float32)[:, 0]
    yields = background + nominal_sum
    curvature = observed / (yields * yields)

    parts = []
    for c in range(chunks):
        packed = pack(starts, event_weights, slot, c * width, width)
        got = lax.all_to_all(packed, "bins", split_axis=0, concat_axis=0, tiled=True)
        got = got.reshape(owners * slot, width)
        parts.append(histogram_of(local, got, bins_dev, block, jnp.bfloat16))
    templates = jnp.concatenate(parts, axis=1)
    weighted = (curvature[:, None] * templates.astype(jnp.float32)).astype(jnp.bfloat16)
    pieces = [templates]
    for shift_by in range(1, groups_count // 2 + 1):
        shifted = [from_behind(part, "params", -shift_by) for part in parts]
        pieces.append(jnp.concatenate(shifted, axis=1))
    partners = jnp.concatenate(pieces, axis=1)
    dims = (((0,), (0,)), ((), ()))
    full = lax.dot_general(weighted, partners, dims, preferred_element_type=jnp.float32)
    full = full.astype(jnp.bfloat16)
    shares = full.reshape(owners, width_g // owners, full.shape[1])
    summed = reduce_shares(shares)
    return summed * (1.0 / (bins_dev * owners))


LANES = 128
TILE = 256


def shift(value, pairs):
    return lax.ppermute(value, "bins", pairs)


def xor_of(a, b, count):
    total, bit = 0, 1
    while bit < count:
        total = total + bit * lax.rem(a // bit + b // bit, 2)
        bit *= 2
    return total


def diagonal():
    rows = lax.broadcasted_iota(jnp.int32, (LANES, LANES), 0)
    return rows == lax.broadcasted_iota(jnp.int32, (LANES, LANES), 1)


def slots_kernel(bins_dev, starts_ref, ids_ref, nominal_ref, out_ref):
    owners = starts_ref.shape[0]
    slot = out_ref.shape[1]
    events = ids_ref.shape[1]
    first = lax.broadcasted_iota(jnp.int32, (8, events), 0) == 0
    table = jnp.where(first, ids_ref[...].astype(jnp.float32), nominal_ref[...].astype(jnp.float32))
    lanes = lax.broadcasted_iota(jnp.int32, (1, slot), 1)
    out_ref[pl.ds(2 * owners, 1), :] = jnp.zeros((1, slot), jnp.float32)

    @pl.loop(0, owners)
    def _(o):
        start = starts_ref[o]
        turned = pltpu.roll(table, lax.rem(events - start * 16, events), axis=1)
        bins = turned[0:1, :slot] - (o * bins_dev).astype(jnp.float32)
        inside = (bins >= 0) & (bins < bins_dev)
        out_ref[pl.ds(o, 1), :] = jnp.where(inside, bins, -1.0)
        out_ref[pl.ds(owners + o, 1), :] = turned[1:2, :slot]
        out_ref[pl.ds(2 * owners, 1), :] += jnp.where(lanes == o, start.astype(jnp.float32), 0.0)


def slots_of(starts, ids, nominal, slot, bins_dev):
    owners, events = starts.shape[0], ids.shape[0]
    return pl.pallas_call(
        functools.partial(slots_kernel, bins_dev),
        out_shape=jax.ShapeDtypeStruct((2 * owners + 1, slot), jnp.float32),
        in_specs=[pl.BlockSpec(memory_space=pltpu.SMEM)]
        + [pl.BlockSpec(memory_space=pltpu.VMEM)] * 2,
        out_specs=pl.BlockSpec(memory_space=pltpu.VMEM),
        name="slots",
    )(starts, ids.reshape(1, events), nominal.reshape(1, events))


def chain_kernel(
    near, far, chunks, pieces, slot, starts_ref, local_ref, data_ref, weights_ref, *refs
):
    firsts = refs[:near]
    out_ref, weighted_ref = refs[near : near + 2]
    rows_refs = refs[near + 2 : near + 2 + chunks]
    (
        heads, sums, got_sums, got_data, levels, curve_ref, stage, stage_sem,
        head_sem, head_keep, sums_send, sums_recv, data_send, data_recv,
        window, acc, own, send_q, send_s, got_q, got_s,
        row_sem, row_send, row_recv, q_send, q_recv, s_send, s_recv,
        own_sem, side_send, side_recv, pair_send, pair_recv,
    ) = refs[near + 2 + chunks :]
    owners = near * far
    here = lax.axis_index("bins")
    core = lax.axis_index("params")
    z, me = here // near, lax.rem(here, near)
    bins_dev = own.shape[1] // near
    width = chunks * LANES
    held = near // pieces
    size = held * bins_dev
    direct = [1, 2]

    def side(d):
        return z * near + xor_of(me, d, near)

    def along(way):
        return (z + 1 - 2 * way) * near + me

    def peer(k):
        return lax.rem(z + k, far)

    barrier = pltpu.get_barrier_semaphore()
    for d in range(1, near):
        pl.semaphore_signal(barrier, inc=1, device_id={"bins": side(d)}, device_id_type=MESH)
    for k in range(1, far):
        pl.semaphore_signal(
            barrier, inc=1, device_id={"bins": peer(k) * near + me}, device_id_type=MESH
        )
    pl.semaphore_signal(barrier, inc=1, device_id={"params": 1 - core}, device_id_type=MESH)
    pl.semaphore_wait(barrier, near + far - 1)

    events = weights_ref.shape[0]
    ahead = firsts[0].shape[0]
    lower = (z < far // 2).astype(jnp.int32)
    head_start = lower * (events - ahead)
    rest_start = (1 - lower) * ahead

    def quarter(d, c):
        start = xor_of(me, d, near) * width + c * LANES
        return pl.ds(pl.multiple_of(start, LANES), LANES)

    def row_part(c):
        if c > 0:
            return pl.ds(0, events)
        return pl.ds(pl.multiple_of(rest_start, 16), events - ahead)

    def row_copy(c, d):
        return pltpu.make_async_remote_copy(
            src_ref=weights_ref.at[row_part(c), quarter(d, c)],
            dst_ref=rows_refs[c].at[d, row_part(c), :],
            send_sem=row_send.at[c, d],
            recv_sem=row_recv.at[c, d],
            device_id={"bins": side(d)},
            device_id_type=MESH,
        )

    def row_local(c):
        return pltpu.make_async_copy(
            weights_ref.at[row_part(c), quarter(0, c)],
            rows_refs[c].at[0, row_part(c), :],
            row_sem.at[c],
        )

    def head_local(d):
        return pltpu.make_async_copy(firsts[d], heads.at[d], head_sem.at[d])

    def head_stay(d):
        part = pl.ds(pl.multiple_of(head_start, 16), ahead)
        return pltpu.make_async_copy(firsts[d], rows_refs[0].at[d, part, :], head_keep.at[d])

    def sums_copy(k):
        lines_from = pl.ds(pl.multiple_of(peer(k) * curve_ref.shape[0], 8), curve_ref.shape[0])
        return pltpu.make_async_remote_copy(
            src_ref=sums.at[lines_from, :],
            dst_ref=got_sums.at[k - 1],
            send_sem=sums_send.at[k - 1],
            recv_sem=sums_recv.at[k - 1],
            device_id={"bins": peer(k) * near + me},
            device_id_type=MESH,
        )

    def data_copy(d):
        return pltpu.make_async_remote_copy(
            src_ref=data_ref,
            dst_ref=got_data.at[d - 1],
            send_sem=data_send.at[d - 1],
            recv_sem=data_recv.at[d - 1],
            device_id={"bins": side(d)},
            device_id_type=MESH,
        )

    for d in range(near):
        head_local(d).start()
    for d in range(1, near):
        data_copy(d).start()
    for c in range(chunks):
        for d in range(1, near):
            row_copy(c, d).start()
    for c in range(chunks):
        row_local(c).start()
    for d in range(near):
        head_stay(d).start()

    def nominal_sums():
        @pl.loop(0, owners)
        def _(o):
            ids = local_ref[pl.ds(o, 1), :].astype(jnp.int32)
            worth = local_ref[pl.ds(owners + o, 1), :]

            @pl.loop(0, bins_dev // TILE)
            def _(k):
                bins = k * TILE + lax.broadcasted_iota(jnp.int32, (TILE, near * slot), 0)
                total = jnp.sum(jnp.where(bins == ids, worth, 0.0), axis=1, keepdims=True)
                for h in range(TILE // LANES):
                    part = total[h * LANES : (h + 1) * LANES]
                    line = o * (bins_dev // LANES) + k * (TILE // LANES) + h
                    sums[pl.ds(line, 1), :] = jnp.sum(
                        jnp.where(diagonal(), part, 0.0), axis=0, keepdims=True
                    )

        for k in range(1, far):
            sums_copy(k).start()

    def finish_sums():
        own_lines = pl.ds(pl.multiple_of(z * curve_ref.shape[0], 8), curve_ref.shape[0])
        total = sums[own_lines, :]
        for k in range(1, far):
            sums_copy(k).wait_recv()
            total += got_sums[k - 1]
        lines_dev = bins_dev // LANES
        levels[0, pl.ds(pl.multiple_of(me * lines_dev, 8), lines_dev), :] = data_ref[0:lines_dev, :]
        levels[1, pl.ds(pl.multiple_of(me * lines_dev, 8), lines_dev), :] = data_ref[
            lines_dev : 2 * lines_dev, :
        ]
        for d in range(1, near):
            data_copy(d).wait_recv()
            part = pl.ds(pl.multiple_of(xor_of(me, d, near) * lines_dev, 8), lines_dev)
            levels[0, part, :] = got_data[d - 1, 0:lines_dev, :]
            levels[1, part, :] = got_data[d - 1, lines_dev : 2 * lines_dev, :]
        yields = levels[0] + total
        curve_ref[...] = levels[1] / (yields * yields)

    def chain_copies(way, c, r, p):
        return [
            pltpu.make_async_remote_copy(
                src_ref=source.at[way, c, r - 1, p],
                dst_ref=target.at[way, c, r - 1, p],
                send_sem=sent.at[way, c, r - 1, p],
                recv_sem=landed.at[way, c, r - 1, p],
                device_id={"bins": along(way)},
                device_id_type=MESH,
            )
            for source, target, sent, landed in (
                (send_q, got_q, q_send, q_recv), (send_s, got_s, s_send, s_recv)
            )
        ]

    def fold(c, plane, p, inputs, finish, early=False):
        @pl.loop(0, held)
        def _(i):
            owner = plane * near + p * held + i
            for s in range(near):
                start = starts_ref[s * owners + owner]
                if early:
                    start = jnp.maximum(start - lower * ((events - ahead) // 16), 0)
                    part = heads[s, pl.ds(start * 16, slot), :]
                else:
                    part = rows_refs[c][s, pl.ds(start * 16, slot), :]
                window[s * slot : (s + 1) * slot, :] = part

            ids = local_ref[pl.ds(owner, 1), :].astype(jnp.int32)

            @pl.loop(0, bins_dev // TILE)
            def _(k):
                bins = k * TILE + lax.broadcasted_iota(jnp.int32, (TILE, near * slot), 0)
                hot = (bins == ids).astype(jnp.bfloat16)
                acc[...] = jnp.dot(hot, window[...], preferred_element_type=jnp.float32)
                base = i * (bins_dev // LANES) + k * (TILE // LANES)
                eye = diagonal()
                for way, r, has in inputs:
                    @pl.when(has)
                    def _():
                        for h in range(TILE // LANES):
                            line = base + h
                            part = pl.ds(pl.multiple_of(line * LANES, LANES), LANES)
                            step = got_s[way, c, r - 1, p, pl.ds(line, 1), :]
                            step = jnp.sum(jnp.where(eye, step, 0.0), axis=1, keepdims=True)
                            coded = got_q[way, c, r - 1, p, part, :].astype(jnp.int32)
                            acc[h * LANES : (h + 1) * LANES, :] += (
                                coded.astype(jnp.float32) * step
                            )
                for h in range(TILE // LANES):
                    line = base + h
                    part = pl.ds(pl.multiple_of(line * LANES, LANES), LANES)
                    finish(acc[h * LANES : (h + 1) * LANES, :], line, part, eye)

    def wait_chain(way, c, r, p):
        for copy in chain_copies(way, c, r, p):
            copy.wait_recv()

    def rounds(c, span, first, last, early=False):
        low, high = span

        @pl.loop(first, last)
        def _(r):
            @pl.loop(low, high)
            def _(p):
                for way in range(2):
                    step_in = z if way == 0 else far - 1 - z

                    @pl.when(step_in < r)
                    def _():
                        inputs = []
                        if first > 1:
                            has = step_in > 0
                            inputs = [(way, r - 1, has)]

                            @pl.when(has)
                            def _():
                                wait_chain(way, c, r - 1, p)

                        def code(value, line, part, eye):
                            most = jnp.max(jnp.abs(value), axis=1, keepdims=True)
                            wide = most * (2.0**23 + 1.0)
                            step = (wide + (most - wide)) * 2.0**-14
                            factor = jnp.where(most > 1e-30, 1.0 / step, 0.0)
                            coded = jnp.round(value * factor).astype(jnp.int32)
                            send_q[way, c, r - 1, p, part, :] = coded.astype(send_q.dtype)
                            send_s[way, c, r - 1, p, pl.ds(line, 1), :] = jnp.sum(
                                jnp.where(eye, step, 0.0), axis=0, keepdims=True
                            )

                        plane = z + (far - r) * (1 - 2 * way)
                        fold(c, plane, p, inputs, code, early)
                        for copy in chain_copies(way, c, r, p):
                            copy.start()

    def rows_part(p):
        return pl.ds(pl.multiple_of(p * size, size), size)

    def side_copy(c, d, p, source=0, hop=None):
        hop = d if hop is None else hop
        origin = own.at[c] if source == 0 else out_ref.at[0, source, c]
        return pltpu.make_async_remote_copy(
            src_ref=origin.at[rows_part(p), :],
            dst_ref=out_ref.at[0, d, c, rows_part(p), :],
            send_sem=side_send.at[c, d, p],
            recv_sem=side_recv.at[c, d, p],
            device_id={"bins": side(hop)},
            device_id_type=MESH,
        )

    def pair_copy(c, d, p):
        source = own.at[c] if d == 0 else out_ref.at[0, d, c]
        return pltpu.make_async_remote_copy(
            src_ref=source.at[rows_part(p), :],
            dst_ref=out_ref.at[1, d, c, rows_part(p), :],
            send_sem=pair_send.at[c, d, p],
            recv_sem=pair_recv.at[c, d, p],
            device_id={"params": 1 - core},
            device_id_type=MESH,
        )

    def keep_copy(c, p):
        return pltpu.make_async_copy(
            own.at[c, rows_part(p), :], out_ref.at[0, 0, c, rows_part(p), :], own_sem.at[c, p]
        )

    def finish(c, p):
        @pl.when(z > 0)
        def _():
            wait_chain(0, c, far - 1, p)

        @pl.when(z < far - 1)
        def _():
            wait_chain(1, c, far - 1, p)

        def store(value, line, part, eye):
            row = pl.ds(pl.multiple_of(p * size + line * LANES, LANES), LANES)
            own[c, row, :] = value.astype(own.dtype)

        fold(c, z, p, [(0, far - 1, z > 0), (1, far - 1, z < far - 1)], store)
        for d in direct:
            side_copy(c, d, p).start()
        pair_copy(c, 0, p).start()
        keep_copy(c, p).start()

    def forward(c, p):
        copies = []
        for half, (source, hop, sem) in enumerate(((1, 2, 3), (2, 1, 0))):
            part = pl.ds(pl.multiple_of(p * size + half * (size // 2), size // 2), size // 2)
            copies.append(
                pltpu.make_async_remote_copy(
                    src_ref=out_ref.at[0, source, c, part, :],
                    dst_ref=out_ref.at[0, 3, c, part, :],
                    send_sem=side_send.at[c, sem, p],
                    recv_sem=side_recv.at[c, sem, p],
                    device_id={"bins": side(hop)},
                    device_id_type=MESH,
                )
            )
        return copies

    def stage_copy(c, d, p):
        return pltpu.make_async_copy(
            out_ref.at[0, d, c, rows_part(p), :], stage.at[p, d - 1], stage_sem.at[p, d - 1]
        )

    def over(c, span, act):
        @pl.loop(span[0], span[1])
        def _(p):
            act(c, p)

    def relay(c, p):
        for d in direct:
            side_copy(c, d, p).wait_recv()
        for copy in forward(c, p):
            copy.start()
        for d in direct:
            pair_copy(c, d, p).start()

    def relay_last(c, p):
        for d in direct:
            stage_copy(c, d, p).start()
        for copy in forward(c, p):
            copy.wait_recv()
        stage_copy(c, 3, p).start()
        pair_copy(c, 3, p).start()

    def weigh(c, p):
        for d in range(1, near):
            stage_copy(c, d, p).wait()
        piece = weighted_ref.shape[0] // near
        depth = 4 * LANES
        rows = lax.broadcasted_iota(jnp.int32, (piece, LANES), 0) + me * piece
        lanes = lax.broadcasted_iota(jnp.int32, (piece, LANES), 1) + c * LANES
        pick = (rows == lanes).astype(jnp.bfloat16)

        @pl.loop(0, size // depth)
        def _(b):
            eye = diagonal()
            curves = []
            for h in range(depth // LANES):
                at = p * (size // LANES) + b * (depth // LANES) + h
                line = curve_ref[pl.ds(at, 1), :]
                curves.append(jnp.sum(jnp.where(eye, line, 0.0), axis=1, keepdims=True))
            curve = jnp.concatenate(curves, axis=0)
            here_part = pl.ds(pl.multiple_of(b * depth, depth), depth)
            part = pl.ds(pl.multiple_of(p * size + b * depth, depth), depth)
            for d in range(near):
                if d == 0:
                    value = own[c, part, :]
                else:
                    value = stage[p, d - 1, here_part, :]
                value = (curve * value.astype(jnp.float32)).astype(jnp.bfloat16)
                picked = lax.dot_general(
                    pick, value, (((1,), (1,)), ((), ())), preferred_element_type=jnp.float32
                ).astype(weighted_ref.dtype)
                block = slice(d * piece, (d + 1) * piece)
                if c == 0:
                    weighted_ref[block, part] = picked
                else:
                    weighted_ref[block, part] += picked

    def weigh_all(c, span):
        over(c, span, relay_last)
        over(c, span, weigh)

    every = (0, pieces)
    groups = [(c, every) for c in range(chunks - 1)]
    groups += [(chunks - 1, (0, pieces // 2)), (chunks - 1, (pieces // 2, pieces))]
    for d in range(near):
        head_local(d).wait()
    for g, (c, span) in enumerate(groups):
        new = g == 0 or groups[g - 1][0] != c
        if new and c > 0:
            row_local(c).wait()
            for d in range(1, near):
                row_copy(c, d).wait_recv()
        rounds(c, span, 1, 2, g == 0)
        if g == 0:
            nominal_sums()
            row_local(0).wait()
            head_stay(0).wait()
            for d in range(1, near):
                head_stay(d).wait()
                row_copy(0, d).wait_recv()
        if g > 0:
            over(*groups[g - 1], finish)
        rounds(c, span, 2, far)
        if g == 0:
            finish_sums()
        if g > 0:
            over(*groups[g - 1], relay)
        if g > 1:
            weigh_all(*groups[g - 2])
    over(*groups[-1], finish)
    weigh_all(*groups[-2])
    over(*groups[-1], relay)
    weigh_all(*groups[-1])

    for k in range(1, far):
        sums_copy(k).wait_send()
    for d in range(1, near):
        data_copy(d).wait_send()
    for c in range(chunks):
        for d in range(1, near):
            row_copy(c, d).wait_send()

        @pl.loop(0, pieces)
        def _(p):
            keep_copy(c, p).wait()
            for d in direct:
                side_copy(c, d, p).wait_send()
            for copy in forward(c, p):
                copy.wait_send()
            for d in range(near):
                pair_copy(c, d, p).wait_send()
                pair_copy(c, d, p).wait_recv()

            @pl.loop(1, far)
            def _(r):
                for way in range(2):
                    step_in = z if way == 0 else far - 1 - z

                    @pl.when(step_in < r)
                    def _():
                        for copy in chain_copies(way, c, r, p):
                            copy.wait_send()


def chain(starts, local, data, weights, firsts, near, far, chunks, slot, bins_dev):
    events = weights.shape[0]
    ahead = firsts[0].shape[0]
    pieces = near
    bins = near * bins_dev
    size = bins // pieces
    hops = (2, chunks, far - 1, pieces)
    lines = bins // LANES
    dma = pltpu.SemaphoreType.DMA
    rows = jnp.bfloat16
    table = jnp.float32
    return pl.pallas_call(
        functools.partial(chain_kernel, near, far, chunks, pieces, slot),
        out_shape=[
            jax.ShapeDtypeStruct((2, near, chunks, bins, LANES), rows),
            jax.ShapeDtypeStruct((chunks * LANES * near // far, bins), rows),
        ],
        in_specs=[pl.BlockSpec(memory_space=pltpu.SMEM)]
        + [pl.BlockSpec(memory_space=pltpu.VMEM)] * 2
        + [pl.BlockSpec(memory_space=pl.ANY)] * (1 + near),
        out_specs=[
            pl.BlockSpec(memory_space=pl.ANY),
            pl.BlockSpec(memory_space=pltpu.VMEM),
        ],
        scratch_shapes=[pltpu.VMEM((near, events, LANES), rows)] * chunks
        + [
            pltpu.VMEM((near, ahead, LANES), rows),
            pltpu.VMEM((far * lines, LANES), table),
            pltpu.VMEM((far - 1, lines, LANES), table),
            pltpu.VMEM((near - 1,) + data.shape, table),
            pltpu.VMEM((2, lines, LANES), table),
            pltpu.VMEM((lines, LANES), table),
            pltpu.VMEM((pieces, near - 1, size, LANES), rows),
            dma((pieces, near - 1)),
            dma((near,)),
            dma((near,)),
            dma((far - 1,)),
            dma((far - 1,)),
            dma((near - 1,)),
            dma((near - 1,)),
            pltpu.VMEM((near * slot, LANES), rows),
            pltpu.VMEM((TILE, LANES), table),
            pltpu.VMEM((chunks, bins, LANES), rows),
            pltpu.VMEM(hops + (size, LANES), jnp.int16),
            pltpu.VMEM(hops + (size // LANES, LANES), table),
            pltpu.VMEM(hops + (size, LANES), jnp.int16),
            pltpu.VMEM(hops + (size // LANES, LANES), table),
            dma((chunks,)),
            dma((chunks, near)),
            dma((chunks, near)),
            dma(hops),
            dma(hops),
            dma(hops),
            dma(hops),
            dma((chunks, pieces)),
            dma((chunks, near, pieces)),
            dma((chunks, near, pieces)),
            dma((chunks, near, pieces)),
            dma((chunks, near, pieces)),
        ],
        compiler_params=pltpu.CompilerParams(
            collective_id=3, has_side_effects=True, vmem_limit_bytes=62 << 20
        ),
        name="chain",
    )(starts, local, data, weights, *firsts)


def tail_kernel(
    near, far, templates_ref, weighted, out_ref, held, total, coded, own, got,
    hand, kept, merged, sems, sends, recvs, hand_recvs,
):
    groups, _, chunks, _, _ = templates_ref.shape
    here = lax.axis_index("bins")
    z, me = here // near, lax.rem(here, near)
    piece = own.shape[0]
    count = groups * near * chunks
    step = 2 * LANES

    def peer(k):
        return lax.rem(z + k, far)

    barrier = pltpu.get_barrier_semaphore()
    for k in range(1, far):
        pl.semaphore_signal(
            barrier, inc=1, device_id={"bins": peer(k) * near + me}, device_id_type=MESH
        )

    def fetch(n):
        part = templates_ref.at[n // (near * chunks), lax.rem(n // chunks, near), lax.rem(n, chunks)]
        return pltpu.make_async_copy(
            part, held.at[:, pl.ds(pl.multiple_of(n * LANES, LANES), LANES)], sems.at[n]
        )

    @pl.loop(0, count)
    def _(n):
        fetch(n).start()

    pl.semaphore_wait(barrier, far - 1)

    def rows_for(target):
        return pl.ds(pl.multiple_of(xor_of(me, target, near) * piece, 16), piece)

    def columns_of(n):
        return pl.ds(pl.multiple_of(n * step, step), step)

    def send(source, target, landed, j, n, to):
        return pltpu.make_async_remote_copy(
            src_ref=source,
            dst_ref=target.at[:, columns_of(n)],
            send_sem=sends.at[j, n],
            recv_sem=landed,
            device_id={"bins": to * near + me},
            device_id_type=MESH,
        )

    half = z // 2
    at_end = (z == 0) | (z == far - 1)
    within = 1 + half
    end = half * (far - 1)

    def to_inner(j, n):
        target = (far - 1 - within, far - 1 - z, within)[j]
        source = coded.at[rows_for(target), columns_of(n)]
        if j == 2:
            return send(source, got.at[half], recvs.at[half, n], j, n, within)
        return send(source, hand.at[j], hand_recvs.at[j, n], j, n, within)

    def from_inner(j, n):
        target = (far - 1 - z, far - 1 - end, end)[j]
        if j == 2:
            source = coded.at[rows_for(target), columns_of(n)]
        else:
            source = merged.at[j, :, columns_of(n)]
        return send(source, got.at[half], recvs.at[half, n], j, n, target)

    def merge(n):
        for j in range(2):
            to_inner(j, n).wait_recv()
            part = kept[j, :, columns_of(n)] + hand[j, :, columns_of(n)].astype(jnp.float32)
            merged[j, :, columns_of(n)] = part.astype(merged.dtype)
            from_inner(j, n).start()

    inner = jnp.logical_not(at_end)
    lag = 2

    @pl.loop(0, count // 2)
    def _(n):
        fetch(2 * n).wait()
        fetch(2 * n + 1).wait()
        total[...] = jnp.dot(
            weighted[...], held[:, columns_of(n)], preferred_element_type=jnp.float32
        )
        coded[:, columns_of(n)] = total[...].astype(coded.dtype)
        own[:, columns_of(n)] = total[rows_for(z), :]

        @pl.when(at_end)
        def _():
            for j in range(3):
                to_inner(j, n).start()

        @pl.when(inner)
        def _():
            from_inner(2, n).start()
            kept[0, :, columns_of(n)] = total[rows_for(far - 1 - z), :]
            kept[1, :, columns_of(n)] = total[rows_for(far - 1 - end), :]

        @pl.when(inner & (n >= lag))
        def _():
            merge(n - lag)

    @pl.when(inner)
    def _():
        @pl.loop(count // 2 - lag, count // 2)
        def _(n):
            merge(n)

    @pl.loop(0, count // 2)
    def _(n):
        for j in range(2):
            send(merged.at[0, :, columns_of(n)], got.at[j], recvs.at[j, n], 0, n, within).wait_recv()
        for side in range(2):
            place = 2 * n + side
            group = place // (near * chunks)
            d = lax.rem(place // chunks, near)
            start = ((group * near + xor_of(me, d, near)) * chunks + lax.rem(place, chunks)) * LANES
            part = pl.ds(pl.multiple_of(place * LANES, LANES), LANES)
            value = own[:, part]
            for j in range(2):
                value += got[j, :, part].astype(jnp.float32)
            out_ref[:, pl.ds(pl.multiple_of(start, LANES), LANES)] = value

    @pl.loop(0, count // 2)
    def _(n):
        for j in range(3):
            @pl.when(at_end)
            def _():
                to_inner(j, n).wait_send()

            @pl.when(inner)
            def _():
                from_inner(j, n).wait_send()


def tail(templates, weighted, near, far):
    groups, _, chunks, bins, _ = templates.shape
    piece = chunks * LANES // far
    columns = groups * near * chunks * LANES
    count = groups * near * chunks
    return pl.pallas_call(
        functools.partial(tail_kernel, near, far),
        out_shape=jax.ShapeDtypeStruct((piece, columns), jnp.float32),
        in_specs=[pl.BlockSpec(memory_space=pl.ANY), pl.BlockSpec(memory_space=pltpu.VMEM)],
        out_specs=pl.BlockSpec(memory_space=pltpu.VMEM),
        scratch_shapes=[
            pltpu.VMEM((bins, columns), jnp.bfloat16),
            pltpu.VMEM((near * piece, 2 * LANES), jnp.float32),
            pltpu.VMEM((near * piece, columns), jnp.bfloat16),
            pltpu.VMEM((piece, columns), jnp.float32),
            pltpu.VMEM((2, piece, columns), jnp.bfloat16),
            pltpu.VMEM((2, piece, columns), jnp.bfloat16),
            pltpu.VMEM((2, piece, columns), jnp.float32),
            pltpu.VMEM((2, piece, columns), jnp.bfloat16),
            pltpu.SemaphoreType.DMA((count,)),
            pltpu.SemaphoreType.DMA((3, count // 2)),
            pltpu.SemaphoreType.DMA((2, count // 2)),
            pltpu.SemaphoreType.DMA((2, count // 2)),
        ],
        compiler_params=pltpu.CompilerParams(
            collective_id=2, has_side_effects=True, vmem_limit_bytes=60 << 20
        ),
        name="tail",
    )(templates, weighted)


def body_by_parameters(event_bins, event_weights, nominal, background, observed):
    owners = lax.axis_size("bins")
    near = math.isqrt(owners)
    far = owners // near
    events = event_bins.shape[0]
    bins_dev = background.shape[0]
    width = event_weights.shape[1] // near
    chunks = width // LANES
    capacity = 3 * events // (2 * owners)
    slot = -(-capacity // 16) * 16 + 16
    ahead = min(-(-near * capacity // 16) * 16 + 16, events - 16)
    here = lax.axis_index("bins")
    z, me = here // near, lax.rem(here, near)
    around = [[(s, s // near * near + (s % near ^ d)) for s in range(owners)] for d in range(near)]

    def spread(value):
        return [value] + [shift(value, around[d]) for d in range(1, near)]

    firsts = []
    first_row = jnp.where(z < far // 2, events - ahead, 0)
    for d in range(near):
        corner = (first_row, (me ^ d) * width)
        firsts.append(lax.dynamic_slice(event_weights, corner, (ahead, LANES)))
    event_bins, firsts = lax.optimization_barrier((event_bins, firsts))
    for d in range(1, near):
        firsts[d] = shift(firsts[d], around[d])

    marks = jnp.arange(owners, dtype=jnp.int32) * bins_dev
    before = jnp.sum((event_bins[None, :] < marks[:, None]).astype(jnp.int32), axis=1)
    starts = jnp.minimum(before // 16, (events - slot) // 16)
    places = slots_of(starts, event_bins, nominal, slot, bins_dev)
    places = jnp.stack(spread(places))

    starts = places[:, 2 * owners, :owners].astype(jnp.int32).reshape(-1)
    places = places.transpose(1, 0, 2).reshape(2 * owners + 1, near * slot)
    data = jnp.concatenate([background, observed]).reshape(-1, LANES)
    templates, weighted = chain(
        starts, places, data, event_weights, firsts, near, far, chunks, slot, bins_dev
    )
    summed = tail(templates, weighted, near, far)
    return summed * (1.0 / (bins_dev * owners))


def splits_by_parameters(mesh, event_bins, event_weights, background):
    owners, groups = mesh.shape["bins"], mesh.shape["params"]
    near = math.isqrt(owners)
    events = event_bins.shape[0] // owners
    width = event_weights.shape[1] // groups // max(near, 1)
    bins_dev = background.shape[0] // owners
    return (
        groups == 2
        and near == 4
        and near * near == owners
        and near & (near - 1) == 0
        and width % LANES == 0
        and width % (16 * near) == 0
        and events % LANES == 0
        and events >= 2 * LANES
        and bins_dev % (8 * LANES) == 0
    )


def solution(mesh):
    in_specs = (P("bins"), P("bins", "params"), P("bins"), P("bins"), P("bins"))
    out_specs = P(("params", "bins"), None)

    def run(event_bins, event_weights, nominal, background, observed):
        fits = splits_by_parameters(mesh, event_bins, event_weights, background)
        chosen = body_by_parameters if fits else body
        mapped = jax.shard_map(
            chosen, mesh=mesh, in_specs=in_specs, out_specs=out_specs, check_vma=False
        )
        return mapped(event_bins, event_weights, nominal, background, observed)

    return run
```

```python
import functools
import math

import jax
import jax.numpy as jnp
from jax import lax
from jax.experimental import pallas as pl
from jax.experimental.pallas import tpu as pltpu
from jax.sharding import PartitionSpec as P


ALIGN = 8
MESH = pl.DeviceIdType.MESH


def from_behind(value, axis, steps):
    count = lax.axis_size(axis)
    pairs = [(source, (source + steps) % count) for source in range(count)]
    return lax.ppermute(value, axis, pairs)


def pack_kernel(owners, slot, first, width, starts_ref, rows_ref, out_ref, held, in_sems, out_sems):
    def fetch(o):
        start = pl.multiple_of(starts_ref[o] * ALIGN, ALIGN)
        return pltpu.make_async_copy(
            rows_ref.at[pl.ds(start, slot), pl.ds(first, width)], held.at[o], in_sems.at[o]
        )

    def store(o):
        return pltpu.make_async_copy(held.at[o], out_ref.at[o], out_sems.at[o])

    @pl.loop(0, owners)
    def _(o):
        fetch(o).start()

    @pl.loop(0, owners)
    def _(o):
        fetch(o).wait()
        store(o).start()

    @pl.loop(0, owners)
    def _(o):
        store(o).wait()


def pack(starts, rows, slot, first, width):
    owners = starts.shape[0]
    return pl.pallas_call(
        functools.partial(pack_kernel, owners, slot, first, width),
        out_shape=jax.ShapeDtypeStruct((owners, slot, width), rows.dtype),
        in_specs=[
            pl.BlockSpec(memory_space=pltpu.SMEM),
            pl.BlockSpec(memory_space=pl.ANY),
        ],
        out_specs=pl.BlockSpec(memory_space=pl.ANY),
        scratch_shapes=[
            pltpu.VMEM((owners, slot, width), rows.dtype),
            pltpu.SemaphoreType.DMA((owners,)),
            pltpu.SemaphoreType.DMA((owners,)),
        ],
        compiler_params=pltpu.CompilerParams(vmem_limit_bytes=32 << 20),
        cost_estimate=pl.CostEstimate(
            flops=0, bytes_accessed=4 * owners * slot * width, transcendentals=0
        ),
        name="pack",
    )(starts, rows)


def meta_kernel(bins_dev, starts_ref, table_ref, out_ref):
    owners, _, slot = out_ref.shape
    events = table_ref.shape[1]
    table = table_ref[...]

    @pl.loop(0, owners)
    def _(o):
        start = starts_ref[o] * ALIGN
        turned = pltpu.roll(table, lax.rem(events - start, events), axis=1)[:, :slot]
        bins = turned[0:1] - (o * bins_dev).astype(jnp.float32)
        inside = (bins >= 0) & (bins < bins_dev)
        out_ref[o, 0:1, :] = jnp.where(inside, bins, -1.0)
        out_ref[o, 1:2, :] = turned[1:2]


def pack_meta(starts, table, slot, bins_dev):
    owners = starts.shape[0]
    return pl.pallas_call(
        functools.partial(meta_kernel, bins_dev),
        out_shape=jax.ShapeDtypeStruct((owners, 2, slot), jnp.float32),
        in_specs=[
            pl.BlockSpec(memory_space=pltpu.SMEM),
            pl.BlockSpec(memory_space=pltpu.VMEM),
        ],
        out_specs=pl.BlockSpec(memory_space=pltpu.VMEM),
        name="pack_meta",
    )(starts, table)


def hist_kernel(chunk, tile, local_ref, rows_ref, out_ref, hot):
    bins, total = hot.shape

    @pl.when(pl.program_id(0) == 0)
    def _():
        ids = lax.broadcasted_iota(jnp.int32, (bins, chunk), 0)

        @pl.loop(0, total // chunk)
        def _(k):
            part = pl.ds(pl.multiple_of(k * chunk, chunk), chunk)
            hot[:, part] = (ids == local_ref[:, part]).astype(jnp.bfloat16)

    @pl.loop(0, bins // tile)
    def _(m):
        part = pl.ds(pl.multiple_of(m * tile, tile), tile)
        out_ref[part, :] = jnp.dot(
            hot[part, :], rows_ref[...], preferred_element_type=jnp.float32
        ).astype(out_ref.dtype)


def histogram_of(local, rows, bins, block, dtype):
    total, width = rows.shape
    return pl.pallas_call(
        functools.partial(hist_kernel, math.gcd(total, 128), math.gcd(bins, 256)),
        grid=(width // block,),
        out_shape=jax.ShapeDtypeStruct((bins, width), dtype),
        in_specs=[
            pl.BlockSpec((1, total), lambda j: (0, 0)),
            pl.BlockSpec((total, block), lambda j: (0, j)),
        ],
        out_specs=pl.BlockSpec((bins, block), lambda j: (0, j)),
        scratch_shapes=[pltpu.VMEM((bins, total), jnp.bfloat16)],
        compiler_params=pltpu.CompilerParams(
            vmem_limit_bytes=40 << 20, dimension_semantics=("arbitrary",)
        ),
        cost_estimate=pl.CostEstimate(
            flops=2 * bins * total * width, bytes_accessed=2 * total * width, transcendentals=0
        ),
        name="histogram",
    )(local, rows)


def reduce_kernel(
    piece, shares_ref, out_ref, own, got_near, sums, got_far,
    own_sem, near_send, near_recv, far_send, far_recv,
):
    far, near, rows, _ = shares_ref.shape
    me = lax.axis_index("bins")
    f, n = me // near, lax.rem(me, near)

    def near_peer(d):
        return lax.rem(n + d, near)

    def far_peer(d):
        return lax.rem(f + d, far)

    barrier = pltpu.get_barrier_semaphore()
    for d in range(1, near):
        pl.semaphore_signal(
            barrier, inc=1, device_id={"bins": f * near + near_peer(d)}, device_id_type=MESH
        )
    for d in range(1, far):
        pl.semaphore_signal(
            barrier, inc=1, device_id={"bins": far_peer(d) * near + n}, device_id_type=MESH
        )
    pl.semaphore_wait(barrier, near + far - 2)

    def part_of(c):
        return pl.ds(pl.multiple_of(c * piece, piece), piece)

    def near_copy(d, c):
        return pltpu.make_async_remote_copy(
            src_ref=shares_ref.at[:, near_peer(d), part_of(c), :],
            dst_ref=got_near.at[d - 1, :, part_of(c), :],
            send_sem=near_send.at[d - 1, c],
            recv_sem=near_recv.at[d - 1, c],
            device_id={"bins": f * near + near_peer(d)},
            device_id_type=MESH,
        )

    def far_copy(d, c):
        return pltpu.make_async_remote_copy(
            src_ref=sums.at[far_peer(d), part_of(c), :],
            dst_ref=got_far.at[d - 1, part_of(c), :],
            send_sem=far_send.at[d - 1, c],
            recv_sem=far_recv.at[d - 1, c],
            device_id={"bins": far_peer(d) * near + n},
            device_id_type=MESH,
        )

    own_copy = pltpu.make_async_copy(shares_ref.at[:, n], own, own_sem)
    own_copy.start()
    pieces = rows // piece

    @pl.loop(0, pieces)
    def _(c):
        for d in range(1, near):
            near_copy(d, c).start()

    own_copy.wait()

    @pl.loop(0, pieces)
    def _(c):
        part = part_of(c)
        for d in range(1, near):
            near_copy(d, c).wait_recv()

        @pl.loop(0, far)
        def _(k):
            total = own[k, part, :].astype(jnp.float32)
            for d in range(1, near):
                total += got_near[d - 1, k, part, :].astype(jnp.float32)
            sums[k, part, :] = total

        for d in range(1, far):
            far_copy(d, c).start()

    @pl.loop(0, pieces)
    def _(c):
        part = part_of(c)
        for d in range(1, far):
            far_copy(d, c).wait_recv()
        total = sums[f, part, :]
        for d in range(1, far):
            total += got_far[d - 1, part, :]
        out_ref[part, :] = total
        for d in range(1, near):
            near_copy(d, c).wait_send()
        for d in range(1, far):
            far_copy(d, c).wait_send()


def reduce_shares(shares):
    owners, rows, cols = shares.shape
    near = math.isqrt(owners)
    while owners % near:
        near -= 1
    far = owners // near
    piece = 16 if rows % 16 == 0 else rows
    pieces = rows // piece
    return pl.pallas_call(
        functools.partial(reduce_kernel, piece),
        out_shape=jax.ShapeDtypeStruct((rows, cols), jnp.float32),
        in_specs=[pl.BlockSpec(memory_space=pl.ANY)],
        out_specs=pl.BlockSpec(memory_space=pltpu.VMEM),
        scratch_shapes=[
            pltpu.VMEM((far, rows, cols), shares.dtype),
            pltpu.VMEM((near - 1, far, rows, cols), shares.dtype),
            pltpu.VMEM((far, rows, cols), jnp.float32),
            pltpu.VMEM((far - 1, rows, cols), jnp.float32),
            pltpu.SemaphoreType.DMA,
            pltpu.SemaphoreType.DMA((near - 1, pieces)),
            pltpu.SemaphoreType.DMA((near - 1, pieces)),
            pltpu.SemaphoreType.DMA((far - 1, pieces)),
            pltpu.SemaphoreType.DMA((far - 1, pieces)),
        ],
        compiler_params=pltpu.CompilerParams(
            collective_id=1, has_side_effects=True, vmem_limit_bytes=40 << 20
        ),
        name="reduce_shares",
    )(shares.reshape(far, near, rows, cols))


def body(event_bins, event_weights, nominal, background, observed):
    owners = lax.axis_size("bins")
    groups_count = lax.axis_size("params")
    events = event_bins.shape[0]
    width_g = event_weights.shape[1]
    bins_dev = background.shape[0]
    capacity = 3 * events // (2 * owners)
    slot = -(-capacity // ALIGN) * ALIGN + ALIGN
    chunks = 2 if width_g % 512 == 0 else 1
    width = width_g // chunks
    block = math.gcd(width, 256)

    destination = event_bins // bins_dev
    targets = jnp.arange(owners, dtype=jnp.int32)
    before = jnp.sum((destination[None, :] < targets[:, None]).astype(jnp.int32), axis=1)
    starts = jnp.minimum(before // ALIGN, (events - slot) // ALIGN)

    table = jnp.stack([event_bins.astype(jnp.float32), nominal.astype(jnp.float32)])
    table = jnp.concatenate([table, jnp.zeros((6, events), jnp.float32)], axis=0)
    meta = pack_meta(starts, table, slot, bins_dev)
    got_meta = lax.all_to_all(meta, "bins", split_axis=0, concat_axis=0, tiled=True)
    local = got_meta[:, 0].astype(jnp.int32).reshape(1, owners * slot)
    got_nominal = got_meta[:, 1].astype(jnp.bfloat16).reshape(owners * slot, 1)
    got_nominal = jnp.broadcast_to(got_nominal, (owners * slot, 128))
    nominal_sum = histogram_of(local, got_nominal, bins_dev, 128, jnp.float32)[:, 0]
    yields = background + nominal_sum
    curvature = observed / (yields * yields)

    parts = []
    for c in range(chunks):
        packed = pack(starts, event_weights, slot, c * width, width)
        got = lax.all_to_all(packed, "bins", split_axis=0, concat_axis=0, tiled=True)
        got = got.reshape(owners * slot, width)
        parts.append(histogram_of(local, got, bins_dev, block, jnp.bfloat16))
    templates = jnp.concatenate(parts, axis=1)
    weighted = (curvature[:, None] * templates.astype(jnp.float32)).astype(jnp.bfloat16)
    pieces = [templates]
    for shift_by in range(1, groups_count // 2 + 1):
        shifted = [from_behind(part, "params", -shift_by) for part in parts]
        pieces.append(jnp.concatenate(shifted, axis=1))
    partners = jnp.concatenate(pieces, axis=1)
    dims = (((0,), (0,)), ((), ()))
    full = lax.dot_general(weighted, partners, dims, preferred_element_type=jnp.float32)
    full = full.astype(jnp.bfloat16)
    shares = full.reshape(owners, width_g // owners, full.shape[1])
    summed = reduce_shares(shares)
    return summed * (1.0 / (bins_dev * owners))


LANES = 128
TILE = 256


def shift(value, pairs):
    return lax.ppermute(value, "bins", pairs)


def xor_of(a, b, count):
    total, bit = 0, 1
    while bit < count:
        total = total + bit * lax.rem(a // bit + b // bit, 2)
        bit *= 2
    return total


def diagonal():
    rows = lax.broadcasted_iota(jnp.int32, (LANES, LANES), 0)
    return rows == lax.broadcasted_iota(jnp.int32, (LANES, LANES), 1)


def slots_kernel(bins_dev, starts_ref, ids_ref, nominal_ref, out_ref):
    owners = starts_ref.shape[0]
    slot = out_ref.shape[1]
    events = ids_ref.shape[1]
    first = lax.broadcasted_iota(jnp.int32, (8, events), 0) == 0
    table = jnp.where(first, ids_ref[...].astype(jnp.float32), nominal_ref[...].astype(jnp.float32))
    lanes = lax.broadcasted_iota(jnp.int32, (1, slot), 1)
    out_ref[pl.ds(2 * owners, 1), :] = jnp.zeros((1, slot), jnp.float32)

    @pl.loop(0, owners)
    def _(o):
        start = starts_ref[o]
        turned = pltpu.roll(table, lax.rem(events - start * 16, events), axis=1)
        bins = turned[0:1, :slot] - (o * bins_dev).astype(jnp.float32)
        inside = (bins >= 0) & (bins < bins_dev)
        out_ref[pl.ds(o, 1), :] = jnp.where(inside, bins, -1.0)
        out_ref[pl.ds(owners + o, 1), :] = turned[1:2, :slot]
        out_ref[pl.ds(2 * owners, 1), :] += jnp.where(lanes == o, start.astype(jnp.float32), 0.0)


def slots_of(starts, ids, nominal, slot, bins_dev):
    owners, events = starts.shape[0], ids.shape[0]
    return pl.pallas_call(
        functools.partial(slots_kernel, bins_dev),
        out_shape=jax.ShapeDtypeStruct((2 * owners + 1, slot), jnp.float32),
        in_specs=[pl.BlockSpec(memory_space=pltpu.SMEM)]
        + [pl.BlockSpec(memory_space=pltpu.VMEM)] * 2,
        out_specs=pl.BlockSpec(memory_space=pltpu.VMEM),
        name="slots",
    )(starts, ids.reshape(1, events), nominal.reshape(1, events))


def chain_kernel(
    near, far, chunks, pieces, slot, starts_ref, local_ref, data_ref, weights_ref, *refs
):
    firsts = refs[:near]
    out_ref, weighted_ref = refs[near : near + 2]
    rows_refs = refs[near + 2 : near + 2 + chunks]
    (
        heads, sums, got_sums, got_data, levels, curve_ref, curve_wide, stage, stage_sem,
        head_sem, head_keep, sums_send, sums_recv, data_send, data_recv,
        window, acc, own, send_q, send_s, got_q, got_s,
        row_sem, row_send, row_recv, q_send, q_recv, s_send, s_recv,
        own_sem, side_send, side_recv, pair_send, pair_recv,
    ) = refs[near + 2 + chunks :]
    owners = near * far
    here = lax.axis_index("bins")
    core = lax.axis_index("params")
    z, me = here // near, lax.rem(here, near)
    bins_dev = own.shape[1] // near
    width = chunks * LANES
    held = near // pieces
    size = held * bins_dev
    direct = [1, 2]

    def side(d):
        return z * near + xor_of(me, d, near)

    def along(way):
        return (z + 1 - 2 * way) * near + me

    def peer(k):
        return lax.rem(z + k, far)

    barrier = pltpu.get_barrier_semaphore()
    for d in range(1, near):
        pl.semaphore_signal(barrier, inc=1, device_id={"bins": side(d)}, device_id_type=MESH)
    for k in range(1, far):
        pl.semaphore_signal(
            barrier, inc=1, device_id={"bins": peer(k) * near + me}, device_id_type=MESH
        )
    pl.semaphore_signal(barrier, inc=1, device_id={"params": 1 - core}, device_id_type=MESH)
    pl.semaphore_wait(barrier, near + far - 1)

    events = weights_ref.shape[0]
    ahead = firsts[0].shape[0]
    lower = (z < far // 2).astype(jnp.int32)
    head_start = lower * (events - ahead)
    rest_start = (1 - lower) * ahead

    def quarter(d, c):
        start = xor_of(me, d, near) * width + c * LANES
        return pl.ds(pl.multiple_of(start, LANES), LANES)

    def row_part(c):
        if c > 0:
            return pl.ds(0, events)
        return pl.ds(pl.multiple_of(rest_start, 16), events - ahead)

    def row_copy(c, d):
        return pltpu.make_async_remote_copy(
            src_ref=weights_ref.at[row_part(c), quarter(d, c)],
            dst_ref=rows_refs[c].at[d, row_part(c), :],
            send_sem=row_send.at[c, d],
            recv_sem=row_recv.at[c, d],
            device_id={"bins": side(d)},
            device_id_type=MESH,
        )

    def row_local(c):
        return pltpu.make_async_copy(
            weights_ref.at[row_part(c), quarter(0, c)],
            rows_refs[c].at[0, row_part(c), :],
            row_sem.at[c],
        )

    def head_local(d):
        return pltpu.make_async_copy(firsts[d], heads.at[d], head_sem.at[d])

    def head_stay(d):
        part = pl.ds(pl.multiple_of(head_start, 16), ahead)
        return pltpu.make_async_copy(firsts[d], rows_refs[0].at[d, part, :], head_keep.at[d])

    def sums_copy(k):
        lines_from = pl.ds(pl.multiple_of(peer(k) * curve_ref.shape[0], 8), curve_ref.shape[0])
        return pltpu.make_async_remote_copy(
            src_ref=sums.at[lines_from, :],
            dst_ref=got_sums.at[k - 1],
            send_sem=sums_send.at[k - 1],
            recv_sem=sums_recv.at[k - 1],
            device_id={"bins": peer(k) * near + me},
            device_id_type=MESH,
        )

    def data_copy(d):
        return pltpu.make_async_remote_copy(
            src_ref=data_ref,
            dst_ref=got_data.at[d - 1],
            send_sem=data_send.at[d - 1],
            recv_sem=data_recv.at[d - 1],
            device_id={"bins": side(d)},
            device_id_type=MESH,
        )

    for d in range(near):
        head_local(d).start()
    for d in range(1, near):
        data_copy(d).start()
    for c in range(chunks):
        for d in range(1, near):
            row_copy(c, d).start()
    for c in range(chunks):
        row_local(c).start()
    for d in range(near):
        head_stay(d).start()

    def nominal_sums():
        @pl.loop(0, owners)
        def _(o):
            ids = local_ref[pl.ds(o, 1), :].astype(jnp.int32)
            worth = local_ref[pl.ds(owners + o, 1), :]

            @pl.loop(0, bins_dev // TILE)
            def _(k):
                bins = k * TILE + lax.broadcasted_iota(jnp.int32, (TILE, near * slot), 0)
                total = jnp.sum(jnp.where(bins == ids, worth, 0.0), axis=1, keepdims=True)
                for h in range(TILE // LANES):
                    part = total[h * LANES : (h + 1) * LANES]
                    line = o * (bins_dev // LANES) + k * (TILE // LANES) + h
                    sums[pl.ds(line, 1), :] = jnp.sum(
                        jnp.where(diagonal(), part, 0.0), axis=0, keepdims=True
                    )

        for k in range(1, far):
            sums_copy(k).start()

    def finish_sums():
        own_lines = pl.ds(pl.multiple_of(z * curve_ref.shape[0], 8), curve_ref.shape[0])
        total = sums[own_lines, :]
        for k in range(1, far):
            sums_copy(k).wait_recv()
            total += got_sums[k - 1]
        lines_dev = bins_dev // LANES
        levels[0, pl.ds(pl.multiple_of(me * lines_dev, 8), lines_dev), :] = data_ref[0:lines_dev, :]
        levels[1, pl.ds(pl.multiple_of(me * lines_dev, 8), lines_dev), :] = data_ref[
            lines_dev : 2 * lines_dev, :
        ]
        for d in range(1, near):
            data_copy(d).wait_recv()
            part = pl.ds(pl.multiple_of(xor_of(me, d, near) * lines_dev, 8), lines_dev)
            levels[0, part, :] = got_data[d - 1, 0:lines_dev, :]
            levels[1, part, :] = got_data[d - 1, lines_dev : 2 * lines_dev, :]
        yields = levels[0] + total
        curve_ref[...] = levels[1] / (yields * yields)

        @pl.loop(0, curve_ref.shape[0])
        def _(n):
            line = jnp.where(diagonal(), curve_ref[pl.ds(n, 1), :], 0.0)
            line = jnp.sum(line, axis=1, keepdims=True)
            part = pl.ds(pl.multiple_of(n * LANES, LANES), LANES)
            curve_wide[part, :] = jnp.broadcast_to(line, (LANES, LANES))

    def chain_copies(way, c, r, p):
        return [
            pltpu.make_async_remote_copy(
                src_ref=source.at[way, c, r - 1, p],
                dst_ref=target.at[way, c, r - 1, p],
                send_sem=sent.at[way, c, r - 1, p],
                recv_sem=landed.at[way, c, r - 1, p],
                device_id={"bins": along(way)},
                device_id_type=MESH,
            )
            for source, target, sent, landed in (
                (send_q, got_q, q_send, q_recv), (send_s, got_s, s_send, s_recv)
            )
        ]

    def fold(c, plane, p, inputs, finish, early=False):
        @pl.loop(0, held)
        def _(i):
            owner = plane * near + p * held + i
            for s in range(near):
                start = starts_ref[s * owners + owner]
                if early:
                    start = jnp.maximum(start - lower * ((events - ahead) // 16), 0)
                    part = heads[s, pl.ds(start * 16, slot), :]
                else:
                    part = rows_refs[c][s, pl.ds(start * 16, slot), :]
                window[s * slot : (s + 1) * slot, :] = part

            ids = local_ref[pl.ds(owner, 1), :].astype(jnp.int32)

            @pl.loop(0, bins_dev // TILE)
            def _(k):
                bins = k * TILE + lax.broadcasted_iota(jnp.int32, (TILE, near * slot), 0)
                hot = (bins == ids).astype(jnp.bfloat16)
                acc[...] = jnp.dot(hot, window[...], preferred_element_type=jnp.float32)
                base = i * (bins_dev // LANES) + k * (TILE // LANES)
                eye = diagonal()
                for way, r, has in inputs:
                    @pl.when(has)
                    def _():
                        for h in range(TILE // LANES):
                            line = base + h
                            part = pl.ds(pl.multiple_of(line * LANES, LANES), LANES)
                            step = got_s[way, c, r - 1, p, pl.ds(line, 1), :]
                            step = jnp.sum(jnp.where(eye, step, 0.0), axis=1, keepdims=True)
                            coded = got_q[way, c, r - 1, p, part, :].astype(jnp.int32)
                            acc[h * LANES : (h + 1) * LANES, :] += (
                                coded.astype(jnp.float32) * step
                            )
                for h in range(TILE // LANES):
                    line = base + h
                    part = pl.ds(pl.multiple_of(line * LANES, LANES), LANES)
                    finish(acc[h * LANES : (h + 1) * LANES, :], line, part, eye)

    def wait_chain(way, c, r, p):
        for copy in chain_copies(way, c, r, p):
            copy.wait_recv()

    def rounds(c, span, first, last, early=False):
        low, high = span

        @pl.loop(first, last)
        def _(r):
            @pl.loop(low, high)
            def _(p):
                for way in range(2):
                    step_in = z if way == 0 else far - 1 - z

                    @pl.when(step_in < r)
                    def _():
                        inputs = []
                        if first > 1:
                            has = step_in > 0
                            inputs = [(way, r - 1, has)]

                            @pl.when(has)
                            def _():
                                wait_chain(way, c, r - 1, p)

                        def code(value, line, part, eye):
                            most = jnp.max(jnp.abs(value), axis=1, keepdims=True)
                            wide = most * (2.0**23 + 1.0)
                            step = (wide + (most - wide)) * 2.0**-14
                            factor = jnp.where(most > 1e-30, 1.0 / step, 0.0)
                            coded = jnp.round(value * factor).astype(jnp.int32)
                            send_q[way, c, r - 1, p, part, :] = coded.astype(send_q.dtype)
                            send_s[way, c, r - 1, p, pl.ds(line, 1), :] = jnp.sum(
                                jnp.where(eye, step, 0.0), axis=0, keepdims=True
                            )

                        plane = z + (far - r) * (1 - 2 * way)
                        fold(c, plane, p, inputs, code, early)
                        for copy in chain_copies(way, c, r, p):
                            copy.start()

    def rows_part(p):
        return pl.ds(pl.multiple_of(p * size, size), size)

    def side_copy(c, d, p, source=0, hop=None):
        hop = d if hop is None else hop
        origin = own.at[c] if source == 0 else out_ref.at[0, source, c]
        return pltpu.make_async_remote_copy(
            src_ref=origin.at[rows_part(p), :],
            dst_ref=out_ref.at[0, d, c, rows_part(p), :],
            send_sem=side_send.at[c, d, p],
            recv_sem=side_recv.at[c, d, p],
            device_id={"bins": side(hop)},
            device_id_type=MESH,
        )

    def pair_copy(c, d, p):
        source = own.at[c] if d == 0 else out_ref.at[0, d, c]
        return pltpu.make_async_remote_copy(
            src_ref=source.at[rows_part(p), :],
            dst_ref=out_ref.at[1, d, c, rows_part(p), :],
            send_sem=pair_send.at[c, d, p],
            recv_sem=pair_recv.at[c, d, p],
            device_id={"params": 1 - core},
            device_id_type=MESH,
        )

    def keep_copy(c, p):
        return pltpu.make_async_copy(
            own.at[c, rows_part(p), :], out_ref.at[0, 0, c, rows_part(p), :], own_sem.at[c, p]
        )

    def finish(c, p):
        @pl.when(z > 0)
        def _():
            wait_chain(0, c, far - 1, p)

        @pl.when(z < far - 1)
        def _():
            wait_chain(1, c, far - 1, p)

        def store(value, line, part, eye):
            row = pl.ds(pl.multiple_of(p * size + line * LANES, LANES), LANES)
            own[c, row, :] = value.astype(own.dtype)

        fold(c, z, p, [(0, far - 1, z > 0), (1, far - 1, z < far - 1)], store)
        for d in direct:
            side_copy(c, d, p).start()
        pair_copy(c, 0, p).start()
        keep_copy(c, p).start()

    def forward(c, p):
        copies = []
        for half, (source, hop, sem) in enumerate(((1, 2, 3), (2, 1, 0))):
            part = pl.ds(pl.multiple_of(p * size + half * (size // 2), size // 2), size // 2)
            copies.append(
                pltpu.make_async_remote_copy(
                    src_ref=out_ref.at[0, source, c, part, :],
                    dst_ref=out_ref.at[0, 3, c, part, :],
                    send_sem=side_send.at[c, sem, p],
                    recv_sem=side_recv.at[c, sem, p],
                    device_id={"bins": side(hop)},
                    device_id_type=MESH,
                )
            )
        return copies

    def stage_copy(c, d, p):
        return pltpu.make_async_copy(
            out_ref.at[0, d, c, rows_part(p), :], stage.at[p, d - 1], stage_sem.at[p, d - 1]
        )

    def over(c, span, act):
        @pl.loop(span[0], span[1])
        def _(p):
            act(c, p)

    def relay(c, p):
        for d in direct:
            side_copy(c, d, p).wait_recv()
        for copy in forward(c, p):
            copy.start()
        for d in direct:
            pair_copy(c, d, p).start()

    def relay_last(c, p):
        for d in direct:
            stage_copy(c, d, p).start()
        for copy in forward(c, p):
            copy.wait_recv()
        stage_copy(c, 3, p).start()
        pair_copy(c, 3, p).start()

    def weigh(c, p):
        for d in range(1, near):
            stage_copy(c, d, p).wait()
        piece = weighted_ref.shape[0] // near
        depth = 4 * LANES
        rows = lax.broadcasted_iota(jnp.int32, (piece, LANES), 0) + me * piece
        lanes = lax.broadcasted_iota(jnp.int32, (piece, LANES), 1) + c * LANES
        pick = (rows == lanes).astype(jnp.bfloat16)

        @pl.loop(0, size // depth)
        def _(b):
            here_part = pl.ds(pl.multiple_of(b * depth, depth), depth)
            part = pl.ds(pl.multiple_of(p * size + b * depth, depth), depth)
            curve = curve_wide[part, :]
            for d in range(near):
                if d == 0:
                    value = own[c, part, :]
                else:
                    value = stage[p, d - 1, here_part, :]
                value = (curve * value.astype(jnp.float32)).astype(jnp.bfloat16)
                picked = lax.dot_general(
                    pick, value, (((1,), (1,)), ((), ())), preferred_element_type=jnp.float32
                ).astype(weighted_ref.dtype)
                block = slice(d * piece, (d + 1) * piece)
                if c == 0:
                    weighted_ref[block, part] = picked
                else:
                    weighted_ref[block, part] += picked

    def weigh_all(c, span):
        over(c, span, relay_last)
        over(c, span, weigh)

    every = (0, pieces)
    groups = [(c, every) for c in range(chunks - 1)]
    groups += [(chunks - 1, (0, pieces // 2)), (chunks - 1, (pieces // 2, pieces))]
    for d in range(near):
        head_local(d).wait()
    for g, (c, span) in enumerate(groups):
        new = g == 0 or groups[g - 1][0] != c
        if new and c > 0:
            row_local(c).wait()
            for d in range(1, near):
                row_copy(c, d).wait_recv()
        rounds(c, span, 1, 2, g == 0)
        if g == 0:
            nominal_sums()
            row_local(0).wait()
            head_stay(0).wait()
            for d in range(1, near):
                head_stay(d).wait()
                row_copy(0, d).wait_recv()
        if g > 0:
            over(*groups[g - 1], finish)
        rounds(c, span, 2, far)
        if g == 0:
            finish_sums()
        if g > 0:
            over(*groups[g - 1], relay)
        if g > 1:
            weigh_all(*groups[g - 2])
    over(*groups[-1], finish)
    weigh_all(*groups[-2])
    over(*groups[-1], relay)
    weigh_all(*groups[-1])

    for k in range(1, far):
        sums_copy(k).wait_send()
    for d in range(1, near):
        data_copy(d).wait_send()
    for c in range(chunks):
        for d in range(1, near):
            row_copy(c, d).wait_send()

        @pl.loop(0, pieces)
        def _(p):
            keep_copy(c, p).wait()
            for d in direct:
                side_copy(c, d, p).wait_send()
            for copy in forward(c, p):
                copy.wait_send()
            for d in range(near):
                pair_copy(c, d, p).wait_send()
                pair_copy(c, d, p).wait_recv()

            @pl.loop(1, far)
            def _(r):
                for way in range(2):
                    step_in = z if way == 0 else far - 1 - z

                    @pl.when(step_in < r)
                    def _():
                        for copy in chain_copies(way, c, r, p):
                            copy.wait_send()


def chain(starts, local, data, weights, firsts, near, far, chunks, slot, bins_dev):
    events = weights.shape[0]
    ahead = firsts[0].shape[0]
    pieces = near
    bins = near * bins_dev
    size = bins // pieces
    hops = (2, chunks, far - 1, pieces)
    lines = bins // LANES
    dma = pltpu.SemaphoreType.DMA
    rows = jnp.bfloat16
    table = jnp.float32
    return pl.pallas_call(
        functools.partial(chain_kernel, near, far, chunks, pieces, slot),
        out_shape=[
            jax.ShapeDtypeStruct((2, near, chunks, bins, LANES), rows),
            jax.ShapeDtypeStruct((chunks * LANES * near // far, bins), rows),
        ],
        in_specs=[pl.BlockSpec(memory_space=pltpu.SMEM)]
        + [pl.BlockSpec(memory_space=pltpu.VMEM)] * 2
        + [pl.BlockSpec(memory_space=pl.ANY)] * (1 + near),
        out_specs=[
            pl.BlockSpec(memory_space=pl.ANY),
            pl.BlockSpec(memory_space=pltpu.VMEM),
        ],
        scratch_shapes=[pltpu.VMEM((near, events, LANES), rows)] * chunks
        + [
            pltpu.VMEM((near, ahead, LANES), rows),
            pltpu.VMEM((far * lines, LANES), table),
            pltpu.VMEM((far - 1, lines, LANES), table),
            pltpu.VMEM((near - 1,) + data.shape, table),
            pltpu.VMEM((2, lines, LANES), table),
            pltpu.VMEM((lines, LANES), table),
            pltpu.VMEM((bins, LANES), table),
            pltpu.VMEM((pieces, near - 1, size, LANES), rows),
            dma((pieces, near - 1)),
            dma((near,)),
            dma((near,)),
            dma((far - 1,)),
            dma((far - 1,)),
            dma((near - 1,)),
            dma((near - 1,)),
            pltpu.VMEM((near * slot, LANES), rows),
            pltpu.VMEM((TILE, LANES), table),
            pltpu.VMEM((chunks, bins, LANES), rows),
            pltpu.VMEM(hops + (size, LANES), jnp.int16),
            pltpu.VMEM(hops + (size // LANES, LANES), table),
            pltpu.VMEM(hops + (size, LANES), jnp.int16),
            pltpu.VMEM(hops + (size // LANES, LANES), table),
            dma((chunks,)),
            dma((chunks, near)),
            dma((chunks, near)),
            dma(hops),
            dma(hops),
            dma(hops),
            dma(hops),
            dma((chunks, pieces)),
            dma((chunks, near, pieces)),
            dma((chunks, near, pieces)),
            dma((chunks, near, pieces)),
            dma((chunks, near, pieces)),
        ],
        compiler_params=pltpu.CompilerParams(
            collective_id=3, has_side_effects=True, vmem_limit_bytes=62 << 20
        ),
        name="chain",
    )(starts, local, data, weights, *firsts)


def tail_kernel(
    near, far, templates_ref, weighted, out_ref, held, total, coded, own, got,
    hand, kept, merged, sems, sends, recvs, hand_recvs,
):
    groups, _, chunks, _, _ = templates_ref.shape
    here = lax.axis_index("bins")
    z, me = here // near, lax.rem(here, near)
    piece = own.shape[0]
    count = groups * near * chunks
    step = 2 * LANES

    def peer(k):
        return lax.rem(z + k, far)

    barrier = pltpu.get_barrier_semaphore()
    for k in range(1, far):
        pl.semaphore_signal(
            barrier, inc=1, device_id={"bins": peer(k) * near + me}, device_id_type=MESH
        )

    def fetch(n):
        part = templates_ref.at[n // (near * chunks), lax.rem(n // chunks, near), lax.rem(n, chunks)]
        return pltpu.make_async_copy(
            part, held.at[:, pl.ds(pl.multiple_of(n * LANES, LANES), LANES)], sems.at[n]
        )

    @pl.loop(0, count)
    def _(n):
        fetch(n).start()

    pl.semaphore_wait(barrier, far - 1)

    def rows_for(target):
        return pl.ds(pl.multiple_of(xor_of(me, target, near) * piece, 16), piece)

    def columns_of(n):
        return pl.ds(pl.multiple_of(n * step, step), step)

    def send(source, target, landed, j, n, to):
        return pltpu.make_async_remote_copy(
            src_ref=source,
            dst_ref=target.at[:, columns_of(n)],
            send_sem=sends.at[j, n],
            recv_sem=landed,
            device_id={"bins": to * near + me},
            device_id_type=MESH,
        )

    half = z // 2
    at_end = (z == 0) | (z == far - 1)
    within = 1 + half
    end = half * (far - 1)

    def to_inner(j, n):
        target = (far - 1 - within, far - 1 - z, within)[j]
        source = coded.at[rows_for(target), columns_of(n)]
        if j == 2:
            return send(source, got.at[half], recvs.at[half, n], j, n, within)
        return send(source, hand.at[j], hand_recvs.at[j, n], j, n, within)

    def from_inner(j, n):
        target = (far - 1 - z, far - 1 - end, end)[j]
        if j == 2:
            source = coded.at[rows_for(target), columns_of(n)]
        else:
            source = merged.at[j, :, columns_of(n)]
        return send(source, got.at[half], recvs.at[half, n], j, n, target)

    def merge(n):
        for j in range(2):
            to_inner(j, n).wait_recv()
            part = kept[j, :, columns_of(n)] + hand[j, :, columns_of(n)].astype(jnp.float32)
            merged[j, :, columns_of(n)] = part.astype(merged.dtype)
            from_inner(j, n).start()

    inner = jnp.logical_not(at_end)
    lag, late = 2, 6

    @pl.loop(0, count // 2)
    def _(n):
        fetch(2 * n).wait()
        fetch(2 * n + 1).wait()
        total[...] = jnp.dot(
            weighted[...], held[:, columns_of(n)], preferred_element_type=jnp.float32
        )
        coded[:, columns_of(n)] = total[...].astype(coded.dtype)
        own[:, columns_of(n)] = total[rows_for(z), :]

        @pl.when(at_end)
        def _():
            for j in range(2):
                to_inner(j, n).start()

        @pl.when(at_end & (n >= late))
        def _():
            to_inner(2, n - late).start()

        @pl.when(inner)
        def _():
            from_inner(2, n).start()
            kept[0, :, columns_of(n)] = total[rows_for(far - 1 - z), :]
            kept[1, :, columns_of(n)] = total[rows_for(far - 1 - end), :]

        @pl.when(inner & (n >= lag))
        def _():
            merge(n - lag)

    @pl.when(at_end)
    def _():
        @pl.loop(count // 2 - late, count // 2)
        def _(n):
            to_inner(2, n).start()

    @pl.when(inner)
    def _():
        @pl.loop(count // 2 - lag, count // 2)
        def _(n):
            merge(n)

    @pl.loop(0, count // 2)
    def _(n):
        for j in range(2):
            send(merged.at[0, :, columns_of(n)], got.at[j], recvs.at[j, n], 0, n, within).wait_recv()
        for side in range(2):
            place = 2 * n + side
            group = place // (near * chunks)
            d = lax.rem(place // chunks, near)
            start = ((group * near + xor_of(me, d, near)) * chunks + lax.rem(place, chunks)) * LANES
            part = pl.ds(pl.multiple_of(place * LANES, LANES), LANES)
            value = own[:, part]
            for j in range(2):
                value += got[j, :, part].astype(jnp.float32)
            out_ref[:, pl.ds(pl.multiple_of(start, LANES), LANES)] = value

    @pl.loop(0, count // 2)
    def _(n):
        for j in range(3):
            @pl.when(at_end)
            def _():
                to_inner(j, n).wait_send()

            @pl.when(inner)
            def _():
                from_inner(j, n).wait_send()


def tail(templates, weighted, near, far):
    groups, _, chunks, bins, _ = templates.shape
    piece = chunks * LANES // far
    columns = groups * near * chunks * LANES
    count = groups * near * chunks
    return pl.pallas_call(
        functools.partial(tail_kernel, near, far),
        out_shape=jax.ShapeDtypeStruct((piece, columns), jnp.float32),
        in_specs=[pl.BlockSpec(memory_space=pl.ANY), pl.BlockSpec(memory_space=pltpu.VMEM)],
        out_specs=pl.BlockSpec(memory_space=pltpu.VMEM),
        scratch_shapes=[
            pltpu.VMEM((bins, columns), jnp.bfloat16),
            pltpu.VMEM((near * piece, 2 * LANES), jnp.float32),
            pltpu.VMEM((near * piece, columns), jnp.bfloat16),
            pltpu.VMEM((piece, columns), jnp.float32),
            pltpu.VMEM((2, piece, columns), jnp.bfloat16),
            pltpu.VMEM((2, piece, columns), jnp.bfloat16),
            pltpu.VMEM((2, piece, columns), jnp.float32),
            pltpu.VMEM((2, piece, columns), jnp.bfloat16),
            pltpu.SemaphoreType.DMA((count,)),
            pltpu.SemaphoreType.DMA((3, count // 2)),
            pltpu.SemaphoreType.DMA((2, count // 2)),
            pltpu.SemaphoreType.DMA((2, count // 2)),
        ],
        compiler_params=pltpu.CompilerParams(
            collective_id=2, has_side_effects=True, vmem_limit_bytes=44 << 20
        ),
        name="tail",
    )(templates, weighted)


def body_by_parameters(event_bins, event_weights, nominal, background, observed):
    owners = lax.axis_size("bins")
    near = math.isqrt(owners)
    far = owners // near
    events = event_bins.shape[0]
    bins_dev = background.shape[0]
    width = event_weights.shape[1] // near
    chunks = width // LANES
    capacity = 3 * events // (2 * owners)
    slot = -(-capacity // 16) * 16 + 16
    ahead = min(-(-near * capacity // 16) * 16 + 16, events - 16)
    here = lax.axis_index("bins")
    z, me = here // near, lax.rem(here, near)
    around = [[(s, s // near * near + (s % near ^ d)) for s in range(owners)] for d in range(near)]

    def spread(value):
        return [value] + [shift(value, around[d]) for d in range(1, near)]

    firsts = []
    first_row = jnp.where(z < far // 2, events - ahead, 0)
    for d in range(near):
        corner = (first_row, (me ^ d) * width)
        firsts.append(lax.dynamic_slice(event_weights, corner, (ahead, LANES)))
    event_bins, firsts = lax.optimization_barrier((event_bins, firsts))
    for d in range(1, near):
        firsts[d] = shift(firsts[d], around[d])

    marks = jnp.arange(owners, dtype=jnp.int32) * bins_dev
    before = jnp.sum((event_bins[None, :] < marks[:, None]).astype(jnp.int32), axis=1)
    starts = jnp.minimum(before // 16, (events - slot) // 16)
    places = slots_of(starts, event_bins, nominal, slot, bins_dev)
    places = jnp.stack(spread(places))

    starts = places[:, 2 * owners, :owners].astype(jnp.int32).reshape(-1)
    places = places.transpose(1, 0, 2).reshape(2 * owners + 1, near * slot)
    data = jnp.concatenate([background, observed]).reshape(-1, LANES)
    templates, weighted = chain(
        starts, places, data, event_weights, firsts, near, far, chunks, slot, bins_dev
    )
    summed = tail(templates, weighted, near, far)
    return summed * (1.0 / (bins_dev * owners))


def splits_by_parameters(mesh, event_bins, event_weights, background):
    owners, groups = mesh.shape["bins"], mesh.shape["params"]
    near = math.isqrt(owners)
    events = event_bins.shape[0] // owners
    width = event_weights.shape[1] // groups // max(near, 1)
    bins_dev = background.shape[0] // owners
    return (
        groups == 2
        and near == 4
        and near * near == owners
        and near & (near - 1) == 0
        and width % LANES == 0
        and width % (16 * near) == 0
        and events % LANES == 0
        and events >= 2 * LANES
        and bins_dev % (8 * LANES) == 0
    )


def solution(mesh):
    in_specs = (P("bins"), P("bins", "params"), P("bins"), P("bins"), P("bins"))
    out_specs = P(("params", "bins"), None)

    def run(event_bins, event_weights, nominal, background, observed):
        fits = splits_by_parameters(mesh, event_bins, event_weights, background)
        chosen = body_by_parameters if fits else body
        mapped = jax.shard_map(
            chosen, mesh=mesh, in_specs=in_specs, out_specs=out_specs, check_vma=False
        )
        return mapped(event_bins, event_weights, nominal, background, observed)

    return run
```

```python
import functools
import math

import jax
import jax.numpy as jnp
from jax import lax
from jax.experimental import pallas as pl
from jax.experimental.pallas import tpu as pltpu
from jax.sharding import PartitionSpec as P


ALIGN = 8
MESH = pl.DeviceIdType.MESH


def from_behind(value, axis, steps):
    count = lax.axis_size(axis)
    pairs = [(source, (source + steps) % count) for source in range(count)]
    return lax.ppermute(value, axis, pairs)


def pack_kernel(owners, slot, first, width, starts_ref, rows_ref, out_ref, held, in_sems, out_sems):
    def fetch(o):
        start = pl.multiple_of(starts_ref[o] * ALIGN, ALIGN)
        return pltpu.make_async_copy(
            rows_ref.at[pl.ds(start, slot), pl.ds(first, width)], held.at[o], in_sems.at[o]
        )

    def store(o):
        return pltpu.make_async_copy(held.at[o], out_ref.at[o], out_sems.at[o])

    @pl.loop(0, owners)
    def _(o):
        fetch(o).start()

    @pl.loop(0, owners)
    def _(o):
        fetch(o).wait()
        store(o).start()

    @pl.loop(0, owners)
    def _(o):
        store(o).wait()


def pack(starts, rows, slot, first, width):
    owners = starts.shape[0]
    return pl.pallas_call(
        functools.partial(pack_kernel, owners, slot, first, width),
        out_shape=jax.ShapeDtypeStruct((owners, slot, width), rows.dtype),
        in_specs=[
            pl.BlockSpec(memory_space=pltpu.SMEM),
            pl.BlockSpec(memory_space=pl.ANY),
        ],
        out_specs=pl.BlockSpec(memory_space=pl.ANY),
        scratch_shapes=[
            pltpu.VMEM((owners, slot, width), rows.dtype),
            pltpu.SemaphoreType.DMA((owners,)),
            pltpu.SemaphoreType.DMA((owners,)),
        ],
        compiler_params=pltpu.CompilerParams(vmem_limit_bytes=32 << 20),
        cost_estimate=pl.CostEstimate(
            flops=0, bytes_accessed=4 * owners * slot * width, transcendentals=0
        ),
        name="pack",
    )(starts, rows)


def meta_kernel(bins_dev, starts_ref, table_ref, out_ref):
    owners, _, slot = out_ref.shape
    events = table_ref.shape[1]
    table = table_ref[...]

    @pl.loop(0, owners)
    def _(o):
        start = starts_ref[o] * ALIGN
        turned = pltpu.roll(table, lax.rem(events - start, events), axis=1)[:, :slot]
        bins = turned[0:1] - (o * bins_dev).astype(jnp.float32)
        inside = (bins >= 0) & (bins < bins_dev)
        out_ref[o, 0:1, :] = jnp.where(inside, bins, -1.0)
        out_ref[o, 1:2, :] = turned[1:2]


def pack_meta(starts, table, slot, bins_dev):
    owners = starts.shape[0]
    return pl.pallas_call(
        functools.partial(meta_kernel, bins_dev),
        out_shape=jax.ShapeDtypeStruct((owners, 2, slot), jnp.float32),
        in_specs=[
            pl.BlockSpec(memory_space=pltpu.SMEM),
            pl.BlockSpec(memory_space=pltpu.VMEM),
        ],
        out_specs=pl.BlockSpec(memory_space=pltpu.VMEM),
        name="pack_meta",
    )(starts, table)


def hist_kernel(chunk, tile, local_ref, rows_ref, out_ref, hot):
    bins, total = hot.shape

    @pl.when(pl.program_id(0) == 0)
    def _():
        ids = lax.broadcasted_iota(jnp.int32, (bins, chunk), 0)

        @pl.loop(0, total // chunk)
        def _(k):
            part = pl.ds(pl.multiple_of(k * chunk, chunk), chunk)
            hot[:, part] = (ids == local_ref[:, part]).astype(jnp.bfloat16)

    @pl.loop(0, bins // tile)
    def _(m):
        part = pl.ds(pl.multiple_of(m * tile, tile), tile)
        out_ref[part, :] = jnp.dot(
            hot[part, :], rows_ref[...], preferred_element_type=jnp.float32
        ).astype(out_ref.dtype)


def histogram_of(local, rows, bins, block, dtype):
    total, width = rows.shape
    return pl.pallas_call(
        functools.partial(hist_kernel, math.gcd(total, 128), math.gcd(bins, 256)),
        grid=(width // block,),
        out_shape=jax.ShapeDtypeStruct((bins, width), dtype),
        in_specs=[
            pl.BlockSpec((1, total), lambda j: (0, 0)),
            pl.BlockSpec((total, block), lambda j: (0, j)),
        ],
        out_specs=pl.BlockSpec((bins, block), lambda j: (0, j)),
        scratch_shapes=[pltpu.VMEM((bins, total), jnp.bfloat16)],
        compiler_params=pltpu.CompilerParams(
            vmem_limit_bytes=40 << 20, dimension_semantics=("arbitrary",)
        ),
        cost_estimate=pl.CostEstimate(
            flops=2 * bins * total * width, bytes_accessed=2 * total * width, transcendentals=0
        ),
        name="histogram",
    )(local, rows)


def reduce_kernel(
    piece, shares_ref, out_ref, own, got_near, sums, got_far,
    own_sem, near_send, near_recv, far_send, far_recv,
):
    far, near, rows, _ = shares_ref.shape
    me = lax.axis_index("bins")
    f, n = me // near, lax.rem(me, near)

    def near_peer(d):
        return lax.rem(n + d, near)

    def far_peer(d):
        return lax.rem(f + d, far)

    barrier = pltpu.get_barrier_semaphore()
    for d in range(1, near):
        pl.semaphore_signal(
            barrier, inc=1, device_id={"bins": f * near + near_peer(d)}, device_id_type=MESH
        )
    for d in range(1, far):
        pl.semaphore_signal(
            barrier, inc=1, device_id={"bins": far_peer(d) * near + n}, device_id_type=MESH
        )
    pl.semaphore_wait(barrier, near + far - 2)

    def part_of(c):
        return pl.ds(pl.multiple_of(c * piece, piece), piece)

    def near_copy(d, c):
        return pltpu.make_async_remote_copy(
            src_ref=shares_ref.at[:, near_peer(d), part_of(c), :],
            dst_ref=got_near.at[d - 1, :, part_of(c), :],
            send_sem=near_send.at[d - 1, c],
            recv_sem=near_recv.at[d - 1, c],
            device_id={"bins": f * near + near_peer(d)},
            device_id_type=MESH,
        )

    def far_copy(d, c):
        return pltpu.make_async_remote_copy(
            src_ref=sums.at[far_peer(d), part_of(c), :],
            dst_ref=got_far.at[d - 1, part_of(c), :],
            send_sem=far_send.at[d - 1, c],
            recv_sem=far_recv.at[d - 1, c],
            device_id={"bins": far_peer(d) * near + n},
            device_id_type=MESH,
        )

    own_copy = pltpu.make_async_copy(shares_ref.at[:, n], own, own_sem)
    own_copy.start()
    pieces = rows // piece

    @pl.loop(0, pieces)
    def _(c):
        for d in range(1, near):
            near_copy(d, c).start()

    own_copy.wait()

    @pl.loop(0, pieces)
    def _(c):
        part = part_of(c)
        for d in range(1, near):
            near_copy(d, c).wait_recv()

        @pl.loop(0, far)
        def _(k):
            total = own[k, part, :].astype(jnp.float32)
            for d in range(1, near):
                total += got_near[d - 1, k, part, :].astype(jnp.float32)
            sums[k, part, :] = total

        for d in range(1, far):
            far_copy(d, c).start()

    @pl.loop(0, pieces)
    def _(c):
        part = part_of(c)
        for d in range(1, far):
            far_copy(d, c).wait_recv()
        total = sums[f, part, :]
        for d in range(1, far):
            total += got_far[d - 1, part, :]
        out_ref[part, :] = total
        for d in range(1, near):
            near_copy(d, c).wait_send()
        for d in range(1, far):
            far_copy(d, c).wait_send()


def reduce_shares(shares):
    owners, rows, cols = shares.shape
    near = math.isqrt(owners)
    while owners % near:
        near -= 1
    far = owners // near
    piece = 16 if rows % 16 == 0 else rows
    pieces = rows // piece
    return pl.pallas_call(
        functools.partial(reduce_kernel, piece),
        out_shape=jax.ShapeDtypeStruct((rows, cols), jnp.float32),
        in_specs=[pl.BlockSpec(memory_space=pl.ANY)],
        out_specs=pl.BlockSpec(memory_space=pltpu.VMEM),
        scratch_shapes=[
            pltpu.VMEM((far, rows, cols), shares.dtype),
            pltpu.VMEM((near - 1, far, rows, cols), shares.dtype),
            pltpu.VMEM((far, rows, cols), jnp.float32),
            pltpu.VMEM((far - 1, rows, cols), jnp.float32),
            pltpu.SemaphoreType.DMA,
            pltpu.SemaphoreType.DMA((near - 1, pieces)),
            pltpu.SemaphoreType.DMA((near - 1, pieces)),
            pltpu.SemaphoreType.DMA((far - 1, pieces)),
            pltpu.SemaphoreType.DMA((far - 1, pieces)),
        ],
        compiler_params=pltpu.CompilerParams(
            collective_id=1, has_side_effects=True, vmem_limit_bytes=40 << 20
        ),
        name="reduce_shares",
    )(shares.reshape(far, near, rows, cols))


def body(event_bins, event_weights, nominal, background, observed):
    owners = lax.axis_size("bins")
    groups_count = lax.axis_size("params")
    events = event_bins.shape[0]
    width_g = event_weights.shape[1]
    bins_dev = background.shape[0]
    capacity = 3 * events // (2 * owners)
    slot = -(-capacity // ALIGN) * ALIGN + ALIGN
    chunks = 2 if width_g % 512 == 0 else 1
    width = width_g // chunks
    block = math.gcd(width, 256)

    destination = event_bins // bins_dev
    targets = jnp.arange(owners, dtype=jnp.int32)
    before = jnp.sum((destination[None, :] < targets[:, None]).astype(jnp.int32), axis=1)
    starts = jnp.minimum(before // ALIGN, (events - slot) // ALIGN)

    table = jnp.stack([event_bins.astype(jnp.float32), nominal.astype(jnp.float32)])
    table = jnp.concatenate([table, jnp.zeros((6, events), jnp.float32)], axis=0)
    meta = pack_meta(starts, table, slot, bins_dev)
    got_meta = lax.all_to_all(meta, "bins", split_axis=0, concat_axis=0, tiled=True)
    local = got_meta[:, 0].astype(jnp.int32).reshape(1, owners * slot)
    got_nominal = got_meta[:, 1].astype(jnp.bfloat16).reshape(owners * slot, 1)
    got_nominal = jnp.broadcast_to(got_nominal, (owners * slot, 128))
    nominal_sum = histogram_of(local, got_nominal, bins_dev, 128, jnp.float32)[:, 0]
    yields = background + nominal_sum
    curvature = observed / (yields * yields)

    parts = []
    for c in range(chunks):
        packed = pack(starts, event_weights, slot, c * width, width)
        got = lax.all_to_all(packed, "bins", split_axis=0, concat_axis=0, tiled=True)
        got = got.reshape(owners * slot, width)
        parts.append(histogram_of(local, got, bins_dev, block, jnp.bfloat16))
    templates = jnp.concatenate(parts, axis=1)
    weighted = (curvature[:, None] * templates.astype(jnp.float32)).astype(jnp.bfloat16)
    pieces = [templates]
    for shift_by in range(1, groups_count // 2 + 1):
        shifted = [from_behind(part, "params", -shift_by) for part in parts]
        pieces.append(jnp.concatenate(shifted, axis=1))
    partners = jnp.concatenate(pieces, axis=1)
    dims = (((0,), (0,)), ((), ()))
    full = lax.dot_general(weighted, partners, dims, preferred_element_type=jnp.float32)
    full = full.astype(jnp.bfloat16)
    shares = full.reshape(owners, width_g // owners, full.shape[1])
    summed = reduce_shares(shares)
    return summed * (1.0 / (bins_dev * owners))


LANES = 128
TILE = 256


def shift(value, pairs):
    return lax.ppermute(value, "bins", pairs)


def xor_of(a, b, count):
    total, bit = 0, 1
    while bit < count:
        total = total + bit * lax.rem(a // bit + b // bit, 2)
        bit *= 2
    return total


def diagonal():
    rows = lax.broadcasted_iota(jnp.int32, (LANES, LANES), 0)
    return rows == lax.broadcasted_iota(jnp.int32, (LANES, LANES), 1)


def slots_kernel(bins_dev, starts_ref, ids_ref, nominal_ref, out_ref):
    owners = starts_ref.shape[0]
    slot = out_ref.shape[1]
    events = ids_ref.shape[1]
    first = lax.broadcasted_iota(jnp.int32, (8, events), 0) == 0
    table = jnp.where(first, ids_ref[...].astype(jnp.float32), nominal_ref[...].astype(jnp.float32))
    lanes = lax.broadcasted_iota(jnp.int32, (1, slot), 1)
    out_ref[pl.ds(2 * owners, 1), :] = jnp.zeros((1, slot), jnp.float32)

    @pl.loop(0, owners)
    def _(o):
        start = starts_ref[o]
        turned = pltpu.roll(table, lax.rem(events - start * 16, events), axis=1)
        bins = turned[0:1, :slot] - (o * bins_dev).astype(jnp.float32)
        inside = (bins >= 0) & (bins < bins_dev)
        out_ref[pl.ds(o, 1), :] = jnp.where(inside, bins, -1.0)
        out_ref[pl.ds(owners + o, 1), :] = turned[1:2, :slot]
        out_ref[pl.ds(2 * owners, 1), :] += jnp.where(lanes == o, start.astype(jnp.float32), 0.0)


def slots_of(starts, ids, nominal, slot, bins_dev):
    owners, events = starts.shape[0], ids.shape[0]
    return pl.pallas_call(
        functools.partial(slots_kernel, bins_dev),
        out_shape=jax.ShapeDtypeStruct((2 * owners + 1, slot), jnp.float32),
        in_specs=[pl.BlockSpec(memory_space=pltpu.SMEM)]
        + [pl.BlockSpec(memory_space=pltpu.VMEM)] * 2,
        out_specs=pl.BlockSpec(memory_space=pltpu.VMEM),
        name="slots",
    )(starts, ids.reshape(1, events), nominal.reshape(1, events))


def chain_kernel(
    near, far, chunks, pieces, slot, starts_ref, local_ref, data_ref, weights_ref, *refs
):
    firsts = refs[:near]
    out_ref, weighted_ref = refs[near : near + 2]
    rows_refs = refs[near + 2 : near + 2 + chunks]
    (
        heads, sums, got_sums, got_data, levels, curve_ref, curve_wide, stage, stage_sem,
        head_sem, head_keep, sums_send, sums_recv, data_send, data_recv,
        window, acc, own, send_q, send_s, got_q, got_s,
        row_sem, row_send, row_recv, q_send, q_recv, s_send, s_recv,
        own_sem, side_send, side_recv, pair_send, pair_recv,
    ) = refs[near + 2 + chunks :]
    owners = near * far
    here = lax.axis_index("bins")
    core = lax.axis_index("params")
    z, me = here // near, lax.rem(here, near)
    bins_dev = own.shape[1] // near
    width = chunks * LANES
    held = near // pieces
    size = held * bins_dev
    direct = [1, 2]

    def side(d):
        return z * near + xor_of(me, d, near)

    def along(way):
        return (z + 1 - 2 * way) * near + me

    def peer(k):
        return lax.rem(z + k, far)

    barrier = pltpu.get_barrier_semaphore()
    for d in range(1, near):
        pl.semaphore_signal(barrier, inc=1, device_id={"bins": side(d)}, device_id_type=MESH)
    for k in range(1, far):
        pl.semaphore_signal(
            barrier, inc=1, device_id={"bins": peer(k) * near + me}, device_id_type=MESH
        )
    pl.semaphore_signal(barrier, inc=1, device_id={"params": 1 - core}, device_id_type=MESH)
    pl.semaphore_wait(barrier, near + far - 1)

    events = weights_ref.shape[0]
    ahead = firsts[0].shape[0]
    lower = (z < far // 2).astype(jnp.int32)
    head_start = lower * (events - ahead)
    rest_start = (1 - lower) * ahead

    def quarter(d, c):
        start = xor_of(me, d, near) * width + c * LANES
        return pl.ds(pl.multiple_of(start, LANES), LANES)

    def row_part(c):
        if c > 0:
            return pl.ds(0, events)
        return pl.ds(pl.multiple_of(rest_start, 16), events - ahead)

    def row_copy(c, d):
        return pltpu.make_async_remote_copy(
            src_ref=weights_ref.at[row_part(c), quarter(d, c)],
            dst_ref=rows_refs[c].at[d, row_part(c), :],
            send_sem=row_send.at[c, d],
            recv_sem=row_recv.at[c, d],
            device_id={"bins": side(d)},
            device_id_type=MESH,
        )

    def row_local(c):
        return pltpu.make_async_copy(
            weights_ref.at[row_part(c), quarter(0, c)],
            rows_refs[c].at[0, row_part(c), :],
            row_sem.at[c],
        )

    def head_local(d):
        return pltpu.make_async_copy(firsts[d], heads.at[d], head_sem.at[d])

    def head_stay(d):
        part = pl.ds(pl.multiple_of(head_start, 16), ahead)
        return pltpu.make_async_copy(firsts[d], rows_refs[0].at[d, part, :], head_keep.at[d])

    def sums_copy(k):
        lines_from = pl.ds(pl.multiple_of(peer(k) * curve_ref.shape[0], 8), curve_ref.shape[0])
        return pltpu.make_async_remote_copy(
            src_ref=sums.at[lines_from, :],
            dst_ref=got_sums.at[k - 1],
            send_sem=sums_send.at[k - 1],
            recv_sem=sums_recv.at[k - 1],
            device_id={"bins": peer(k) * near + me},
            device_id_type=MESH,
        )

    def data_copy(d):
        return pltpu.make_async_remote_copy(
            src_ref=data_ref,
            dst_ref=got_data.at[d - 1],
            send_sem=data_send.at[d - 1],
            recv_sem=data_recv.at[d - 1],
            device_id={"bins": side(d)},
            device_id_type=MESH,
        )

    for d in range(near):
        head_local(d).start()
    for d in range(1, near):
        data_copy(d).start()
    for c in range(chunks):
        for d in range(1, near):
            row_copy(c, d).start()
    for c in range(chunks):
        row_local(c).start()
    for d in range(near):
        head_stay(d).start()

    def nominal_sums():
        @pl.loop(0, owners)
        def _(o):
            ids = local_ref[pl.ds(o, 1), :].astype(jnp.int32)
            worth = local_ref[pl.ds(owners + o, 1), :]

            @pl.loop(0, bins_dev // TILE)
            def _(k):
                bins = k * TILE + lax.broadcasted_iota(jnp.int32, (TILE, near * slot), 0)
                total = jnp.sum(jnp.where(bins == ids, worth, 0.0), axis=1, keepdims=True)
                for h in range(TILE // LANES):
                    part = total[h * LANES : (h + 1) * LANES]
                    line = o * (bins_dev // LANES) + k * (TILE // LANES) + h
                    sums[pl.ds(line, 1), :] = jnp.sum(
                        jnp.where(diagonal(), part, 0.0), axis=0, keepdims=True
                    )

        for k in range(1, far):
            sums_copy(k).start()

    def finish_sums():
        own_lines = pl.ds(pl.multiple_of(z * curve_ref.shape[0], 8), curve_ref.shape[0])
        total = sums[own_lines, :]
        for k in range(1, far):
            sums_copy(k).wait_recv()
            total += got_sums[k - 1]
        lines_dev = bins_dev // LANES
        levels[0, pl.ds(pl.multiple_of(me * lines_dev, 8), lines_dev), :] = data_ref[0:lines_dev, :]
        levels[1, pl.ds(pl.multiple_of(me * lines_dev, 8), lines_dev), :] = data_ref[
            lines_dev : 2 * lines_dev, :
        ]
        for d in range(1, near):
            data_copy(d).wait_recv()
            part = pl.ds(pl.multiple_of(xor_of(me, d, near) * lines_dev, 8), lines_dev)
            levels[0, part, :] = got_data[d - 1, 0:lines_dev, :]
            levels[1, part, :] = got_data[d - 1, lines_dev : 2 * lines_dev, :]
        yields = levels[0] + total
        curve_ref[...] = levels[1] / (yields * yields)

        @pl.loop(0, curve_ref.shape[0])
        def _(n):
            line = jnp.where(diagonal(), curve_ref[pl.ds(n, 1), :], 0.0)
            line = jnp.sum(line, axis=1, keepdims=True)
            part = pl.ds(pl.multiple_of(n * LANES, LANES), LANES)
            curve_wide[part, :] = jnp.broadcast_to(line, (LANES, LANES))

    def chain_copies(way, c, r, p):
        return [
            pltpu.make_async_remote_copy(
                src_ref=source.at[way, c, r - 1, p],
                dst_ref=target.at[way, c, r - 1, p],
                send_sem=sent.at[way, c, r - 1, p],
                recv_sem=landed.at[way, c, r - 1, p],
                device_id={"bins": along(way)},
                device_id_type=MESH,
            )
            for source, target, sent, landed in (
                (send_q, got_q, q_send, q_recv), (send_s, got_s, s_send, s_recv)
            )
        ]

    def fold(c, plane, p, inputs, finish, early=False):
        @pl.loop(0, held)
        def _(i):
            owner = plane * near + p * held + i
            for s in range(near):
                start = starts_ref[s * owners + owner]
                if early:
                    start = jnp.maximum(start - lower * ((events - ahead) // 16), 0)
                    part = heads[s, pl.ds(start * 16, slot), :]
                else:
                    part = rows_refs[c][s, pl.ds(start * 16, slot), :]
                window[s * slot : (s + 1) * slot, :] = part

            ids = local_ref[pl.ds(owner, 1), :].astype(jnp.int32)

            @pl.loop(0, bins_dev // TILE)
            def _(k):
                bins = k * TILE + lax.broadcasted_iota(jnp.int32, (TILE, near * slot), 0)
                hot = (bins == ids).astype(jnp.bfloat16)
                acc[...] = jnp.dot(hot, window[...], preferred_element_type=jnp.float32)
                base = i * (bins_dev // LANES) + k * (TILE // LANES)
                eye = diagonal()
                for way, r, has in inputs:
                    @pl.when(has)
                    def _():
                        for h in range(TILE // LANES):
                            line = base + h
                            part = pl.ds(pl.multiple_of(line * LANES, LANES), LANES)
                            step = got_s[way, c, r - 1, p, pl.ds(line, 1), :]
                            step = jnp.sum(jnp.where(eye, step, 0.0), axis=1, keepdims=True)
                            coded = got_q[way, c, r - 1, p, part, :].astype(jnp.int32)
                            acc[h * LANES : (h + 1) * LANES, :] += (
                                coded.astype(jnp.float32) * step
                            )
                for h in range(TILE // LANES):
                    line = base + h
                    part = pl.ds(pl.multiple_of(line * LANES, LANES), LANES)
                    finish(acc[h * LANES : (h + 1) * LANES, :], line, part, eye)

    def wait_chain(way, c, r, p):
        for copy in chain_copies(way, c, r, p):
            copy.wait_recv()

    def rounds(c, span, first, last, early=False):
        low, high = span

        @pl.loop(first, last)
        def _(r):
            @pl.loop(low, high)
            def _(p):
                for way in range(2):
                    step_in = z if way == 0 else far - 1 - z

                    @pl.when(step_in < r)
                    def _():
                        inputs = []
                        if first > 1:
                            has = step_in > 0
                            inputs = [(way, r - 1, has)]

                            @pl.when(has)
                            def _():
                                wait_chain(way, c, r - 1, p)

                        def code(value, line, part, eye):
                            most = jnp.max(jnp.abs(value), axis=1, keepdims=True)
                            wide = most * (2.0**23 + 1.0)
                            step = (wide + (most - wide)) * 2.0**-14
                            factor = jnp.where(most > 1e-30, 1.0 / step, 0.0)
                            coded = jnp.round(value * factor).astype(jnp.int32)
                            send_q[way, c, r - 1, p, part, :] = coded.astype(send_q.dtype)
                            send_s[way, c, r - 1, p, pl.ds(line, 1), :] = jnp.sum(
                                jnp.where(eye, step, 0.0), axis=0, keepdims=True
                            )

                        plane = z + (far - r) * (1 - 2 * way)
                        fold(c, plane, p, inputs, code, early)
                        for copy in chain_copies(way, c, r, p):
                            copy.start()

    def rows_part(p):
        return pl.ds(pl.multiple_of(p * size, size), size)

    def side_copy(c, d, p, source=0, hop=None):
        hop = d if hop is None else hop
        origin = own.at[c] if source == 0 else out_ref.at[0, source, c]
        return pltpu.make_async_remote_copy(
            src_ref=origin.at[rows_part(p), :],
            dst_ref=out_ref.at[0, d, c, rows_part(p), :],
            send_sem=side_send.at[c, d, p],
            recv_sem=side_recv.at[c, d, p],
            device_id={"bins": side(hop)},
            device_id_type=MESH,
        )

    def pair_copy(c, d, p):
        source = own.at[c] if d == 0 else out_ref.at[0, d, c]
        return pltpu.make_async_remote_copy(
            src_ref=source.at[rows_part(p), :],
            dst_ref=out_ref.at[1, d, c, rows_part(p), :],
            send_sem=pair_send.at[c, d, p],
            recv_sem=pair_recv.at[c, d, p],
            device_id={"params": 1 - core},
            device_id_type=MESH,
        )

    def keep_copy(c, p):
        return pltpu.make_async_copy(
            own.at[c, rows_part(p), :], out_ref.at[0, 0, c, rows_part(p), :], own_sem.at[c, p]
        )

    def finish(c, p):
        @pl.when(z > 0)
        def _():
            wait_chain(0, c, far - 1, p)

        @pl.when(z < far - 1)
        def _():
            wait_chain(1, c, far - 1, p)

        def store(value, line, part, eye):
            row = pl.ds(pl.multiple_of(p * size + line * LANES, LANES), LANES)
            own[c, row, :] = value.astype(own.dtype)

        fold(c, z, p, [(0, far - 1, z > 0), (1, far - 1, z < far - 1)], store)
        for d in direct:
            side_copy(c, d, p).start()
        pair_copy(c, 0, p).start()
        keep_copy(c, p).start()

    def forward(c, p):
        copies = []
        for half, (source, hop, sem) in enumerate(((1, 2, 3), (2, 1, 0))):
            part = pl.ds(pl.multiple_of(p * size + half * (size // 2), size // 2), size // 2)
            copies.append(
                pltpu.make_async_remote_copy(
                    src_ref=out_ref.at[0, source, c, part, :],
                    dst_ref=out_ref.at[0, 3, c, part, :],
                    send_sem=side_send.at[c, sem, p],
                    recv_sem=side_recv.at[c, sem, p],
                    device_id={"bins": side(hop)},
                    device_id_type=MESH,
                )
            )
        return copies

    def stage_copy(c, d, p):
        return pltpu.make_async_copy(
            out_ref.at[0, d, c, rows_part(p), :], stage.at[p, d - 1], stage_sem.at[p, d - 1]
        )

    def over(c, span, act):
        @pl.loop(span[0], span[1])
        def _(p):
            act(c, p)

    def relay(c, p):
        for d in direct:
            side_copy(c, d, p).wait_recv()
        for copy in forward(c, p):
            copy.start()
        for d in direct:
            pair_copy(c, d, p).start()

    def relay_last(c, p):
        for d in direct:
            stage_copy(c, d, p).start()
        for copy in forward(c, p):
            copy.wait_recv()
        stage_copy(c, 3, p).start()
        pair_copy(c, 3, p).start()

    def weigh(c, p):
        for d in range(1, near):
            stage_copy(c, d, p).wait()
        piece = weighted_ref.shape[0] // near
        depth = 4 * LANES
        rows = lax.broadcasted_iota(jnp.int32, (piece, LANES), 0) + me * piece
        lanes = lax.broadcasted_iota(jnp.int32, (piece, LANES), 1) + c * LANES
        pick = (rows == lanes).astype(jnp.bfloat16)

        @pl.loop(0, size // depth)
        def _(b):
            here_part = pl.ds(pl.multiple_of(b * depth, depth), depth)
            part = pl.ds(pl.multiple_of(p * size + b * depth, depth), depth)
            curve = curve_wide[part, :]
            for d in range(near):
                if d == 0:
                    value = own[c, part, :]
                else:
                    value = stage[p, d - 1, here_part, :]
                value = (curve * value.astype(jnp.float32)).astype(jnp.bfloat16)
                picked = lax.dot_general(
                    pick, value, (((1,), (1,)), ((), ())), preferred_element_type=jnp.float32
                ).astype(weighted_ref.dtype)
                block = slice(d * piece, (d + 1) * piece)
                if c == 0:
                    weighted_ref[block, part] = picked
                else:
                    weighted_ref[block, part] += picked

    def weigh_all(c, span):
        over(c, span, relay_last)
        over(c, span, weigh)

    every = (0, pieces)
    groups = [(c, every) for c in range(chunks - 1)]
    groups += [(chunks - 1, (0, pieces // 2)), (chunks - 1, (pieces // 2, pieces))]
    for d in range(near):
        head_local(d).wait()
    for g, (c, span) in enumerate(groups):
        new = g == 0 or groups[g - 1][0] != c
        if new and c > 0:
            row_local(c).wait()
            for d in range(1, near):
                row_copy(c, d).wait_recv()
        rounds(c, span, 1, 2, g == 0)
        if g == 0:
            nominal_sums()
            row_local(0).wait()
            head_stay(0).wait()
            for d in range(1, near):
                head_stay(d).wait()
                row_copy(0, d).wait_recv()
        if g > 0:
            over(*groups[g - 1], finish)
        rounds(c, span, 2, far)
        if g == 0:
            finish_sums()
        if g > 0:
            over(*groups[g - 1], relay)
        if g > 1:
            weigh_all(*groups[g - 2])
    over(*groups[-1], finish)
    weigh_all(*groups[-2])
    over(*groups[-1], relay)
    weigh_all(*groups[-1])

    for k in range(1, far):
        sums_copy(k).wait_send()
    for d in range(1, near):
        data_copy(d).wait_send()
    for c in range(chunks):
        for d in range(1, near):
            row_copy(c, d).wait_send()

        @pl.loop(0, pieces)
        def _(p):
            keep_copy(c, p).wait()
            for d in direct:
                side_copy(c, d, p).wait_send()
            for copy in forward(c, p):
                copy.wait_send()
            for d in range(near):
                pair_copy(c, d, p).wait_send()
                pair_copy(c, d, p).wait_recv()

            @pl.loop(1, far)
            def _(r):
                for way in range(2):
                    step_in = z if way == 0 else far - 1 - z

                    @pl.when(step_in < r)
                    def _():
                        for copy in chain_copies(way, c, r, p):
                            copy.wait_send()


def chain(starts, local, data, weights, firsts, near, far, chunks, slot, bins_dev):
    events = weights.shape[0]
    ahead = firsts[0].shape[0]
    pieces = near
    bins = near * bins_dev
    size = bins // pieces
    hops = (2, chunks, far - 1, pieces)
    lines = bins // LANES
    dma = pltpu.SemaphoreType.DMA
    rows = jnp.bfloat16
    table = jnp.float32
    return pl.pallas_call(
        functools.partial(chain_kernel, near, far, chunks, pieces, slot),
        out_shape=[
            jax.ShapeDtypeStruct((2, near, chunks, bins, LANES), rows),
            jax.ShapeDtypeStruct((chunks * LANES * near // far, bins), rows),
        ],
        in_specs=[pl.BlockSpec(memory_space=pltpu.SMEM)]
        + [pl.BlockSpec(memory_space=pltpu.VMEM)] * 2
        + [pl.BlockSpec(memory_space=pl.ANY)] * (1 + near),
        out_specs=[
            pl.BlockSpec(memory_space=pl.ANY),
            pl.BlockSpec(memory_space=pltpu.VMEM),
        ],
        scratch_shapes=[pltpu.VMEM((near, events, LANES), rows)] * chunks
        + [
            pltpu.VMEM((near, ahead, LANES), rows),
            pltpu.VMEM((far * lines, LANES), table),
            pltpu.VMEM((far - 1, lines, LANES), table),
            pltpu.VMEM((near - 1,) + data.shape, table),
            pltpu.VMEM((2, lines, LANES), table),
            pltpu.VMEM((lines, LANES), table),
            pltpu.VMEM((bins, LANES), table),
            pltpu.VMEM((pieces, near - 1, size, LANES), rows),
            dma((pieces, near - 1)),
            dma((near,)),
            dma((near,)),
            dma((far - 1,)),
            dma((far - 1,)),
            dma((near - 1,)),
            dma((near - 1,)),
            pltpu.VMEM((near * slot, LANES), rows),
            pltpu.VMEM((TILE, LANES), table),
            pltpu.VMEM((chunks, bins, LANES), rows),
            pltpu.VMEM(hops + (size, LANES), jnp.int16),
            pltpu.VMEM(hops + (size // LANES, LANES), table),
            pltpu.VMEM(hops + (size, LANES), jnp.int16),
            pltpu.VMEM(hops + (size // LANES, LANES), table),
            dma((chunks,)),
            dma((chunks, near)),
            dma((chunks, near)),
            dma(hops),
            dma(hops),
            dma(hops),
            dma(hops),
            dma((chunks, pieces)),
            dma((chunks, near, pieces)),
            dma((chunks, near, pieces)),
            dma((chunks, near, pieces)),
            dma((chunks, near, pieces)),
        ],
        compiler_params=pltpu.CompilerParams(
            collective_id=3, has_side_effects=True, vmem_limit_bytes=62 << 20
        ),
        name="chain",
    )(starts, local, data, weights, *firsts)


def tail_kernel(
    near, far, templates_ref, weighted_ref, out_ref, held, weighted, total, coded, own, got,
    hand, kept, merged, weighted_sem, sems, sends, recvs, hand_recvs,
):
    groups, _, chunks, _, _ = templates_ref.shape
    here = lax.axis_index("bins")
    z, me = here // near, lax.rem(here, near)
    piece = own.shape[0]
    count = groups * near * chunks
    step = 2 * LANES

    def peer(k):
        return lax.rem(z + k, far)

    barrier = pltpu.get_barrier_semaphore()
    for k in range(1, far):
        pl.semaphore_signal(
            barrier, inc=1, device_id={"bins": peer(k) * near + me}, device_id_type=MESH
        )

    def fetch(n):
        part = templates_ref.at[n // (near * chunks), lax.rem(n // chunks, near), lax.rem(n, chunks)]
        return pltpu.make_async_copy(
            part, held.at[:, pl.ds(pl.multiple_of(n * LANES, LANES), LANES)], sems.at[n]
        )

    take = pltpu.make_async_copy(weighted_ref, weighted, weighted_sem)
    take.start()

    @pl.loop(0, count)
    def _(n):
        fetch(n).start()

    pl.semaphore_wait(barrier, far - 1)
    take.wait()

    def rows_for(target):
        return pl.ds(pl.multiple_of(xor_of(me, target, near) * piece, 16), piece)

    def columns_of(n):
        return pl.ds(pl.multiple_of(n * step, step), step)

    def send(source, target, landed, j, n, to):
        return pltpu.make_async_remote_copy(
            src_ref=source,
            dst_ref=target.at[:, columns_of(n)],
            send_sem=sends.at[j, n],
            recv_sem=landed,
            device_id={"bins": to * near + me},
            device_id_type=MESH,
        )

    half = z // 2
    at_end = (z == 0) | (z == far - 1)
    within = 1 + half
    end = half * (far - 1)

    def to_inner(j, n):
        target = (far - 1 - within, far - 1 - z, within)[j]
        source = coded.at[rows_for(target), columns_of(n)]
        if j == 2:
            return send(source, got.at[half], recvs.at[half, n], j, n, within)
        return send(source, hand.at[j], hand_recvs.at[j, n], j, n, within)

    def from_inner(j, n):
        target = (far - 1 - z, far - 1 - end, end)[j]
        if j == 2:
            source = coded.at[rows_for(target), columns_of(n)]
        else:
            source = merged.at[j, :, columns_of(n)]
        return send(source, got.at[half], recvs.at[half, n], j, n, target)

    def merge(n):
        for j in range(2):
            to_inner(j, n).wait_recv()
            part = kept[j, :, columns_of(n)] + hand[j, :, columns_of(n)].astype(jnp.float32)
            merged[j, :, columns_of(n)] = part.astype(merged.dtype)
            from_inner(j, n).start()

    inner = jnp.logical_not(at_end)
    lag, late = 2, 6

    @pl.loop(0, count // 2)
    def _(n):
        fetch(2 * n).wait()
        fetch(2 * n + 1).wait()
        total[...] = jnp.dot(
            weighted[...], held[:, columns_of(n)], preferred_element_type=jnp.float32
        )
        coded[:, columns_of(n)] = total[...].astype(coded.dtype)
        own[:, columns_of(n)] = total[rows_for(z), :]

        @pl.when(at_end)
        def _():
            for j in range(2):
                to_inner(j, n).start()

        @pl.when(at_end & (n >= late))
        def _():
            to_inner(2, n - late).start()

        @pl.when(inner)
        def _():
            from_inner(2, n).start()
            kept[0, :, columns_of(n)] = total[rows_for(far - 1 - z), :]
            kept[1, :, columns_of(n)] = total[rows_for(far - 1 - end), :]

        @pl.when(inner & (n >= lag))
        def _():
            merge(n - lag)

    @pl.when(at_end)
    def _():
        @pl.loop(count // 2 - late, count // 2)
        def _(n):
            to_inner(2, n).start()

    @pl.when(inner)
    def _():
        @pl.loop(count // 2 - lag, count // 2)
        def _(n):
            merge(n)

    @pl.loop(0, count // 2)
    def _(n):
        for j in range(2):
            send(merged.at[0, :, columns_of(n)], got.at[j], recvs.at[j, n], 0, n, within).wait_recv()
        for side in range(2):
            place = 2 * n + side
            group = place // (near * chunks)
            d = lax.rem(place // chunks, near)
            start = ((group * near + xor_of(me, d, near)) * chunks + lax.rem(place, chunks)) * LANES
            part = pl.ds(pl.multiple_of(place * LANES, LANES), LANES)
            value = own[:, part]
            for j in range(2):
                value += got[j, :, part].astype(jnp.float32)
            out_ref[:, pl.ds(pl.multiple_of(start, LANES), LANES)] = value

    @pl.loop(0, count // 2)
    def _(n):
        for j in range(3):
            @pl.when(at_end)
            def _():
                to_inner(j, n).wait_send()

            @pl.when(inner)
            def _():
                from_inner(j, n).wait_send()


def tail(templates, weighted, near, far):
    groups, _, chunks, bins, _ = templates.shape
    piece = chunks * LANES // far
    columns = groups * near * chunks * LANES
    count = groups * near * chunks
    return pl.pallas_call(
        functools.partial(tail_kernel, near, far),
        out_shape=jax.ShapeDtypeStruct((piece, columns), jnp.float32),
        in_specs=[pl.BlockSpec(memory_space=pl.ANY)] * 2,
        out_specs=pl.BlockSpec(memory_space=pltpu.VMEM),
        scratch_shapes=[
            pltpu.VMEM((bins, columns), jnp.bfloat16),
            pltpu.VMEM((near * piece, bins), jnp.bfloat16),
            pltpu.VMEM((near * piece, 2 * LANES), jnp.float32),
            pltpu.VMEM((near * piece, columns), jnp.bfloat16),
            pltpu.VMEM((piece, columns), jnp.float32),
            pltpu.VMEM((2, piece, columns), jnp.bfloat16),
            pltpu.VMEM((2, piece, columns), jnp.bfloat16),
            pltpu.VMEM((2, piece, columns), jnp.float32),
            pltpu.VMEM((2, piece, columns), jnp.bfloat16),
            pltpu.SemaphoreType.DMA,
            pltpu.SemaphoreType.DMA((count,)),
            pltpu.SemaphoreType.DMA((3, count // 2)),
            pltpu.SemaphoreType.DMA((2, count // 2)),
            pltpu.SemaphoreType.DMA((2, count // 2)),
        ],
        compiler_params=pltpu.CompilerParams(
            collective_id=2, has_side_effects=True, vmem_limit_bytes=58 << 20
        ),
        name="tail",
    )(templates, weighted)


def body_by_parameters(event_bins, event_weights, nominal, background, observed):
    owners = lax.axis_size("bins")
    near = math.isqrt(owners)
    far = owners // near
    events = event_bins.shape[0]
    bins_dev = background.shape[0]
    width = event_weights.shape[1] // near
    chunks = width // LANES
    capacity = 3 * events // (2 * owners)
    slot = -(-capacity // 16) * 16 + 16
    ahead = min(-(-near * capacity // 16) * 16 + 16, events - 16)
    here = lax.axis_index("bins")
    z, me = here // near, lax.rem(here, near)
    around = [[(s, s // near * near + (s % near ^ d)) for s in range(owners)] for d in range(near)]

    def spread(value):
        return [value] + [shift(value, around[d]) for d in range(1, near)]

    firsts = []
    first_row = jnp.where(z < far // 2, events - ahead, 0)
    for d in range(near):
        corner = (first_row, (me ^ d) * width)
        firsts.append(lax.dynamic_slice(event_weights, corner, (ahead, LANES)))
    event_bins, firsts = lax.optimization_barrier((event_bins, firsts))
    for d in range(1, near):
        firsts[d] = shift(firsts[d], around[d])

    marks = jnp.arange(owners, dtype=jnp.int32) * bins_dev
    before = jnp.sum((event_bins[None, :] < marks[:, None]).astype(jnp.int32), axis=1)
    starts = jnp.minimum(before // 16, (events - slot) // 16)
    places = slots_of(starts, event_bins, nominal, slot, bins_dev)
    places = jnp.stack(spread(places))

    starts = places[:, 2 * owners, :owners].astype(jnp.int32).reshape(-1)
    places = places.transpose(1, 0, 2).reshape(2 * owners + 1, near * slot)
    data = jnp.concatenate([background, observed]).reshape(-1, LANES)
    templates, weighted = chain(
        starts, places, data, event_weights, firsts, near, far, chunks, slot, bins_dev
    )
    summed = tail(templates, weighted, near, far)
    return summed * (1.0 / (bins_dev * owners))


def splits_by_parameters(mesh, event_bins, event_weights, background):
    owners, groups = mesh.shape["bins"], mesh.shape["params"]
    near = math.isqrt(owners)
    events = event_bins.shape[0] // owners
    width = event_weights.shape[1] // groups // max(near, 1)
    bins_dev = background.shape[0] // owners
    return (
        groups == 2
        and near == 4
        and near * near == owners
        and near & (near - 1) == 0
        and width % LANES == 0
        and width % (16 * near) == 0
        and events % LANES == 0
        and events >= 2 * LANES
        and bins_dev % (8 * LANES) == 0
    )


def solution(mesh):
    in_specs = (P("bins"), P("bins", "params"), P("bins"), P("bins"), P("bins"))
    out_specs = P(("params", "bins"), None)

    def run(event_bins, event_weights, nominal, background, observed):
        fits = splits_by_parameters(mesh, event_bins, event_weights, background)
        chosen = body_by_parameters if fits else body
        mapped = jax.shard_map(
            chosen, mesh=mesh, in_specs=in_specs, out_specs=out_specs, check_vma=False
        )
        return mapped(event_bins, event_weights, nominal, background, observed)

    return run
```
